32 devices in a mesh: narrow: 4 (over z), wide: 8 (over y, x, core).
Axes of the slice: x: 2, y: 2, z: 4, core: 2. Of those that a mesh axis runs over, the one named last changes fastest.
Arguments:
- layer_input: bfloat16 [32, 512, 640], P(('narrow', 'wide')), may hold values from -6 to 6
- segments: int32 [32, 512], P(('narrow', 'wide')), may hold values from 0 to 7, never falling along the last dimension, each value on 1 to 192 neighbouring positions
- targets: int32 [32, 512], P(('narrow', 'wide')), may hold values from 0 to 24
- loss_mask: int32 [32, 512], P(('narrow', 'wide')), may hold values from 0 to 1
- readout: bfloat16 [640, 25], replicated, may hold values from -0.29882812 to 0.29882812
- attend_gain: bfloat16 [640], P('wide'), may hold values from 0.5 to 1.5
- attend_shift: bfloat16 [640], P('wide'), may hold values from -1.1953125 to 1.1953125
- heads_weight: bfloat16 [640, 1920], P('wide'), may hold values from -0.25 to 0.25
- query_bias: bfloat16 [640], P('wide'), may hold values from -1.1953125 to 1.1953125
- value_bias: bfloat16 [640], P('wide'), may hold values from -1.1953125 to 1.1953125
- output_weight: bfloat16 [640, 640], P('wide'), may hold values from -1.25 to 1.25
- output_bias: bfloat16 [640], P('wide'), may hold values from -1.1953125 to 1.1953125
- forward_gain: bfloat16 [640], P('wide'), may hold values from 0.5 to 1.5
- forward_shift: bfloat16 [640], P('wide'), may hold values from -1.1953125 to 1.1953125
- up_weight: bfloat16 [640, 5120], P('wide'), may hold values from -0.25 to 0.25
- up_bias: bfloat16 [5120], P('wide'), may hold values from -1.1953125 to 1.1953125
- down_weight: bfloat16 [5120, 640], P('wide'), may hold values from -0.125 to 0.125
- down_bias: bfloat16 [640], P('wide'), may hold values from -1.1953125 to 1.1953125
Outputs:
- layer_output: bfloat16 [32, 512, 640], P(('narrow', 'wide'))
- input_grad: float32 [32, 512, 640], P(('narrow', 'wide'))
- attend_gain_grad: float32 [640], P('wide')
- attend_shift_grad: float32 [640], P('wide')
- heads_weight_grad: float32 [640, 1920], P('wide')
- query_bias_grad: float32 [640], P('wide')
- value_bias_grad: float32 [640], P('wide')
- output_weight_grad: float32 [640, 640], P('wide')
- output_bias_grad: float32 [640], P('wide')
- forward_gain_grad: float32 [640], P('wide')
- forward_shift_grad: float32 [640], P('wide')
- up_weight_grad: float32 [640, 5120], P('wide')
- up_bias_grad: float32 [5120], P('wide')
- down_weight_grad: float32 [5120, 640], P('wide')
- down_bias_grad: float32 [640], P('wide')
- loss_sum: float32 [], replicated
- token_count: int32 [], replicated
The draws below stay inside these ranges and needn't reach their ends.
All inputs are finite; a program needn't handle non-finite values.
Results may differ from the reference program's by a relative error of at most 0.013.
Values may be sent and summed in bfloat16 or wider, within the bound.
No kernel may reach another device: no remote copies, remote signals or barrier semaphores. Data moves between devices by JAX's collectives and lax.ppermute only.
A program may use at most 192 MiB of HBM per device.

```python
import math
import jax
import jax.numpy as jnp
import numpy as np
from jax import lax

D = 640
HEADS = 20
HEAD_DIM = 32
FF = 5120
VOCAB = 25
LENGTH = 512
SEQS = 32
NSEG = 8
SEG_MOST = 192


def draw_loss_mask(key, part):
    row_index = lax.broadcasted_iota(jnp.int32, (SEQS, LENGTH), 0)
    threshold = 100 + 300 * row_index // SEQS
    random_draw = jax.random.randint(key, (SEQS, LENGTH), 0, 1000)
    return (random_draw < threshold).astype(jnp.int32)


def set_ends(values, own_key, low, largest):
    extent = values.shape
    index_at = [jax.random.randint(jax.random.fold_in(own_key, axis), (), 0, extent[axis]) for axis in range(len(extent))]
    values = values.at[tuple(index_at)].set(low)
    longest = extent.index(max(extent))
    index_at[longest] = (index_at[longest] + 1) % extent[longest]
    return values.at[tuple(index_at)].set(largest)


def shard_levels(key, shape, cuts, smallest, top_value):
    def one(axis_at, blocks):
        steps = jax.random.uniform(jax.random.fold_in(jax.random.fold_in(key, 6), axis_at), (blocks,), jnp.float32, smallest / len(cuts), top_value / len(cuts))
        return jnp.repeat(jnp.exp(steps), shape[axis_at] // blocks).reshape((-1,) + (1,) * (len(shape) - axis_at - 1))

    factor_of = one(*cuts[0])
    for cut in cuts[1:]:
        factor_of = factor_of * one(*cut)
    return factor_of


def split_up(amount, total, most, skew):
    portions = [(1 << 20) // math.isqrt(standing ** skew) + 1 for standing in range(2, amount + 1)]
    surplus, counts = total - most - (amount - 1), [1] * (amount - 1)
    while surplus > 0:
        movable = [i for i in range(amount - 1) if counts[i] < most]
        mass, budget = sum([portions[i] for i in movable]), surplus
        for i in movable:
            addition = min(most - counts[i], max(1, budget * portions[i] // mass), surplus)
            counts[i] = counts[i] + addition
            surplus = surplus - addition
    return np.array([most] + counts)


def ragged(own_key, amount, total, bound, slope):
    if amount == 2:
        one = jax.random.randint(own_key, (), max(1, total - bound), min(bound, total - 1) + 1)
        return jnp.stack([one, total - one])
    tallies = jnp.asarray(split_up(amount, total, bound, slope), jnp.int32)
    couples = (amount - 1) // 2
    giver, taker = tallies[1:1 + 2 * couples:2], tallies[2:2 + 2 * couples:2]
    slack = jnp.minimum(giver - 1, bound - taker)
    passed = jax.random.randint(jax.random.fold_in(own_key, 1), (couples,), 0, 1 << 20) % (slack + 1)
    tallies = tallies.at[1:1 + 2 * couples:2].set(giver - passed).at[2:2 + 2 * couples:2].set(taker + passed)
    return tallies[jax.random.permutation(jax.random.fold_in(own_key, 2), amount)]


def gaussian(rng, extent, scale, most, split=(), dtype=jnp.bfloat16):
    entries = scale * jax.random.normal(rng, extent, jnp.float32)
    if split:
        entries = entries * shard_levels(rng, extent, split, -0.22, 0.18)
    return jnp.clip(entries, -most, most).astype(dtype)


def setup_inputs(seed: int = 0) -> dict:
    seeds = jax.random.split(jax.random.key(seed), 19)
    return {
        "layer_input": gaussian(seeds[0], (SEQS, LENGTH, D), 1.0, 6.0, ((0, 32),)),
        "segments": jax.vmap(lambda own: jnp.searchsorted(jnp.cumsum(ragged(own, NSEG, LENGTH, SEG_MOST, 2)), jnp.arange(LENGTH), side="right"))(jax.random.split(seeds[1], SEQS)).reshape((SEQS, LENGTH)).astype(jnp.int32),
        "targets": set_ends(jax.random.randint(seeds[2], (SEQS, LENGTH), 0, VOCAB), jax.random.fold_in(seeds[2], 1), 0, VOCAB - 1).astype(jnp.int32),
        "loss_mask": draw_loss_mask(jax.random.fold_in(seeds[18], 71), 0),
        "readout": gaussian(seeds[4], (D, VOCAB), 0.05, 0.29882812),
        "attend_gain": jnp.clip(1.0 + 0.1 * jax.random.normal(seeds[5], (D,), jnp.float32), 0.5, 1.5).astype(jnp.bfloat16),
        "attend_shift": gaussian(seeds[6], (D,), 0.2, 1.1953125, ((0, 8),)),
        "heads_weight": gaussian(seeds[7], (D, 3 * D), D ** -0.5, 0.25, ((0, 8),)),
        "query_bias": gaussian(seeds[8], (D,), 0.2, 1.1953125, ((0, 8),)),
        "value_bias": gaussian(seeds[9], (D,), 0.2, 1.1953125, ((0, 8),)),
        "output_weight": gaussian(seeds[10], (D, D), (D // 32) ** -0.5, 1.25, ((0, 8),)),
        "output_bias": gaussian(seeds[11], (D,), 0.2, 1.1953125, ((0, 8),)),
        "forward_gain": jnp.clip(1.0 + 0.1 * jax.random.normal(seeds[12], (D,), jnp.float32), 0.5, 1.5).astype(jnp.bfloat16),
        "forward_shift": gaussian(seeds[13], (D,), 0.2, 1.1953125, ((0, 8),)),
        "up_weight": gaussian(seeds[14], (D, FF), D ** -0.5, 0.25, ((0, 8),)),
        "up_bias": gaussian(seeds[15], (FF,), 0.2, 1.1953125, ((0, 8),)),
        "down_weight": gaussian(seeds[16], (FF, D), (FF // 2) ** -0.5, 0.125, ((0, 8),)),
        "down_bias": gaussian(seeds[17], (D,), 0.2, 1.1953125, ((0, 8),)),
    }


@jax.custom_vjp
def low(v):
    return lax.optimization_barrier(v.astype(jnp.bfloat16)).astype(jnp.float32)

@jax.custom_vjp
def low_back(v):
    return v

def low_keep(v):
    return (low(v), None)

def low_pass(kept, grad):
    return (grad,)

def back_keep(v):
    return (v, None)

def back_low(kept, grad):
    return (low(grad),)
low.defvjp(low_keep, low_pass)
low_back.defvjp(back_keep, back_low)

def project(left, right):
    return jnp.einsum('...i,ij->...j', left, right, precision=lax.Precision.HIGHEST)

def normalize(values, gain, shift):
    average = lax.optimization_barrier(jnp.mean(values, axis=-1, keepdims=True))
    centred = values - average
    spread = lax.optimization_barrier(jnp.mean(centred * centred, axis=-1, keepdims=True))
    return centred * lax.rsqrt(spread + 1e-05) * gain + shift

def layer_loss(params, inputs, segment, target, weight_mask, readout_table):
    attend_gain, attend_shift, heads_weight, query_bias, value_bias, output_weight, output_bias, forward_gain, forward_shift, up_weight, up_bias, down_weight, down_bias = params
    batch = inputs.shape[0]
    length = inputs.shape[1]
    width = inputs.shape[2]
    first_normed = low(normalize(inputs, attend_gain, attend_shift))
    bias_row = jnp.concatenate([query_bias, jnp.zeros_like(query_bias), value_bias])
    joined = low(low_back(project(first_normed, heads_weight) + bias_row))
    split_heads = joined.reshape(batch, length, 3, HEADS, HEAD_DIM)
    queryset = split_heads[:, :, 0]
    keyset = split_heads[:, :, 1]
    valueset = split_heads[:, :, 2]
    scores = jnp.einsum('bqhd,bkhd->bhqk', queryset, keyset, precision=lax.Precision.HIGHEST) * (1.0 / math.sqrt(HEAD_DIM))
    allowed = (segment[:, :, None] == segment[:, None, :])[:, None]
    scores = low_back(jnp.where(allowed, scores, -1e+30))
    probs = low(jax.nn.softmax(scores, axis=-1))
    attended = jnp.einsum('bhqk,bkhd->bqhd', probs, valueset, precision=lax.Precision.HIGHEST).reshape(batch, length, width)
    attended = low(low_back(attended))
    middle = inputs + low_back(project(attended, output_weight) + output_bias)
    second_normed = low(normalize(middle, forward_gain, forward_shift))
    upward = low_back(project(second_normed, up_weight) + up_bias)
    activated = low(jax.nn.gelu(upward, approximate=False))
    result = low(middle + low_back(project(activated, down_weight) + down_bias))
    logits = low_back(project(result, readout_table))
    log_total = jax.nn.logsumexp(logits, axis=-1)
    onehot = jnp.arange(VOCAB)[None, None, :] == target[:, :, None]
    picked = lax.optimization_barrier(jnp.sum(jnp.where(onehot, logits, 0.0), axis=-1))
    return (result, jnp.sum((log_total - picked) * weight_mask))

def reference(layer_input, segments, targets, loss_mask, readout, attend_gain, attend_shift, heads_weight, query_bias, value_bias, output_weight, output_bias, forward_gain, forward_shift, up_weight, up_bias, down_weight, down_bias):
    params = tuple((item.astype(jnp.float32) for item in (attend_gain, attend_shift, heads_weight, query_bias, value_bias, output_weight, output_bias, forward_gain, forward_shift, up_weight, up_bias, down_weight, down_bias)))
    readout_table = readout.astype(jnp.float32)
    group = math.gcd(SEQS, 4)
    count_groups = SEQS // group
    inputs = layer_input.astype(jnp.float32).reshape(count_groups, group, LENGTH, D)
    segment_groups = segments.reshape(count_groups, group, LENGTH)
    target_groups = targets.reshape(count_groups, group, LENGTH)
    mask_groups = loss_mask.astype(jnp.float32).reshape(count_groups, group, LENGTH)

    def step_group(carry, pieces):
        grads_total, loss_total = carry
        inputs_block, segment_block, target_block, mask_block = pieces

        def closed(params_in, inputs_in):
            return layer_loss(params_in, inputs_in, segment_block, target_block, mask_block, readout_table)
        (result, loss), puller = jax.vjp(closed, params, inputs_block)
        param_grads, input_grads = puller((jnp.zeros_like(result), jnp.ones_like(loss)))
        grads_total = jax.tree.map(jnp.add, grads_total, param_grads)
        return ((grads_total, loss_total + loss), (result.astype(jnp.bfloat16), input_grads))
    start = (jax.tree.map(jnp.zeros_like, params), jnp.zeros((), jnp.float32))
    (grads_total, loss_total), (outputs, input_grads) = lax.scan(step_group, start, (inputs, segment_groups, target_groups, mask_groups))
    layer_output = outputs.reshape(SEQS, LENGTH, D)
    input_grad = input_grads.reshape(SEQS, LENGTH, D)
    token_count = jnp.sum(loss_mask).astype(jnp.int32)
    return (layer_output, input_grad, grads_total[0], grads_total[1], grads_total[2], grads_total[3], grads_total[4], grads_total[5], grads_total[6], grads_total[7], grads_total[8], grads_total[9], grads_total[10], grads_total[11], grads_total[12], loss_total, token_count)
```

```python
import math

import jax
import jax.numpy as jnp
from jax import lax
from jax.sharding import PartitionSpec as P

HEADS = 20
HEAD_DIM = 32
LOSS_LANES = 128


def normalize(values, gain, shift):
    average = jnp.mean(values, axis=-1, keepdims=True)
    centred = values - average
    spread = jnp.mean(centred * centred, axis=-1, keepdims=True)
    return centred * lax.rsqrt(spread + 1e-05) * gain + shift


def exact_gelu(values):
    return jax.nn.gelu(values, approximate=False)


def swap(values, bit):
    return lax.ppermute(values, "wide", [(i, i ^ bit) for i in range(lax.axis_size("wide"))])


def same_core_groups():
    chips = lax.axis_size("wide") // 2
    return [[2 * chip + core for chip in range(chips)] for core in range(2)]


def spread_chips(shard):
    if lax.axis_size("wide") != 8:
        return lax.all_gather(shard, "wide", axis=0, axis_index_groups=same_core_groups())
    chip = lax.axis_index("wide") // 2
    half = shard.shape[0] // 2
    along_x = swap(shard, 2)
    along_y = swap(shard, 4)
    across = jnp.concatenate([swap(along_y[:half], 2), swap(along_x[half:], 4)])
    whole = jnp.zeros((4,) + shard.shape, shard.dtype)
    for offset, part in enumerate((shard, along_x, along_y, across)):
        whole = lax.dynamic_update_index_in_dim(whole, part, chip ^ offset, 0)
    return whole


def add_low(left, right):
    return (left.astype(jnp.float32) + right.astype(jnp.float32)).astype(jnp.bfloat16)


def collect_chips(parts):
    if lax.axis_size("wide") != 8:
        return lax.psum_scatter(
            parts, "wide", scatter_dimension=0, axis_index_groups=same_core_groups()
        )
    chip = lax.axis_index("wide") // 2
    half = parts.shape[1] // 2

    def pick(offset, low, high):
        return lax.dynamic_index_in_dim(parts, chip ^ offset, 0, keepdims=False)[low:high]

    size = parts.shape[1]
    from_x = swap(jnp.stack([pick(1, 0, half), pick(3, 0, half)]), 2)
    from_y = swap(jnp.stack([pick(2, half, size), pick(3, half, size)]), 4)
    upper_far = add_low(pick(2, 0, half), from_x[1])
    lower_far = add_low(pick(1, half, size), from_y[1])
    upper_got = swap(upper_far, 4)
    lower_got = swap(lower_far, 2)
    upper = add_low(add_low(pick(0, 0, half), from_x[0]), upper_got)
    lower = add_low(add_low(pick(0, half, size), from_y[0]), lower_got)
    return jnp.concatenate([upper, lower])


def sum_narrow(shard):
    if lax.axis_size("narrow") != 4:
        return lax.psum(shard, "narrow")
    place = lax.axis_index("narrow")
    inner = (place == 1) | (place == 2)
    half = add_low(shard, lax.ppermute(shard, "narrow", [(0, 1), (3, 2)]))
    total = add_low(half, lax.ppermute(half, "narrow", [(1, 2), (2, 1)]))
    outer = lax.ppermute(total, "narrow", [(1, 0), (2, 3)])
    return jnp.where(inner, total, outer)


def local(
    layer_input,
    segments,
    targets,
    loss_mask,
    readout,
    attend_gain,
    attend_shift,
    heads_weight,
    query_bias,
    value_bias,
    output_weight,
    output_bias,
    forward_gain,
    forward_shift,
    up_weight,
    up_bias,
    down_weight,
    down_bias,
):
    length = layer_input.shape[1]
    width = layer_input.shape[2]
    wide = lax.axis_size("wide")
    chips = wide // 2
    core = lax.axis_index("wide") % 2
    rows = heads_weight.shape[0]
    hidden = up_bias.shape[0]
    half = chips * hidden
    scale = 1.0 / math.sqrt(HEAD_DIM)
    inputs = layer_input[0].astype(jnp.float32)
    segment_row = segments[0]

    def by_core(mine, other, axis):
        return jnp.where(
            core == 0, jnp.stack([mine, other], axis), jnp.stack([other, mine], axis)
        )

    def mine_of(values, axis, flip=0):
        return lax.dynamic_index_in_dim(values, core ^ flip, axis, keepdims=False)

    attend_slab = jnp.concatenate([heads_weight, output_weight], axis=1)
    attend_mine = spread_chips(attend_slab)
    small = lax.all_gather(
        jnp.concatenate(
            [
                attend_gain,
                attend_shift,
                query_bias,
                value_bias,
                output_bias,
                forward_gain,
                forward_shift,
                down_bias,
                up_bias,
            ]
        ),
        "wide",
        axis=0,
    ).astype(jnp.float32)
    vectors = small[:, : 8 * rows].reshape(wide, 8, rows).transpose(1, 0, 2).reshape(8, width)
    up_bias_half = mine_of(small[:, 8 * rows :].reshape(chips, 2, hidden), 1).reshape(half)
    up_view = up_weight.reshape(rows, chips, 2, hidden)
    up_pair = by_core(mine_of(up_view, 2), swap(mine_of(up_view, 2, 1), 1), 0)
    up_half = spread_chips(up_pair.reshape(2 * rows, half)).reshape(width, half)
    down_half = spread_chips(down_weight).reshape(half, width)
    attend_full = by_core(attend_mine, swap(attend_mine, 1), 1).reshape(width, 4 * width)
    heads_full = attend_full[:, : 3 * width]
    output_full = attend_full[:, 3 * width :]

    first_normed, first_pull = jax.vjp(normalize, inputs, vectors[0], vectors[1])
    first_low = first_normed.astype(jnp.bfloat16)
    bias_row = jnp.concatenate([vectors[2], jnp.zeros_like(vectors[2]), vectors[3]])
    joined = (
        jnp.dot(first_low, heads_full, preferred_element_type=jnp.float32) + bias_row
    ).astype(jnp.bfloat16)
    split_heads = joined.reshape(length, 3, HEADS, HEAD_DIM)
    queryset = split_heads[:, 0]
    keyset = split_heads[:, 1]
    valueset = split_heads[:, 2]

    def masked_scores():
        scores = (
            jnp.einsum("qhd,khd->hqk", queryset, keyset, preferred_element_type=jnp.float32)
            * scale
        )
        allowed = (segment_row[:, None] == segment_row[None, :])[None]
        return jnp.where(allowed, scores, -1e30)

    scores = masked_scores()
    highest = jnp.max(scores, axis=-1, keepdims=True)
    shifted = jnp.exp(scores - highest)
    totals = jnp.sum(shifted, axis=-1, keepdims=True)
    probs_low = (shifted / totals).astype(jnp.bfloat16)
    attended = (
        jnp.einsum("hqk,khd->qhd", probs_low, valueset, preferred_element_type=jnp.float32)
        .astype(jnp.bfloat16)
        .reshape(length, width)
    )
    lse = highest + jnp.log(totals)
    middle = (
        inputs + jnp.dot(attended, output_full, preferred_element_type=jnp.float32) + vectors[4]
    )

    second_normed, second_pull = jax.vjp(normalize, middle, vectors[5], vectors[6])
    second_low = second_normed.astype(jnp.bfloat16)
    second_both = jnp.concatenate([second_low, swap(second_low, 1)])
    upward = jnp.dot(second_both, up_half, preferred_element_type=jnp.float32) + up_bias_half
    activated, gelu_pull = jax.vjp(exact_gelu, upward)
    activated_low = activated.astype(jnp.bfloat16)
    outward = jnp.dot(activated_low, down_half, preferred_element_type=jnp.float32)
    outward_got = swap(outward[length:].astype(jnp.bfloat16), 1)
    result = middle + (outward[:length] + outward_got.astype(jnp.float32)) + vectors[7]
    result_low = result.astype(jnp.bfloat16)

    logits = jnp.dot(result_low, readout, preferred_element_type=jnp.float32)
    highest_logit = jnp.max(logits, axis=-1, keepdims=True)
    shifted_logits = jnp.exp(logits - highest_logit)
    logit_totals = jnp.sum(shifted_logits, axis=-1, keepdims=True)
    log_total = highest_logit[:, 0] + jnp.log(logit_totals[:, 0])
    onehot = lax.broadcasted_iota(jnp.int32, logits.shape, 1) == targets[0][:, None]
    picked = jnp.sum(jnp.where(onehot, logits, 0.0), axis=-1)
    weights_row = loss_mask[0].astype(jnp.float32)
    loss_lanes = jnp.sum(((log_total - picked) * weights_row).reshape(-1, LOSS_LANES), axis=0)
    count_lanes = jnp.sum(weights_row.reshape(-1, LOSS_LANES), axis=0)
    grad_logits = (
        weights_row[:, None] * (shifted_logits / logit_totals - onehot.astype(jnp.float32))
    ).astype(jnp.bfloat16)
    grad_result = jnp.einsum("lv,dv->ld", grad_logits, readout, preferred_element_type=jnp.float32)

    grad_down = grad_result.astype(jnp.bfloat16)
    grad_down_both = jnp.concatenate([grad_down, swap(grad_down, 1)])
    down_weight_part = jnp.einsum(
        "lf,ld->fd", activated_low, grad_down_both, preferred_element_type=jnp.float32
    ).astype(jnp.bfloat16)
    down_weight_sum = collect_chips(down_weight_part.reshape(chips, hidden, width))
    down_weight_sum = sum_narrow(down_weight_sum)
    down_bias_part = jnp.sum(grad_down, axis=0, dtype=jnp.float32)
    grad_activated = jnp.einsum(
        "ld,fd->lf", grad_down_both, down_half, preferred_element_type=jnp.float32
    )
    grad_up = gelu_pull(grad_activated)[0].astype(jnp.bfloat16)
    up_weight_part = jnp.einsum(
        "ld,lf->df", second_both, grad_up, preferred_element_type=jnp.float32
    ).astype(jnp.bfloat16)
    up_weight_sum = collect_chips(up_weight_part.reshape(chips, 2 * rows, half))
    up_weight_sum = up_weight_sum.reshape(2, rows, half)
    up_weight_sum = by_core(
        mine_of(up_weight_sum, 0).reshape(rows, chips, hidden),
        swap(mine_of(up_weight_sum, 0, 1), 1).reshape(rows, chips, hidden),
        2,
    ).reshape(rows, 2 * half)
    up_weight_sum = sum_narrow(up_weight_sum)
    up_bias_part = jnp.sum(grad_up, axis=0, dtype=jnp.float32)
    inward = jnp.einsum("lf,df->ld", grad_up, up_half, preferred_element_type=jnp.float32)
    inward_got = swap(inward[length:].astype(jnp.bfloat16), 1)
    grad_second = inward[:length] + inward_got.astype(jnp.float32)
    middle_part, forward_gain_part, forward_shift_part = second_pull(grad_second)
    grad_middle = grad_result + middle_part

    grad_branch = grad_middle.astype(jnp.bfloat16)
    output_weight_part = jnp.einsum(
        "ld,le->de", attended, grad_branch, preferred_element_type=jnp.float32
    ).astype(jnp.bfloat16)
    output_bias_part = jnp.sum(grad_branch, axis=0, dtype=jnp.float32)
    grad_attended = (
        jnp.einsum("le,de->ld", grad_branch, output_full, preferred_element_type=jnp.float32)
        .astype(jnp.bfloat16)
        .reshape(length, HEADS, HEAD_DIM)
    )
    probs = jnp.exp(masked_scores() - lse)
    grad_value = jnp.einsum(
        "hqk,qhd->khd",
        probs.astype(jnp.bfloat16),
        grad_attended,
        preferred_element_type=jnp.float32,
    )
    grad_probs = jnp.einsum(
        "qhd,khd->hqk", grad_attended, valueset, preferred_element_type=jnp.float32
    )
    inner = jnp.sum(probs * grad_probs, axis=-1, keepdims=True)
    grad_scores = (probs * (grad_probs - inner)).astype(jnp.bfloat16)
    grad_query = (
        jnp.einsum("hqk,khd->qhd", grad_scores, keyset, preferred_element_type=jnp.float32)
        * scale
    )
    grad_key = (
        jnp.einsum("hqk,qhd->khd", grad_scores, queryset, preferred_element_type=jnp.float32)
        * scale
    )
    grad_joined = jnp.concatenate(
        [
            grad_query.reshape(length, width),
            grad_key.reshape(length, width),
            grad_value.reshape(length, width),
        ],
        axis=1,
    ).astype(jnp.bfloat16)
    heads_weight_part = jnp.einsum(
        "ld,le->de", first_low, grad_joined, preferred_element_type=jnp.float32
    ).astype(jnp.bfloat16)
    query_bias_part = jnp.sum(grad_joined[:, :width], axis=0, dtype=jnp.float32)
    value_bias_part = jnp.sum(grad_joined[:, 2 * width :], axis=0, dtype=jnp.float32)
    grad_first = jnp.einsum(
        "le,de->ld", grad_joined, heads_full, preferred_element_type=jnp.float32
    )
    input_part, attend_gain_part, attend_shift_part = first_pull(grad_first)
    input_grad = grad_middle + input_part

    short = jnp.stack(
        [
            attend_gain_part,
            attend_shift_part,
            query_bias_part,
            value_bias_part,
            output_bias_part,
            forward_gain_part,
            forward_shift_part,
            down_bias_part,
        ]
    )
    short = short.reshape(8, wide, rows).transpose(1, 0, 2).reshape(wide, 8 * rows)
    blank = jnp.zeros((chips, hidden), jnp.float32)
    up_bias_rows = by_core(up_bias_part.reshape(chips, hidden), blank, 1).reshape(wide, hidden)
    lanes = jnp.broadcast_to(
        jnp.concatenate([loss_lanes, count_lanes])[None], (wide, 2 * LOSS_LANES)
    )
    row = jnp.concatenate([short, up_bias_rows, lanes], axis=1).astype(jnp.bfloat16)
    used = row.shape[1]
    row = jnp.pad(row[:, None], ((0, 0), (0, 0), (0, 4 * width - used)))
    slab = jnp.concatenate(
        [
            jnp.concatenate(
                [
                    heads_weight_part.reshape(wide, rows, 3 * width),
                    output_weight_part.reshape(wide, rows, width),
                ],
                axis=2,
            ),
            row,
        ],
        axis=1,
    )
    slab = slab.reshape(chips, 2, rows + 1, 4 * width)
    slab = add_low(mine_of(slab, 1), swap(mine_of(slab, 1, 1), 1))
    slab = sum_narrow(collect_chips(slab)).astype(jnp.float32)
    last = slab[rows]
    vectors_sum = last[: 8 * rows].reshape(8, rows)
    lanes_sum = last[8 * rows + hidden : used].reshape(2, LOSS_LANES)
    return (
        result_low[None],
        input_grad[None],
        vectors_sum[0],
        vectors_sum[1],
        slab[:rows, : 3 * width],
        vectors_sum[2],
        vectors_sum[3],
        slab[:rows, 3 * width :],
        vectors_sum[4],
        vectors_sum[5],
        vectors_sum[6],
        up_weight_sum.astype(jnp.float32),
        last[8 * rows : 8 * rows + hidden],
        down_weight_sum.astype(jnp.float32),
        vectors_sum[7],
        jnp.sum(lanes_sum[0]),
        jnp.round(jnp.sum(lanes_sum[1])).astype(jnp.int32),
    )


def solution(mesh):
    in_specs = (
        P(("narrow", "wide"), None, None),
        P(("narrow", "wide"), None),
        P(("narrow", "wide"), None),
        P(("narrow", "wide"), None),
        P(),
        P("wide"),
        P("wide"),
        P("wide", None),
        P("wide"),
        P("wide"),
        P("wide", None),
        P("wide"),
        P("wide"),
        P("wide"),
        P("wide", None),
        P("wide"),
        P("wide", None),
        P("wide"),
    )
    out_specs = (
        P(("narrow", "wide"), None, None),
        P(("narrow", "wide"), None, None),
        P("wide"),
        P("wide"),
        P("wide", None),
        P("wide"),
        P("wide"),
        P("wide", None),
        P("wide"),
        P("wide"),
        P("wide"),
        P("wide", None),
        P("wide"),
        P("wide", None),
        P("wide"),
        P(),
        P(),
    )
    return jax.shard_map(local, mesh=mesh, in_specs=in_specs, out_specs=out_specs, check_vma=False)
```

```python
import functools
import math

import jax
import jax.numpy as jnp
from jax import lax
from jax.experimental import pallas as pl
from jax.experimental.pallas import tpu as pltpu
from jax.sharding import PartitionSpec as P

HEADS = 20
HEAD_DIM = 32
LANES = 128
SUBLANES = 8
SEGMENTS = 8
REACH = 192
CHUNK = 256
ROWS = 128
SCALE = 1.0 / math.sqrt(HEAD_DIM)
SCALE2 = math.log2(math.e) * SCALE
F32 = jnp.float32
BF16 = jnp.bfloat16
VECTORS = 8
ATTEND_GAIN, ATTEND_SHIFT, QUERY_BIAS, VALUE_BIAS = 0, 1, 2, 3
OUTPUT_BIAS, FORWARD_GAIN, FORWARD_SHIFT, DOWN_BIAS = 4, 5, 6, 7


def nn(left, right):
    return lax.dot_general(left, right, (((1,), (0,)), ((), ())), preferred_element_type=F32)


def nt(left, right):
    return lax.dot_general(left, right, (((1,), (1,)), ((), ())), preferred_element_type=F32)


def tn(left, right):
    return lax.dot_general(left, right, (((0,), (0,)), ((), ())), preferred_element_type=F32)


def call(kernel, outs, args, positions=None, grid=None, in_specs=None, out_specs=None, scratch=(),
         mib=16):
    whole = pl.BlockSpec(memory_space=pltpu.VMEM)
    in_specs = in_specs or [whole] * len(args)
    out_specs = out_specs or [whole] * len(outs)
    shapes = [jax.ShapeDtypeStruct(shape, dtype) for shape, dtype in outs]
    extra = [] if positions is None else [positions]
    return pl.pallas_call(
        kernel,
        out_shape=shapes,
        grid_spec=pltpu.PrefetchScalarGridSpec(
            num_scalar_prefetch=len(extra),
            grid=grid or (),
            in_specs=in_specs,
            out_specs=out_specs,
            scratch_shapes=list(scratch),
        ),
        compiler_params=pltpu.CompilerParams(vmem_limit_bytes=mib * 1024 * 1024),
        cost_estimate=pl.CostEstimate(flops=1, bytes_accessed=1, transcendentals=0),
    )(*extra, *args)


def unit(values):
    centred = values - jnp.mean(values, axis=-1, keepdims=True)
    spread = jnp.mean(centred * centred, axis=-1, keepdims=True)
    inverse = lax.rsqrt(spread + 1e-05)
    return centred * inverse, inverse


def unit_back(grad, normal, inverse, gain):
    scaled = grad * gain
    mean = jnp.mean(scaled, axis=-1, keepdims=True)
    along = jnp.mean(scaled * normal, axis=-1, keepdims=True)
    return inverse * (scaled - mean - normal * along)


def spans(length):
    chunk = min(CHUNK, length)
    return [
        (at, at + chunk, max(0, at - REACH), min(length, at + chunk + REACH))
        for at in range(0, length, chunk)
    ]


def split3(values):
    first = values.astype(BF16).astype(F32)
    rest = values - first
    second = rest.astype(BF16).astype(F32)
    return [first, second, rest - second]


def key_marks(segment_column):
    lane = lax.broadcasted_iota(jnp.int32, (segment_column.shape[0], LANES), 1)
    ones = (lane >= SEGMENTS) & (lane < SEGMENTS + 3)
    return jnp.where((lane == segment_column) | ones, 1.0, 0.0).astype(BF16)


def query_marks(segment_row):
    row = lax.broadcasted_iota(jnp.int32, (SEGMENTS, segment_row.shape[1]), 0)
    return jnp.where(row == segment_row, 0.0, -1e30)


def place(rows, head, marks):
    count = rows.shape[1]
    parts = [rows, marks, jnp.zeros((LANES - marks.shape[0], count), BF16)]
    if head < LANES // HEAD_DIM - 1:
        parts.insert(1, jnp.zeros((LANES - HEAD_DIM * (head + 1), count), BF16))
    if head:
        parts.insert(0, jnp.zeros((HEAD_DIM * head, count), BF16))
    return jnp.concatenate(parts, axis=0)


def attend_kernel(column_ref, row_ref, q_ref, k_ref, v_ref, out_ref, across_ref, lse_ref, marks_ref):
    @pl.when(pl.program_id(0) == 0)
    def _():
        marks_ref[...] = key_marks(column_ref[...])

    length = q_ref.shape[0]
    heads = LANES // HEAD_DIM
    queries = q_ref[...].T
    values = v_ref[...].T
    keys = jnp.concatenate([k_ref[...], marks_ref[...]], axis=1)
    blank = jnp.zeros((SUBLANES, length), F32)
    marks = jnp.concatenate([query_marks(row_ref[...]), blank], axis=0).astype(BF16)
    ones = jnp.ones((SUBLANES, length), BF16)
    bodies = [(head, span) for head in range(heads) for span in spans(length)]

    def rows(head):
        return slice(HEAD_DIM * head, HEAD_DIM * (head + 1))

    summed = [jnp.concatenate([values[rows(head)], ones], axis=0) for head in range(heads)]

    def score(head, span):
        begin, end, low, high = span
        return nn(keys[low:high], place(queries[rows(head), begin:end], head, marks[:, begin:end]))

    def finish(head, span, top, probs):
        begin, end, low, high = span
        out = nn(summed[head][:, low:high], probs)
        total = out[HEAD_DIM : HEAD_DIM + 1]
        across_ref[rows(head), begin:end] = out[:HEAD_DIM] * (1.0 / total)
        lse_ref[head : head + 1, begin:end] = (top + jnp.log2(total)) * (1.0 / SCALE2)

    scores = [score(*body) for body in bodies[:2]]
    waiting = None
    for at, body in enumerate(bodies):
        current = scores.pop(0)
        if at + 2 < len(bodies):
            scores.append(score(*bodies[at + 2]))
        top = jnp.max(current, axis=0, keepdims=True) * SCALE2
        probs = jnp.exp2(current * SCALE2 - top).astype(BF16)
        if waiting is not None:
            finish(*waiting)
        waiting = (*body, top, probs)
    finish(*waiting)
    lse_ref[heads:, :] = jnp.zeros((SUBLANES - heads, length), F32)
    out_ref[...] = across_ref[...].T.astype(BF16)


def attend_back_kernel(
    column_ref, row_ref, q_ref, k_ref, v_ref, grad_ref, across_ref, lse_ref,
    gq_ref, gk_ref, gv_ref, marks_ref, turned_ref,
):
    @pl.when(pl.program_id(0) == 0)
    def _():
        marks_ref[...] = key_marks(column_ref[...])

    length = q_ref.shape[0]
    grad = grad_ref[...]
    queries = q_ref[...].T
    turned_keys = k_ref[...].T
    grads = grad.T
    keys = jnp.concatenate([k_ref[...], marks_ref[...]], axis=1)
    values = jnp.concatenate([v_ref[...], marks_ref[...]], axis=1)
    low_marks = query_marks(row_ref[...])
    blank = jnp.zeros((SUBLANES, length), F32)
    lane = lax.broadcasted_iota(jnp.int32, (1, LANES), 1) // HEAD_DIM
    heads = []
    for head in range(LANES // HEAD_DIM):
        rows = slice(HEAD_DIM * head, HEAD_DIM * (head + 1))
        inner = jnp.sum(grads[rows].astype(F32) * across_ref[rows, :], axis=0, keepdims=True)
        lse = lse_ref[head : head + 1, :]
        score_marks = jnp.concatenate([low_marks, *split3(-lse), blank[:5]], axis=0)
        inner_marks = jnp.concatenate([blank, *split3(-inner), blank[:5]], axis=0)
        zero = jnp.zeros_like(grad)
        heads.append(
            (
                rows,
                score_marks.astype(BF16),
                inner_marks.astype(BF16),
                jnp.where(lane == head, q_ref[...], zero),
                jnp.where(lane == head, grad, zero),
            )
        )
    bodies = [
        (head, at, span) for head in range(len(heads)) for at, span in enumerate(spans(length))
    ]
    sums = [[None, None] for _ in spans(length)]

    def pair(head, at, span):
        begin, end, low, high = span
        rows, score_marks, inner_marks, _, _ = heads[head]
        return (
            nn(keys[low:high], place(queries[rows, begin:end], head, score_marks[:, begin:end])),
            nn(values[low:high], place(grads[rows, begin:end], head, inner_marks[:, begin:end])),
        )

    def finish(head, at, span, score_grads, probs):
        begin, end, low, high = span
        rows, _, _, own_queries, own_grads = heads[head]
        for which, (left, right) in enumerate(
            ((score_grads, own_queries[begin:end]), (probs, own_grads[begin:end]))
        ):
            part = nn(left, right)
            sums[at][which] = part if sums[at][which] is None else sums[at][which] + part
        turned_ref[rows, begin:end] = nn(turned_keys[rows, low:high], score_grads)

    ahead = [pair(*bodies[0])]
    waiting = None
    for at, body in enumerate(bodies):
        scores, differences = ahead.pop(0)
        if at + 1 < len(bodies):
            ahead.append(pair(*bodies[at + 1]))
        probs = jnp.exp2(scores * SCALE2)
        score_grads = (probs * differences).astype(BF16)
        if waiting is not None:
            finish(*waiting)
        waiting = (*body, score_grads, probs.astype(BF16))
    finish(*waiting)
    gq_ref[...] = (turned_ref[...].T * SCALE).astype(BF16)
    for which, (ref, factor) in enumerate(((gk_ref, SCALE), (gv_ref, 1.0))):
        total = None
        for at, (_, _, low, high) in enumerate(spans(length)):
            parts = [sums[at][which]]
            if low:
                parts.insert(0, jnp.zeros((low, LANES), F32))
            if high < length:
                parts.append(jnp.zeros((length - high, LANES), F32))
            part = jnp.concatenate(parts, axis=0) if len(parts) > 1 else parts[0]
            total = part if total is None else total + part
        ref[...] = (total * factor).astype(BF16)


def attention_specs(length, width):
    tiles = width // LANES

    def tile(at):
        return pl.BlockSpec((length, LANES), lambda i: (0, at + i))

    return (
        tiles,
        tile,
        pl.BlockSpec((length, 1), lambda i: (0, 0)),
        pl.BlockSpec((1, length), lambda i: (0, 0)),
        pl.BlockSpec((LANES, length), lambda i: (i, 0)),
        pl.BlockSpec((SUBLANES, length), lambda i: (i, 0)),
    )


def attend(joined, column, row):
    length = joined.shape[0]
    width = joined.shape[1] // 3
    tiles, tile, column_spec, row_spec, across_spec, lse_spec = attention_specs(length, width)
    return call(
        attend_kernel,
        [((length, width), BF16), ((width, length), F32), ((SUBLANES * tiles, length), F32)],
        (column, row, joined, joined, joined),
        grid=(tiles,),
        in_specs=[column_spec, row_spec, tile(0), tile(tiles), tile(2 * tiles)],
        out_specs=[tile(0), across_spec, lse_spec],
        scratch=[pltpu.VMEM((length, LANES), BF16)],
    )


def attend_back(joined, column, row, grad, across, lse):
    length = joined.shape[0]
    width = joined.shape[1] // 3
    tiles, tile, column_spec, row_spec, across_spec, lse_spec = attention_specs(length, width)
    return call(
        attend_back_kernel,
        [((length, width), BF16)] * 3,
        (column, row, joined, joined, joined, grad, across, lse),
        grid=(tiles,),
        in_specs=[column_spec, row_spec, tile(0), tile(tiles), tile(2 * tiles), tile(0), across_spec, lse_spec],
        out_specs=[tile(0)] * 3,
        scratch=[pltpu.VMEM((length, LANES), BF16), pltpu.VMEM((LANES, length), F32)],
        mib=24,
    )


def slab_kernel(heads_ref, out_ref, short_ref, up_ref, slab_ref):
    rows = heads_ref.shape[0]
    width = out_ref.shape[1]
    slab_ref[:rows, : 3 * width] = heads_ref[...]
    slab_ref[:rows, 3 * width :] = out_ref[...]
    slab_ref[rows:, :] = jnp.zeros((VECTORS, 4 * width), BF16)
    slab_ref[rows:, :rows] = short_ref[...]
    slab_ref[rows:, LANES : LANES + up_ref.shape[1]] = jnp.broadcast_to(
        up_ref[...], (VECTORS, up_ref.shape[1])
    )


def halves_kernel(hidden, position_ref, up_ref, mine_ref, other_ref):
    for at in range(mine_ref.shape[1] // hidden):
        here = slice(hidden * at, hidden * (at + 1))
        for core, ref in enumerate((mine_ref, other_ref)):
            begin = (2 * at + (position_ref[0] + core) % 2) * hidden
            ref[:, here] = up_ref[:, pl.ds(pl.multiple_of(begin, LANES), hidden)]


def project_kernel(count, rows, hidden, position_ref, x_ref, *refs):
    slabs, refs = refs[:count], refs[count:]
    length, width = x_ref.shape
    if count:
        low_ref, joined_ref, heads_ref, out_ref, vector_ref, bias_ref, short_ref, sems = refs
        copies = []
        for at, slab in enumerate(slabs):
            begin = pl.multiple_of(position_ref[at] * rows, SUBLANES)
            here = pl.ds(begin, rows)
            for which, (source, target) in enumerate(
                (
                    (slab.at[pl.ds(0, rows), pl.ds(0, 3 * width)], heads_ref.at[here]),
                    (slab.at[pl.ds(0, rows), pl.ds(3 * width, width)], out_ref.at[here]),
                    (slab.at[pl.ds(rows, VECTORS), pl.ds(0, LANES + hidden)], short_ref.at[at]),
                )
            ):
                copy = pltpu.make_async_copy(source, target, sems.at[at, which])
                copy.start()
                copies.append(copy)
    else:
        heads_ref, vector_ref, low_ref, joined_ref = refs
    if count:
        for copy in copies:
            copy.wait()
        vectors = jnp.zeros((VECTORS, width), F32)
        for at in range(count):
            begin = position_ref[at] * rows
            short = short_ref[at, :, :LANES].astype(F32)
            lane = lax.broadcasted_iota(jnp.int32, short.shape, 1)
            short = jnp.where(lane < rows, short, 0.0)
            short = jnp.concatenate([short, jnp.zeros((VECTORS, width - LANES), F32)], axis=1)
            vectors = vectors + pltpu.roll(short, begin, 1)
            if at < count // 2:
                begin = pl.multiple_of(lax.div(position_ref[at], 2) * hidden, LANES)
                bias_ref[:, pl.ds(begin, hidden)] = short_ref[at, :, LANES:].astype(F32)
        vector_ref[...] = vectors
    zero = jnp.zeros((1, width), F32)
    vector = vector_ref[...]
    bias = jnp.concatenate(
        [vector[QUERY_BIAS : QUERY_BIAS + 1], zero, vector[VALUE_BIAS : VALUE_BIAS + 1]], axis=1
    )
    for at in range(0, length, ROWS):
        normal, _ = unit(x_ref[at : at + ROWS, :].astype(F32))
        low_ref[at : at + ROWS, :] = (
            normal * vector[ATTEND_GAIN : ATTEND_GAIN + 1]
            + vector[ATTEND_SHIFT : ATTEND_SHIFT + 1]
        ).astype(BF16)
    for at in range(0, 3 * width, width):
        here = slice(at, at + width)
        joined_ref[:, here] = (nn(low_ref[...], heads_ref[:, here]) + bias[:, here]).astype(BF16)


def middle_kernel(x_ref, attended_ref, out_ref, vector_ref, middle_ref, low_ref):
    vector = vector_ref[...]
    for at in range(0, x_ref.shape[0], ROWS):
        here = slice(at, at + ROWS)
        middle = (
            x_ref[here, :].astype(F32)
            + nn(attended_ref[here, :], out_ref[...])
            + vector[OUTPUT_BIAS : OUTPUT_BIAS + 1]
        )
        middle_ref[here, :] = middle
        normal, _ = unit(middle)
        low_ref[here, :] = (
            normal * vector[FORWARD_GAIN : FORWARD_GAIN + 1]
            + vector[FORWARD_SHIFT : FORWARD_SHIFT + 1]
        ).astype(BF16)


def up_kernel(position_ref, own_ref, other_ref, bias_ref, *refs):
    parts, (act_ref, slope_ref, full_ref) = refs[: len(refs) - 3], refs[len(refs) - 3 :]
    for at, part in enumerate(parts):
        rows = part.shape[0]
        begin = pl.multiple_of(position_ref[at] * rows, SUBLANES)
        full_ref[pl.ds(begin, rows), :] = part[...]
    weight = full_ref[...]
    bias = bias_ref[:1, :]
    length = own_ref.shape[0]
    for which, ref in enumerate((own_ref, other_ref)):
        for at in range(0, length, ROWS):
            upward = nn(ref[at : at + ROWS, :], weight) + bias
            share = 0.5 + 0.5 * lax.erf(upward * math.sqrt(0.5))
            bell = jnp.exp2((upward * upward) * (-0.5 * math.log2(math.e)))
            here = slice(which * length + at, which * length + at + ROWS)
            act_ref[here, :] = (upward * share).astype(BF16)
            slope = share + upward * (bell * (1.0 / math.sqrt(2.0 * math.pi)))
            slope_ref[here, :] = slope.astype(BF16)


def column_specs(half, block):
    block = min(block, half)

    def column(height):
        return pl.BlockSpec((height, block), lambda i, at: (0, i))

    return half // block, block, column


def whole_spec(shape):
    return pl.BlockSpec(shape, lambda i, at: (0,) * len(shape))


def up_project(own, other, bias, parts, positions):
    length, width = own.shape
    half = parts[0].shape[1]
    steps, _, column = column_specs(half, 512)
    whole = whole_spec((length, width))
    return call(
        up_kernel,
        [((2 * length, half), BF16), ((2 * length, half), BF16), ((width, half), BF16)],
        (own, other, bias, *parts),
        positions,
        grid=(steps,),
        in_specs=[whole, whole, column(bias.shape[0])] + [column(part.shape[0]) for part in parts],
        out_specs=[column(2 * length), column(2 * length), column(width)],
    )


def down_kernel(position_ref, act_ref, *refs):
    parts, (own_ref, other_ref, full_ref) = refs[: len(refs) - 3], refs[len(refs) - 3 :]
    length = own_ref.shape[0]
    for at, part in enumerate(parts):
        rows = part.shape[0]
        begin = pl.multiple_of(position_ref[at] * rows, SUBLANES)
        full_ref[pl.ds(begin, rows), :] = part[...]
    for which, ref in enumerate((own_ref, other_ref)):
        here = slice(which * length, (which + 1) * length)
        ref[...] = nn(act_ref[here, :], full_ref[...]).astype(ref.dtype)


def down_project(act, parts, positions):
    length = act.shape[0] // 2
    half = act.shape[1]
    width = parts[0].shape[1]
    return call(
        down_kernel,
        [((length, width), F32), ((length, width), BF16), ((half, width), BF16)],
        (act, *parts),
        positions,
        mib=20,
    )


def loss_kernel(
    middle_ref, own_ref, got_ref, vector_ref, readout_ref, target_ref, mask_ref,
    low_ref, down_ref, grad_ref, lanes_ref, sums_ref,
):
    result = (
        middle_ref[...]
        + (own_ref[...] + got_ref[...].astype(F32))
        + vector_ref[DOWN_BIAS : DOWN_BIAS + 1, :]
    ).astype(BF16)
    low_ref[...] = result
    logits = nt(readout_ref[...], result)
    length = logits.shape[1]
    top = jnp.max(logits, axis=0, keepdims=True)
    shifted = jnp.exp(logits - top)
    total = jnp.sum(shifted, axis=0, keepdims=True)
    onehot = lax.broadcasted_iota(jnp.int32, logits.shape, 0) == target_ref[...]
    picked = jnp.sum(jnp.where(onehot, logits, 0.0), axis=0, keepdims=True)
    weight = mask_ref[...].astype(F32)
    loss = (top + jnp.log(total) - picked) * weight
    loss_lanes = jnp.zeros((1, LANES), F32)
    count_lanes = jnp.zeros((1, LANES), F32)
    for at in range(0, length, LANES):
        loss_lanes = loss_lanes + loss[:, at : at + LANES]
        count_lanes = count_lanes + weight[:, at : at + LANES]
    blank = jnp.zeros((SUBLANES - 2, LANES), F32)
    lanes_ref[...] = jnp.concatenate([loss_lanes, count_lanes, blank], axis=0)
    grad_logits = (weight * (shifted / total - onehot.astype(F32))).astype(BF16)
    grad = tn(grad_logits, readout_ref[...])
    grad_ref[...] = grad
    low = grad.astype(BF16)
    down_ref[...] = low
    sums_ref[...] = jnp.sum(low.astype(F32), axis=0, keepdims=True)


def down_grad_kernel(chips, position_ref, act_ref, own_ref, other_ref, *out_refs):
    length = own_ref.shape[0]
    hidden = act_ref.shape[1] // chips
    for offset in range(chips):
        if len(out_refs) == 1:
            begin = offset * hidden
        else:
            begin = pl.multiple_of((position_ref[0] ^ offset) * hidden, LANES)
        here = pl.ds(begin, hidden)
        part = tn(act_ref[:length, here], own_ref[...]) + tn(act_ref[length:, here], other_ref[...])
        part = part.astype(BF16)
        if len(out_refs) == 1:
            out_refs[0][begin : begin + hidden, :] = part
            continue
        keep_x, send_x, keep_y, send_y = out_refs
        half = hidden // 2
        (send_x if offset % 2 else keep_x)[offset // 2, :, :] = part[:half]
        (send_y if offset // 2 else keep_y)[offset % 2, :, :] = part[half:]


def down_grad(act, own, other, chips, position):
    half = act.shape[1]
    width = own.shape[1]
    if square():
        outs = [((2, half // chips // 2, width), BF16)] * 4
    else:
        outs = [((half, width), BF16)]
    return call(
        functools.partial(down_grad_kernel, chips), outs, (act, own, other), position, mib=20
    )


def up_grad_kernel(
    rows, position_ref, own_ref, other_ref, slope_ref, second_ref, second_other_ref, down_ref,
    up_ref, bias_ref, *refs,
):
    out_refs, part_ref = refs[:-1], refs[-1]
    length = own_ref.shape[0]
    total = None
    grads = []
    for which, ref in enumerate((own_ref, other_ref)):
        for at in range(0, length, 2 * ROWS):
            here = slice(which * length + at, which * length + at + 2 * ROWS)
            grad = nt(ref[at : at + 2 * ROWS, :], down_ref[...]) * slope_ref[here, :].astype(F32)
            low = grad.astype(BF16)
            up_ref[here, :] = low
            part = jnp.sum(low.astype(F32), axis=0, keepdims=True)
            total = part if total is None else total + part
    bias_ref[...] = total
    part = tn(second_ref[...], up_ref[:length, :]) + tn(second_other_ref[...], up_ref[length:, :])
    if len(out_refs) == 1:
        out_refs[0][...] = part.astype(BF16)
        return
    part_ref[...] = part
    keep_x, send_x, keep_y, send_y = out_refs
    for offset in range(4):
        begin = pl.multiple_of((position_ref[0] ^ offset) * (2 * rows), SUBLANES)
        upper = part_ref[pl.ds(begin, rows), :].astype(BF16)
        lower = part_ref[pl.ds(begin + rows, rows), :].astype(BF16)
        (send_x if offset % 2 else keep_x)[offset // 2, :, :] = upper
        (send_y if offset // 2 else keep_y)[offset % 2, :, :] = lower


def up_grad(own, other, slope, second, second_other, down_full, rows, position):
    length, width = own.shape
    half = slope.shape[1]
    steps, block, column = column_specs(half, 512)
    whole = whole_spec((length, width))
    if square():
        outs = [((2, rows, half), BF16)] * 4
        specs = [pl.BlockSpec((2, rows, block), lambda i, at: (0, 0, i))] * 4
    else:
        outs = [((width, half), BF16)]
        specs = [column(width)]
    return call(
        functools.partial(up_grad_kernel, rows),
        [((2 * length, half), BF16), ((1, half), F32), *outs],
        (own, other, slope, second, second_other, down_full),
        position,
        grid=(steps,),
        in_specs=[
            whole, whole, column(2 * length), whole, whole,
            pl.BlockSpec((block, width), lambda i, at: (i, 0)),
        ],
        out_specs=[column(2 * length), column(1), *specs],
        scratch=[pltpu.VMEM((width, block), F32)],
        mib=20,
    )


def inward_kernel(grad_ref, up_ref, own_ref, other_ref):
    length = own_ref.shape[0]
    other_ref[...] = nt(grad_ref[length:, :], up_ref[...]).astype(BF16)
    own_ref[...] = nt(grad_ref[:length, :], up_ref[...])


def join_kernel(hidden, position_ref, mine_ref, other_ref, out_ref):
    for at in range(mine_ref.shape[1] // hidden):
        here = slice(hidden * at, hidden * (at + 1))
        for core, ref in enumerate((mine_ref, other_ref)):
            begin = (2 * at + (position_ref[0] + core) % 2) * hidden
            out_ref[:, pl.ds(pl.multiple_of(begin, LANES), hidden)] = ref[:, here].astype(F32)


def branch_kernel(
    own_ref, got_ref, middle_ref, result_ref, out_ref, vector_ref,
    grad_ref, branch_ref, attended_ref, sums_ref,
):
    width = own_ref.shape[1]
    gain = vector_ref[FORWARD_GAIN : FORWARD_GAIN + 1, :]
    sums = [jnp.zeros((1, width), F32) for _ in range(3)]
    for at in range(0, own_ref.shape[0], ROWS):
        here = slice(at, at + ROWS)
        grad = own_ref[here, :] + got_ref[here, :].astype(F32)
        normal, inverse = unit(middle_ref[here, :])
        middle = result_ref[here, :] + unit_back(grad, normal, inverse, gain)
        grad_ref[here, :] = middle
        branch = middle.astype(BF16)
        branch_ref[here, :] = branch
        attended_ref[here, :] = nt(branch, out_ref[...]).astype(BF16)
        for which, part in enumerate((grad * normal, grad, branch.astype(F32))):
            sums[which] = sums[which] + jnp.sum(part, axis=0, keepdims=True)
    blank = jnp.zeros((SUBLANES - 3, width), F32)
    sums_ref[...] = jnp.concatenate([*sums, blank], axis=0)


def last_kernel(
    count, rows, hidden, position_ref,
    x_ref, low_ref, gq_ref, gk_ref, gv_ref, heads_ref, attended_ref, branch_ref, grad_ref,
    vector_ref, sums_ref, down_ref, up_ref, lanes_ref, *refs,
):
    slabs, (input_ref, vectors_ref, full_ref) = refs[:count], refs[count:]
    width = x_ref.shape[1]
    for at, ref in enumerate((gq_ref, gk_ref, gv_ref)):
        part = tn(low_ref[...], ref[...])
        full_ref[:, width * at : width * (at + 1)] = part.astype(BF16)
    full_ref[:, 3 * width :] = tn(attended_ref[...], branch_ref[...]).astype(BF16)
    gain = vector_ref[ATTEND_GAIN : ATTEND_GAIN + 1, :]
    sums = [jnp.zeros((1, width), F32) for _ in range(4)]
    for at in range(0, x_ref.shape[0], ROWS):
        here = slice(at, at + ROWS)
        grad = (
            nt(gq_ref[here, :], heads_ref[:, :width])
            + nt(gk_ref[here, :], heads_ref[:, width : 2 * width])
            + nt(gv_ref[here, :], heads_ref[:, 2 * width :])
        )
        normal, inverse = unit(x_ref[here, :].astype(F32))
        input_ref[here, :] = grad_ref[here, :] + unit_back(grad, normal, inverse, gain)
        parts = (grad * normal, grad, gq_ref[here, :].astype(F32), gv_ref[here, :].astype(F32))
        for which, part in enumerate(parts):
            sums[which] = sums[which] + jnp.sum(part, axis=0, keepdims=True)
    vectors = jnp.concatenate(
        [*sums, sums_ref[2:3, :], sums_ref[0:1, :], sums_ref[1:2, :], down_ref[...]], axis=0
    )
    vectors_ref[...] = vectors
    blank = jnp.zeros((VECTORS - 1, hidden), F32)
    for at, slab in enumerate(slabs):
        place_at = position_ref[at]
        begin = pl.multiple_of(place_at * rows, SUBLANES)
        slab[:rows, :] = full_ref[pl.ds(begin, rows), :]
        short = pltpu.roll(vectors, width - begin, 1)[:, :LANES]
        if at < count // 2:
            hidden_at = pl.multiple_of(lax.div(place_at, 2) * hidden, LANES)
            bias = jnp.concatenate([up_ref[:, pl.ds(hidden_at, hidden)], blank], axis=0)
        else:
            bias = jnp.zeros((VECTORS, hidden), F32)
        row = jnp.concatenate([short, bias, lanes_ref[...]], axis=1).astype(BF16)
        pad = jnp.zeros((VECTORS, 4 * width - row.shape[1]), BF16)
        slab[rows:, :] = jnp.concatenate([row, pad], axis=1)


def swap(values, bit):
    return lax.ppermute(values, "wide", [(i, i ^ bit) for i in range(lax.axis_size("wide"))])


def same_core_groups():
    chips = lax.axis_size("wide") // 2
    return [[2 * chip + core for chip in range(chips)] for core in range(2)]


def square():
    return lax.axis_size("wide") == 8


def spread_chips(shard):
    return lax.all_gather(shard, "wide", axis=0, axis_index_groups=same_core_groups())


def add_low(*parts):
    return sum(part.astype(F32) for part in parts).astype(BF16)


def collect_chips(parts):
    return lax.psum_scatter(
        parts, "wide", scatter_dimension=0, axis_index_groups=same_core_groups()
    )


def collect_square(keep_x, send_x, keep_y, send_y):
    from_x = swap(send_x, 2)
    from_y = swap(send_y, 4)
    upper = swap(add_low(keep_x[1], from_x[1]), 4)
    lower = swap(add_low(keep_y[1], from_y[1]), 2)
    return add_low(keep_x[0], from_x[0], upper), add_low(keep_y[0], from_y[0], lower)


def sum_narrow(shard):
    if lax.axis_size("narrow") != 4:
        return lax.psum(shard, "narrow")
    place_at = lax.axis_index("narrow")
    inner = (place_at == 1) | (place_at == 2)
    half = add_low(shard, lax.ppermute(shard, "narrow", [(0, 1), (3, 2)]))
    total = add_low(half, lax.ppermute(half, "narrow", [(1, 2), (2, 1)]))
    outer = lax.ppermute(total, "narrow", [(1, 0), (2, 3)])
    return jnp.where(inner, total, outer)


def local(
    layer_input, segments, targets, loss_mask, readout,
    attend_gain, attend_shift, heads_weight, query_bias, value_bias, output_weight, output_bias,
    forward_gain, forward_shift, up_weight, up_bias, down_weight, down_bias,
):
    length = layer_input.shape[1]
    width = layer_input.shape[2]
    wide = lax.axis_size("wide")
    chips = wide // 2
    core = lax.axis_index("wide") % 2
    chip = lax.axis_index("wide") // 2
    rows = heads_weight.shape[0]
    hidden = up_bias.shape[0]
    half = chips * hidden
    x = layer_input[0]
    column = segments.reshape(length, 1)

    def by_core(mine, other, axis):
        return jnp.where(
            core == 0, jnp.stack([mine, other], axis), jnp.stack([other, mine], axis)
        )

    def mine_of(values, axis, flip=0):
        return lax.dynamic_index_in_dim(values, core ^ flip, axis, keepdims=False)

    short = jnp.stack(
        [
            attend_gain, attend_shift, query_bias, value_bias,
            output_bias, forward_gain, forward_shift, down_bias,
        ]
    )
    core_position = core.reshape(1).astype(jnp.int32)
    chip_position = chip.reshape(1).astype(jnp.int32)
    if square():
        offsets = jnp.arange(4, dtype=jnp.int32)
        (slab,) = call(
            slab_kernel,
            [((rows + VECTORS, 4 * width), BF16)],
            (heads_weight, output_weight, short, up_bias[None]),
        )
        slabs = [slab, swap(slab, 2), swap(slab, 4), swap(slab, 6)]
        slabs = slabs + [swap(part, 1) for part in slabs]
        devices = 2 * (chip ^ offsets) + core
        positions = jnp.concatenate([devices, devices ^ 1]).astype(jnp.int32)
        first_low, joined, heads_full, output_full, vectors, up_bias_half = call(
            functools.partial(project_kernel, len(slabs), rows, hidden),
            [
                ((length, width), BF16), ((length, 3 * width), BF16), ((width, 3 * width), BF16),
                ((width, width), BF16), ((VECTORS, width), F32), ((VECTORS, half), F32),
            ],
            (x, *slabs),
            positions,
            in_specs=[pl.BlockSpec(memory_space=pltpu.VMEM)]
            + [pl.BlockSpec(memory_space=pl.ANY)] * len(slabs),
            scratch=[
                pltpu.VMEM((len(slabs), VECTORS, LANES + hidden), BF16),
                pltpu.SemaphoreType.DMA((len(slabs), 3)),
            ],
            mib=20,
        )
        up_mine, up_other = call(
            functools.partial(halves_kernel, hidden),
            [((rows, half), BF16)] * 2,
            (up_weight,),
            core_position,
        )
        mine_x, other_x = swap(up_mine, 2), swap(up_other, 3)
        mine_y, other_y = swap(up_mine, 4), swap(up_other, 5)
        up_parts = [
            up_mine, mine_x, mine_y, swap(mine_y, 2),
            swap(up_other, 1), other_x, other_y, swap(other_x, 4),
        ]
        down_x, down_y = swap(down_weight, 2), swap(down_weight, 4)
        middle_row = hidden // 2
        down_parts = [
            down_weight, down_x, down_y,
            swap(down_y[:middle_row], 2), swap(down_x[middle_row:], 4),
        ]
        up_positions = positions
        chip_at = chip ^ offsets
        down_positions = jnp.concatenate(
            [chip_at[:3], 2 * chip_at[3:], 2 * chip_at[3:] + 1]
        ).astype(jnp.int32)
    else:
        tail = jnp.concatenate([short.reshape(1, 8 * rows), up_bias[None]], axis=1)
        tail = jnp.pad(tail, ((0, 0), (0, 4 * width - tail.shape[1])))
        slab = jnp.concatenate(
            [jnp.concatenate([heads_weight, output_weight], axis=1), tail], axis=0
        )
        slabs = lax.all_gather(slab, "wide", axis=0)
        attend_full = slabs[:, :rows].reshape(width, 4 * width)
        heads_full = attend_full[:, : 3 * width]
        output_full = attend_full[:, 3 * width :]
        last = slabs[:, rows].astype(F32)
        vectors = last[:, : 8 * rows].reshape(wide, 8, rows).transpose(1, 0, 2).reshape(8, width)
        up_bias_half = mine_of(last[:, 8 * rows : 8 * rows + hidden].reshape(chips, 2, hidden), 1)
        up_bias_half = jnp.broadcast_to(up_bias_half.reshape(1, half), (VECTORS, half))
        positions = jnp.zeros((1,), jnp.int32)
        first_low, joined = call(
            functools.partial(project_kernel, 0, rows, hidden),
            [((length, width), BF16), ((length, 3 * width), BF16)],
            (x, heads_full, vectors),
            positions,
            mib=20,
        )
        up_view = up_weight.reshape(rows, chips, 2, hidden)
        up_pair = by_core(
            mine_of(up_view, 2).reshape(rows, half),
            swap(mine_of(up_view, 2, 1).reshape(rows, half), 1),
            0,
        ).reshape(2 * rows, half)
        up_parts = [spread_chips(up_pair).reshape(width, half)]
        down_parts = [spread_chips(down_weight).reshape(half, width)]
        up_positions = down_positions = positions

    attended, across, lse = attend(joined, column, segments)
    middle, second_low = call(
        middle_kernel,
        [((length, width), F32), ((length, width), BF16)],
        (x, attended, output_full, vectors),
    )

    second_other = swap(second_low, 1)
    activated, slope, up_full = up_project(
        second_low, second_other, up_bias_half, up_parts, up_positions
    )
    outward, outward_other, down_full = down_project(activated, down_parts, down_positions)
    result_low, grad_down, grad_result, lanes, down_bias_part = call(
        loss_kernel,
        [
            ((length, width), BF16), ((length, width), BF16), ((length, width), F32),
            ((SUBLANES, LANES), F32), ((1, width), F32),
        ],
        (middle, outward, swap(outward_other, 1), vectors, readout.T, targets, loss_mask),
    )

    grad_down_other = swap(grad_down, 1)
    down_parts = down_grad(activated, grad_down, grad_down_other, chips, chip_position)
    grad_up, up_bias_part, *up_parts = up_grad(
        grad_down, grad_down_other, slope, second_low, second_other, down_full, rows, chip_position
    )
    inward, inward_other = call(
        inward_kernel,
        [((length, width), F32), ((length, width), BF16)],
        (grad_up, up_full),
        mib=20,
    )
    grad_middle, grad_branch, grad_attended, branch_sums = call(
        branch_kernel,
        [
            ((length, width), F32), ((length, width), BF16), ((length, width), BF16),
            ((SUBLANES, width), F32),
        ],
        (inward, swap(inward_other, 1), middle, grad_result, output_full, vectors),
    )
    if square():
        down_sums = [sum_narrow(part) for part in collect_square(*down_parts)]
        down_weight_sum = jnp.concatenate(down_sums).astype(F32)
        upper, lower = [sum_narrow(part) for part in collect_square(*up_parts)]
        first = core == 0
        (up_weight_sum,) = call(
            functools.partial(join_kernel, hidden),
            [((rows, 2 * half), F32)],
            (jnp.where(first, upper, lower), swap(jnp.where(first, lower, upper), 1)),
            core_position,
        )
    else:
        down_weight_sum = collect_chips(down_parts[0].reshape(chips, hidden, width))
        down_weight_sum = sum_narrow(down_weight_sum).astype(F32)
        up_sum = sum_narrow(collect_chips(up_parts[0].reshape(chips, 2 * rows, half)))
        up_sum = up_sum.reshape(2, rows, chips, hidden)
        up_weight_sum = by_core(mine_of(up_sum, 0), swap(mine_of(up_sum, 0, 1), 1), 2)
        up_weight_sum = up_weight_sum.reshape(rows, 2 * half).astype(F32)

    grad_query, grad_key, grad_value = attend_back(
        joined, column, segments, grad_attended, across, lse
    )
    slab_shape = ((rows + VECTORS, 4 * width), BF16)
    *slabs, input_grad, short_sums, attend_part = call(
        functools.partial(last_kernel, 8 if square() else 0, rows, hidden),
        ([slab_shape] * 8 if square() else [])
        + [((length, width), F32), ((VECTORS, width), F32), ((width, 4 * width), BF16)],
        (
            x, first_low, grad_query, grad_key, grad_value, heads_full, attended, grad_branch,
            grad_middle, vectors, branch_sums, down_bias_part, up_bias_part, lanes,
        ),
        positions,
        mib=40,
    )
    if square():
        both = [add_low(slabs[at], swap(slabs[4 + at], 1)) for at in (3, 1, 2, 0)]
        got = [swap(both[0], 6), swap(both[1], 2), swap(both[2], 4)]
        slab = sum_narrow(add_low(both[3], *got)).astype(F32)
        vectors_sum = slab[rows:, :rows]
        up_bias_grad = slab[rows, LANES : LANES + hidden]
        lanes_sum = slab[rows : rows + 2, LANES + hidden : 2 * LANES + hidden]
    else:
        short = short_sums.reshape(8, wide, rows).transpose(1, 0, 2).reshape(wide, 8 * rows)
        up_bias_rows = up_bias_part.reshape(chips, hidden)
        up_bias_rows = by_core(up_bias_rows, jnp.zeros_like(up_bias_rows), 1).reshape(wide, hidden)
        shared = jnp.broadcast_to(lanes[:2].reshape(1, 2 * LANES), (wide, 2 * LANES))
        row = jnp.concatenate([short, up_bias_rows, shared], axis=1).astype(BF16)
        row = jnp.pad(row, ((0, 0), (0, 4 * width - row.shape[1])))
        slab = jnp.concatenate([attend_part.reshape(wide, rows, 4 * width), row[:, None]], axis=1)
        slab = sum_narrow(lax.psum_scatter(slab, "wide", scatter_dimension=0)).astype(F32)
        vectors_sum = slab[rows, : 8 * rows].reshape(8, rows)
        up_bias_grad = slab[rows, 8 * rows : 8 * rows + hidden]
        lanes_sum = slab[rows, 8 * rows + hidden : 8 * rows + hidden + 2 * LANES].reshape(2, LANES)
    return (
        result_low[None],
        input_grad[None],
        vectors_sum[ATTEND_GAIN],
        vectors_sum[ATTEND_SHIFT],
        slab[:rows, : 3 * width],
        vectors_sum[QUERY_BIAS],
        vectors_sum[VALUE_BIAS],
        slab[:rows, 3 * width :],
        vectors_sum[OUTPUT_BIAS],
        vectors_sum[FORWARD_GAIN],
        vectors_sum[FORWARD_SHIFT],
        up_weight_sum,
        up_bias_grad,
        down_weight_sum,
        vectors_sum[DOWN_BIAS],
        jnp.sum(lanes_sum[0]),
        jnp.round(jnp.sum(lanes_sum[1])).astype(jnp.int32),
    )


def solution(mesh):
    in_specs = (
        P(("narrow", "wide"), None, None),
        P(("narrow", "wide"), None),
        P(("narrow", "wide"), None),
        P(("narrow", "wide"), None),
        P(),
        P("wide"),
        P("wide"),
        P("wide", None),
        P("wide"),
        P("wide"),
        P("wide", None),
        P("wide"),
        P("wide"),
        P("wide"),
        P("wide", None),
        P("wide"),
        P("wide", None),
        P("wide"),
    )
    out_specs = (
        P(("narrow", "wide"), None, None),
        P(("narrow", "wide"), None, None),
        P("wide"),
        P("wide"),
        P("wide", None),
        P("wide"),
        P("wide"),
        P("wide", None),
        P("wide"),
        P("wide"),
        P("wide"),
        P("wide", None),
        P("wide"),
        P("wide", None),
        P("wide"),
        P(),
        P(),
    )
    return jax.shard_map(local, mesh=mesh, in_specs=in_specs, out_specs=out_specs, check_vma=False)
```

```python
import functools
import math

import jax
import jax.numpy as jnp
from jax import lax
from jax.experimental import pallas as pl
from jax.experimental.pallas import tpu as pltpu
from jax.sharding import PartitionSpec as P

HEADS = 20
HEAD_DIM = 32
LANES = 128
SUBLANES = 8
SEGMENTS = 8
REACH = 192
CHUNK = 256
ROWS = 128
SCALE = 1.0 / math.sqrt(HEAD_DIM)
SCALE2 = math.log2(math.e) * SCALE
F32 = jnp.float32
BF16 = jnp.bfloat16
VECTORS = 8
ATTEND_GAIN, ATTEND_SHIFT, QUERY_BIAS, VALUE_BIAS = 0, 1, 2, 3
OUTPUT_BIAS, FORWARD_GAIN, FORWARD_SHIFT, DOWN_BIAS = 4, 5, 6, 7


def nn(left, right):
    return lax.dot_general(left, right, (((1,), (0,)), ((), ())), preferred_element_type=F32)


def nt(left, right):
    return lax.dot_general(left, right, (((1,), (1,)), ((), ())), preferred_element_type=F32)


def tn(left, right):
    return lax.dot_general(left, right, (((0,), (0,)), ((), ())), preferred_element_type=F32)


def call(kernel, outs, args, positions=None, grid=None, in_specs=None, out_specs=None, scratch=(),
         mib=16):
    whole = pl.BlockSpec(memory_space=pltpu.VMEM)
    in_specs = in_specs or [whole] * len(args)
    out_specs = out_specs or [whole] * len(outs)
    shapes = [jax.ShapeDtypeStruct(shape, dtype) for shape, dtype in outs]
    extra = [] if positions is None else [positions]
    return pl.pallas_call(
        kernel,
        out_shape=shapes,
        grid_spec=pltpu.PrefetchScalarGridSpec(
            num_scalar_prefetch=len(extra),
            grid=grid or (),
            in_specs=in_specs,
            out_specs=out_specs,
            scratch_shapes=list(scratch),
        ),
        compiler_params=pltpu.CompilerParams(vmem_limit_bytes=mib * 1024 * 1024),
        cost_estimate=pl.CostEstimate(flops=1, bytes_accessed=1, transcendentals=0),
    )(*extra, *args)


def unit(values):
    centred = values - jnp.mean(values, axis=-1, keepdims=True)
    spread = jnp.mean(centred * centred, axis=-1, keepdims=True)
    inverse = lax.rsqrt(spread + 1e-05)
    return centred * inverse, inverse


def unit_back(grad, normal, inverse, gain):
    scaled = grad * gain
    mean = jnp.mean(scaled, axis=-1, keepdims=True)
    along = jnp.mean(scaled * normal, axis=-1, keepdims=True)
    return inverse * (scaled - mean - normal * along)


def spans(length):
    chunk = min(CHUNK, length)
    return [
        (at, at + chunk, max(0, at - REACH), min(length, at + chunk + REACH))
        for at in range(0, length, chunk)
    ]


def split3(values):
    first = values.astype(BF16).astype(F32)
    rest = values - first
    second = rest.astype(BF16).astype(F32)
    return [first, second, rest - second]


def key_marks(segment_column):
    lane = lax.broadcasted_iota(jnp.int32, (segment_column.shape[0], LANES), 1)
    ones = (lane >= SEGMENTS) & (lane < SEGMENTS + 3)
    return jnp.where((lane == segment_column) | ones, 1.0, 0.0).astype(BF16)


def query_marks(segment_row):
    row = lax.broadcasted_iota(jnp.int32, (SEGMENTS, segment_row.shape[1]), 0)
    return jnp.where(row == segment_row, 0.0, -1e30)


def place(rows, head, marks):
    count = rows.shape[1]
    parts = [rows, marks, jnp.zeros((LANES - marks.shape[0], count), BF16)]
    if head < LANES // HEAD_DIM - 1:
        parts.insert(1, jnp.zeros((LANES - HEAD_DIM * (head + 1), count), BF16))
    if head:
        parts.insert(0, jnp.zeros((HEAD_DIM * head, count), BF16))
    return jnp.concatenate(parts, axis=0)


def attend_kernel(column_ref, row_ref, q_ref, k_ref, v_ref, out_ref, across_ref, lse_ref, marks_ref):
    @pl.when(pl.program_id(0) == 0)
    def _():
        marks_ref[...] = key_marks(column_ref[...])

    length = q_ref.shape[0]
    heads = LANES // HEAD_DIM
    queries = q_ref[...].T
    values = v_ref[...].T
    keys = jnp.concatenate([k_ref[...], marks_ref[...]], axis=1)
    blank = jnp.zeros((SUBLANES, length), F32)
    marks = jnp.concatenate([query_marks(row_ref[...]), blank], axis=0).astype(BF16)
    ones = jnp.ones((SUBLANES, length), BF16)
    bodies = [(head, span) for head in range(heads) for span in spans(length)]

    def rows(head):
        return slice(HEAD_DIM * head, HEAD_DIM * (head + 1))

    summed = [jnp.concatenate([values[rows(head)], ones], axis=0) for head in range(heads)]

    def score(head, span):
        begin, end, low, high = span
        return nn(keys[low:high], place(queries[rows(head), begin:end], head, marks[:, begin:end]))

    def finish(head, span, top, probs):
        begin, end, low, high = span
        out = nn(summed[head][:, low:high], probs)
        total = out[HEAD_DIM : HEAD_DIM + 1]
        across_ref[rows(head), begin:end] = out[:HEAD_DIM] * (1.0 / total)
        lse_ref[head : head + 1, begin:end] = (top + jnp.log2(total)) * (1.0 / SCALE2)

    scores = [score(*body) for body in bodies[:2]]
    waiting = None
    for at, body in enumerate(bodies):
        current = scores.pop(0)
        if at + 2 < len(bodies):
            scores.append(score(*bodies[at + 2]))
        top = jnp.max(current, axis=0, keepdims=True) * SCALE2
        probs = jnp.exp2(current * SCALE2 - top).astype(BF16)
        if waiting is not None:
            finish(*waiting)
        waiting = (*body, top, probs)
    finish(*waiting)
    lse_ref[heads:, :] = jnp.zeros((SUBLANES - heads, length), F32)
    out_ref[...] = across_ref[...].T.astype(BF16)


def attend_back_kernel(
    column_ref, row_ref, q_ref, k_ref, v_ref, grad_ref, across_ref, lse_ref,
    gq_ref, gk_ref, gv_ref, marks_ref, turned_ref,
):
    @pl.when(pl.program_id(0) == 0)
    def _():
        marks_ref[...] = key_marks(column_ref[...])

    length = q_ref.shape[0]
    grad = grad_ref[...]
    queries = q_ref[...].T
    turned_keys = k_ref[...].T
    grads = grad.T
    keys = jnp.concatenate([k_ref[...], marks_ref[...]], axis=1)
    values = jnp.concatenate([v_ref[...], marks_ref[...]], axis=1)
    low_marks = query_marks(row_ref[...])
    blank = jnp.zeros((SUBLANES, length), F32)
    lane = lax.broadcasted_iota(jnp.int32, (1, LANES), 1) // HEAD_DIM
    heads = []
    for head in range(LANES // HEAD_DIM):
        rows = slice(HEAD_DIM * head, HEAD_DIM * (head + 1))
        inner = jnp.sum(grads[rows].astype(F32) * across_ref[rows, :], axis=0, keepdims=True)
        lse = lse_ref[head : head + 1, :]
        score_marks = jnp.concatenate([low_marks, *split3(-lse), blank[:5]], axis=0)
        inner_marks = jnp.concatenate([blank, *split3(-inner), blank[:5]], axis=0)
        zero = jnp.zeros_like(grad)
        heads.append(
            (
                rows,
                score_marks.astype(BF16),
                inner_marks.astype(BF16),
                jnp.where(lane == head, q_ref[...], zero),
                jnp.where(lane == head, grad, zero),
            )
        )
    bodies = [
        (head, at, span) for head in range(len(heads)) for at, span in enumerate(spans(length))
    ]
    sums = [[None, None] for _ in spans(length)]

    def pair(head, at, span):
        begin, end, low, high = span
        rows, score_marks, inner_marks, _, _ = heads[head]
        return (
            nn(keys[low:high], place(queries[rows, begin:end], head, score_marks[:, begin:end])),
            nn(values[low:high], place(grads[rows, begin:end], head, inner_marks[:, begin:end])),
        )

    def finish(head, at, span, score_grads, probs):
        begin, end, low, high = span
        rows, _, _, own_queries, own_grads = heads[head]
        for which, (left, right) in enumerate(
            ((score_grads, own_queries[begin:end]), (probs, own_grads[begin:end]))
        ):
            part = nn(left, right)
            sums[at][which] = part if sums[at][which] is None else sums[at][which] + part
        turned_ref[rows, begin:end] = nn(turned_keys[rows, low:high], score_grads)

    ahead = [pair(*bodies[0])]
    waiting = None
    for at, body in enumerate(bodies):
        scores, differences = ahead.pop(0)
        if at + 1 < len(bodies):
            ahead.append(pair(*bodies[at + 1]))
        probs = jnp.exp2(scores * SCALE2)
        score_grads = (probs * differences).astype(BF16)
        if waiting is not None:
            finish(*waiting)
        waiting = (*body, score_grads, probs.astype(BF16))
    finish(*waiting)
    gq_ref[...] = (turned_ref[...].T * SCALE).astype(BF16)
    for which, (ref, factor) in enumerate(((gk_ref, SCALE), (gv_ref, 1.0))):
        total = None
        for at, (_, _, low, high) in enumerate(spans(length)):
            parts = [sums[at][which]]
            if low:
                parts.insert(0, jnp.zeros((low, LANES), F32))
            if high < length:
                parts.append(jnp.zeros((length - high, LANES), F32))
            part = jnp.concatenate(parts, axis=0) if len(parts) > 1 else parts[0]
            total = part if total is None else total + part
        ref[...] = (total * factor).astype(BF16)


def attention_specs(length, width, begin=0):
    tiles = width // LANES

    def tile(at, begin=begin):
        return pl.BlockSpec((length, LANES), lambda i: (0, at + begin + i))

    return (
        tiles,
        tile,
        pl.BlockSpec((length, 1), lambda i: (0, 0)),
        pl.BlockSpec((1, length), lambda i: (0, 0)),
        pl.BlockSpec((LANES, length), lambda i: (begin + i, 0)),
        pl.BlockSpec((SUBLANES, length), lambda i: (begin + i, 0)),
    )


def attend(joined, column, row):
    length = joined.shape[0]
    width = joined.shape[1] // 3
    tiles, tile, column_spec, row_spec, across_spec, lse_spec = attention_specs(length, width)
    return call(
        attend_kernel,
        [((length, width), BF16), ((width, length), F32), ((SUBLANES * tiles, length), F32)],
        (column, row, joined, joined, joined),
        grid=(tiles,),
        in_specs=[column_spec, row_spec, tile(0), tile(tiles), tile(2 * tiles)],
        out_specs=[tile(0), across_spec, lse_spec],
        scratch=[pltpu.VMEM((length, LANES), BF16)],
    )


def attend_back(joined, column, row, grad, across, lse, begin=0, end=None):
    length = joined.shape[0]
    width = joined.shape[1] // 3
    specs = attention_specs(length, width, begin)
    tiles, tile, column_spec, row_spec, across_spec, lse_spec = specs
    count = (end or tiles) - begin
    return call(
        attend_back_kernel,
        [((length, count * LANES), BF16)] * 3,
        (column, row, joined, joined, joined, grad, across, lse),
        grid=(count,),
        in_specs=[column_spec, row_spec, tile(0), tile(tiles), tile(2 * tiles), tile(0), across_spec, lse_spec],
        out_specs=[tile(0, 0)] * 3,
        scratch=[pltpu.VMEM((length, LANES), BF16), pltpu.VMEM((LANES, length), F32)],
        mib=24,
    )


def slab_kernel(heads_ref, out_ref, short_ref, up_ref, slab_ref):
    rows = heads_ref.shape[0]
    width = out_ref.shape[1]
    slab_ref[:rows, : 3 * width] = heads_ref[...]
    slab_ref[:rows, 3 * width :] = out_ref[...]
    slab_ref[rows:, :] = jnp.zeros((VECTORS, 4 * width), BF16)
    slab_ref[rows:, :rows] = short_ref[...]
    slab_ref[rows:, LANES : LANES + up_ref.shape[1]] = jnp.broadcast_to(
        up_ref[...], (VECTORS, up_ref.shape[1])
    )


def halves_kernel(hidden, position_ref, up_ref, mine_ref, other_ref):
    for at in range(mine_ref.shape[1] // hidden):
        here = slice(hidden * at, hidden * (at + 1))
        for core, ref in enumerate((mine_ref, other_ref)):
            begin = (2 * at + (position_ref[0] + core) % 2) * hidden
            ref[:, here] = up_ref[:, pl.ds(pl.multiple_of(begin, LANES), hidden)]


def project_kernel(count, rows, hidden, position_ref, x_ref, *refs):
    slabs, refs = refs[:count], refs[count:]
    length, width = x_ref.shape
    if count:
        low_ref, joined_ref, heads_ref, out_ref, vector_ref, bias_ref, short_ref, sems = refs
        copies = []
        for at, slab in enumerate(slabs):
            begin = pl.multiple_of(position_ref[at] * rows, SUBLANES)
            here = pl.ds(begin, rows)
            for which, (source, target) in enumerate(
                (
                    (slab.at[pl.ds(0, rows), pl.ds(0, 3 * width)], heads_ref.at[here]),
                    (slab.at[pl.ds(0, rows), pl.ds(3 * width, width)], out_ref.at[here]),
                    (slab.at[pl.ds(rows, VECTORS), pl.ds(0, LANES + hidden)], short_ref.at[at]),
                )
            ):
                copy = pltpu.make_async_copy(source, target, sems.at[at, which])
                copy.start()
                copies.append(copy)
    else:
        heads_ref, vector_ref, low_ref, joined_ref = refs
    if count:
        for copy in copies:
            copy.wait()
        vectors = jnp.zeros((VECTORS, width), F32)
        for at in range(count):
            begin = position_ref[at] * rows
            short = short_ref[at, :, :LANES].astype(F32)
            lane = lax.broadcasted_iota(jnp.int32, short.shape, 1)
            short = jnp.where(lane < rows, short, 0.0)
            short = jnp.concatenate([short, jnp.zeros((VECTORS, width - LANES), F32)], axis=1)
            vectors = vectors + pltpu.roll(short, begin, 1)
            if at < count // 2:
                begin = pl.multiple_of(lax.div(position_ref[at], 2) * hidden, LANES)
                bias_ref[:, pl.ds(begin, hidden)] = short_ref[at, :, LANES:].astype(F32)
        vector_ref[...] = vectors
    zero = jnp.zeros((1, width), F32)
    vector = vector_ref[...]
    bias = jnp.concatenate(
        [vector[QUERY_BIAS : QUERY_BIAS + 1], zero, vector[VALUE_BIAS : VALUE_BIAS + 1]], axis=1
    )
    for at in range(0, length, ROWS):
        normal, _ = unit(x_ref[at : at + ROWS, :].astype(F32))
        low_ref[at : at + ROWS, :] = (
            normal * vector[ATTEND_GAIN : ATTEND_GAIN + 1]
            + vector[ATTEND_SHIFT : ATTEND_SHIFT + 1]
        ).astype(BF16)
    for at in range(0, 3 * width, width):
        here = slice(at, at + width)
        joined_ref[:, here] = (nn(low_ref[...], heads_ref[:, here]) + bias[:, here]).astype(BF16)


def middle_kernel(x_ref, attended_ref, out_ref, vector_ref, middle_ref, low_ref):
    vector = vector_ref[...]
    for at in range(0, x_ref.shape[0], ROWS):
        here = slice(at, at + ROWS)
        middle = (
            x_ref[here, :].astype(F32)
            + nn(attended_ref[here, :], out_ref[...])
            + vector[OUTPUT_BIAS : OUTPUT_BIAS + 1]
        )
        middle_ref[here, :] = middle
        normal, _ = unit(middle)
        low_ref[here, :] = (
            normal * vector[FORWARD_GAIN : FORWARD_GAIN + 1]
            + vector[FORWARD_SHIFT : FORWARD_SHIFT + 1]
        ).astype(BF16)


def up_kernel(position_ref, own_ref, other_ref, bias_ref, *refs):
    parts, (act_ref, slope_ref, full_ref) = refs[: len(refs) - 3], refs[len(refs) - 3 :]
    for at, part in enumerate(parts):
        rows = part.shape[0]
        begin = pl.multiple_of(position_ref[at] * rows, SUBLANES)
        full_ref[pl.ds(begin, rows), :] = part[...]
    weight = full_ref[...]
    bias = bias_ref[:1, :]
    length = own_ref.shape[0]
    for which, ref in enumerate((own_ref, other_ref)):
        for at in range(0, length, ROWS):
            upward = nn(ref[at : at + ROWS, :], weight) + bias
            share = 0.5 + 0.5 * lax.erf(upward * math.sqrt(0.5))
            bell = jnp.exp2((upward * upward) * (-0.5 * math.log2(math.e)))
            here = slice(which * length + at, which * length + at + ROWS)
            act_ref[here, :] = (upward * share).astype(BF16)
            slope = share + upward * (bell * (1.0 / math.sqrt(2.0 * math.pi)))
            slope_ref[here, :] = slope.astype(BF16)


def column_specs(half, block):
    block = min(block, half)

    def column(height):
        return pl.BlockSpec((height, block), lambda i, at: (0, i))

    return half // block, block, column


def whole_spec(shape):
    return pl.BlockSpec(shape, lambda i, at: (0,) * len(shape))


def up_project(own, other, bias, parts, positions):
    length, width = own.shape
    half = parts[0].shape[1]
    steps, _, column = column_specs(half, 512)
    whole = whole_spec((length, width))
    return call(
        up_kernel,
        [((2 * length, half), BF16), ((2 * length, half), BF16), ((width, half), BF16)],
        (own, other, bias, *parts),
        positions,
        grid=(steps,),
        in_specs=[whole, whole, column(bias.shape[0])] + [column(part.shape[0]) for part in parts],
        out_specs=[column(2 * length), column(2 * length), column(width)],
    )


def down_kernel(position_ref, act_ref, *refs):
    parts, (own_ref, other_ref, full_ref) = refs[: len(refs) - 3], refs[len(refs) - 3 :]
    length = own_ref.shape[0]
    for at, part in enumerate(parts):
        rows = part.shape[0]
        begin = pl.multiple_of(position_ref[at] * rows, SUBLANES)
        full_ref[pl.ds(begin, rows), :] = part[...]
    for which, ref in enumerate((own_ref, other_ref)):
        here = slice(which * length, (which + 1) * length)
        ref[...] = nn(act_ref[here, :], full_ref[...]).astype(ref.dtype)


def down_project(act, parts, positions):
    length = act.shape[0] // 2
    half = act.shape[1]
    width = parts[0].shape[1]
    return call(
        down_kernel,
        [((length, width), F32), ((length, width), BF16), ((half, width), BF16)],
        (act, *parts),
        positions,
        mib=20,
    )


def loss_kernel(
    middle_ref, own_ref, got_ref, vector_ref, readout_ref, target_ref, mask_ref,
    low_ref, down_ref, grad_ref, lanes_ref, sums_ref,
):
    result = (
        middle_ref[...]
        + (own_ref[...] + got_ref[...].astype(F32))
        + vector_ref[DOWN_BIAS : DOWN_BIAS + 1, :]
    ).astype(BF16)
    low_ref[...] = result
    logits = nt(readout_ref[...], result)
    length = logits.shape[1]
    top = jnp.max(logits, axis=0, keepdims=True)
    shifted = jnp.exp(logits - top)
    total = jnp.sum(shifted, axis=0, keepdims=True)
    onehot = lax.broadcasted_iota(jnp.int32, logits.shape, 0) == target_ref[...]
    picked = jnp.sum(jnp.where(onehot, logits, 0.0), axis=0, keepdims=True)
    weight = mask_ref[...].astype(F32)
    loss = (top + jnp.log(total) - picked) * weight
    loss_lanes = jnp.zeros((1, LANES), F32)
    count_lanes = jnp.zeros((1, LANES), F32)
    for at in range(0, length, LANES):
        loss_lanes = loss_lanes + loss[:, at : at + LANES]
        count_lanes = count_lanes + weight[:, at : at + LANES]
    blank = jnp.zeros((SUBLANES - 2, LANES), F32)
    lanes_ref[...] = jnp.concatenate([loss_lanes, count_lanes, blank], axis=0)
    grad_logits = (weight * (shifted / total - onehot.astype(F32))).astype(BF16)
    grad = tn(grad_logits, readout_ref[...])
    grad_ref[...] = grad
    low = grad.astype(BF16)
    down_ref[...] = low
    sums_ref[...] = jnp.sum(low.astype(F32), axis=0, keepdims=True)


def down_grad_kernel(chips, position_ref, act_ref, own_ref, other_ref, *out_refs):
    length = own_ref.shape[0]
    hidden = act_ref.shape[1] // chips
    for offset in range(chips):
        if len(out_refs) == 1:
            begin = offset * hidden
        else:
            begin = pl.multiple_of((position_ref[0] ^ offset) * hidden, LANES)
        here = pl.ds(begin, hidden)
        part = tn(act_ref[:length, here], own_ref[...]) + tn(act_ref[length:, here], other_ref[...])
        part = part.astype(BF16)
        if len(out_refs) == 1:
            out_refs[0][begin : begin + hidden, :] = part
            continue
        keep_x, send_x, keep_y, send_y = out_refs
        half = hidden // 2
        (send_x if offset % 2 else keep_x)[offset // 2, :, :] = part[:half]
        (send_y if offset // 2 else keep_y)[offset % 2, :, :] = part[half:]


def down_grad(act, own, other, chips, position):
    half = act.shape[1]
    width = own.shape[1]
    if square():
        outs = [((2, half // chips // 2, width), BF16)] * 4
    else:
        outs = [((half, width), BF16)]
    return call(
        functools.partial(down_grad_kernel, chips), outs, (act, own, other), position, mib=20
    )


def up_grad_kernel(
    rows, position_ref, own_ref, other_ref, slope_ref, second_ref, second_other_ref, down_ref,
    up_ref, bias_ref, *refs,
):
    out_refs, part_ref = refs[:-1], refs[-1]
    length = own_ref.shape[0]
    total = None
    grads = []
    for which, ref in enumerate((own_ref, other_ref)):
        for at in range(0, length, 2 * ROWS):
            here = slice(which * length + at, which * length + at + 2 * ROWS)
            grad = nt(ref[at : at + 2 * ROWS, :], down_ref[...]) * slope_ref[here, :].astype(F32)
            low = grad.astype(BF16)
            up_ref[here, :] = low
            part = jnp.sum(low.astype(F32), axis=0, keepdims=True)
            total = part if total is None else total + part
    bias_ref[...] = total
    part = tn(second_ref[...], up_ref[:length, :]) + tn(second_other_ref[...], up_ref[length:, :])
    if len(out_refs) == 1:
        out_refs[0][...] = part.astype(BF16)
        return
    part_ref[...] = part
    keep_x, send_x, keep_y, send_y = out_refs
    for offset in range(4):
        begin = pl.multiple_of((position_ref[0] ^ offset) * (2 * rows), SUBLANES)
        upper = part_ref[pl.ds(begin, rows), :].astype(BF16)
        lower = part_ref[pl.ds(begin + rows, rows), :].astype(BF16)
        (send_x if offset % 2 else keep_x)[offset // 2, :, :] = upper
        (send_y if offset // 2 else keep_y)[offset % 2, :, :] = lower


def up_grad(own, other, slope, second, second_other, down_full, rows, position):
    length, width = own.shape
    half = slope.shape[1]
    steps, block, column = column_specs(half, 512)
    whole = whole_spec((length, width))
    if square():
        outs = [((2, rows, half), BF16)] * 4
        specs = [pl.BlockSpec((2, rows, block), lambda i, at: (0, 0, i))] * 4
    else:
        outs = [((width, half), BF16)]
        specs = [column(width)]
    return call(
        functools.partial(up_grad_kernel, rows),
        [((2 * length, half), BF16), ((1, half), F32), *outs],
        (own, other, slope, second, second_other, down_full),
        position,
        grid=(steps,),
        in_specs=[
            whole, whole, column(2 * length), whole, whole,
            pl.BlockSpec((block, width), lambda i, at: (i, 0)),
        ],
        out_specs=[column(2 * length), column(1), *specs],
        scratch=[pltpu.VMEM((width, block), F32)],
        mib=20,
    )


def inward_kernel(grad_ref, up_ref, own_ref, other_ref):
    length = own_ref.shape[0]
    other_ref[...] = nt(grad_ref[length:, :], up_ref[...]).astype(BF16)
    own_ref[...] = nt(grad_ref[:length, :], up_ref[...])


def join_kernel(hidden, position_ref, mine_ref, other_ref, out_ref):
    for at in range(mine_ref.shape[1] // hidden):
        here = slice(hidden * at, hidden * (at + 1))
        for core, ref in enumerate((mine_ref, other_ref)):
            begin = (2 * at + (position_ref[0] + core) % 2) * hidden
            out_ref[:, pl.ds(pl.multiple_of(begin, LANES), hidden)] = ref[:, here].astype(F32)


def branch_kernel(
    own_ref, got_ref, middle_ref, result_ref, out_ref, vector_ref,
    grad_ref, branch_ref, attended_ref, sums_ref,
):
    width = own_ref.shape[1]
    gain = vector_ref[FORWARD_GAIN : FORWARD_GAIN + 1, :]
    sums = [jnp.zeros((1, width), F32) for _ in range(3)]
    for at in range(0, own_ref.shape[0], ROWS):
        here = slice(at, at + ROWS)
        grad = own_ref[here, :] + got_ref[here, :].astype(F32)
        normal, inverse = unit(middle_ref[here, :])
        middle = result_ref[here, :] + unit_back(grad, normal, inverse, gain)
        grad_ref[here, :] = middle
        branch = middle.astype(BF16)
        branch_ref[here, :] = branch
        attended_ref[here, :] = nt(branch, out_ref[...]).astype(BF16)
        for which, part in enumerate((grad * normal, grad, branch.astype(F32))):
            sums[which] = sums[which] + jnp.sum(part, axis=0, keepdims=True)
    blank = jnp.zeros((SUBLANES - 3, width), F32)
    sums_ref[...] = jnp.concatenate([*sums, blank], axis=0)


def last_kernel(count, rows, hidden, pieces, position_ref, x_ref, low_ref, *refs):
    grad_refs, refs = refs[: 3 * pieces], refs[3 * pieces :]
    heads_ref, attended_ref, branch_ref, grad_ref, vector_ref, *refs = refs
    sums_ref, down_ref, up_ref, lanes_ref, *refs = refs
    slabs, (input_ref, vectors_ref, full_ref) = refs[:count], refs[count:]
    width = x_ref.shape[1]

    def grads(which, here):
        parts = [ref[here, :] for ref in grad_refs[which::3]]
        return jnp.concatenate(parts, axis=1) if pieces > 1 else parts[0]

    for at in range(3):
        part = tn(low_ref[...], grads(at, slice(None)))
        full_ref[:, width * at : width * (at + 1)] = part.astype(BF16)
    full_ref[:, 3 * width :] = tn(attended_ref[...], branch_ref[...]).astype(BF16)
    gain = vector_ref[ATTEND_GAIN : ATTEND_GAIN + 1, :]
    sums = [jnp.zeros((1, width), F32) for _ in range(4)]
    for at in range(0, x_ref.shape[0], ROWS):
        here = slice(at, at + ROWS)
        grad_query, grad_key, grad_value = [grads(at, here) for at in range(3)]
        grad = (
            nt(grad_query, heads_ref[:, :width])
            + nt(grad_key, heads_ref[:, width : 2 * width])
            + nt(grad_value, heads_ref[:, 2 * width :])
        )
        normal, inverse = unit(x_ref[here, :].astype(F32))
        input_ref[here, :] = grad_ref[here, :] + unit_back(grad, normal, inverse, gain)
        parts = (grad * normal, grad, grad_query.astype(F32), grad_value.astype(F32))
        for which, part in enumerate(parts):
            sums[which] = sums[which] + jnp.sum(part, axis=0, keepdims=True)
    vectors = jnp.concatenate(
        [*sums, sums_ref[2:3, :], sums_ref[0:1, :], sums_ref[1:2, :], down_ref[...]], axis=0
    )
    vectors_ref[...] = vectors
    blank = jnp.zeros((VECTORS - 1, hidden), F32)
    for at, slab in enumerate(slabs):
        place_at = position_ref[at]
        begin = pl.multiple_of(place_at * rows, SUBLANES)
        slab[:rows, :] = full_ref[pl.ds(begin, rows), :]
        short = pltpu.roll(vectors, width - begin, 1)[:, :LANES]
        if at < count // 2:
            hidden_at = pl.multiple_of(lax.div(place_at, 2) * hidden, LANES)
            bias = jnp.concatenate([up_ref[:, pl.ds(hidden_at, hidden)], blank], axis=0)
        else:
            bias = jnp.zeros((VECTORS, hidden), F32)
        row = jnp.concatenate([short, bias, lanes_ref[...]], axis=1).astype(BF16)
        pad = jnp.zeros((VECTORS, 4 * width - row.shape[1]), BF16)
        slab[rows:, :] = jnp.concatenate([row, pad], axis=1)


def swap(values, bit):
    return lax.ppermute(values, "wide", [(i, i ^ bit) for i in range(lax.axis_size("wide"))])


def same_core_groups():
    chips = lax.axis_size("wide") // 2
    return [[2 * chip + core for chip in range(chips)] for core in range(2)]


def square():
    return lax.axis_size("wide") == 8


def spread_chips(shard):
    return lax.all_gather(shard, "wide", axis=0, axis_index_groups=same_core_groups())


def add_low(*parts):
    return sum(part.astype(F32) for part in parts).astype(BF16)


def collect_chips(parts):
    return lax.psum_scatter(
        parts, "wide", scatter_dimension=0, axis_index_groups=same_core_groups()
    )


def after(values, *gates):
    leaves, tree = jax.tree.flatten(values)
    held = lax.optimization_barrier((*leaves, *jax.tree.leaves(gates)))
    return jax.tree.unflatten(tree, held[: len(leaves)])


INWARD, ACROSS, OUTWARD = [(0, 1), (3, 2)], [(1, 2), (2, 1)], [(1, 0), (2, 3)]


def hop(parts, pairs):
    return [lax.ppermute(part, "narrow", pairs) for part in parts]


def add_each(left, right):
    return [add_low(a, b) for a, b in zip(left, right)]


def settle(total, outer):
    place_at = lax.axis_index("narrow")
    return jnp.where((place_at == 1) | (place_at == 2), total, outer)


def sum_narrow(shard):
    if lax.axis_size("narrow") != 4:
        return lax.psum(shard, "narrow")
    half = add_low(shard, *hop([shard], INWARD))
    total = add_low(half, *hop([half], ACROSS))
    return settle(total, *hop([total], OUTWARD))


def local(
    layer_input, segments, targets, loss_mask, readout,
    attend_gain, attend_shift, heads_weight, query_bias, value_bias, output_weight, output_bias,
    forward_gain, forward_shift, up_weight, up_bias, down_weight, down_bias,
):
    length = layer_input.shape[1]
    width = layer_input.shape[2]
    wide = lax.axis_size("wide")
    chips = wide // 2
    core = lax.axis_index("wide") % 2
    chip = lax.axis_index("wide") // 2
    rows = heads_weight.shape[0]
    hidden = up_bias.shape[0]
    half = chips * hidden
    x = layer_input[0]
    column = segments.reshape(length, 1)

    def by_core(mine, other, axis):
        return jnp.where(
            core == 0, jnp.stack([mine, other], axis), jnp.stack([other, mine], axis)
        )

    def mine_of(values, axis, flip=0):
        return lax.dynamic_index_in_dim(values, core ^ flip, axis, keepdims=False)

    short = jnp.stack(
        [
            attend_gain, attend_shift, query_bias, value_bias,
            output_bias, forward_gain, forward_shift, down_bias,
        ]
    )
    core_position = core.reshape(1).astype(jnp.int32)
    chip_position = chip.reshape(1).astype(jnp.int32)
    if square():
        offsets = jnp.arange(4, dtype=jnp.int32)
        (slab,) = call(
            slab_kernel,
            [((rows + VECTORS, 4 * width), BF16)],
            (heads_weight, output_weight, short, up_bias[None]),
        )
        near_x, near_y, far = swap(slab, 2), swap(slab, 4), swap(slab, 6)
        (up_weight,) = after([up_weight], near_x)
        up_mine, up_other = call(
            functools.partial(halves_kernel, hidden),
            [((rows, half), BF16)] * 2,
            (up_weight,),
            core_position,
        )
        other_x, mine_y = swap(up_other, 3), swap(up_mine, 4)
        mine_x, other_y = swap(up_mine, 2), swap(up_other, 5)
        (far,) = after([far], up_mine)
        slabs = [slab, near_x, near_y, far]
        slabs = slabs + [swap(part, 1) for part in slabs]
        devices = 2 * (chip ^ offsets) + core
        positions = jnp.concatenate([devices, devices ^ 1]).astype(jnp.int32)
        up_positions = positions
        first_low, joined, heads_full, output_full, vectors, up_bias_half = call(
            functools.partial(project_kernel, len(slabs), rows, hidden),
            [
                ((length, width), BF16), ((length, 3 * width), BF16), ((width, 3 * width), BF16),
                ((width, width), BF16), ((VECTORS, width), F32), ((VECTORS, half), F32),
            ],
            (x, *slabs),
            positions,
            in_specs=[pl.BlockSpec(memory_space=pltpu.VMEM)]
            + [pl.BlockSpec(memory_space=pltpu.HBM)] * len(slabs),
            scratch=[
                pltpu.VMEM((len(slabs), VECTORS, LANES + hidden), BF16),
                pltpu.SemaphoreType.DMA((len(slabs), 3)),
            ],
            mib=20,
        )
    else:
        tail = jnp.concatenate([short.reshape(1, 8 * rows), up_bias[None]], axis=1)
        tail = jnp.pad(tail, ((0, 0), (0, 4 * width - tail.shape[1])))
        slab = jnp.concatenate(
            [jnp.concatenate([heads_weight, output_weight], axis=1), tail], axis=0
        )
        slabs = lax.all_gather(slab, "wide", axis=0)
        attend_full = slabs[:, :rows].reshape(width, 4 * width)
        heads_full = attend_full[:, : 3 * width]
        output_full = attend_full[:, 3 * width :]
        last = slabs[:, rows].astype(F32)
        vectors = last[:, : 8 * rows].reshape(wide, 8, rows).transpose(1, 0, 2).reshape(8, width)
        up_bias_half = mine_of(last[:, 8 * rows : 8 * rows + hidden].reshape(chips, 2, hidden), 1)
        up_bias_half = jnp.broadcast_to(up_bias_half.reshape(1, half), (VECTORS, half))
        positions = jnp.zeros((1,), jnp.int32)
        first_low, joined = call(
            functools.partial(project_kernel, 0, rows, hidden),
            [((length, width), BF16), ((length, 3 * width), BF16)],
            (x, heads_full, vectors),
            positions,
            mib=20,
        )
        up_view = up_weight.reshape(rows, chips, 2, hidden)
        up_pair = by_core(
            mine_of(up_view, 2).reshape(rows, half),
            swap(mine_of(up_view, 2, 1).reshape(rows, half), 1),
            0,
        ).reshape(2 * rows, half)
        up_parts = [spread_chips(up_pair).reshape(width, half)]
        down_parts = [spread_chips(down_weight).reshape(half, width)]
        up_positions = down_positions = positions

    attended, across, lse = attend(joined, column, segments)
    if square():
        passed_y, passed_x = after([mine_y, other_x], attended)
        up_parts = [
            up_mine, mine_x, mine_y, swap(passed_y, 2),
            swap(up_other, 1), other_x, other_y, swap(passed_x, 4),
        ]
        middle_row = hidden // 2
        upper, lower = after(
            [down_weight[:middle_row], down_weight[middle_row:]], mine_x, other_y, attended
        )
        lower_x, upper_y = swap(lower, 2), swap(upper, 4)
        upper_x, lower_y = swap(upper, 2), swap(lower, 4)
        down_parts = [
            down_weight, upper_x, lower_x, upper_y, lower_y, swap(upper_y, 2), swap(lower_x, 4)
        ]
        at = jnp.arange(7, dtype=jnp.int32)
        down_positions = jnp.where(at == 0, chip, 2 * (chip ^ ((at + 1) // 2)) + (at + 1) % 2)
    middle, second_low = call(
        middle_kernel,
        [((length, width), F32), ((length, width), BF16)],
        (x, attended, output_full, vectors),
    )

    second_other = swap(second_low, 1)
    activated, slope, up_full = up_project(
        second_low, second_other, up_bias_half, up_parts, up_positions
    )
    outward, outward_other, down_full = down_project(activated, down_parts, down_positions)
    result_low, grad_down, grad_result, lanes, down_bias_part = call(
        loss_kernel,
        [
            ((length, width), BF16), ((length, width), BF16), ((length, width), F32),
            ((SUBLANES, LANES), F32), ((1, width), F32),
        ],
        (middle, outward, swap(outward_other, 1), vectors, readout.T, targets, loss_mask),
    )

    grad_down_other = swap(grad_down, 1)
    down_parts = down_grad(activated, grad_down, grad_down_other, chips, chip_position)
    if square():
        keep_dx, send_dx, keep_dy, send_dy = down_parts
        down_first = [swap(send_dx, 2), swap(send_dy, 4)]
        (grad_down_other,) = after([grad_down_other], send_dx)
    grad_up, up_bias_part, *up_parts = up_grad(
        grad_down, grad_down_other, slope, second_low, second_other, down_full, rows, chip_position
    )
    inward, inward_other = call(
        inward_kernel,
        [((length, width), F32), ((length, width), BF16)],
        (grad_up, up_full),
        mib=20,
    )
    got_inward = swap(inward_other, 1)
    if square():
        down_second = [
            add_low(keep_dx[1], down_first[0][1]), add_low(keep_dy[1], down_first[1][1])
        ]
        (got_inward,) = after([got_inward], down_second)
        keep_ux, send_ux, keep_uy, send_uy = up_parts
        send_ux, send_uy = after([send_ux, send_uy], down_second)
        down_got = [swap(down_second[0], 4), swap(down_second[1], 2)]
        up_first = [swap(send_ux, 2), swap(send_uy, 4)]
    grad_middle, grad_branch, grad_attended, branch_sums = call(
        branch_kernel,
        [
            ((length, width), F32), ((length, width), BF16), ((length, width), BF16),
            ((SUBLANES, width), F32),
        ],
        (inward, got_inward, middle, grad_result, output_full, vectors),
    )

    if square():
        early = 3
        first_grads = attend_back(
            joined, column, segments, grad_attended, across, lse, 0, early
        )
        down_narrow = [
            add_low(keep_dx[0], down_first[0][0], after([down_got[0]], first_grads[0])[0]),
            add_low(keep_dy[0], down_first[1][0], after([down_got[1]], first_grads[0])[0]),
        ]
        down_in = hop(down_narrow, INWARD)
        (grad_attended,) = after([grad_attended], down_narrow)
        last_grads = attend_back(
            joined, column, segments, grad_attended, across, lse, early
        )
        attend_grads = [*first_grads, *last_grads]
    else:
        attend_grads = attend_back(joined, column, segments, grad_attended, across, lse)
    slab_shape = ((rows + VECTORS, 4 * width), BF16)
    *slabs, input_grad, short_sums, attend_part = call(
        functools.partial(last_kernel, 8 if square() else 0, rows, hidden, len(attend_grads) // 3),
        ([slab_shape] * 8 if square() else [])
        + [((length, width), F32), ((VECTORS, width), F32), ((width, 4 * width), BF16)],
        (
            x, first_low, *attend_grads, heads_full, attended, grad_branch,
            grad_middle, vectors, branch_sums, down_bias_part, up_bias_part, lanes,
        ),
        positions,
        mib=40,
    )
    if square():
        slab_got = [swap(slabs[4 + at], 1) for at in (3, 1, 2, 0)]
        up_first = after(up_first, slabs[7])
        up_second = [add_low(keep_ux[1], up_first[0][1]), add_low(keep_uy[1], up_first[1][1])]
        up_got = [swap(up_second[0], 4), swap(up_second[1], 2)]

        down_half, down_mid = [], []
        gate = up_second
        for at in range(2):
            (came,) = after([down_in[at]], gate)
            down_half.append(add_low(down_narrow[at], came))
            down_mid += hop(down_half[-1:], ACROSS)
            gate = down_half[-1:]

        slab_got = after(slab_got, gate)
        both = [add_low(slabs[at], got) for at, got in zip((3, 1, 2, 0), slab_got)]
        slab_far = [swap(both[0], 6), swap(both[1], 2), swap(both[2], 4)]

        up_got = after(up_got, both)
        up_narrow = [
            add_low(keep_ux[0], up_first[0][0], up_got[0]),
            add_low(keep_uy[0], up_first[1][0], up_got[1]),
        ]
        up_in = hop(up_narrow, INWARD)

        gate = up_narrow
        down_total, down_out = [], []
        for at in range(2):
            (came,) = after([down_mid[at]], gate)
            down_total.append(add_low(down_half[at], came))
            down_out += hop(down_total[-1:], OUTWARD)
            gate = down_total[-1:]

        up_half, up_mid = [], []
        (came,) = after(up_in[:1], gate)
        up_half.append(add_low(up_narrow[0], came))
        up_mid += hop(up_half, ACROSS)

        slab_far = after(slab_far, up_half)
        cut = rows // 2 // SUBLANES * SUBLANES
        slab_narrow = [
            add_low(both[3][part], *[far[part] for far in slab_far])
            for part in (slice(0, cut), slice(cut, None))
        ]
        slab_in = hop(slab_narrow, INWARD)

        (came,) = after(up_in[1:], slab_narrow)
        up_half.append(add_low(up_narrow[1], came))
        up_mid += hop(up_half[1:], ACROSS)

        (came,) = after(up_mid[:1], up_half[1])
        up_total = [add_low(up_half[0], came)]
        up_out = hop(up_total, OUTWARD)

        gate = up_total
        slab_half, slab_mid = [], []
        for at in range(2):
            (came,) = after([slab_in[at]], gate)
            slab_half.append(add_low(slab_narrow[at], came))
            slab_mid += hop(slab_half[-1:], ACROSS)
            gate = slab_half[-1:]

        (came,) = after(up_mid[1:], gate)
        up_total.append(add_low(up_half[1], came))
        up_out += hop(up_total[1:], OUTWARD)

        gate = up_total[1]
        slab_total, slab_out = [], []
        for at in range(2):
            (came,) = after([slab_mid[at]], gate)
            slab_total.append(add_low(slab_half[at], came))
            slab_out += hop(slab_total[-1:], OUTWARD)
            gate = slab_total[-1:]

        down_out = after(down_out, gate)
        down_weight_sum = jnp.concatenate(
            [settle(*pair) for pair in zip(down_total, down_out)]
        ).astype(F32)
        up_out = after(up_out, gate)
        upper, lower = [settle(*pair) for pair in zip(up_total, up_out)]
        first = core == 0
        (up_weight_sum,) = call(
            functools.partial(join_kernel, hidden),
            [((rows, 2 * half), F32)],
            (jnp.where(first, upper, lower), swap(jnp.where(first, lower, upper), 1)),
            core_position,
        )
        slab = jnp.concatenate([settle(*pair) for pair in zip(slab_total, slab_out)]).astype(F32)
        vectors_sum = slab[rows:, :rows]
        up_bias_grad = slab[rows, LANES : LANES + hidden]
        lanes_sum = slab[rows : rows + 2, LANES + hidden : 2 * LANES + hidden]
        loss_sum = jnp.sum(lanes_sum[0])
        token_count = jnp.round(jnp.sum(lanes_sum[1])).astype(jnp.int32)
    else:
        down_weight_sum = collect_chips(down_parts[0].reshape(chips, hidden, width))
        down_weight_sum = sum_narrow(down_weight_sum).astype(F32)
        up_sum = sum_narrow(collect_chips(up_parts[0].reshape(chips, 2 * rows, half)))
        up_sum = up_sum.reshape(2, rows, chips, hidden)
        up_weight_sum = by_core(mine_of(up_sum, 0), swap(mine_of(up_sum, 0, 1), 1), 2)
        up_weight_sum = up_weight_sum.reshape(rows, 2 * half).astype(F32)
        short = short_sums.reshape(8, wide, rows).transpose(1, 0, 2).reshape(wide, 8 * rows)
        up_bias_rows = up_bias_part.reshape(chips, hidden)
        up_bias_rows = by_core(up_bias_rows, jnp.zeros_like(up_bias_rows), 1).reshape(wide, hidden)
        shared = jnp.broadcast_to(lanes[:1], (wide, LANES))
        row = jnp.concatenate([short, up_bias_rows, shared], axis=1).astype(BF16)
        row = jnp.pad(row, ((0, 0), (0, 4 * width - row.shape[1])))
        slab = jnp.concatenate([attend_part.reshape(wide, rows, 4 * width), row[:, None]], axis=1)
        slab = sum_narrow(lax.psum_scatter(slab, "wide", scatter_dimension=0)).astype(F32)
        vectors_sum = slab[rows, : 8 * rows].reshape(8, rows)
        up_bias_grad = slab[rows, 8 * rows : 8 * rows + hidden]
        loss_sum = jnp.sum(slab[rows, 8 * rows + hidden : 8 * rows + hidden + LANES])
        token_count = lax.psum(jnp.sum(loss_mask), ("narrow", "wide"))
    return (
        result_low[None],
        input_grad[None],
        vectors_sum[ATTEND_GAIN],
        vectors_sum[ATTEND_SHIFT],
        slab[:rows, : 3 * width],
        vectors_sum[QUERY_BIAS],
        vectors_sum[VALUE_BIAS],
        slab[:rows, 3 * width :],
        vectors_sum[OUTPUT_BIAS],
        vectors_sum[FORWARD_GAIN],
        vectors_sum[FORWARD_SHIFT],
        up_weight_sum,
        up_bias_grad,
        down_weight_sum,
        vectors_sum[DOWN_BIAS],
        loss_sum,
        token_count,
    )


def solution(mesh):
    in_specs = (
        P(("narrow", "wide"), None, None),
        P(("narrow", "wide"), None),
        P(("narrow", "wide"), None),
        P(("narrow", "wide"), None),
        P(),
        P("wide"),
        P("wide"),
        P("wide", None),
        P("wide"),
        P("wide"),
        P("wide", None),
        P("wide"),
        P("wide"),
        P("wide"),
        P("wide", None),
        P("wide"),
        P("wide", None),
        P("wide"),
    )
    out_specs = (
        P(("narrow", "wide"), None, None),
        P(("narrow", "wide"), None, None),
        P("wide"),
        P("wide"),
        P("wide", None),
        P("wide"),
        P("wide"),
        P("wide", None),
        P("wide"),
        P("wide"),
        P("wide"),
        P("wide", None),
        P("wide"),
        P("wide", None),
        P("wide"),
        P(),
        P(),
    )
    return jax.shard_map(local, mesh=mesh, in_specs=in_specs, out_specs=out_specs, check_vma=False)
```

```python
import functools
import math

import jax
import jax.numpy as jnp
from jax import lax
from jax.experimental import pallas as pl
from jax.experimental.pallas import tpu as pltpu
from jax.sharding import PartitionSpec as P

HEADS = 20
HEAD_DIM = 32
LANES = 128
SUBLANES = 8
SEGMENTS = 8
REACH = 192
CHUNK = 256
ROWS = 128
SCALE = 1.0 / math.sqrt(HEAD_DIM)
SCALE2 = math.log2(math.e) * SCALE
F32 = jnp.float32
BF16 = jnp.bfloat16
VECTORS = 8
ATTEND_GAIN, ATTEND_SHIFT, QUERY_BIAS, VALUE_BIAS = 0, 1, 2, 3
OUTPUT_BIAS, FORWARD_GAIN, FORWARD_SHIFT, DOWN_BIAS = 4, 5, 6, 7


def nn(left, right):
    return lax.dot_general(left, right, (((1,), (0,)), ((), ())), preferred_element_type=F32)


def nt(left, right):
    return lax.dot_general(left, right, (((1,), (1,)), ((), ())), preferred_element_type=F32)


def tn(left, right):
    return lax.dot_general(left, right, (((0,), (0,)), ((), ())), preferred_element_type=F32)


def call(kernel, outs, args, positions=None, grid=None, in_specs=None, out_specs=None, scratch=(),
         mib=16):
    whole = pl.BlockSpec(memory_space=pltpu.VMEM)
    in_specs = in_specs or [whole] * len(args)
    args = [
        pltpu.with_memory_space_constraint(arg, pltpu.HBM)
        if spec.memory_space == pltpu.HBM
        else arg
        for arg, spec in zip(args, in_specs)
    ]
    out_specs = out_specs or [whole] * len(outs)
    shapes = [jax.ShapeDtypeStruct(shape, dtype) for shape, dtype in outs]
    extra = [] if positions is None else [positions]
    return pl.pallas_call(
        kernel,
        out_shape=shapes,
        grid_spec=pltpu.PrefetchScalarGridSpec(
            num_scalar_prefetch=len(extra),
            grid=grid or (),
            in_specs=in_specs,
            out_specs=out_specs,
            scratch_shapes=list(scratch),
        ),
        compiler_params=pltpu.CompilerParams(vmem_limit_bytes=mib * 1024 * 1024),
        cost_estimate=pl.CostEstimate(flops=1, bytes_accessed=1, transcendentals=0),
    )(*extra, *args)


def unit(values):
    centred = values - jnp.mean(values, axis=-1, keepdims=True)
    spread = jnp.mean(centred * centred, axis=-1, keepdims=True)
    inverse = lax.rsqrt(spread + 1e-05)
    return centred * inverse, inverse


def unit_back(grad, normal, inverse, gain):
    scaled = grad * gain
    mean = jnp.mean(scaled, axis=-1, keepdims=True)
    along = jnp.mean(scaled * normal, axis=-1, keepdims=True)
    return inverse * (scaled - mean - normal * along)


def spans(length):
    chunk = min(CHUNK, length)
    return [
        (at, at + chunk, max(0, at - REACH), min(length, at + chunk + REACH))
        for at in range(0, length, chunk)
    ]


def split3(values):
    first = values.astype(BF16).astype(F32)
    rest = values - first
    second = rest.astype(BF16).astype(F32)
    return [first, second, rest - second]


def key_marks(segment_column):
    lane = lax.broadcasted_iota(jnp.int32, (segment_column.shape[0], LANES), 1)
    ones = (lane >= SEGMENTS) & (lane < SEGMENTS + 3)
    return jnp.where((lane == segment_column) | ones, 1.0, 0.0).astype(BF16)


def query_marks(segment_row):
    row = lax.broadcasted_iota(jnp.int32, (SEGMENTS, segment_row.shape[1]), 0)
    return jnp.where(row == segment_row, 0.0, -1e30)


def place(rows, head, marks):
    count = rows.shape[1]
    parts = [rows, marks, jnp.zeros((LANES - marks.shape[0], count), BF16)]
    if head < LANES // HEAD_DIM - 1:
        parts.insert(1, jnp.zeros((LANES - HEAD_DIM * (head + 1), count), BF16))
    if head:
        parts.insert(0, jnp.zeros((HEAD_DIM * head, count), BF16))
    return jnp.concatenate(parts, axis=0)


def attend_kernel(column_ref, row_ref, q_ref, k_ref, v_ref, out_ref, across_ref, lse_ref, marks_ref):
    @pl.when(pl.program_id(0) == 0)
    def _():
        marks_ref[...] = key_marks(column_ref[...])

    length = q_ref.shape[0]
    heads = LANES // HEAD_DIM
    queries = q_ref[...].T
    values = v_ref[...].T
    keys = jnp.concatenate([k_ref[...], marks_ref[...]], axis=1)
    blank = jnp.zeros((SUBLANES, length), F32)
    marks = jnp.concatenate([query_marks(row_ref[...]), blank], axis=0).astype(BF16)
    ones = jnp.ones((SUBLANES, length), BF16)
    bodies = [(head, span) for head in range(heads) for span in spans(length)]

    def rows(head):
        return slice(HEAD_DIM * head, HEAD_DIM * (head + 1))

    summed = [jnp.concatenate([values[rows(head)], ones], axis=0) for head in range(heads)]

    def score(head, span):
        begin, end, low, high = span
        return nn(keys[low:high], place(queries[rows(head), begin:end], head, marks[:, begin:end]))

    def finish(head, span, top, probs):
        begin, end, low, high = span
        out = nn(summed[head][:, low:high], probs)
        total = out[HEAD_DIM : HEAD_DIM + 1]
        across_ref[rows(head), begin:end] = out[:HEAD_DIM] * (1.0 / total)
        lse_ref[head : head + 1, begin:end] = (top + jnp.log2(total)) * (1.0 / SCALE2)

    scores = [score(*body) for body in bodies[:2]]
    waiting = None
    for at, body in enumerate(bodies):
        current = scores.pop(0)
        if at + 2 < len(bodies):
            scores.append(score(*bodies[at + 2]))
        top = jnp.max(current, axis=0, keepdims=True) * SCALE2
        probs = jnp.exp2(current * SCALE2 - top).astype(BF16)
        if waiting is not None:
            finish(*waiting)
        waiting = (*body, top, probs)
    finish(*waiting)
    lse_ref[heads:, :] = jnp.zeros((SUBLANES - heads, length), F32)
    out_ref[...] = across_ref[...].T.astype(BF16)


def attend_back_kernel(
    column_ref, row_ref, q_ref, k_ref, v_ref, grad_ref, across_ref, lse_ref,
    gq_ref, gk_ref, gv_ref, marks_ref, turned_ref,
):
    @pl.when(pl.program_id(0) == 0)
    def _():
        marks_ref[...] = key_marks(column_ref[...])

    length = q_ref.shape[0]
    grad = grad_ref[...]
    queries = q_ref[...].T
    turned_keys = k_ref[...].T
    grads = grad.T
    keys = jnp.concatenate([k_ref[...], marks_ref[...]], axis=1)
    values = jnp.concatenate([v_ref[...], marks_ref[...]], axis=1)
    low_marks = query_marks(row_ref[...])
    blank = jnp.zeros((SUBLANES, length), F32)
    lane = lax.broadcasted_iota(jnp.int32, (1, LANES), 1) // HEAD_DIM
    heads = []
    for head in range(LANES // HEAD_DIM):
        rows = slice(HEAD_DIM * head, HEAD_DIM * (head + 1))
        inner = jnp.sum(grads[rows].astype(F32) * across_ref[rows, :], axis=0, keepdims=True)
        lse = lse_ref[head : head + 1, :]
        score_marks = jnp.concatenate([low_marks, *split3(-lse), blank[:5]], axis=0)
        inner_marks = jnp.concatenate([blank, *split3(-inner), blank[:5]], axis=0)
        zero = jnp.zeros_like(grad)
        heads.append(
            (
                rows,
                score_marks.astype(BF16),
                inner_marks.astype(BF16),
                jnp.where(lane == head, q_ref[...], zero),
                jnp.where(lane == head, grad, zero),
            )
        )
    bodies = [
        (head, at, span) for head in range(len(heads)) for at, span in enumerate(spans(length))
    ]
    sums = [[None, None] for _ in spans(length)]

    def pair(head, at, span):
        begin, end, low, high = span
        rows, score_marks, inner_marks, _, _ = heads[head]
        return (
            nn(keys[low:high], place(queries[rows, begin:end], head, score_marks[:, begin:end])),
            nn(values[low:high], place(grads[rows, begin:end], head, inner_marks[:, begin:end])),
        )

    def finish(head, at, span, score_grads, probs):
        begin, end, low, high = span
        rows, _, _, own_queries, own_grads = heads[head]
        for which, (left, right) in enumerate(
            ((score_grads, own_queries[begin:end]), (probs, own_grads[begin:end]))
        ):
            part = nn(left, right)
            sums[at][which] = part if sums[at][which] is None else sums[at][which] + part
        turned_ref[rows, begin:end] = nn(turned_keys[rows, low:high], score_grads)

    ahead = [pair(*bodies[0])]
    waiting = None
    for at, body in enumerate(bodies):
        scores, differences = ahead.pop(0)
        if at + 1 < len(bodies):
            ahead.append(pair(*bodies[at + 1]))
        probs = jnp.exp2(scores * SCALE2)
        score_grads = (probs * differences).astype(BF16)
        if waiting is not None:
            finish(*waiting)
        waiting = (*body, score_grads, probs.astype(BF16))
    finish(*waiting)
    gq_ref[...] = (turned_ref[...].T * SCALE).astype(BF16)
    for which, (ref, factor) in enumerate(((gk_ref, SCALE), (gv_ref, 1.0))):
        total = None
        for at, (_, _, low, high) in enumerate(spans(length)):
            parts = [sums[at][which]]
            if low:
                parts.insert(0, jnp.zeros((low, LANES), F32))
            if high < length:
                parts.append(jnp.zeros((length - high, LANES), F32))
            part = jnp.concatenate(parts, axis=0) if len(parts) > 1 else parts[0]
            total = part if total is None else total + part
        ref[...] = (total * factor).astype(BF16)


def attention_specs(length, width, begin=0):
    tiles = width // LANES

    def tile(at, begin=begin):
        return pl.BlockSpec((length, LANES), lambda i: (0, at + begin + i))

    return (
        tiles,
        tile,
        pl.BlockSpec((length, 1), lambda i: (0, 0)),
        pl.BlockSpec((1, length), lambda i: (0, 0)),
        pl.BlockSpec((LANES, length), lambda i: (begin + i, 0)),
        pl.BlockSpec((SUBLANES, length), lambda i: (begin + i, 0)),
    )


def attend(joined, column, row):
    length = joined.shape[0]
    width = joined.shape[1] // 3
    tiles, tile, column_spec, row_spec, across_spec, lse_spec = attention_specs(length, width)
    return call(
        attend_kernel,
        [((length, width), BF16), ((width, length), F32), ((SUBLANES * tiles, length), F32)],
        (column, row, joined, joined, joined),
        grid=(tiles,),
        in_specs=[column_spec, row_spec, tile(0), tile(tiles), tile(2 * tiles)],
        out_specs=[tile(0), across_spec, lse_spec],
        scratch=[pltpu.VMEM((length, LANES), BF16)],
    )


def attend_back(joined, column, row, grad, across, lse, begin=0, end=None):
    length = joined.shape[0]
    width = joined.shape[1] // 3
    specs = attention_specs(length, width, begin)
    tiles, tile, column_spec, row_spec, across_spec, lse_spec = specs
    count = (end or tiles) - begin
    return call(
        attend_back_kernel,
        [((length, count * LANES), BF16)] * 3,
        (column, row, joined, joined, joined, grad, across, lse),
        grid=(count,),
        in_specs=[column_spec, row_spec, tile(0), tile(tiles), tile(2 * tiles), tile(0), across_spec, lse_spec],
        out_specs=[tile(0, 0)] * 3,
        scratch=[pltpu.VMEM((length, LANES), BF16), pltpu.VMEM((LANES, length), F32)],
        mib=24,
    )


def slab_kernel(heads_ref, out_ref, short_ref, up_ref, slab_ref):
    rows = heads_ref.shape[0]
    width = out_ref.shape[1]
    slab_ref[:rows, : 3 * width] = heads_ref[...]
    slab_ref[:rows, 3 * width :] = out_ref[...]
    slab_ref[rows:, :] = jnp.zeros((VECTORS, 4 * width), BF16)
    slab_ref[rows:, :rows] = short_ref[...]
    slab_ref[rows:, LANES : LANES + up_ref.shape[1]] = jnp.broadcast_to(
        up_ref[...], (VECTORS, up_ref.shape[1])
    )


def halves_kernel(hidden, position_ref, up_ref, mine_ref, other_ref):
    for at in range(mine_ref.shape[1] // hidden):
        here = slice(hidden * at, hidden * (at + 1))
        for core, ref in enumerate((mine_ref, other_ref)):
            begin = (2 * at + (position_ref[0] + core) % 2) * hidden
            ref[:, here] = up_ref[:, pl.ds(pl.multiple_of(begin, LANES), hidden)]


def project_kernel(count, rows, hidden, position_ref, x_ref, *refs):
    slabs, refs = refs[:count], refs[count:]
    length, width = x_ref.shape
    if count:
        low_ref, joined_ref, heads_ref, out_ref, vector_ref, bias_ref, short_ref, sems = refs
        copies = []
        for at, slab in enumerate(slabs):
            begin = pl.multiple_of(position_ref[at] * rows, SUBLANES)
            here = pl.ds(begin, rows)
            for which, (source, target) in enumerate(
                (
                    (slab.at[pl.ds(0, rows), pl.ds(0, 3 * width)], heads_ref.at[here]),
                    (slab.at[pl.ds(0, rows), pl.ds(3 * width, width)], out_ref.at[here]),
                    (slab.at[pl.ds(rows, VECTORS), pl.ds(0, LANES + hidden)], short_ref.at[at]),
                )
            ):
                copy = pltpu.make_async_copy(source, target, sems.at[at, which])
                copy.start()
                copies.append(copy)
    else:
        heads_ref, vector_ref, low_ref, joined_ref = refs
    if count:
        for copy in copies:
            copy.wait()
        vectors = jnp.zeros((VECTORS, width), F32)
        for at in range(count):
            begin = position_ref[at] * rows
            short = short_ref[at, :, :LANES].astype(F32)
            lane = lax.broadcasted_iota(jnp.int32, short.shape, 1)
            short = jnp.where(lane < rows, short, 0.0)
            short = jnp.concatenate([short, jnp.zeros((VECTORS, width - LANES), F32)], axis=1)
            vectors = vectors + pltpu.roll(short, begin, 1)
            if at < count // 2:
                begin = pl.multiple_of(lax.div(position_ref[at], 2) * hidden, LANES)
                bias_ref[:, pl.ds(begin, hidden)] = short_ref[at, :, LANES:].astype(F32)
        vector_ref[...] = vectors
    zero = jnp.zeros((1, width), F32)
    vector = vector_ref[...]
    bias = jnp.concatenate(
        [vector[QUERY_BIAS : QUERY_BIAS + 1], zero, vector[VALUE_BIAS : VALUE_BIAS + 1]], axis=1
    )
    for at in range(0, length, ROWS):
        normal, _ = unit(x_ref[at : at + ROWS, :].astype(F32))
        low_ref[at : at + ROWS, :] = (
            normal * vector[ATTEND_GAIN : ATTEND_GAIN + 1]
            + vector[ATTEND_SHIFT : ATTEND_SHIFT + 1]
        ).astype(BF16)
    for at in range(0, 3 * width, width):
        here = slice(at, at + width)
        joined_ref[:, here] = (nn(low_ref[...], heads_ref[:, here]) + bias[:, here]).astype(BF16)


def middle_kernel(x_ref, attended_ref, out_ref, vector_ref, middle_ref, low_ref):
    vector = vector_ref[...]
    for at in range(0, x_ref.shape[0], ROWS):
        here = slice(at, at + ROWS)
        middle = (
            x_ref[here, :].astype(F32)
            + nn(attended_ref[here, :], out_ref[...])
            + vector[OUTPUT_BIAS : OUTPUT_BIAS + 1]
        )
        middle_ref[here, :] = middle
        normal, _ = unit(middle)
        low_ref[here, :] = (
            normal * vector[FORWARD_GAIN : FORWARD_GAIN + 1]
            + vector[FORWARD_SHIFT : FORWARD_SHIFT + 1]
        ).astype(BF16)


def up_kernel(position_ref, own_ref, other_ref, bias_ref, *refs):
    parts, (act_ref, slope_ref, full_ref) = refs[: len(refs) - 3], refs[len(refs) - 3 :]
    for at, part in enumerate(parts):
        rows = part.shape[0]
        begin = pl.multiple_of(position_ref[at] * rows, SUBLANES)
        full_ref[pl.ds(begin, rows), :] = part[...]
    weight = full_ref[...]
    bias = bias_ref[:1, :]
    length = own_ref.shape[0]
    for which, ref in enumerate((own_ref, other_ref)):
        for at in range(0, length, ROWS):
            upward = nn(ref[at : at + ROWS, :], weight) + bias
            share = 0.5 + 0.5 * lax.erf(upward * math.sqrt(0.5))
            bell = jnp.exp2((upward * upward) * (-0.5 * math.log2(math.e)))
            here = slice(which * length + at, which * length + at + ROWS)
            act_ref[here, :] = (upward * share).astype(BF16)
            slope = share + upward * (bell * (1.0 / math.sqrt(2.0 * math.pi)))
            slope_ref[here, :] = slope.astype(BF16)


def column_specs(half, block):
    block = min(block, half)

    def column(height):
        return pl.BlockSpec((height, block), lambda i, at: (0, i))

    return half // block, block, column


def whole_spec(shape):
    return pl.BlockSpec(shape, lambda i, at: (0,) * len(shape))


def up_project(own, other, bias, parts, positions):
    length, width = own.shape
    half = parts[0].shape[1]
    steps, _, column = column_specs(half, 512)
    whole = whole_spec((length, width))
    return call(
        up_kernel,
        [((2 * length, half), BF16), ((2 * length, half), BF16), ((width, half), BF16)],
        (own, other, bias, *parts),
        positions,
        grid=(steps,),
        in_specs=[whole, whole, column(bias.shape[0])] + [column(part.shape[0]) for part in parts],
        out_specs=[column(2 * length), column(2 * length), column(width)],
    )


def down_kernel(position_ref, act_ref, *refs):
    parts, (own_ref, other_ref, full_ref) = refs[: len(refs) - 3], refs[len(refs) - 3 :]
    length = own_ref.shape[0]
    for at, part in enumerate(parts):
        rows = part.shape[0]
        begin = pl.multiple_of(position_ref[at] * rows, SUBLANES)
        full_ref[pl.ds(begin, rows), :] = part[...]
    for which, ref in enumerate((own_ref, other_ref)):
        here = slice(which * length, (which + 1) * length)
        ref[...] = nn(act_ref[here, :], full_ref[...]).astype(ref.dtype)


def down_project(act, parts, positions):
    length = act.shape[0] // 2
    half = act.shape[1]
    width = parts[0].shape[1]
    return call(
        down_kernel,
        [((length, width), F32), ((length, width), BF16), ((half, width), BF16)],
        (act, *parts),
        positions,
        mib=20,
    )


def loss_kernel(
    middle_ref, own_ref, got_ref, vector_ref, readout_ref, target_ref, mask_ref,
    low_ref, down_ref, grad_ref, sums_ref,
):
    result = (
        middle_ref[...]
        + (own_ref[...] + got_ref[...].astype(F32))
        + vector_ref[DOWN_BIAS : DOWN_BIAS + 1, :]
    ).astype(BF16)
    low_ref[...] = result
    logits = nt(readout_ref[...], result)
    length = logits.shape[1]
    top = jnp.max(logits, axis=0, keepdims=True)
    shifted = jnp.exp(logits - top)
    total = jnp.sum(shifted, axis=0, keepdims=True)
    onehot = lax.broadcasted_iota(jnp.int32, logits.shape, 0) == target_ref[...]
    picked = jnp.sum(jnp.where(onehot, logits, 0.0), axis=0, keepdims=True)
    weight = mask_ref[...].astype(F32)
    loss = (top + jnp.log(total) - picked) * weight
    loss_lanes = jnp.zeros((1, LANES), F32)
    count_lanes = jnp.zeros((1, LANES), F32)
    for at in range(0, length, LANES):
        loss_lanes = loss_lanes + loss[:, at : at + LANES]
        count_lanes = count_lanes + weight[:, at : at + LANES]
    lanes = jnp.concatenate([loss_lanes, count_lanes], axis=0)
    lanes = jnp.concatenate([lanes, jnp.zeros((2, result.shape[1] - LANES), F32)], axis=1)
    grad_logits = (weight * (shifted / total - onehot.astype(F32))).astype(BF16)
    grad = tn(grad_logits, readout_ref[...])
    grad_ref[...] = grad
    low = grad.astype(BF16)
    down_ref[...] = low
    sums = jnp.sum(low.astype(F32), axis=0, keepdims=True)
    blank = jnp.zeros((SUBLANES - 3, result.shape[1]), F32)
    sums_ref[...] = jnp.concatenate([lanes, sums, blank], axis=0)


def down_grad_kernel(chips, position_ref, act_ref, own_ref, other_ref, *out_refs):
    length = own_ref.shape[0]
    hidden = act_ref.shape[1] // chips
    for offset in range(chips):
        if len(out_refs) == 1:
            begin = offset * hidden
        else:
            begin = pl.multiple_of((position_ref[0] ^ offset) * hidden, LANES)
        here = pl.ds(begin, hidden)
        part = tn(act_ref[:length, here], own_ref[...]) + tn(act_ref[length:, here], other_ref[...])
        part = part.astype(BF16)
        if len(out_refs) == 1:
            out_refs[0][begin : begin + hidden, :] = part
            continue
        keep_x, send_x, keep_y, send_y = out_refs
        half = hidden // 2
        (send_x if offset % 2 else keep_x)[offset // 2, :, :] = part[:half]
        (send_y if offset // 2 else keep_y)[offset % 2, :, :] = part[half:]


def down_grad(act, own, other, chips, position):
    half = act.shape[1]
    width = own.shape[1]
    if square():
        outs = [((2, half // chips // 2, width), BF16)] * 4
    else:
        outs = [((half, width), BF16)]
    return call(
        functools.partial(down_grad_kernel, chips), outs, (act, own, other), position, mib=20
    )


def up_grad_kernel(
    rows, position_ref, own_ref, other_ref, slope_ref, second_ref, second_other_ref, down_ref,
    up_ref, bias_ref, *refs,
):
    out_refs, part_ref = refs[:-1], refs[-1]
    length = own_ref.shape[0]
    total = None
    grads = []
    for which, ref in enumerate((own_ref, other_ref)):
        for at in range(0, length, 2 * ROWS):
            here = slice(which * length + at, which * length + at + 2 * ROWS)
            grad = nt(ref[at : at + 2 * ROWS, :], down_ref[...]) * slope_ref[here, :].astype(F32)
            low = grad.astype(BF16)
            up_ref[here, :] = low
            part = jnp.sum(low.astype(F32), axis=0, keepdims=True)
            total = part if total is None else total + part
    bias_ref[...] = total
    part = tn(second_ref[...], up_ref[:length, :]) + tn(second_other_ref[...], up_ref[length:, :])
    if len(out_refs) == 1:
        out_refs[0][...] = part.astype(BF16)
        return
    part_ref[...] = part
    keep_x, send_x, keep_y, send_y = out_refs
    for offset in range(4):
        begin = pl.multiple_of((position_ref[0] ^ offset) * (2 * rows), SUBLANES)
        upper = part_ref[pl.ds(begin, rows), :].astype(BF16)
        lower = part_ref[pl.ds(begin + rows, rows), :].astype(BF16)
        (send_x if offset % 2 else keep_x)[offset // 2, :, :] = upper
        (send_y if offset // 2 else keep_y)[offset % 2, :, :] = lower


def up_grad(own, other, slope, second, second_other, down_full, rows, position):
    length, width = own.shape
    half = slope.shape[1]
    steps, block, column = column_specs(half, 512)
    whole = whole_spec((length, width))
    if square():
        outs = [((2, rows, half), BF16)] * 4
        specs = [pl.BlockSpec((2, rows, block), lambda i, at: (0, 0, i))] * 4
    else:
        outs = [((width, half), BF16)]
        specs = [column(width)]
    return call(
        functools.partial(up_grad_kernel, rows),
        [((2 * length, half), BF16), ((1, half), F32), *outs],
        (own, other, slope, second, second_other, down_full),
        position,
        grid=(steps,),
        in_specs=[
            whole, whole, column(2 * length), whole, whole,
            pl.BlockSpec((block, width), lambda i, at: (i, 0)),
        ],
        out_specs=[column(2 * length), column(1), *specs],
        scratch=[pltpu.VMEM((width, block), F32)],
        mib=20,
    )


def inward_kernel(grad_ref, up_ref, own_ref, other_ref):
    length = own_ref.shape[0]
    other_ref[...] = nt(grad_ref[length:, :], up_ref[...]).astype(BF16)
    own_ref[...] = nt(grad_ref[:length, :], up_ref[...])


def join_kernel(hidden, position_ref, mine_ref, other_ref, out_ref):
    for at in range(mine_ref.shape[1] // hidden):
        here = slice(hidden * at, hidden * (at + 1))
        for core, ref in enumerate((mine_ref, other_ref)):
            begin = (2 * at + (position_ref[0] + core) % 2) * hidden
            out_ref[:, pl.ds(pl.multiple_of(begin, LANES), hidden)] = ref[:, here].astype(F32)


def branch_kernel(
    got_ref, own_far, middle_far, result_far, out_ref, vector_ref,
    grad_ref, branch_ref, attended_ref, sums_ref, own_ref, middle_ref, result_ref, sems,
):
    width = own_ref.shape[1]
    blocks = range(0, own_ref.shape[0], ROWS)
    copies = []
    for at in blocks:
        here = pl.ds(at, ROWS)
        copies.append(
            [
                pltpu.make_async_copy(far.at[here], ref.at[here], sems.at[at // ROWS, which])
                for which, (far, ref) in enumerate(
                    ((own_far, own_ref), (middle_far, middle_ref), (result_far, result_ref))
                )
            ]
        )
        for copy in copies[-1]:
            copy.start()
    gain = vector_ref[FORWARD_GAIN : FORWARD_GAIN + 1, :]
    sums = [jnp.zeros((1, width), F32) for _ in range(3)]
    for at in blocks:
        for copy in copies[at // ROWS]:
            copy.wait()
        here = slice(at, at + ROWS)
        grad = own_ref[here, :] + got_ref[here, :].astype(F32)
        normal, inverse = unit(middle_ref[here, :])
        middle = result_ref[here, :] + unit_back(grad, normal, inverse, gain)
        grad_ref[here, :] = middle
        branch = middle.astype(BF16)
        branch_ref[here, :] = branch
        attended_ref[here, :] = nt(branch, out_ref[...]).astype(BF16)
        for which, part in enumerate((grad * normal, grad, branch.astype(F32))):
            sums[which] = sums[which] + jnp.sum(part, axis=0, keepdims=True)
    blank = jnp.zeros((SUBLANES - 3, width), F32)
    sums_ref[...] = jnp.concatenate([*sums, blank], axis=0)


def last_kernel(count, rows, hidden, pieces, position_ref, x_ref, low_ref, *refs):
    grad_refs, refs = refs[: 3 * pieces], refs[3 * pieces :]
    heads_ref, attended_ref, branch_ref, grad_ref, vector_ref, *refs = refs
    sums_ref, loss_ref, up_ref, *refs = refs
    slabs, (input_ref, vectors_ref, full_ref) = refs[:count], refs[count:]
    width = x_ref.shape[1]

    def grads(which, here):
        parts = [ref[here, :] for ref in grad_refs[which::3]]
        return jnp.concatenate(parts, axis=1) if pieces > 1 else parts[0]

    for at in range(3):
        part = tn(low_ref[...], grads(at, slice(None)))
        full_ref[:, width * at : width * (at + 1)] = part.astype(BF16)
    full_ref[:, 3 * width :] = tn(attended_ref[...], branch_ref[...]).astype(BF16)
    gain = vector_ref[ATTEND_GAIN : ATTEND_GAIN + 1, :]
    sums = [jnp.zeros((1, width), F32) for _ in range(4)]
    for at in range(0, x_ref.shape[0], ROWS):
        here = slice(at, at + ROWS)
        grad_query, grad_key, grad_value = [grads(at, here) for at in range(3)]
        grad = (
            nt(grad_query, heads_ref[:, :width])
            + nt(grad_key, heads_ref[:, width : 2 * width])
            + nt(grad_value, heads_ref[:, 2 * width :])
        )
        normal, inverse = unit(x_ref[here, :].astype(F32))
        input_ref[here, :] = grad_ref[here, :] + unit_back(grad, normal, inverse, gain)
        parts = (grad * normal, grad, grad_query.astype(F32), grad_value.astype(F32))
        for which, part in enumerate(parts):
            sums[which] = sums[which] + jnp.sum(part, axis=0, keepdims=True)
    vectors = jnp.concatenate(
        [*sums, sums_ref[2:3, :], sums_ref[0:1, :], sums_ref[1:2, :], loss_ref[2:3, :]], axis=0
    )
    vectors_ref[...] = vectors
    blank = jnp.zeros((VECTORS - 1, hidden), F32)
    lanes = jnp.concatenate([loss_ref[:2, :LANES], jnp.zeros((VECTORS - 2, LANES), F32)], axis=0)
    for at, slab in enumerate(slabs):
        place_at = position_ref[at]
        begin = pl.multiple_of(place_at * rows, SUBLANES)
        slab[:rows, :] = full_ref[pl.ds(begin, rows), :]
        short = pltpu.roll(vectors, width - begin, 1)[:, :LANES]
        if at < count // 2:
            hidden_at = pl.multiple_of(lax.div(place_at, 2) * hidden, LANES)
            bias = jnp.concatenate([up_ref[:, pl.ds(hidden_at, hidden)], blank], axis=0)
        else:
            bias = jnp.zeros((VECTORS, hidden), F32)
        row = jnp.concatenate([short, bias, lanes], axis=1).astype(BF16)
        pad = jnp.zeros((VECTORS, 4 * width - row.shape[1]), BF16)
        slab[rows:, :] = jnp.concatenate([row, pad], axis=1)


def settle_kernel(cut, rows, place_ref, *refs):
    totals, outers, (heads_ref, out_ref, short_ref) = refs[:2], refs[2:4], refs[4:]
    width = out_ref.shape[1]
    inner = (place_ref[0] == 1) | (place_ref[0] == 2)
    chosen = [
        jnp.where(inner, total[...], outer[...]).astype(F32) for total, outer in zip(totals, outers)
    ]
    for begin, end, values in ((0, cut, chosen[0]), (cut, rows, chosen[1])):
        heads_ref[begin:end, :] = values[: end - begin, : 3 * width]
        out_ref[begin:end, :] = values[: end - begin, 3 * width :]
    short_ref[...] = chosen[1][rows - cut :]


def swap(values, bit):
    return lax.ppermute(values, "wide", [(i, i ^ bit) for i in range(lax.axis_size("wide"))])


def same_core_groups():
    chips = lax.axis_size("wide") // 2
    return [[2 * chip + core for chip in range(chips)] for core in range(2)]


def square():
    return lax.axis_size("wide") == 8


def spread_chips(shard):
    return lax.all_gather(shard, "wide", axis=0, axis_index_groups=same_core_groups())


def add_low(*parts):
    return sum(part.astype(F32) for part in parts).astype(BF16)


def collect_chips(parts):
    return lax.psum_scatter(
        parts, "wide", scatter_dimension=0, axis_index_groups=same_core_groups()
    )


def after(values, *gates):
    leaves, tree = jax.tree.flatten(values)
    held = lax.optimization_barrier((*leaves, *jax.tree.leaves(gates)))
    return jax.tree.unflatten(tree, held[: len(leaves)])


INWARD, ACROSS, OUTWARD = [(0, 1), (3, 2)], [(1, 2), (2, 1)], [(1, 0), (2, 3)]


def hop(parts, pairs):
    return [lax.ppermute(part, "narrow", pairs) for part in parts]


def add_each(left, right):
    return [add_low(a, b) for a, b in zip(left, right)]


def settle(total, outer):
    place_at = lax.axis_index("narrow")
    return jnp.where((place_at == 1) | (place_at == 2), total, outer)


def sum_narrow(shard):
    if lax.axis_size("narrow") != 4:
        return lax.psum(shard, "narrow")
    half = add_low(shard, *hop([shard], INWARD))
    total = add_low(half, *hop([half], ACROSS))
    return settle(total, *hop([total], OUTWARD))


def local(
    layer_input, segments, targets, loss_mask, readout,
    attend_gain, attend_shift, heads_weight, query_bias, value_bias, output_weight, output_bias,
    forward_gain, forward_shift, up_weight, up_bias, down_weight, down_bias,
):
    length = layer_input.shape[1]
    width = layer_input.shape[2]
    wide = lax.axis_size("wide")
    chips = wide // 2
    core = lax.axis_index("wide") % 2
    chip = lax.axis_index("wide") // 2
    rows = heads_weight.shape[0]
    hidden = up_bias.shape[0]
    half = chips * hidden
    x = layer_input[0]
    vmem = pl.BlockSpec(memory_space=pltpu.VMEM)
    far_away = pl.BlockSpec(memory_space=pltpu.HBM)
    column = segments.reshape(length, 1)

    def by_core(mine, other, axis):
        return jnp.where(
            core == 0, jnp.stack([mine, other], axis), jnp.stack([other, mine], axis)
        )

    def mine_of(values, axis, flip=0):
        return lax.dynamic_index_in_dim(values, core ^ flip, axis, keepdims=False)

    short = jnp.stack(
        [
            attend_gain, attend_shift, query_bias, value_bias,
            output_bias, forward_gain, forward_shift, down_bias,
        ]
    )
    core_position = core.reshape(1).astype(jnp.int32)
    chip_position = chip.reshape(1).astype(jnp.int32)
    if square():
        offsets = jnp.arange(4, dtype=jnp.int32)
        (slab,) = call(
            slab_kernel,
            [((rows + VECTORS, 4 * width), BF16)],
            (heads_weight, output_weight, short, up_bias[None]),
        )
        near_x, near_y, far = swap(slab, 2), swap(slab, 4), swap(slab, 6)
        (up_weight,) = after([up_weight], near_x)
        up_mine, up_other = call(
            functools.partial(halves_kernel, hidden),
            [((rows, half), BF16)] * 2,
            (up_weight,),
            core_position,
        )
        other_x, mine_y = swap(up_other, 3), swap(up_mine, 4)
        mine_x, other_y = swap(up_mine, 2), swap(up_other, 5)
        near_y, far = after([near_y, far], up_mine)
        slabs = [slab, near_x, near_y, far]
        slabs = slabs + [swap(part, 1) for part in slabs]
        devices = 2 * (chip ^ offsets) + core
        positions = jnp.concatenate([devices, devices ^ 1]).astype(jnp.int32)
        up_positions = positions
        first_low, joined, heads_full, output_full, vectors, up_bias_half = call(
            functools.partial(project_kernel, len(slabs), rows, hidden),
            [
                ((length, width), BF16), ((length, 3 * width), BF16), ((width, 3 * width), BF16),
                ((width, width), BF16), ((VECTORS, width), F32), ((VECTORS, half), F32),
            ],
            (x, *slabs),
            positions,
            in_specs=[pl.BlockSpec(memory_space=pltpu.VMEM)]
            + [pl.BlockSpec(memory_space=pltpu.HBM)] * len(slabs),
            scratch=[
                pltpu.VMEM((len(slabs), VECTORS, LANES + hidden), BF16),
                pltpu.SemaphoreType.DMA((len(slabs), 3)),
            ],
            mib=20,
        )
    else:
        tail = jnp.concatenate([short.reshape(1, 8 * rows), up_bias[None]], axis=1)
        tail = jnp.pad(tail, ((0, 0), (0, 4 * width - tail.shape[1])))
        slab = jnp.concatenate(
            [jnp.concatenate([heads_weight, output_weight], axis=1), tail], axis=0
        )
        slabs = lax.all_gather(slab, "wide", axis=0)
        attend_full = slabs[:, :rows].reshape(width, 4 * width)
        heads_full = attend_full[:, : 3 * width]
        output_full = attend_full[:, 3 * width :]
        last = slabs[:, rows].astype(F32)
        vectors = last[:, : 8 * rows].reshape(wide, 8, rows).transpose(1, 0, 2).reshape(8, width)
        up_bias_half = mine_of(last[:, 8 * rows : 8 * rows + hidden].reshape(chips, 2, hidden), 1)
        up_bias_half = jnp.broadcast_to(up_bias_half.reshape(1, half), (VECTORS, half))
        positions = jnp.zeros((1,), jnp.int32)
        first_low, joined = call(
            functools.partial(project_kernel, 0, rows, hidden),
            [((length, width), BF16), ((length, 3 * width), BF16)],
            (x, heads_full, vectors),
            positions,
            mib=20,
        )
        up_view = up_weight.reshape(rows, chips, 2, hidden)
        up_pair = by_core(
            mine_of(up_view, 2).reshape(rows, half),
            swap(mine_of(up_view, 2, 1).reshape(rows, half), 1),
            0,
        ).reshape(2 * rows, half)
        up_parts = [spread_chips(up_pair).reshape(width, half)]
        down_parts = [spread_chips(down_weight).reshape(half, width)]
        up_positions = down_positions = positions

    attended, across, lse = attend(joined, column, segments)
    if square():
        passed_y, passed_x = after([mine_y, other_x], attended)
        up_parts = [
            up_mine, mine_x, mine_y, swap(passed_y, 2),
            swap(up_other, 1), other_x, other_y, swap(passed_x, 4),
        ]
        middle_row = hidden // 2
        upper, lower = after(
            [down_weight[:middle_row], down_weight[middle_row:]], mine_x, other_y, attended
        )
        lower_x, upper_y = swap(lower, 2), swap(upper, 4)
        upper_x, lower_y = swap(upper, 2), swap(lower, 4)
        down_parts = [
            down_weight, upper_x, lower_x, upper_y, lower_y
        ]
        at = jnp.arange(7, dtype=jnp.int32)
        down_positions = jnp.where(at == 0, chip, 2 * (chip ^ ((at + 1) // 2)) + (at + 1) % 2)
    middle, second_low = call(
        middle_kernel,
        [((length, width), F32), ((length, width), BF16)],
        (x, attended, output_full, vectors),
    )

    second_other = swap(second_low, 1)
    activated, slope, up_full = up_project(
        second_low, second_other, up_bias_half, up_parts, up_positions
    )
    if square():
        passed_x, passed_y = after([upper_y, lower_x], activated)
        down_parts = down_parts + [swap(passed_x, 2), swap(passed_y, 4)]
    outward, outward_other, down_full = down_project(activated, down_parts, down_positions)
    result_low, grad_down, grad_result, loss_sums = call(
        loss_kernel,
        [
            ((length, width), BF16), ((length, width), BF16), ((length, width), F32),
            ((SUBLANES, width), F32),
        ],
        (middle, outward, swap(outward_other, 1), vectors, readout.T, targets, loss_mask),
    )

    grad_down_other = swap(grad_down, 1)
    down_parts = down_grad(activated, grad_down, grad_down_other, chips, chip_position)
    if square():
        keep_dx, send_dx, keep_dy, send_dy = down_parts
        down_first = [swap(send_dx, 2), swap(send_dy, 4)]
        (grad_down_other,) = after([grad_down_other], send_dx)
    grad_up, up_bias_part, *up_parts = up_grad(
        grad_down, grad_down_other, slope, second_low, second_other, down_full, rows, chip_position
    )
    inward, inward_other = call(
        inward_kernel,
        [((length, width), F32), ((length, width), BF16)],
        (grad_up, up_full),
        mib=20,
    )
    got_inward = swap(inward_other, 1)
    if square():
        down_second = [
            add_low(keep_dx[1], down_first[0][1]), add_low(keep_dy[1], down_first[1][1])
        ]
        (got_inward,) = after([got_inward], down_second)
        keep_ux, send_ux, keep_uy, send_uy = up_parts
        send_ux, send_uy = after([send_ux, send_uy], down_second)
        down_got = [swap(down_second[0], 4), swap(down_second[1], 2)]
        up_first = [swap(send_ux, 2), swap(send_uy, 4)]
    grad_middle, grad_branch, grad_attended, branch_sums = call(
        branch_kernel,
        [
            ((length, width), F32), ((length, width), BF16), ((length, width), BF16),
            ((SUBLANES, width), F32),
        ],
        (got_inward, inward, middle, grad_result, output_full, vectors),
        in_specs=[vmem, far_away, far_away, far_away, vmem, vmem],
        scratch=[
            *[pltpu.VMEM((length, width), F32)] * 3,
            pltpu.SemaphoreType.DMA((length // ROWS, 3)),
        ],
        mib=24,
    )

    if square():
        attend_grads = attend_back(joined, column, segments, grad_attended, across, lse)
        down_narrow = [
            add_low(keep_dx[0], down_first[0][0], after([down_got[0]], attend_grads[0])[0]),
            add_low(keep_dy[0], down_first[1][0], after([down_got[1]], attend_grads[0])[0]),
        ]
        down_in = hop(down_narrow, INWARD)
        attend_grads = after(attend_grads, down_narrow)
    else:
        attend_grads = attend_back(joined, column, segments, grad_attended, across, lse)
    slab_shape = ((rows + VECTORS, 4 * width), BF16)
    *slabs, input_grad, short_sums, attend_part = call(
        functools.partial(last_kernel, 8 if square() else 0, rows, hidden, len(attend_grads) // 3),
        ([slab_shape] * 8 if square() else [])
        + [((length, width), F32), ((VECTORS, width), F32), ((width, 4 * width), BF16)],
        (
            x, first_low, *attend_grads, heads_full, attended, grad_branch,
            grad_middle, vectors, branch_sums, loss_sums, up_bias_part,
        ),
        positions,
        mib=40,
    )
    if square():
        slab_got = [swap(slabs[4 + at], 1) for at in (3, 1, 2, 0)]
        up_first = after(up_first, slabs[7])
        up_second = [add_low(keep_ux[1], up_first[0][1]), add_low(keep_uy[1], up_first[1][1])]
        up_got = [swap(up_second[0], 4), swap(up_second[1], 2)]

        down_half, down_mid = [], []
        gate = up_second
        for at in range(2):
            (came,) = after([down_in[at]], gate)
            down_half.append(add_low(down_narrow[at], came))
            down_mid += hop(down_half[-1:], ACROSS)
            gate = down_half[-1:]

        slab_got = after(slab_got, gate)
        both = [add_low(slabs[at], got) for at, got in zip((3, 1, 2, 0), slab_got)]
        slab_far = [swap(both[0], 6), swap(both[1], 2), swap(both[2], 4)]

        up_got = after(up_got, both)
        up_narrow = [
            add_low(keep_ux[0], up_first[0][0], up_got[0]),
            add_low(keep_uy[0], up_first[1][0], up_got[1]),
        ]
        up_in = hop(up_narrow, INWARD)

        gate = up_narrow
        down_total, down_out = [], []
        for at in range(2):
            (came,) = after([down_mid[at]], gate)
            down_total.append(add_low(down_half[at], came))
            down_out += hop(down_total[-1:], OUTWARD)
            gate = down_total[-1:]

        up_half, up_mid = [], []
        (came,) = after(up_in[:1], gate)
        up_half.append(add_low(up_narrow[0], came))
        up_mid += hop(up_half, ACROSS)

        slab_far = after(slab_far, up_half)
        cut = rows // 2 // SUBLANES * SUBLANES
        slab_narrow = [
            add_low(both[3][part], *[far[part] for far in slab_far])
            for part in (slice(0, cut), slice(cut, None))
        ]
        slab_in = hop(slab_narrow, INWARD)

        (came,) = after(up_in[1:], slab_narrow)
        up_half.append(add_low(up_narrow[1], came))
        up_mid += hop(up_half[1:], ACROSS)

        (came,) = after(up_mid[:1], up_half[1])
        up_total = [add_low(up_half[0], came)]
        up_out = hop(up_total, OUTWARD)

        gate = up_total
        slab_half, slab_mid = [], []
        for at in range(2):
            (came,) = after([slab_in[at]], gate)
            slab_half.append(add_low(slab_narrow[at], came))
            slab_mid += hop(slab_half[-1:], ACROSS)
            gate = slab_half[-1:]

        (came,) = after(up_mid[1:], gate)
        up_total.append(add_low(up_half[1], came))
        up_out += hop(up_total[1:], OUTWARD)

        gate = up_total[1]
        slab_total, slab_out = [], []
        for at in range(2):
            (came,) = after([slab_mid[at]], gate)
            slab_total.append(add_low(slab_half[at], came))
            slab_out += hop(slab_total[-1:], OUTWARD)
            gate = slab_total[-1:]

        down_out = after(down_out, gate)
        down_weight_sum = jnp.concatenate(
            [settle(*pair) for pair in zip(down_total, down_out)]
        ).astype(F32)
        up_out = after(up_out, gate)
        upper, lower = [settle(*pair) for pair in zip(up_total, up_out)]
        first = core == 0
        (up_weight_sum,) = call(
            functools.partial(join_kernel, hidden),
            [((rows, 2 * half), F32)],
            (jnp.where(first, upper, lower), swap(jnp.where(first, lower, upper), 1)),
            core_position,
        )
        slab_out = after(slab_out, up_weight_sum)
        heads_sum, output_sum, short = call(
            functools.partial(settle_kernel, cut, rows),
            [((rows, 3 * width), F32), ((rows, width), F32), ((VECTORS, 4 * width), F32)],
            (*slab_total, *slab_out),
            lax.axis_index("narrow").reshape(1).astype(jnp.int32),
        )
        vectors_sum = short[:, :rows]
        up_bias_grad = short[0, LANES : LANES + hidden]
        lanes_sum = short[:2, LANES + hidden : 2 * LANES + hidden]
        loss_sum = jnp.sum(lanes_sum[0])
        token_count = jnp.round(jnp.sum(lanes_sum[1])).astype(jnp.int32)
    else:
        down_weight_sum = collect_chips(down_parts[0].reshape(chips, hidden, width))
        down_weight_sum = sum_narrow(down_weight_sum).astype(F32)
        up_sum = sum_narrow(collect_chips(up_parts[0].reshape(chips, 2 * rows, half)))
        up_sum = up_sum.reshape(2, rows, chips, hidden)
        up_weight_sum = by_core(mine_of(up_sum, 0), swap(mine_of(up_sum, 0, 1), 1), 2)
        up_weight_sum = up_weight_sum.reshape(rows, 2 * half).astype(F32)
        short = short_sums.reshape(8, wide, rows).transpose(1, 0, 2).reshape(wide, 8 * rows)
        up_bias_rows = up_bias_part.reshape(chips, hidden)
        up_bias_rows = by_core(up_bias_rows, jnp.zeros_like(up_bias_rows), 1).reshape(wide, hidden)
        shared = jnp.broadcast_to(loss_sums[:1, :LANES], (wide, LANES))
        row = jnp.concatenate([short, up_bias_rows, shared], axis=1).astype(BF16)
        row = jnp.pad(row, ((0, 0), (0, 4 * width - row.shape[1])))
        slab = jnp.concatenate([attend_part.reshape(wide, rows, 4 * width), row[:, None]], axis=1)
        slab = sum_narrow(lax.psum_scatter(slab, "wide", scatter_dimension=0)).astype(F32)
        vectors_sum = slab[rows, : 8 * rows].reshape(8, rows)
        heads_sum, output_sum = slab[:rows, : 3 * width], slab[:rows, 3 * width :]
        up_bias_grad = slab[rows, 8 * rows : 8 * rows + hidden]
        loss_sum = jnp.sum(slab[rows, 8 * rows + hidden : 8 * rows + hidden + LANES])
        token_count = lax.psum(jnp.sum(loss_mask), ("narrow", "wide"))
    return (
        result_low[None],
        input_grad[None],
        vectors_sum[ATTEND_GAIN],
        vectors_sum[ATTEND_SHIFT],
        heads_sum,
        vectors_sum[QUERY_BIAS],
        vectors_sum[VALUE_BIAS],
        output_sum,
        vectors_sum[OUTPUT_BIAS],
        vectors_sum[FORWARD_GAIN],
        vectors_sum[FORWARD_SHIFT],
        up_weight_sum,
        up_bias_grad,
        down_weight_sum,
        vectors_sum[DOWN_BIAS],
        loss_sum,
        token_count,
    )


def solution(mesh):
    in_specs = (
        P(("narrow", "wide"), None, None),
        P(("narrow", "wide"), None),
        P(("narrow", "wide"), None),
        P(("narrow", "wide"), None),
        P(),
        P("wide"),
        P("wide"),
        P("wide", None),
        P("wide"),
        P("wide"),
        P("wide", None),
        P("wide"),
        P("wide"),
        P("wide"),
        P("wide", None),
        P("wide"),
        P("wide", None),
        P("wide"),
    )
    out_specs = (
        P(("narrow", "wide"), None, None),
        P(("narrow", "wide"), None, None),
        P("wide"),
        P("wide"),
        P("wide", None),
        P("wide"),
        P("wide"),
        P("wide", None),
        P("wide"),
        P("wide"),
        P("wide"),
        P("wide", None),
        P("wide"),
        P("wide", None),
        P("wide"),
        P(),
        P(),
    )
    return jax.shard_map(local, mesh=mesh, in_specs=in_specs, out_specs=out_specs, check_vma=False)
```

```python
import functools
import math

import jax
import jax.numpy as jnp
from jax import lax
from jax.experimental import pallas as pl
from jax.experimental.pallas import tpu as pltpu
from jax.sharding import PartitionSpec as P

HEADS = 20
HEAD_DIM = 32
LANES = 128
SUBLANES = 8
SEGMENTS = 8
REACH = 192
CHUNK = 256
ROWS = 128
SCALE = 1.0 / math.sqrt(HEAD_DIM)
SCALE2 = math.log2(math.e) * SCALE
F32 = jnp.float32
BF16 = jnp.bfloat16
VECTORS = 8
ATTEND_GAIN, ATTEND_SHIFT, QUERY_BIAS, VALUE_BIAS = 0, 1, 2, 3
OUTPUT_BIAS, FORWARD_GAIN, FORWARD_SHIFT, DOWN_BIAS = 4, 5, 6, 7


def nn(left, right):
    return lax.dot_general(left, right, (((1,), (0,)), ((), ())), preferred_element_type=F32)


def nt(left, right):
    return lax.dot_general(left, right, (((1,), (1,)), ((), ())), preferred_element_type=F32)


def tn(left, right):
    return lax.dot_general(left, right, (((0,), (0,)), ((), ())), preferred_element_type=F32)


def call(kernel, outs, args, positions=None, grid=None, in_specs=None, out_specs=None, scratch=(),
         mib=16):
    whole = pl.BlockSpec(memory_space=pltpu.VMEM)
    in_specs = in_specs or [whole] * len(args)
    args = [
        pltpu.with_memory_space_constraint(arg, pltpu.HBM)
        if spec.memory_space == pltpu.HBM
        else arg
        for arg, spec in zip(args, in_specs)
    ]
    out_specs = out_specs or [whole] * len(outs)
    shapes = [jax.ShapeDtypeStruct(shape, dtype) for shape, dtype in outs]
    extra = [] if positions is None else [positions]
    return pl.pallas_call(
        kernel,
        out_shape=shapes,
        grid_spec=pltpu.PrefetchScalarGridSpec(
            num_scalar_prefetch=len(extra),
            grid=grid or (),
            in_specs=in_specs,
            out_specs=out_specs,
            scratch_shapes=list(scratch),
        ),
        compiler_params=pltpu.CompilerParams(vmem_limit_bytes=mib * 1024 * 1024),
        cost_estimate=pl.CostEstimate(flops=1, bytes_accessed=1, transcendentals=0),
    )(*extra, *args)


def unit(values):
    centred = values - jnp.mean(values, axis=-1, keepdims=True)
    spread = jnp.mean(centred * centred, axis=-1, keepdims=True)
    inverse = lax.rsqrt(spread + 1e-05)
    return centred * inverse, inverse


def unit_back(grad, normal, inverse, gain):
    scaled = grad * gain
    mean = jnp.mean(scaled, axis=-1, keepdims=True)
    along = jnp.mean(scaled * normal, axis=-1, keepdims=True)
    return inverse * (scaled - mean - normal * along)


def spans(length):
    chunk = min(CHUNK, length)
    return [
        (at, at + chunk, max(0, at - REACH), min(length, at + chunk + REACH))
        for at in range(0, length, chunk)
    ]


def split3(values):
    first = values.astype(BF16).astype(F32)
    rest = values - first
    second = rest.astype(BF16).astype(F32)
    return [first, second, rest - second]


def key_marks(segment_column):
    lane = lax.broadcasted_iota(jnp.int32, (segment_column.shape[0], LANES), 1)
    ones = (lane >= SEGMENTS) & (lane < SEGMENTS + 3)
    return jnp.where((lane == segment_column) | ones, 1.0, 0.0).astype(BF16)


def query_marks(segment_row):
    row = lax.broadcasted_iota(jnp.int32, (SEGMENTS, segment_row.shape[1]), 0)
    return jnp.where(row == segment_row, 0.0, -1e30)


def place(rows, head, marks):
    count = rows.shape[1]
    parts = [rows, marks, jnp.zeros((LANES - marks.shape[0], count), BF16)]
    if head < LANES // HEAD_DIM - 1:
        parts.insert(1, jnp.zeros((LANES - HEAD_DIM * (head + 1), count), BF16))
    if head:
        parts.insert(0, jnp.zeros((HEAD_DIM * head, count), BF16))
    return jnp.concatenate(parts, axis=0)


def attend_kernel(column_ref, row_ref, q_ref, k_ref, v_ref, out_ref, across_ref, lse_ref, marks_ref):
    @pl.when(pl.program_id(0) == 0)
    def _():
        marks_ref[...] = key_marks(column_ref[...])

    length = q_ref.shape[0]
    heads = LANES // HEAD_DIM
    queries = q_ref[...].T
    values = v_ref[...].T
    keys = jnp.concatenate([k_ref[...], marks_ref[...]], axis=1)
    blank = jnp.zeros((SUBLANES, length), F32)
    marks = jnp.concatenate([query_marks(row_ref[...]), blank], axis=0).astype(BF16)
    ones = jnp.ones((SUBLANES, length), BF16)
    bodies = [(head, span) for head in range(heads) for span in spans(length)]

    def rows(head):
        return slice(HEAD_DIM * head, HEAD_DIM * (head + 1))

    summed = [jnp.concatenate([values[rows(head)], ones], axis=0) for head in range(heads)]

    def score(head, span):
        begin, end, low, high = span
        return nn(keys[low:high], place(queries[rows(head), begin:end], head, marks[:, begin:end]))

    def finish(head, span, top, probs):
        begin, end, low, high = span
        out = nn(summed[head][:, low:high], probs)
        total = out[HEAD_DIM : HEAD_DIM + 1]
        across_ref[rows(head), begin:end] = out[:HEAD_DIM] * (1.0 / total)
        lse_ref[head : head + 1, begin:end] = (top + jnp.log2(total)) * (1.0 / SCALE2)

    scores = [score(*body) for body in bodies[:2]]
    waiting = None
    for at, body in enumerate(bodies):
        current = scores.pop(0)
        if at + 2 < len(bodies):
            scores.append(score(*bodies[at + 2]))
        top = jnp.max(current, axis=0, keepdims=True) * SCALE2
        probs = jnp.exp2(current * SCALE2 - top).astype(BF16)
        if waiting is not None:
            finish(*waiting)
        waiting = (*body, top, probs)
    finish(*waiting)
    lse_ref[heads:, :] = jnp.zeros((SUBLANES - heads, length), F32)
    out_ref[...] = across_ref[...].T.astype(BF16)


def attend_back_kernel(
    column_ref, row_ref, q_ref, k_ref, v_ref, grad_ref, across_ref, lse_ref,
    gq_ref, gk_ref, gv_ref, marks_ref, turned_ref,
):
    @pl.when(pl.program_id(0) == 0)
    def _():
        marks_ref[...] = key_marks(column_ref[...])

    length = q_ref.shape[0]
    grad = grad_ref[...]
    queries = q_ref[...].T
    turned_keys = k_ref[...].T
    grads = grad.T
    keys = jnp.concatenate([k_ref[...], marks_ref[...]], axis=1)
    values = jnp.concatenate([v_ref[...], marks_ref[...]], axis=1)
    low_marks = query_marks(row_ref[...])
    blank = jnp.zeros((SUBLANES, length), F32)
    lane = lax.broadcasted_iota(jnp.int32, (1, LANES), 1) // HEAD_DIM
    heads = []
    for head in range(LANES // HEAD_DIM):
        rows = slice(HEAD_DIM * head, HEAD_DIM * (head + 1))
        inner = jnp.sum(grads[rows].astype(F32) * across_ref[rows, :], axis=0, keepdims=True)
        lse = lse_ref[head : head + 1, :]
        score_marks = jnp.concatenate([low_marks, *split3(-lse), blank[:5]], axis=0)
        inner_marks = jnp.concatenate([blank, *split3(-inner), blank[:5]], axis=0)
        zero = jnp.zeros_like(grad)
        heads.append(
            (
                rows,
                score_marks.astype(BF16),
                inner_marks.astype(BF16),
                jnp.where(lane == head, q_ref[...], zero),
                jnp.where(lane == head, grad, zero),
            )
        )
    bodies = [
        (head, at, span) for head in range(len(heads)) for at, span in enumerate(spans(length))
    ]
    sums = [[None, None] for _ in spans(length)]

    def pair(head, at, span):
        begin, end, low, high = span
        rows, score_marks, inner_marks, _, _ = heads[head]
        return (
            nn(keys[low:high], place(queries[rows, begin:end], head, score_marks[:, begin:end])),
            nn(values[low:high], place(grads[rows, begin:end], head, inner_marks[:, begin:end])),
        )

    def finish(head, at, span, score_grads, probs):
        begin, end, low, high = span
        rows, _, _, own_queries, own_grads = heads[head]
        for which, (left, right) in enumerate(
            ((score_grads, own_queries[begin:end]), (probs, own_grads[begin:end]))
        ):
            part = nn(left, right)
            sums[at][which] = part if sums[at][which] is None else sums[at][which] + part
        turned_ref[rows, begin:end] = nn(turned_keys[rows, low:high], score_grads)

    ahead = [pair(*bodies[0])]
    waiting = None
    for at, body in enumerate(bodies):
        scores, differences = ahead.pop(0)
        if at + 1 < len(bodies):
            ahead.append(pair(*bodies[at + 1]))
        probs = jnp.exp2(scores * SCALE2)
        score_grads = (probs * differences).astype(BF16)
        if waiting is not None:
            finish(*waiting)
        waiting = (*body, score_grads, probs.astype(BF16))
    finish(*waiting)
    gq_ref[...] = (turned_ref[...].T * SCALE).astype(BF16)
    for which, (ref, factor) in enumerate(((gk_ref, SCALE), (gv_ref, 1.0))):
        total = None
        for at, (_, _, low, high) in enumerate(spans(length)):
            parts = [sums[at][which]]
            if low:
                parts.insert(0, jnp.zeros((low, LANES), F32))
            if high < length:
                parts.append(jnp.zeros((length - high, LANES), F32))
            part = jnp.concatenate(parts, axis=0) if len(parts) > 1 else parts[0]
            total = part if total is None else total + part
        ref[...] = (total * factor).astype(BF16)


def attention_specs(length, width, begin=0):
    tiles = width // LANES

    def tile(at, begin=begin):
        return pl.BlockSpec((length, LANES), lambda i: (0, at + begin + i))

    return (
        tiles,
        tile,
        pl.BlockSpec((length, 1), lambda i: (0, 0)),
        pl.BlockSpec((1, length), lambda i: (0, 0)),
        pl.BlockSpec((LANES, length), lambda i: (begin + i, 0)),
        pl.BlockSpec((SUBLANES, length), lambda i: (begin + i, 0)),
    )


def attend(joined, column, row):
    length = joined.shape[0]
    width = joined.shape[1] // 3
    tiles, tile, column_spec, row_spec, across_spec, lse_spec = attention_specs(length, width)
    return call(
        attend_kernel,
        [((length, width), BF16), ((width, length), F32), ((SUBLANES * tiles, length), F32)],
        (column, row, joined, joined, joined),
        grid=(tiles,),
        in_specs=[column_spec, row_spec, tile(0), tile(tiles), tile(2 * tiles)],
        out_specs=[tile(0), across_spec, lse_spec],
        scratch=[pltpu.VMEM((length, LANES), BF16)],
    )


def attend_back(joined, column, row, grad, across, lse, begin=0, end=None):
    length = joined.shape[0]
    width = joined.shape[1] // 3
    specs = attention_specs(length, width, begin)
    tiles, tile, column_spec, row_spec, across_spec, lse_spec = specs
    count = (end or tiles) - begin
    return call(
        attend_back_kernel,
        [((length, count * LANES), BF16)] * 3,
        (column, row, joined, joined, joined, grad, across, lse),
        grid=(count,),
        in_specs=[column_spec, row_spec, tile(0), tile(tiles), tile(2 * tiles), tile(0), across_spec, lse_spec],
        out_specs=[tile(0, 0)] * 3,
        scratch=[pltpu.VMEM((length, LANES), BF16), pltpu.VMEM((LANES, length), F32)],
        mib=24,
    )


def slab_kernel(heads_ref, out_ref, short_ref, up_ref, slab_ref):
    rows = heads_ref.shape[0]
    width = out_ref.shape[1]
    slab_ref[:rows, : 3 * width] = heads_ref[...]
    slab_ref[:rows, 3 * width :] = out_ref[...]
    slab_ref[rows:, :] = jnp.zeros((VECTORS, 4 * width), BF16)
    slab_ref[rows:, :rows] = short_ref[...]
    slab_ref[rows:, LANES : LANES + up_ref.shape[1]] = jnp.broadcast_to(
        up_ref[...], (VECTORS, up_ref.shape[1])
    )


def halves_kernel(hidden, position_ref, up_ref, mine_ref, other_ref):
    for at in range(mine_ref.shape[1] // hidden):
        here = slice(hidden * at, hidden * (at + 1))
        for core, ref in enumerate((mine_ref, other_ref)):
            begin = (2 * at + (position_ref[0] + core) % 2) * hidden
            ref[:, here] = up_ref[:, pl.ds(pl.multiple_of(begin, LANES), hidden)]


def project_kernel(count, rows, hidden, position_ref, x_ref, *refs):
    slabs, refs = refs[:count], refs[count:]
    length, width = x_ref.shape
    if count:
        low_ref, joined_ref, heads_ref, out_ref, vector_ref, bias_ref, short_ref, sems = refs
        copies = []
        for at, slab in enumerate(slabs):
            begin = pl.multiple_of(position_ref[at] * rows, SUBLANES)
            here = pl.ds(begin, rows)
            for which, (source, target) in enumerate(
                (
                    (slab.at[pl.ds(0, rows), pl.ds(0, 3 * width)], heads_ref.at[here]),
                    (slab.at[pl.ds(0, rows), pl.ds(3 * width, width)], out_ref.at[here]),
                    (slab.at[pl.ds(rows, VECTORS), pl.ds(0, LANES + hidden)], short_ref.at[at]),
                )
            ):
                copy = pltpu.make_async_copy(source, target, sems.at[at, which])
                copy.start()
                copies.append(copy)
    else:
        heads_ref, vector_ref, low_ref, joined_ref = refs
    if count:
        for copy in copies:
            copy.wait()
        vectors = jnp.zeros((VECTORS, width), F32)
        for at in range(count):
            begin = position_ref[at] * rows
            short = short_ref[at, :, :LANES].astype(F32)
            lane = lax.broadcasted_iota(jnp.int32, short.shape, 1)
            short = jnp.where(lane < rows, short, 0.0)
            short = jnp.concatenate([short, jnp.zeros((VECTORS, width - LANES), F32)], axis=1)
            vectors = vectors + pltpu.roll(short, begin, 1)
            if at < count // 2:
                begin = pl.multiple_of(lax.div(position_ref[at], 2) * hidden, LANES)
                bias_ref[:, pl.ds(begin, hidden)] = short_ref[at, :, LANES:].astype(F32)
        vector_ref[...] = vectors
    zero = jnp.zeros((1, width), F32)
    vector = vector_ref[...]
    bias = jnp.concatenate(
        [vector[QUERY_BIAS : QUERY_BIAS + 1], zero, vector[VALUE_BIAS : VALUE_BIAS + 1]], axis=1
    )
    for at in range(0, length, ROWS):
        normal, _ = unit(x_ref[at : at + ROWS, :].astype(F32))
        low_ref[at : at + ROWS, :] = (
            normal * vector[ATTEND_GAIN : ATTEND_GAIN + 1]
            + vector[ATTEND_SHIFT : ATTEND_SHIFT + 1]
        ).astype(BF16)
    for at in range(0, 3 * width, width):
        here = slice(at, at + width)
        joined_ref[:, here] = (nn(low_ref[...], heads_ref[:, here]) + bias[:, here]).astype(BF16)


def middle_kernel(x_ref, attended_ref, out_ref, vector_ref, middle_ref, low_ref):
    vector = vector_ref[...]
    for at in range(0, x_ref.shape[0], ROWS):
        here = slice(at, at + ROWS)
        middle = (
            x_ref[here, :].astype(F32)
            + nn(attended_ref[here, :], out_ref[...])
            + vector[OUTPUT_BIAS : OUTPUT_BIAS + 1]
        )
        middle_ref[here, :] = middle
        normal, _ = unit(middle)
        low_ref[here, :] = (
            normal * vector[FORWARD_GAIN : FORWARD_GAIN + 1]
            + vector[FORWARD_SHIFT : FORWARD_SHIFT + 1]
        ).astype(BF16)


def up_kernel(position_ref, own_ref, other_ref, bias_ref, *refs):
    parts, (act_ref, slope_ref, full_ref) = refs[: len(refs) - 3], refs[len(refs) - 3 :]
    for at, part in enumerate(parts):
        rows = part.shape[0]
        begin = pl.multiple_of(position_ref[at] * rows, SUBLANES)
        full_ref[pl.ds(begin, rows), :] = part[...]
    weight = full_ref[...]
    bias = bias_ref[:1, :]
    length = own_ref.shape[0]
    for which, ref in enumerate((own_ref, other_ref)):
        for at in range(0, length, ROWS):
            upward = nn(ref[at : at + ROWS, :], weight) + bias
            share = 0.5 + 0.5 * lax.erf(upward * math.sqrt(0.5))
            bell = jnp.exp2((upward * upward) * (-0.5 * math.log2(math.e)))
            here = slice(which * length + at, which * length + at + ROWS)
            act_ref[here, :] = (upward * share).astype(BF16)
            slope = share + upward * (bell * (1.0 / math.sqrt(2.0 * math.pi)))
            slope_ref[here, :] = slope.astype(BF16)


def column_specs(half, block):
    block = min(block, half)

    def column(height):
        return pl.BlockSpec((height, block), lambda i, at: (0, i))

    return half // block, block, column


def whole_spec(shape):
    return pl.BlockSpec(shape, lambda i, at: (0,) * len(shape))


def up_project(own, other, bias, parts, positions):
    length, width = own.shape
    half = parts[0].shape[1]
    steps, _, column = column_specs(half, 512)
    whole = whole_spec((length, width))
    return call(
        up_kernel,
        [((2 * length, half), BF16), ((2 * length, half), BF16), ((width, half), BF16)],
        (own, other, bias, *parts),
        positions,
        grid=(steps,),
        in_specs=[whole, whole, column(bias.shape[0])] + [column(part.shape[0]) for part in parts],
        out_specs=[column(2 * length), column(2 * length), column(width)],
    )


def down_kernel(position_ref, act_ref, *refs):
    parts, (own_ref, other_ref, full_ref) = refs[: len(refs) - 3], refs[len(refs) - 3 :]
    length = own_ref.shape[0]
    for at, part in enumerate(parts):
        rows = part.shape[0]
        begin = pl.multiple_of(position_ref[at] * rows, SUBLANES)
        full_ref[pl.ds(begin, rows), :] = part[...]
    for which, ref in enumerate((own_ref, other_ref)):
        here = slice(which * length, (which + 1) * length)
        ref[...] = nn(act_ref[here, :], full_ref[...]).astype(ref.dtype)


def down_project(act, parts, positions):
    length = act.shape[0] // 2
    half = act.shape[1]
    width = parts[0].shape[1]
    return call(
        down_kernel,
        [((length, width), F32), ((length, width), BF16), ((half, width), BF16)],
        (act, *parts),
        positions,
        mib=20,
    )


def loss_kernel(
    middle_ref, own_ref, got_ref, vector_ref, readout_ref, target_ref, mask_ref,
    low_ref, down_ref, grad_ref, sums_ref,
):
    result = (
        middle_ref[...]
        + (own_ref[...] + got_ref[...].astype(F32))
        + vector_ref[DOWN_BIAS : DOWN_BIAS + 1, :]
    ).astype(BF16)
    low_ref[...] = result
    logits = nt(readout_ref[...], result)
    length = logits.shape[1]
    top = jnp.max(logits, axis=0, keepdims=True)
    shifted = jnp.exp(logits - top)
    total = jnp.sum(shifted, axis=0, keepdims=True)
    onehot = lax.broadcasted_iota(jnp.int32, logits.shape, 0) == target_ref[...]
    picked = jnp.sum(jnp.where(onehot, logits, 0.0), axis=0, keepdims=True)
    weight = mask_ref[...].astype(F32)
    loss = (top + jnp.log(total) - picked) * weight
    loss_lanes = jnp.zeros((1, LANES), F32)
    count_lanes = jnp.zeros((1, LANES), F32)
    for at in range(0, length, LANES):
        loss_lanes = loss_lanes + loss[:, at : at + LANES]
        count_lanes = count_lanes + weight[:, at : at + LANES]
    lanes = jnp.concatenate([loss_lanes, count_lanes], axis=0)
    lanes = jnp.concatenate([lanes, jnp.zeros((2, result.shape[1] - LANES), F32)], axis=1)
    grad_logits = (weight * (shifted / total - onehot.astype(F32))).astype(BF16)
    grad = tn(grad_logits, readout_ref[...])
    grad_ref[...] = grad
    low = grad.astype(BF16)
    down_ref[...] = low
    sums = jnp.sum(low.astype(F32), axis=0, keepdims=True)
    blank = jnp.zeros((SUBLANES - 3, result.shape[1]), F32)
    sums_ref[...] = jnp.concatenate([lanes, sums, blank], axis=0)


def down_grad_kernel(chips, position_ref, act_ref, own_ref, other_ref, *out_refs):
    length = own_ref.shape[0]
    hidden = act_ref.shape[1] // chips
    for offset in range(chips):
        if len(out_refs) == 1:
            begin = offset * hidden
        else:
            begin = pl.multiple_of((position_ref[0] ^ offset) * hidden, LANES)
        here = pl.ds(begin, hidden)
        part = tn(act_ref[:length, here], own_ref[...]) + tn(act_ref[length:, here], other_ref[...])
        part = part.astype(BF16)
        if len(out_refs) == 1:
            out_refs[0][begin : begin + hidden, :] = part
            continue
        keep_x, send_x, keep_y, send_y = out_refs
        half = hidden // 2
        (send_x if offset % 2 else keep_x)[offset // 2, :, :] = part[:half]
        (send_y if offset // 2 else keep_y)[offset % 2, :, :] = part[half:]


def down_grad(act, own, other, chips, position):
    half = act.shape[1]
    width = own.shape[1]
    if square():
        outs = [((2, half // chips // 2, width), BF16)] * 4
    else:
        outs = [((half, width), BF16)]
    return call(
        functools.partial(down_grad_kernel, chips), outs, (act, own, other), position, mib=20
    )


def up_grad_kernel(
    rows, position_ref, own_ref, other_ref, slope_ref, second_ref, second_other_ref, down_ref,
    up_ref, bias_ref, *refs,
):
    out_refs, part_ref = refs[:-1], refs[-1]
    length = own_ref.shape[0]
    total = None
    grads = []
    for which, ref in enumerate((own_ref, other_ref)):
        for at in range(0, length, 2 * ROWS):
            here = slice(which * length + at, which * length + at + 2 * ROWS)
            grad = nt(ref[at : at + 2 * ROWS, :], down_ref[...]) * slope_ref[here, :].astype(F32)
            low = grad.astype(BF16)
            up_ref[here, :] = low
            part = jnp.sum(low.astype(F32), axis=0, keepdims=True)
            total = part if total is None else total + part
    bias_ref[...] = total
    part = tn(second_ref[...], up_ref[:length, :]) + tn(second_other_ref[...], up_ref[length:, :])
    if len(out_refs) == 1:
        out_refs[0][...] = part.astype(BF16)
        return
    part_ref[...] = part
    keep_x, send_x, keep_y, send_y = out_refs
    for offset in range(4):
        begin = pl.multiple_of((position_ref[0] ^ offset) * (2 * rows), SUBLANES)
        upper = part_ref[pl.ds(begin, rows), :].astype(BF16)
        lower = part_ref[pl.ds(begin + rows, rows), :].astype(BF16)
        (send_x if offset % 2 else keep_x)[offset // 2, :, :] = upper
        (send_y if offset // 2 else keep_y)[offset % 2, :, :] = lower


def up_grad(own, other, slope, second, second_other, down_full, rows, position):
    length, width = own.shape
    half = slope.shape[1]
    steps, block, column = column_specs(half, 512)
    whole = whole_spec((length, width))
    if square():
        outs = [((2, rows, half), BF16)] * 4
        specs = [pl.BlockSpec((2, rows, block), lambda i, at: (0, 0, i))] * 4
    else:
        outs = [((width, half), BF16)]
        specs = [column(width)]
    return call(
        functools.partial(up_grad_kernel, rows),
        [((2 * length, half), BF16), ((1, half), F32), *outs],
        (own, other, slope, second, second_other, down_full),
        position,
        grid=(steps,),
        in_specs=[
            whole, whole, column(2 * length), whole, whole,
            pl.BlockSpec((block, width), lambda i, at: (i, 0)),
        ],
        out_specs=[column(2 * length), column(1), *specs],
        scratch=[pltpu.VMEM((width, block), F32)],
        mib=20,
    )


def inward_kernel(grad_ref, up_ref, own_ref, other_ref):
    length = own_ref.shape[0]
    other_ref[...] = nt(grad_ref[length:, :], up_ref[...]).astype(BF16)
    own_ref[...] = nt(grad_ref[:length, :], up_ref[...])


def join_kernel(hidden, position_ref, mine_ref, other_ref, out_ref):
    for at in range(mine_ref.shape[1] // hidden):
        here = slice(hidden * at, hidden * (at + 1))
        for core, ref in enumerate((mine_ref, other_ref)):
            begin = (2 * at + (position_ref[0] + core) % 2) * hidden
            out_ref[:, pl.ds(pl.multiple_of(begin, LANES), hidden)] = ref[:, here].astype(F32)


def branch_kernel(
    got_ref, own_far, middle_far, result_far, out_ref, vector_ref,
    grad_ref, branch_ref, attended_ref, sums_ref, own_ref, middle_ref, result_ref, sems,
):
    width = own_ref.shape[1]
    blocks = range(0, own_ref.shape[0], ROWS)
    copies = []
    for at in blocks:
        here = pl.ds(at, ROWS)
        copies.append(
            [
                pltpu.make_async_copy(far.at[here], ref.at[here], sems.at[at // ROWS, which])
                for which, (far, ref) in enumerate(
                    ((own_far, own_ref), (middle_far, middle_ref), (result_far, result_ref))
                )
            ]
        )
        for copy in copies[-1]:
            copy.start()
    gain = vector_ref[FORWARD_GAIN : FORWARD_GAIN + 1, :]
    sums = [jnp.zeros((1, width), F32) for _ in range(3)]
    for at in blocks:
        for copy in copies[at // ROWS]:
            copy.wait()
        here = slice(at, at + ROWS)
        grad = own_ref[here, :] + got_ref[here, :].astype(F32)
        normal, inverse = unit(middle_ref[here, :])
        middle = result_ref[here, :] + unit_back(grad, normal, inverse, gain)
        grad_ref[here, :] = middle
        branch = middle.astype(BF16)
        branch_ref[here, :] = branch
        attended_ref[here, :] = nt(branch, out_ref[...]).astype(BF16)
        for which, part in enumerate((grad * normal, grad, branch.astype(F32))):
            sums[which] = sums[which] + jnp.sum(part, axis=0, keepdims=True)
    blank = jnp.zeros((SUBLANES - 3, width), F32)
    sums_ref[...] = jnp.concatenate([*sums, blank], axis=0)


def last_kernel(count, rows, hidden, pieces, position_ref, x_ref, low_ref, *refs):
    grad_refs, refs = refs[: 3 * pieces], refs[3 * pieces :]
    heads_ref, attended_ref, branch_ref, grad_ref, vector_ref, *refs = refs
    sums_ref, loss_ref, up_ref, *refs = refs
    stacks, (input_ref, vectors_ref, full_ref) = refs[:-3], refs[-3:]
    width = x_ref.shape[1]

    def grads(which, here):
        parts = [ref[here, :] for ref in grad_refs[which::3]]
        return jnp.concatenate(parts, axis=1) if pieces > 1 else parts[0]

    for at in range(3):
        part = tn(low_ref[...], grads(at, slice(None)))
        full_ref[:, width * at : width * (at + 1)] = part.astype(BF16)
    full_ref[:, 3 * width :] = tn(attended_ref[...], branch_ref[...]).astype(BF16)
    gain = vector_ref[ATTEND_GAIN : ATTEND_GAIN + 1, :]
    sums = [jnp.zeros((1, width), F32) for _ in range(4)]
    for at in range(0, x_ref.shape[0], ROWS):
        here = slice(at, at + ROWS)
        grad_query, grad_key, grad_value = [grads(at, here) for at in range(3)]
        grad = (
            nt(grad_query, heads_ref[:, :width])
            + nt(grad_key, heads_ref[:, width : 2 * width])
            + nt(grad_value, heads_ref[:, 2 * width :])
        )
        normal, inverse = unit(x_ref[here, :].astype(F32))
        input_ref[here, :] = grad_ref[here, :] + unit_back(grad, normal, inverse, gain)
        parts = (grad * normal, grad, grad_query.astype(F32), grad_value.astype(F32))
        for which, part in enumerate(parts):
            sums[which] = sums[which] + jnp.sum(part, axis=0, keepdims=True)
    vectors = jnp.concatenate(
        [*sums, sums_ref[2:3, :], sums_ref[0:1, :], sums_ref[1:2, :], loss_ref[2:3, :]], axis=0
    )
    vectors_ref[...] = vectors
    blank = jnp.zeros((VECTORS - 1, hidden), F32)
    lanes = jnp.concatenate([loss_ref[:2, :LANES], jnp.zeros((VECTORS - 2, LANES), F32)], axis=0)
    for at in range(count):
        slab = stacks[at // (count // 2)].at[at % (count // 2)]
        place_at = position_ref[at]
        begin = pl.multiple_of(place_at * rows, SUBLANES)
        slab[:rows, :] = full_ref[pl.ds(begin, rows), :]
        short = pltpu.roll(vectors, width - begin, 1)[:, :LANES]
        if at < count // 2:
            hidden_at = pl.multiple_of(lax.div(place_at, 2) * hidden, LANES)
            bias = jnp.concatenate([up_ref[:, pl.ds(hidden_at, hidden)], blank], axis=0)
        else:
            bias = jnp.zeros((VECTORS, hidden), F32)
        row = jnp.concatenate([short, bias, lanes], axis=1).astype(BF16)
        pad = jnp.zeros((VECTORS, 4 * width - row.shape[1]), BF16)
        slab[rows:, :] = jnp.concatenate([row, pad], axis=1)


def settle_kernel(cut, rows, hidden, place_ref, *refs):
    totals, outers, refs = refs[:2], refs[2:4], refs[4:]
    heads_ref, out_ref, short_ref, loss_ref, count_ref = refs
    width = out_ref.shape[1]
    inner = (place_ref[0] == 1) | (place_ref[0] == 2)
    chosen = [
        jnp.where(inner, total[...], outer[...]).astype(F32) for total, outer in zip(totals, outers)
    ]
    for begin, end, values in ((0, cut, chosen[0]), (cut, rows, chosen[1])):
        heads_ref[begin:end, :] = values[: end - begin, : 3 * width]
        out_ref[begin:end, :] = values[: end - begin, 3 * width :]
    short = chosen[1][rows - cut :]
    short_ref[...] = short
    lanes = short[:, LANES + hidden : 2 * LANES + hidden]
    loss_ref[0] = jnp.sum(lanes[0:1])
    count_ref[0] = jnp.sum(lanes[1:2]).astype(jnp.int32)


def swap(values, bit):
    return lax.ppermute(values, "wide", [(i, i ^ bit) for i in range(lax.axis_size("wide"))])


def same_core_groups():
    chips = lax.axis_size("wide") // 2
    return [[2 * chip + core for chip in range(chips)] for core in range(2)]


def square():
    return lax.axis_size("wide") == 8


def spread_chips(shard):
    return lax.all_gather(shard, "wide", axis=0, axis_index_groups=same_core_groups())


def add_low(*parts):
    return sum(part.astype(F32) for part in parts).astype(BF16)


def collect_chips(parts):
    return lax.psum_scatter(
        parts, "wide", scatter_dimension=0, axis_index_groups=same_core_groups()
    )


def after(values, *gates):
    leaves, tree = jax.tree.flatten(values)
    held = lax.optimization_barrier((*leaves, *jax.tree.leaves(gates)))
    return jax.tree.unflatten(tree, held[: len(leaves)])


INWARD, ACROSS, OUTWARD = [(0, 1), (3, 2)], [(1, 2), (2, 1)], [(1, 0), (2, 3)]


def hop(parts, pairs):
    return [lax.ppermute(part, "narrow", pairs) for part in parts]


def add_each(left, right):
    return [add_low(a, b) for a, b in zip(left, right)]


def settle(total, outer):
    place_at = lax.axis_index("narrow")
    return jnp.where((place_at == 1) | (place_at == 2), total, outer)


def sum_narrow(shard):
    if lax.axis_size("narrow") != 4:
        return lax.psum(shard, "narrow")
    half = add_low(shard, *hop([shard], INWARD))
    total = add_low(half, *hop([half], ACROSS))
    return settle(total, *hop([total], OUTWARD))


def local(
    layer_input, segments, targets, loss_mask, readout,
    attend_gain, attend_shift, heads_weight, query_bias, value_bias, output_weight, output_bias,
    forward_gain, forward_shift, up_weight, up_bias, down_weight, down_bias,
):
    length = layer_input.shape[1]
    width = layer_input.shape[2]
    wide = lax.axis_size("wide")
    chips = wide // 2
    core = lax.axis_index("wide") % 2
    chip = lax.axis_index("wide") // 2
    rows = heads_weight.shape[0]
    hidden = up_bias.shape[0]
    half = chips * hidden
    x = layer_input[0]
    vmem = pl.BlockSpec(memory_space=pltpu.VMEM)
    far_away = pl.BlockSpec(memory_space=pltpu.HBM)
    column = segments.reshape(length, 1)

    def by_core(mine, other, axis):
        return jnp.where(
            core == 0, jnp.stack([mine, other], axis), jnp.stack([other, mine], axis)
        )

    def mine_of(values, axis, flip=0):
        return lax.dynamic_index_in_dim(values, core ^ flip, axis, keepdims=False)

    short = jnp.stack(
        [
            attend_gain, attend_shift, query_bias, value_bias,
            output_bias, forward_gain, forward_shift, down_bias,
        ]
    )
    core_position = core.reshape(1).astype(jnp.int32)
    chip_position = chip.reshape(1).astype(jnp.int32)
    if square():
        offsets = jnp.arange(4, dtype=jnp.int32)
        (slab,) = call(
            slab_kernel,
            [((rows + VECTORS, 4 * width), BF16)],
            (heads_weight, output_weight, short, up_bias[None]),
        )
        near_x, near_y, far = swap(slab, 2), swap(slab, 4), swap(slab, 6)
        devices = 2 * (chip ^ offsets) + core
        positions = jnp.concatenate([devices, devices ^ 1]).astype(jnp.int32)
        up_positions = positions
        up_weight, column, positions = after([up_weight, column, positions], near_x)
        up_mine, up_other = call(
            functools.partial(halves_kernel, hidden),
            [((rows, half), BF16)] * 2,
            (up_weight,),
            core_position,
        )
        other_x, mine_y = swap(up_other, 3), swap(up_mine, 4)
        mine_x, other_y = swap(up_mine, 2), swap(up_other, 5)
        swapped = [swap(slab, 1), swap(near_x, 1)]
        near_y, far = after([near_y, far], up_mine, swapped)
        slabs = [slab, near_x, near_y, far, *swapped, swap(near_y, 1), swap(far, 1)]
        first_low, joined, heads_full, output_full, vectors, up_bias_half = call(
            functools.partial(project_kernel, len(slabs), rows, hidden),
            [
                ((length, width), BF16), ((length, 3 * width), BF16), ((width, 3 * width), BF16),
                ((width, width), BF16), ((VECTORS, width), F32), ((VECTORS, half), F32),
            ],
            (x, *slabs),
            positions,
            in_specs=[pl.BlockSpec(memory_space=pltpu.VMEM)]
            + [pl.BlockSpec(memory_space=pltpu.HBM)] * len(slabs),
            scratch=[
                pltpu.VMEM((len(slabs), VECTORS, LANES + hidden), BF16),
                pltpu.SemaphoreType.DMA((len(slabs), 3)),
            ],
            mib=20,
        )
    else:
        tail = jnp.concatenate([short.reshape(1, 8 * rows), up_bias[None]], axis=1)
        tail = jnp.pad(tail, ((0, 0), (0, 4 * width - tail.shape[1])))
        slab = jnp.concatenate(
            [jnp.concatenate([heads_weight, output_weight], axis=1), tail], axis=0
        )
        slabs = lax.all_gather(slab, "wide", axis=0)
        attend_full = slabs[:, :rows].reshape(width, 4 * width)
        heads_full = attend_full[:, : 3 * width]
        output_full = attend_full[:, 3 * width :]
        last = slabs[:, rows].astype(F32)
        vectors = last[:, : 8 * rows].reshape(wide, 8, rows).transpose(1, 0, 2).reshape(8, width)
        up_bias_half = mine_of(last[:, 8 * rows : 8 * rows + hidden].reshape(chips, 2, hidden), 1)
        up_bias_half = jnp.broadcast_to(up_bias_half.reshape(1, half), (VECTORS, half))
        positions = jnp.zeros((1,), jnp.int32)
        first_low, joined = call(
            functools.partial(project_kernel, 0, rows, hidden),
            [((length, width), BF16), ((length, 3 * width), BF16)],
            (x, heads_full, vectors),
            positions,
            mib=20,
        )
        up_view = up_weight.reshape(rows, chips, 2, hidden)
        up_pair = by_core(
            mine_of(up_view, 2).reshape(rows, half),
            swap(mine_of(up_view, 2, 1).reshape(rows, half), 1),
            0,
        ).reshape(2 * rows, half)
        up_parts = [spread_chips(up_pair).reshape(width, half)]
        down_parts = [spread_chips(down_weight).reshape(half, width)]
        up_positions = down_positions = positions

    attended, across, lse = attend(joined, column, segments)
    if square():
        passed_y, passed_x = after([mine_y, other_x], attended)
        up_parts = [
            up_mine, mine_x, mine_y, swap(passed_y, 2),
            swap(up_other, 1), other_x, other_y, swap(passed_x, 4),
        ]
        middle_row = hidden // 2
        upper, lower = after(
            [down_weight[:middle_row], down_weight[middle_row:]], mine_x, other_y, attended
        )
        lower_x, upper_y = swap(lower, 2), swap(upper, 4)
        upper_x, lower_y = swap(upper, 2), swap(lower, 4)
        down_parts = [
            down_weight, upper_x, lower_x, upper_y, lower_y
        ]
        at = jnp.arange(7, dtype=jnp.int32)
        down_positions = jnp.where(at == 0, chip, 2 * (chip ^ ((at + 1) // 2)) + (at + 1) % 2)
    middle, second_low = call(
        middle_kernel,
        [((length, width), F32), ((length, width), BF16)],
        (x, attended, output_full, vectors),
    )

    second_other = swap(second_low, 1)
    activated, slope, up_full = up_project(
        second_low, second_other, up_bias_half, up_parts, up_positions
    )
    if square():
        passed_x, passed_y = after([upper_y, lower_x], activated)
        down_parts = down_parts + [swap(passed_x, 2), swap(passed_y, 4)]
    outward, outward_other, down_full = down_project(activated, down_parts, down_positions)
    result_low, grad_down, grad_result, loss_sums = call(
        loss_kernel,
        [
            ((length, width), BF16), ((length, width), BF16), ((length, width), F32),
            ((SUBLANES, width), F32),
        ],
        (middle, outward, swap(outward_other, 1), vectors, readout.T, targets, loss_mask),
    )

    grad_down_other = swap(grad_down, 1)
    down_parts = down_grad(activated, grad_down, grad_down_other, chips, chip_position)
    if square():
        keep_dx, send_dx, keep_dy, send_dy = down_parts
        down_first = [swap(send_dx, 2), swap(send_dy, 4)]
        (grad_down_other,) = after([grad_down_other], send_dx)
    grad_up, up_bias_part, *up_parts = up_grad(
        grad_down, grad_down_other, slope, second_low, second_other, down_full, rows, chip_position
    )
    inward, inward_other = call(
        inward_kernel,
        [((length, width), F32), ((length, width), BF16)],
        (grad_up, up_full),
        mib=20,
    )
    got_inward = swap(inward_other, 1)
    if square():
        down_second = [
            add_low(keep_dx[1], down_first[0][1]), add_low(keep_dy[1], down_first[1][1])
        ]
        (got_inward,) = after([got_inward], down_second)
        keep_ux, send_ux, keep_uy, send_uy = up_parts
        send_ux, send_uy = after([send_ux, send_uy], down_second)
        down_got = [swap(down_second[0], 4), swap(down_second[1], 2)]
        up_first = [swap(send_ux, 2), swap(send_uy, 4)]
    grad_middle, grad_branch, grad_attended, branch_sums = call(
        branch_kernel,
        [
            ((length, width), F32), ((length, width), BF16), ((length, width), BF16),
            ((SUBLANES, width), F32),
        ],
        (got_inward, inward, middle, grad_result, output_full, vectors),
        in_specs=[vmem, far_away, far_away, far_away, vmem, vmem],
        scratch=[
            *[pltpu.VMEM((length, width), F32)] * 3,
            pltpu.SemaphoreType.DMA((length // ROWS, 3)),
        ],
        mib=24,
    )

    if square():
        attend_grads = attend_back(joined, column, segments, grad_attended, across, lse)
        down_got = after(down_got, attend_grads[0])
        down_narrow = [
            add_low(keep_dx[0], down_first[0][0], down_got[0]),
            add_low(keep_dy[0], down_first[1][0], down_got[1]),
        ]
        down_in = hop(down_narrow, INWARD)
        attend_grads = after(attend_grads, down_narrow)
    else:
        attend_grads = attend_back(joined, column, segments, grad_attended, across, lse)
    stack_shape = ((4, rows + VECTORS, 4 * width), BF16)
    *stacks, input_grad, short_sums, attend_part = call(
        functools.partial(last_kernel, 8 if square() else 0, rows, hidden, len(attend_grads) // 3),
        ([stack_shape] * 2 if square() else [])
        + [((length, width), F32), ((VECTORS, width), F32), ((width, 4 * width), BF16)],
        (
            x, first_low, *attend_grads, heads_full, attended, grad_branch,
            grad_middle, vectors, branch_sums, loss_sums, up_bias_part,
        ),
        positions,
        mib=40,
    )
    if square():
        mine, others = stacks
        mine_got = swap(others, 1)
        up_first = after(up_first, mine)
        up_second = [add_low(keep_ux[1], up_first[0][1]), add_low(keep_uy[1], up_first[1][1])]
        up_got = [swap(up_second[0], 4), swap(up_second[1], 2)]

        down_in = after(down_in, up_second)
        down_half = jnp.concatenate(add_each(down_narrow, down_in))
        (down_mid,) = hop([down_half], ACROSS)

        (mine_got,) = after([mine_got], down_half)
        both = [add_low(mine[at], mine_got[at]) for at in range(4)]
        slab_far = [swap(both[3], 6), swap(both[1], 2), swap(both[2], 4)]

        up_got = after(up_got, both)
        up_narrow = [
            add_low(keep_ux[0], up_first[0][0], up_got[0]),
            add_low(keep_uy[0], up_first[1][0], up_got[1]),
        ]
        up_in = hop(up_narrow, INWARD)

        (came,) = after(up_in[:1], up_narrow)
        up_half = [add_low(up_narrow[0], came)]
        up_mid = hop(up_half, ACROSS)

        (down_mid,) = after([down_mid], up_half)
        down_total = add_low(down_half, down_mid)
        (down_out,) = hop([down_total], OUTWARD)

        (came,) = after(up_in[1:], down_total)
        up_half.append(add_low(up_narrow[1], came))
        up_mid += hop(up_half[1:], ACROSS)

        slab_far = after(slab_far, up_half[1])
        cut = rows // 2 // SUBLANES * SUBLANES
        slab_narrow = [
            add_low(both[0][part], *[far[part] for far in slab_far])
            for part in (slice(0, cut), slice(cut, None))
        ]
        slab_in = hop(slab_narrow, INWARD)

        (came,) = after(up_mid[:1], slab_narrow)
        up_total = [add_low(up_half[0], came)]
        up_out = hop(up_total, OUTWARD)

        (came,) = after(slab_in[:1], up_total)
        slab_half = [add_low(slab_narrow[0], came)]
        slab_mid = hop(slab_half, ACROSS)

        (came,) = after(up_mid[1:], slab_half)
        up_total.append(add_low(up_half[1], came))
        up_out += hop(up_total[1:], OUTWARD)

        (came,) = after(slab_in[1:], up_total[1])
        slab_half.append(add_low(slab_narrow[1], came))
        slab_mid += hop(slab_half[1:], ACROSS)

        gate = slab_half[1]
        slab_total, slab_out = [], []
        for at in range(2):
            (came,) = after([slab_mid[at]], gate)
            slab_total.append(add_low(slab_half[at], came))
            slab_out += hop(slab_total[-1:], OUTWARD)
            gate = slab_total[-1:]

        (down_out,) = after([down_out], gate)
        down_weight_sum = settle(down_total, down_out).astype(F32)
        up_out = after(up_out, gate)
        upper, lower = [settle(*pair) for pair in zip(up_total, up_out)]
        first = core == 0
        (up_weight_sum,) = call(
            functools.partial(join_kernel, hidden),
            [((rows, 2 * half), F32)],
            (jnp.where(first, upper, lower), swap(jnp.where(first, lower, upper), 1)),
            core_position,
        )
        slab_out = after(slab_out, up_weight_sum)
        scalar = pl.BlockSpec(memory_space=pltpu.SMEM)
        heads_sum, output_sum, short, loss_sum, token_count = call(
            functools.partial(settle_kernel, cut, rows, hidden),
            [
                ((rows, 3 * width), F32), ((rows, width), F32), ((VECTORS, 4 * width), F32),
                ((1,), F32), ((1,), jnp.int32),
            ],
            (*slab_total, *slab_out),
            lax.axis_index("narrow").reshape(1).astype(jnp.int32),
            out_specs=[vmem, vmem, vmem, scalar, scalar],
        )
        vectors_sum = short[:, :rows]
        up_bias_grad = short[0, LANES : LANES + hidden]
        loss_sum, token_count = loss_sum.reshape(()), token_count.reshape(())
    else:
        down_weight_sum = collect_chips(down_parts[0].reshape(chips, hidden, width))
        down_weight_sum = sum_narrow(down_weight_sum).astype(F32)
        up_sum = sum_narrow(collect_chips(up_parts[0].reshape(chips, 2 * rows, half)))
        up_sum = up_sum.reshape(2, rows, chips, hidden)
        up_weight_sum = by_core(mine_of(up_sum, 0), swap(mine_of(up_sum, 0, 1), 1), 2)
        up_weight_sum = up_weight_sum.reshape(rows, 2 * half).astype(F32)
        short = short_sums.reshape(8, wide, rows).transpose(1, 0, 2).reshape(wide, 8 * rows)
        up_bias_rows = up_bias_part.reshape(chips, hidden)
        up_bias_rows = by_core(up_bias_rows, jnp.zeros_like(up_bias_rows), 1).reshape(wide, hidden)
        shared = jnp.broadcast_to(loss_sums[:1, :LANES], (wide, LANES))
        row = jnp.concatenate([short, up_bias_rows, shared], axis=1).astype(BF16)
        row = jnp.pad(row, ((0, 0), (0, 4 * width - row.shape[1])))
        slab = jnp.concatenate([attend_part.reshape(wide, rows, 4 * width), row[:, None]], axis=1)
        slab = sum_narrow(lax.psum_scatter(slab, "wide", scatter_dimension=0)).astype(F32)
        vectors_sum = slab[rows, : 8 * rows].reshape(8, rows)
        heads_sum, output_sum = slab[:rows, : 3 * width], slab[:rows, 3 * width :]
        up_bias_grad = slab[rows, 8 * rows : 8 * rows + hidden]
        loss_sum = jnp.sum(slab[rows, 8 * rows + hidden : 8 * rows + hidden + LANES])
        token_count = lax.psum(jnp.sum(loss_mask), ("narrow", "wide"))
    return (
        result_low[None],
        input_grad[None],
        vectors_sum[ATTEND_GAIN],
        vectors_sum[ATTEND_SHIFT],
        heads_sum,
        vectors_sum[QUERY_BIAS],
        vectors_sum[VALUE_BIAS],
        output_sum,
        vectors_sum[OUTPUT_BIAS],
        vectors_sum[FORWARD_GAIN],
        vectors_sum[FORWARD_SHIFT],
        up_weight_sum,
        up_bias_grad,
        down_weight_sum,
        vectors_sum[DOWN_BIAS],
        loss_sum,
        token_count,
    )


def solution(mesh):
    in_specs = (
        P(("narrow", "wide"), None, None),
        P(("narrow", "wide"), None),
        P(("narrow", "wide"), None),
        P(("narrow", "wide"), None),
        P(),
        P("wide"),
        P("wide"),
        P("wide", None),
        P("wide"),
        P("wide"),
        P("wide", None),
        P("wide"),
        P("wide"),
        P("wide"),
        P("wide", None),
        P("wide"),
        P("wide", None),
        P("wide"),
    )
    out_specs = (
        P(("narrow", "wide"), None, None),
        P(("narrow", "wide"), None, None),
        P("wide"),
        P("wide"),
        P("wide", None),
        P("wide"),
        P("wide"),
        P("wide", None),
        P("wide"),
        P("wide"),
        P("wide"),
        P("wide", None),
        P("wide"),
        P("wide", None),
        P("wide"),
        P(),
        P(),
    )
    return jax.shard_map(local, mesh=mesh, in_specs=in_specs, out_specs=out_specs, check_vma=False)
```

```python
import functools
import math

import jax
import jax.numpy as jnp
from jax import lax
from jax.experimental import pallas as pl
from jax.experimental.pallas import tpu as pltpu
from jax.sharding import PartitionSpec as P

HEADS = 20
HEAD_DIM = 32
LANES = 128
SUBLANES = 8
SEGMENTS = 8
REACH = 192
CHUNK = 256
ROWS = 128
SCALE = 1.0 / math.sqrt(HEAD_DIM)
SCALE2 = math.log2(math.e) * SCALE
F32 = jnp.float32
BF16 = jnp.bfloat16
VECTORS = 8
ATTEND_GAIN, ATTEND_SHIFT, QUERY_BIAS, VALUE_BIAS = 0, 1, 2, 3
OUTPUT_BIAS, FORWARD_GAIN, FORWARD_SHIFT, DOWN_BIAS = 4, 5, 6, 7


def nn(left, right):
    return lax.dot_general(left, right, (((1,), (0,)), ((), ())), preferred_element_type=F32)


def nt(left, right):
    return lax.dot_general(left, right, (((1,), (1,)), ((), ())), preferred_element_type=F32)


def tn(left, right):
    return lax.dot_general(left, right, (((0,), (0,)), ((), ())), preferred_element_type=F32)


def call(kernel, outs, args, positions=None, grid=None, in_specs=None, out_specs=None, scratch=(),
         mib=16):
    whole = pl.BlockSpec(memory_space=pltpu.VMEM)
    in_specs = in_specs or [whole] * len(args)
    args = [
        pltpu.with_memory_space_constraint(arg, pltpu.HBM)
        if spec.memory_space == pltpu.HBM
        else arg
        for arg, spec in zip(args, in_specs)
    ]
    out_specs = out_specs or [whole] * len(outs)
    shapes = [
        pltpu.HBM(*out) if spec.memory_space == pltpu.HBM else jax.ShapeDtypeStruct(*out)
        for out, spec in zip(outs, out_specs)
    ]
    extra = [] if positions is None else [positions]
    return pl.pallas_call(
        kernel,
        out_shape=shapes,
        grid_spec=pltpu.PrefetchScalarGridSpec(
            num_scalar_prefetch=len(extra),
            grid=grid or (),
            in_specs=in_specs,
            out_specs=out_specs,
            scratch_shapes=list(scratch),
        ),
        compiler_params=pltpu.CompilerParams(vmem_limit_bytes=mib * 1024 * 1024),
        cost_estimate=pl.CostEstimate(flops=1, bytes_accessed=1, transcendentals=0),
    )(*extra, *args)


def unit(values):
    centred = values - jnp.mean(values, axis=-1, keepdims=True)
    spread = jnp.mean(centred * centred, axis=-1, keepdims=True)
    inverse = lax.rsqrt(spread + 1e-05)
    return centred * inverse, inverse


def unit_back(grad, normal, inverse, gain):
    scaled = grad * gain
    mean = jnp.mean(scaled, axis=-1, keepdims=True)
    along = jnp.mean(scaled * normal, axis=-1, keepdims=True)
    return inverse * (scaled - mean - normal * along)


def spans(length):
    chunk = min(CHUNK, length)
    return [
        (at, at + chunk, max(0, at - REACH), min(length, at + chunk + REACH))
        for at in range(0, length, chunk)
    ]


def split3(values):
    first = values.astype(BF16).astype(F32)
    rest = values - first
    second = rest.astype(BF16).astype(F32)
    return [first, second, rest - second]


def key_marks(segment_row):
    at = lax.broadcasted_iota(jnp.int32, (LANES, segment_row.shape[1]), 0)
    ones = (at >= SEGMENTS) & (at < SEGMENTS + 3)
    return jnp.where((at == segment_row) | ones, 1.0, 0.0).astype(BF16).T


def query_marks(segment_row):
    row = lax.broadcasted_iota(jnp.int32, (SEGMENTS, segment_row.shape[1]), 0)
    return jnp.where(row == segment_row, 0.0, -1e30)


def place(rows, head, marks):
    count = rows.shape[1]
    parts = [rows, marks, jnp.zeros((LANES - marks.shape[0], count), BF16)]
    if head < LANES // HEAD_DIM - 1:
        parts.insert(1, jnp.zeros((LANES - HEAD_DIM * (head + 1), count), BF16))
    if head:
        parts.insert(0, jnp.zeros((HEAD_DIM * head, count), BF16))
    return jnp.concatenate(parts, axis=0)


def attend_kernel(row_ref, q_ref, k_ref, v_ref, out_ref, across_ref, lse_ref, marks_ref):
    @pl.when(pl.program_id(0) == 0)
    def _():
        marks_ref[...] = key_marks(row_ref[...])

    length = q_ref.shape[0]
    heads = LANES // HEAD_DIM
    queries = q_ref[...].T
    values = v_ref[...].T
    keys = jnp.concatenate([k_ref[...], marks_ref[...]], axis=1)
    blank = jnp.zeros((SUBLANES, length), F32)
    marks = jnp.concatenate([query_marks(row_ref[...]), blank], axis=0).astype(BF16)
    ones = jnp.ones((SUBLANES, length), BF16)
    bodies = [(head, span) for head in range(heads) for span in spans(length)]

    def rows(head):
        return slice(HEAD_DIM * head, HEAD_DIM * (head + 1))

    summed = [jnp.concatenate([values[rows(head)], ones], axis=0) for head in range(heads)]

    def score(head, span):
        begin, end, low, high = span
        return nn(keys[low:high], place(queries[rows(head), begin:end], head, marks[:, begin:end]))

    def finish(head, span, top, probs):
        begin, end, low, high = span
        out = nn(summed[head][:, low:high], probs)
        total = out[HEAD_DIM : HEAD_DIM + 1]
        across_ref[rows(head), begin:end] = out[:HEAD_DIM] * (1.0 / total)
        lse_ref[head : head + 1, begin:end] = (top + jnp.log2(total)) * (1.0 / SCALE2)

    scores = [score(*body) for body in bodies[:2]]
    waiting = None
    for at, body in enumerate(bodies):
        current = scores.pop(0)
        if at + 2 < len(bodies):
            scores.append(score(*bodies[at + 2]))
        top = jnp.max(current, axis=0, keepdims=True) * SCALE2
        probs = jnp.exp2(current * SCALE2 - top).astype(BF16)
        if waiting is not None:
            finish(*waiting)
        waiting = (*body, top, probs)
    finish(*waiting)
    lse_ref[heads:, :] = jnp.zeros((SUBLANES - heads, length), F32)
    out_ref[...] = across_ref[...].T.astype(BF16)


def attend_back_kernel(
    row_ref, q_ref, k_ref, v_ref, grad_ref, across_ref, lse_ref,
    gq_ref, gk_ref, gv_ref, marks_ref, turned_ref,
):
    @pl.when(pl.program_id(0) == 0)
    def _():
        marks_ref[...] = key_marks(row_ref[...])

    length = q_ref.shape[0]
    grad = grad_ref[...]
    queries = q_ref[...].T
    turned_keys = k_ref[...].T
    grads = grad.T
    keys = jnp.concatenate([k_ref[...], marks_ref[...]], axis=1)
    values = jnp.concatenate([v_ref[...], marks_ref[...]], axis=1)
    low_marks = query_marks(row_ref[...])
    blank = jnp.zeros((SUBLANES, length), F32)
    lane = lax.broadcasted_iota(jnp.int32, (1, LANES), 1) // HEAD_DIM
    heads = []
    for head in range(LANES // HEAD_DIM):
        rows = slice(HEAD_DIM * head, HEAD_DIM * (head + 1))
        inner = jnp.sum(grads[rows].astype(F32) * across_ref[rows, :], axis=0, keepdims=True)
        lse = lse_ref[head : head + 1, :]
        score_marks = jnp.concatenate([low_marks, *split3(-lse), blank[:5]], axis=0)
        inner_marks = jnp.concatenate([blank, *split3(-inner), blank[:5]], axis=0)
        zero = jnp.zeros_like(grad)
        heads.append(
            (
                rows,
                score_marks.astype(BF16),
                inner_marks.astype(BF16),
                jnp.where(lane == head, q_ref[...], zero),
                jnp.where(lane == head, grad, zero),
            )
        )
    bodies = [
        (head, at, span) for head in range(len(heads)) for at, span in enumerate(spans(length))
    ]
    sums = [[None, None] for _ in spans(length)]

    def pair(head, at, span):
        begin, end, low, high = span
        rows, score_marks, inner_marks, _, _ = heads[head]
        return (
            nn(keys[low:high], place(queries[rows, begin:end], head, score_marks[:, begin:end])),
            nn(values[low:high], place(grads[rows, begin:end], head, inner_marks[:, begin:end])),
        )

    def finish(head, at, span, score_grads, probs):
        begin, end, low, high = span
        rows, _, _, own_queries, own_grads = heads[head]
        for which, (left, right) in enumerate(
            ((score_grads, own_queries[begin:end]), (probs, own_grads[begin:end]))
        ):
            part = nn(left, right)
            sums[at][which] = part if sums[at][which] is None else sums[at][which] + part
        turned_ref[rows, begin:end] = nn(turned_keys[rows, low:high], score_grads)

    ahead = [pair(*bodies[0])]
    waiting = None
    for at, body in enumerate(bodies):
        scores, differences = ahead.pop(0)
        if at + 1 < len(bodies):
            ahead.append(pair(*bodies[at + 1]))
        probs = jnp.exp2(scores * SCALE2)
        score_grads = (probs * differences).astype(BF16)
        if waiting is not None:
            finish(*waiting)
        waiting = (*body, score_grads, probs.astype(BF16))
    finish(*waiting)
    gq_ref[...] = (turned_ref[...].T * SCALE).astype(BF16)
    for which, (ref, factor) in enumerate(((gk_ref, SCALE), (gv_ref, 1.0))):
        total = None
        for at, (_, _, low, high) in enumerate(spans(length)):
            parts = [sums[at][which]]
            if low:
                parts.insert(0, jnp.zeros((low, LANES), F32))
            if high < length:
                parts.append(jnp.zeros((length - high, LANES), F32))
            part = jnp.concatenate(parts, axis=0) if len(parts) > 1 else parts[0]
            total = part if total is None else total + part
        ref[...] = (total * factor).astype(BF16)


def attention_specs(length, width, begin=0):
    tiles = width // LANES

    def tile(at, begin=begin):
        return pl.BlockSpec((length, LANES), lambda i: (0, at + begin + i))

    return (
        tiles,
        tile,
        pl.BlockSpec((1, length), lambda i: (0, 0)),
        pl.BlockSpec((LANES, length), lambda i: (begin + i, 0)),
        pl.BlockSpec((SUBLANES, length), lambda i: (begin + i, 0)),
    )


def attend(joined, row):
    length = joined.shape[0]
    width = joined.shape[1] // 3
    tiles, tile, row_spec, across_spec, lse_spec = attention_specs(length, width)
    return call(
        attend_kernel,
        [((length, width), BF16), ((width, length), F32), ((SUBLANES * tiles, length), F32)],
        (row, joined, joined, joined),
        grid=(tiles,),
        in_specs=[row_spec, tile(0), tile(tiles), tile(2 * tiles)],
        out_specs=[tile(0), across_spec, lse_spec],
        scratch=[pltpu.VMEM((length, LANES), BF16)],
    )


def attend_back(joined, row, grad, across, lse, begin=0, end=None):
    length = joined.shape[0]
    width = joined.shape[1] // 3
    specs = attention_specs(length, width, begin)
    tiles, tile, row_spec, across_spec, lse_spec = specs
    count = (end or tiles) - begin
    return call(
        attend_back_kernel,
        [((length, count * LANES), BF16)] * 3,
        (row, joined, joined, joined, grad, across, lse),
        grid=(count,),
        in_specs=[row_spec, tile(0), tile(tiles), tile(2 * tiles), tile(0), across_spec, lse_spec],
        out_specs=[tile(0, 0)] * 3,
        scratch=[pltpu.VMEM((length, LANES), BF16), pltpu.VMEM((LANES, length), F32)],
        mib=24,
    )


def slab_kernel(heads_ref, out_ref, short_ref, up_ref, slab_ref):
    rows = heads_ref.shape[0]
    width = out_ref.shape[1]
    slab_ref[:rows, : 3 * width] = heads_ref[...]
    slab_ref[:rows, 3 * width :] = out_ref[...]
    slab_ref[rows:, :] = jnp.zeros((VECTORS, 4 * width), BF16)
    slab_ref[rows:, :rows] = short_ref[...]
    slab_ref[rows:, LANES : LANES + up_ref.shape[1]] = jnp.broadcast_to(
        up_ref[...], (VECTORS, up_ref.shape[1])
    )


def halves_kernel(hidden, position_ref, up_ref, mine_ref, other_ref):
    for at in range(mine_ref.shape[1] // hidden):
        here = slice(hidden * at, hidden * (at + 1))
        for core, ref in enumerate((mine_ref, other_ref)):
            begin = (2 * at + (position_ref[0] + core) % 2) * hidden
            ref[:, here] = up_ref[:, pl.ds(pl.multiple_of(begin, LANES), hidden)]


def project_kernel(count, rows, hidden, position_ref, x_ref, *refs):
    slabs, refs = refs[:count], refs[count:]
    length, width = x_ref.shape
    if count:
        low_ref, joined_ref, heads_ref, out_ref, vector_ref, bias_ref, short_ref, sems = refs
        copies = []
        for at, slab in enumerate(slabs):
            begin = pl.multiple_of(position_ref[at] * rows, SUBLANES)
            here = pl.ds(begin, rows)
            for which, (source, target) in enumerate(
                (
                    (slab.at[pl.ds(0, rows), pl.ds(0, 3 * width)], heads_ref.at[here]),
                    (slab.at[pl.ds(0, rows), pl.ds(3 * width, width)], out_ref.at[here]),
                    (slab.at[pl.ds(rows, VECTORS), pl.ds(0, LANES + hidden)], short_ref.at[at]),
                )
            ):
                copy = pltpu.make_async_copy(source, target, sems.at[at, which])
                copy.start()
                copies.append(copy)
    else:
        heads_ref, vector_ref, low_ref, joined_ref = refs
    if count:
        for copy in copies:
            copy.wait()
        vectors = jnp.zeros((VECTORS, width), F32)
        for at in range(count):
            begin = position_ref[at] * rows
            short = short_ref[at, :, :LANES].astype(F32)
            lane = lax.broadcasted_iota(jnp.int32, short.shape, 1)
            short = jnp.where(lane < rows, short, 0.0)
            short = jnp.concatenate([short, jnp.zeros((VECTORS, width - LANES), F32)], axis=1)
            vectors = vectors + pltpu.roll(short, begin, 1)
            if at < count // 2:
                begin = pl.multiple_of(lax.div(position_ref[at], 2) * hidden, LANES)
                bias_ref[:, pl.ds(begin, hidden)] = short_ref[at, :, LANES:].astype(F32)
        vector_ref[...] = vectors
    zero = jnp.zeros((1, width), F32)
    vector = vector_ref[...]
    bias = jnp.concatenate(
        [vector[QUERY_BIAS : QUERY_BIAS + 1], zero, vector[VALUE_BIAS : VALUE_BIAS + 1]], axis=1
    )
    for at in range(0, length, ROWS):
        normal, _ = unit(x_ref[at : at + ROWS, :].astype(F32))
        low_ref[at : at + ROWS, :] = (
            normal * vector[ATTEND_GAIN : ATTEND_GAIN + 1]
            + vector[ATTEND_SHIFT : ATTEND_SHIFT + 1]
        ).astype(BF16)
    for at in range(0, 3 * width, width):
        here = slice(at, at + width)
        joined_ref[:, here] = (nn(low_ref[...], heads_ref[:, here]) + bias[:, here]).astype(BF16)


def middle_kernel(x_ref, attended_ref, out_ref, vector_ref, middle_ref, low_ref):
    vector = vector_ref[...]
    for at in range(0, x_ref.shape[0], ROWS):
        here = slice(at, at + ROWS)
        middle = (
            x_ref[here, :].astype(F32)
            + nn(attended_ref[here, :], out_ref[...])
            + vector[OUTPUT_BIAS : OUTPUT_BIAS + 1]
        )
        middle_ref[here, :] = middle
        normal, _ = unit(middle)
        low_ref[here, :] = (
            normal * vector[FORWARD_GAIN : FORWARD_GAIN + 1]
            + vector[FORWARD_SHIFT : FORWARD_SHIFT + 1]
        ).astype(BF16)


def up_kernel(position_ref, own_ref, other_ref, bias_ref, *refs):
    parts, (act_ref, slope_ref, full_ref) = refs[: len(refs) - 3], refs[len(refs) - 3 :]
    for at, part in enumerate(parts):
        rows = part.shape[0]
        begin = pl.multiple_of(position_ref[at] * rows, SUBLANES)
        full_ref[pl.ds(begin, rows), :] = part[...]
    weight = full_ref[...]
    bias = bias_ref[:1, :]
    length = own_ref.shape[0]
    for which, ref in enumerate((own_ref, other_ref)):
        for at in range(0, length, ROWS):
            upward = nn(ref[at : at + ROWS, :], weight) + bias
            share = 0.5 + 0.5 * lax.erf(upward * math.sqrt(0.5))
            bell = jnp.exp2((upward * upward) * (-0.5 * math.log2(math.e)))
            here = slice(which * length + at, which * length + at + ROWS)
            act_ref[here, :] = (upward * share).astype(BF16)
            slope = share + upward * (bell * (1.0 / math.sqrt(2.0 * math.pi)))
            slope_ref[here, :] = slope.astype(BF16)


def column_specs(half, block):
    block = min(block, half)

    def column(height):
        return pl.BlockSpec((height, block), lambda i, at: (0, i))

    return half // block, block, column


def whole_spec(shape):
    return pl.BlockSpec(shape, lambda i, at: (0,) * len(shape))


def up_project(own, other, bias, parts, positions):
    length, width = own.shape
    half = parts[0].shape[1]
    steps, _, column = column_specs(half, 512)
    whole = whole_spec((length, width))
    return call(
        up_kernel,
        [((2 * length, half), BF16), ((2 * length, half), BF16), ((width, half), BF16)],
        (own, other, bias, *parts),
        positions,
        grid=(steps,),
        in_specs=[whole, whole, column(bias.shape[0])] + [column(part.shape[0]) for part in parts],
        out_specs=[column(2 * length), column(2 * length), column(width)],
    )


def down_kernel(position_ref, act_ref, *refs):
    parts, (own_ref, other_ref, full_ref) = refs[: len(refs) - 3], refs[len(refs) - 3 :]
    length = own_ref.shape[0]
    for at, part in enumerate(parts):
        rows = part.shape[0]
        begin = pl.multiple_of(position_ref[at] * rows, SUBLANES)
        full_ref[pl.ds(begin, rows), :] = part[...]
    for which, ref in enumerate((own_ref, other_ref)):
        here = slice(which * length, (which + 1) * length)
        ref[...] = nn(act_ref[here, :], full_ref[...]).astype(ref.dtype)


def down_project(act, parts, positions):
    length = act.shape[0] // 2
    half = act.shape[1]
    width = parts[0].shape[1]
    return call(
        down_kernel,
        [((length, width), F32), ((length, width), BF16), ((half, width), BF16)],
        (act, *parts),
        positions,
        mib=20,
    )


def loss_kernel(
    middle_ref, own_ref, got_ref, vector_ref, readout_ref, target_ref, mask_ref,
    low_ref, down_ref, grad_ref, sums_ref,
):
    result = (
        middle_ref[...]
        + (own_ref[...] + got_ref[...].astype(F32))
        + vector_ref[DOWN_BIAS : DOWN_BIAS + 1, :]
    ).astype(BF16)
    low_ref[...] = result
    logits = nt(readout_ref[...], result)
    length = logits.shape[1]
    top = jnp.max(logits, axis=0, keepdims=True)
    shifted = jnp.exp(logits - top)
    total = jnp.sum(shifted, axis=0, keepdims=True)
    onehot = lax.broadcasted_iota(jnp.int32, logits.shape, 0) == target_ref[...]
    picked = jnp.sum(jnp.where(onehot, logits, 0.0), axis=0, keepdims=True)
    weight = mask_ref[...].astype(F32)
    loss = (top + jnp.log(total) - picked) * weight
    loss_lanes = jnp.zeros((1, LANES), F32)
    count_lanes = jnp.zeros((1, LANES), F32)
    for at in range(0, length, LANES):
        loss_lanes = loss_lanes + loss[:, at : at + LANES]
        count_lanes = count_lanes + weight[:, at : at + LANES]
    lanes = jnp.concatenate([loss_lanes, count_lanes], axis=0)
    lanes = jnp.concatenate([lanes, jnp.zeros((2, result.shape[1] - LANES), F32)], axis=1)
    grad_logits = (weight * (shifted / total - onehot.astype(F32))).astype(BF16)
    grad_ref[...] = grad_logits
    low = tn(grad_logits, readout_ref[...]).astype(BF16)
    down_ref[...] = low
    sums = jnp.sum(low.astype(F32), axis=0, keepdims=True)
    blank = jnp.zeros((SUBLANES - 3, result.shape[1]), F32)
    sums_ref[...] = jnp.concatenate([lanes, sums, blank], axis=0)


def down_grad_kernel(chips, position_ref, act_ref, own_ref, other_ref, *out_refs):
    length = own_ref.shape[0]
    hidden = act_ref.shape[1] // chips
    for offset in range(chips):
        if len(out_refs) == 1:
            begin = offset * hidden
        else:
            begin = pl.multiple_of((position_ref[0] ^ offset) * hidden, LANES)
        here = pl.ds(begin, hidden)
        part = tn(act_ref[:length, here], own_ref[...]) + tn(act_ref[length:, here], other_ref[...])
        part = part.astype(BF16)
        if len(out_refs) == 1:
            out_refs[0][begin : begin + hidden, :] = part
            continue
        keep_x, send_x, keep_y, send_y = out_refs
        half = hidden // 2
        (send_x if offset % 2 else keep_x)[offset // 2, :, :] = part[:half]
        (send_y if offset // 2 else keep_y)[offset % 2, :, :] = part[half:]


def down_grad(act, own, other, chips, position):
    half = act.shape[1]
    width = own.shape[1]
    if square():
        outs = [((2, half // chips // 2, width), BF16)] * 4
    else:
        outs = [((half, width), BF16)]
    return call(
        functools.partial(down_grad_kernel, chips), outs, (act, own, other), position, mib=20
    )


def up_grad_kernel(
    rows, position_ref, own_ref, other_ref, slope_ref, second_ref, second_other_ref, down_ref,
    up_ref, bias_ref, *refs,
):
    out_refs, part_ref = refs[:-1], refs[-1]
    length = own_ref.shape[0]
    total = None
    grads = []
    for which, ref in enumerate((own_ref, other_ref)):
        for at in range(0, length, 2 * ROWS):
            here = slice(which * length + at, which * length + at + 2 * ROWS)
            grad = nt(ref[at : at + 2 * ROWS, :], down_ref[...]) * slope_ref[here, :].astype(F32)
            low = grad.astype(BF16)
            up_ref[here, :] = low
            part = jnp.sum(low.astype(F32), axis=0, keepdims=True)
            total = part if total is None else total + part
    bias_ref[...] = total
    part = tn(second_ref[...], up_ref[:length, :]) + tn(second_other_ref[...], up_ref[length:, :])
    if len(out_refs) == 1:
        out_refs[0][...] = part.astype(BF16)
        return
    part_ref[...] = part
    keep_x, send_x, keep_y, send_y = out_refs
    for offset in range(4):
        begin = pl.multiple_of((position_ref[0] ^ offset) * (2 * rows), SUBLANES)
        upper = part_ref[pl.ds(begin, rows), :].astype(BF16)
        lower = part_ref[pl.ds(begin + rows, rows), :].astype(BF16)
        (send_x if offset % 2 else keep_x)[offset // 2, :, :] = upper
        (send_y if offset // 2 else keep_y)[offset % 2, :, :] = lower


def up_grad(own, other, slope, second, second_other, down_full, rows, position):
    length, width = own.shape
    half = slope.shape[1]
    steps, block, column = column_specs(half, 512)
    whole = whole_spec((length, width))
    if square():
        outs = [((2, rows, half), BF16)] * 4
        specs = [pl.BlockSpec((2, rows, block), lambda i, at: (0, 0, i))] * 4
    else:
        outs = [((width, half), BF16)]
        specs = [column(width)]
    return call(
        functools.partial(up_grad_kernel, rows),
        [((2 * length, half), BF16), ((1, half), F32), *outs],
        (own, other, slope, second, second_other, down_full),
        position,
        grid=(steps,),
        in_specs=[
            whole, whole, column(2 * length), whole, whole,
            pl.BlockSpec((block, width), lambda i, at: (i, 0)),
        ],
        out_specs=[column(2 * length), column(1), *specs],
        scratch=[pltpu.VMEM((width, block), F32)],
        mib=20,
    )


def inward_kernel(grad_ref, up_ref, own_far, other_ref, own_ref, sem):
    length = other_ref.shape[0]
    own_ref[...] = nt(grad_ref[:length, :], up_ref[...])
    copy = pltpu.make_async_copy(own_ref, own_far, sem)
    copy.start()
    other_ref[...] = nt(grad_ref[length:, :], up_ref[...]).astype(BF16)
    copy.wait()


def join_kernel(hidden, position_ref, mine_ref, other_ref, out_ref):
    for at in range(mine_ref.shape[1] // hidden):
        here = slice(hidden * at, hidden * (at + 1))
        for core, ref in enumerate((mine_ref, other_ref)):
            begin = (2 * at + (position_ref[0] + core) % 2) * hidden
            out_ref[:, pl.ds(pl.multiple_of(begin, LANES), hidden)] = ref[:, here].astype(F32)


def branch_kernel(
    got_ref, own_far, middle_far, logits_ref, classes_ref, out_ref, vector_ref,
    grad_ref, branch_ref, attended_ref, sums_ref, own_ref, middle_ref, sems,
):
    width = own_ref.shape[1]
    blocks = range(0, own_ref.shape[0], ROWS)
    copies = []
    for at in blocks:
        here = pl.ds(at, ROWS)
        copies.append(
            [
                pltpu.make_async_copy(far.at[here], ref.at[here], sems.at[at // ROWS, which])
                for which, (far, ref) in enumerate(((own_far, own_ref), (middle_far, middle_ref)))
            ]
        )
        for copy in copies[-1]:
            copy.start()
    gain = vector_ref[FORWARD_GAIN : FORWARD_GAIN + 1, :]
    sums = [jnp.zeros((1, width), F32) for _ in range(3)]
    for at in blocks:
        for copy in copies[at // ROWS]:
            copy.wait()
        here = slice(at, at + ROWS)
        grad = own_ref[here, :] + got_ref[here, :].astype(F32)
        normal, inverse = unit(middle_ref[here, :])
        result = tn(logits_ref[:, here], classes_ref[...])
        middle = result + unit_back(grad, normal, inverse, gain)
        grad_ref[here, :] = middle
        branch = middle.astype(BF16)
        branch_ref[here, :] = branch
        attended_ref[here, :] = nt(branch, out_ref[...]).astype(BF16)
        for which, part in enumerate((grad * normal, grad, branch.astype(F32))):
            sums[which] = sums[which] + jnp.sum(part, axis=0, keepdims=True)
    blank = jnp.zeros((SUBLANES - 3, width), F32)
    sums_ref[...] = jnp.concatenate([*sums, blank], axis=0)


def last_kernel(count, rows, hidden, pieces, position_ref, x_ref, low_ref, *refs):
    grad_refs, refs = refs[: 3 * pieces], refs[3 * pieces :]
    heads_ref, attended_ref, branch_ref, grad_ref, vector_ref, *refs = refs
    sums_ref, loss_ref, up_ref, *refs = refs
    stacks, (input_ref, vectors_ref, full_ref) = refs[:-3], refs[-3:]
    width = x_ref.shape[1]

    def grads(which, here):
        parts = [ref[here, :] for ref in grad_refs[which::3]]
        return jnp.concatenate(parts, axis=1) if pieces > 1 else parts[0]

    for at in range(3):
        part = tn(low_ref[...], grads(at, slice(None)))
        full_ref[:, width * at : width * (at + 1)] = part.astype(BF16)
    full_ref[:, 3 * width :] = tn(attended_ref[...], branch_ref[...]).astype(BF16)
    gain = vector_ref[ATTEND_GAIN : ATTEND_GAIN + 1, :]
    sums = [jnp.zeros((1, width), F32) for _ in range(4)]
    for at in range(0, x_ref.shape[0], ROWS):
        here = slice(at, at + ROWS)
        grad_query, grad_key, grad_value = [grads(at, here) for at in range(3)]
        grad = (
            nt(grad_query, heads_ref[:, :width])
            + nt(grad_key, heads_ref[:, width : 2 * width])
            + nt(grad_value, heads_ref[:, 2 * width :])
        )
        normal, inverse = unit(x_ref[here, :].astype(F32))
        input_ref[here, :] = grad_ref[here, :] + unit_back(grad, normal, inverse, gain)
        parts = (grad * normal, grad, grad_query.astype(F32), grad_value.astype(F32))
        for which, part in enumerate(parts):
            sums[which] = sums[which] + jnp.sum(part, axis=0, keepdims=True)
    vectors = jnp.concatenate(
        [*sums, sums_ref[2:3, :], sums_ref[0:1, :], sums_ref[1:2, :], loss_ref[2:3, :]], axis=0
    )
    vectors_ref[...] = vectors
    blank = jnp.zeros((VECTORS - 1, hidden), F32)
    lanes = jnp.concatenate([loss_ref[:2, :LANES], jnp.zeros((VECTORS - 2, LANES), F32)], axis=0)
    for at in range(count):
        stack = stacks[at // (count // 2)]
        place_at = position_ref[at]
        begin = pl.multiple_of(place_at * rows, SUBLANES)
        cuts = [
            (pick, slice(2 * width * side, 2 * width * (side + 1)))
            for side, pick in enumerate(((0, 2, 1, 3)[at % 4], 4 + at % 4))
        ]
        for pick, here in cuts:
            stack[pick, :rows, :] = full_ref[pl.ds(begin, rows), here]
        short = pltpu.roll(vectors, width - begin, 1)[:, :LANES]
        if at < count // 2:
            hidden_at = pl.multiple_of(lax.div(place_at, 2) * hidden, LANES)
            bias = jnp.concatenate([up_ref[:, pl.ds(hidden_at, hidden)], blank], axis=0)
        else:
            bias = jnp.zeros((VECTORS, hidden), F32)
        row = jnp.concatenate([short, bias, lanes], axis=1).astype(BF16)
        pad = jnp.zeros((VECTORS, 4 * width - row.shape[1]), BF16)
        row = jnp.concatenate([row, pad], axis=1)
        for pick, here in cuts:
            stack[pick, rows:, :] = row[:, here]


def settle_kernel(rows, hidden, place_ref, *refs):
    totals, outers, refs = refs[:2], refs[2:4], refs[4:]
    heads_ref, out_ref, short_ref, loss_ref, count_ref = refs
    width = out_ref.shape[1]
    inner = (place_ref[0] == 1) | (place_ref[0] == 2)
    left, right = [
        jnp.where(inner, total[...], outer[...]).astype(F32) for total, outer in zip(totals, outers)
    ]
    heads_ref[:, : 2 * width] = left[:rows]
    heads_ref[:, 2 * width :] = right[:rows, :width]
    out_ref[...] = right[:rows, width:]
    short_ref[...] = left[rows:]
    lanes = left[rows:, LANES + hidden : 2 * LANES + hidden]
    loss_ref[0] = jnp.sum(lanes[0:1])
    count_ref[0] = jnp.sum(lanes[1:2]).astype(jnp.int32)


def swap(values, bit):
    return lax.ppermute(values, "wide", [(i, i ^ bit) for i in range(lax.axis_size("wide"))])


def same_core_groups():
    chips = lax.axis_size("wide") // 2
    return [[2 * chip + core for chip in range(chips)] for core in range(2)]


def square():
    return lax.axis_size("wide") == 8


def spread_chips(shard):
    return lax.all_gather(shard, "wide", axis=0, axis_index_groups=same_core_groups())


def add_low(*parts):
    return sum(part.astype(F32) for part in parts).astype(BF16)


def collect_chips(parts):
    return lax.psum_scatter(
        parts, "wide", scatter_dimension=0, axis_index_groups=same_core_groups()
    )


def after(values, *gates):
    leaves, tree = jax.tree.flatten(values)
    held = lax.optimization_barrier((*leaves, *jax.tree.leaves(gates)))
    return jax.tree.unflatten(tree, held[: len(leaves)])


INWARD, ACROSS, OUTWARD = [(0, 1), (3, 2)], [(1, 2), (2, 1)], [(1, 0), (2, 3)]


def hop(parts, pairs):
    return [lax.ppermute(part, "narrow", pairs) for part in parts]


def add_each(left, right):
    return [add_low(a, b) for a, b in zip(left, right)]


def settle(total, outer):
    place_at = lax.axis_index("narrow")
    return jnp.where((place_at == 1) | (place_at == 2), total, outer)


def sum_narrow(shard):
    if lax.axis_size("narrow") != 4:
        return lax.psum(shard, "narrow")
    half = add_low(shard, *hop([shard], INWARD))
    total = add_low(half, *hop([half], ACROSS))
    return settle(total, *hop([total], OUTWARD))


def local(
    layer_input, segments, targets, loss_mask, readout,
    attend_gain, attend_shift, heads_weight, query_bias, value_bias, output_weight, output_bias,
    forward_gain, forward_shift, up_weight, up_bias, down_weight, down_bias,
):
    length = layer_input.shape[1]
    width = layer_input.shape[2]
    wide = lax.axis_size("wide")
    chips = wide // 2
    core = lax.axis_index("wide") % 2
    chip = lax.axis_index("wide") // 2
    rows = heads_weight.shape[0]
    hidden = up_bias.shape[0]
    half = chips * hidden
    x = layer_input[0]
    classes = readout.T
    vmem = pl.BlockSpec(memory_space=pltpu.VMEM)
    far_away = pl.BlockSpec(memory_space=pltpu.HBM)

    def by_core(mine, other, axis):
        return jnp.where(
            core == 0, jnp.stack([mine, other], axis), jnp.stack([other, mine], axis)
        )

    def mine_of(values, axis, flip=0):
        return lax.dynamic_index_in_dim(values, core ^ flip, axis, keepdims=False)

    short = jnp.stack(
        [
            attend_gain, attend_shift, query_bias, value_bias,
            output_bias, forward_gain, forward_shift, down_bias,
        ]
    )
    core_position = core.reshape(1).astype(jnp.int32)
    chip_position = chip.reshape(1).astype(jnp.int32)
    if square():
        offsets = jnp.arange(4, dtype=jnp.int32)
        (slab,) = call(
            slab_kernel,
            [((rows + VECTORS, 4 * width), BF16)],
            (heads_weight, output_weight, short, up_bias[None]),
        )
        near_x, near_y, far = swap(slab, 2), swap(slab, 4), swap(slab, 6)
        devices = 2 * (chip ^ offsets) + core
        positions = jnp.concatenate([devices, devices ^ 1]).astype(jnp.int32)
        up_positions = positions
        up_weight, positions = after([up_weight, positions], near_x)
        up_mine, up_other = call(
            functools.partial(halves_kernel, hidden),
            [((rows, half), BF16)] * 2,
            (up_weight,),
            core_position,
        )
        other_x, mine_y = swap(up_other, 3), swap(up_mine, 4)
        mine_x, other_y = swap(up_mine, 2), swap(up_other, 5)
        swapped = [swap(slab, 1), swap(near_x, 1)]
        near_y, far = after([near_y, far], up_mine, swapped)
        slabs = [slab, near_x, near_y, far, *swapped, swap(near_y, 1), swap(far, 1)]
        first_low, joined, heads_full, output_full, vectors, up_bias_half = call(
            functools.partial(project_kernel, len(slabs), rows, hidden),
            [
                ((length, width), BF16), ((length, 3 * width), BF16), ((width, 3 * width), BF16),
                ((width, width), BF16), ((VECTORS, width), F32), ((VECTORS, half), F32),
            ],
            (x, *slabs),
            positions,
            in_specs=[pl.BlockSpec(memory_space=pltpu.VMEM)]
            + [pl.BlockSpec(memory_space=pltpu.HBM)] * len(slabs),
            scratch=[
                pltpu.VMEM((len(slabs), VECTORS, LANES + hidden), BF16),
                pltpu.SemaphoreType.DMA((len(slabs), 3)),
            ],
            mib=20,
        )
    else:
        tail = jnp.concatenate([short.reshape(1, 8 * rows), up_bias[None]], axis=1)
        tail = jnp.pad(tail, ((0, 0), (0, 4 * width - tail.shape[1])))
        slab = jnp.concatenate(
            [jnp.concatenate([heads_weight, output_weight], axis=1), tail], axis=0
        )
        slabs = lax.all_gather(slab, "wide", axis=0)
        attend_full = slabs[:, :rows].reshape(width, 4 * width)
        heads_full = attend_full[:, : 3 * width]
        output_full = attend_full[:, 3 * width :]
        last = slabs[:, rows].astype(F32)
        vectors = last[:, : 8 * rows].reshape(wide, 8, rows).transpose(1, 0, 2).reshape(8, width)
        up_bias_half = mine_of(last[:, 8 * rows : 8 * rows + hidden].reshape(chips, 2, hidden), 1)
        up_bias_half = jnp.broadcast_to(up_bias_half.reshape(1, half), (VECTORS, half))
        positions = jnp.zeros((1,), jnp.int32)
        first_low, joined = call(
            functools.partial(project_kernel, 0, rows, hidden),
            [((length, width), BF16), ((length, 3 * width), BF16)],
            (x, heads_full, vectors),
            positions,
            mib=20,
        )
        up_view = up_weight.reshape(rows, chips, 2, hidden)
        up_pair = by_core(
            mine_of(up_view, 2).reshape(rows, half),
            swap(mine_of(up_view, 2, 1).reshape(rows, half), 1),
            0,
        ).reshape(2 * rows, half)
        up_parts = [spread_chips(up_pair).reshape(width, half)]
        down_parts = [spread_chips(down_weight).reshape(half, width)]
        up_positions = down_positions = positions

    attended, across, lse = attend(joined, segments)
    if square():
        passed_y, passed_x = after([mine_y, other_x], attended)
        up_parts = [
            up_mine, mine_x, mine_y, swap(passed_y, 2),
            swap(up_other, 1), other_x, other_y, swap(passed_x, 4),
        ]
        middle_row = hidden // 2
        upper, lower = after(
            [down_weight[:middle_row], down_weight[middle_row:]], mine_x, other_y, attended
        )
        lower_x, upper_y = swap(lower, 2), swap(upper, 4)
        upper_x, lower_y = swap(upper, 2), swap(lower, 4)
        down_parts = [
            down_weight, upper_x, lower_x, upper_y, lower_y
        ]
        at = jnp.arange(7, dtype=jnp.int32)
        down_positions = jnp.where(at == 0, chip, 2 * (chip ^ ((at + 1) // 2)) + (at + 1) % 2)
    middle, second_low = call(
        middle_kernel,
        [((length, width), F32), ((length, width), BF16)],
        (x, attended, output_full, vectors),
    )

    second_other = swap(second_low, 1)
    activated, slope, up_full = up_project(
        second_low, second_other, up_bias_half, up_parts, up_positions
    )
    if square():
        passed_x, passed_y = after([upper_y, lower_x], activated)
        down_parts = down_parts + [swap(passed_x, 2), swap(passed_y, 4)]
    outward, outward_other, down_full = down_project(activated, down_parts, down_positions)
    result_low, grad_down, grad_logits, loss_sums = call(
        loss_kernel,
        [
            ((length, width), BF16), ((length, width), BF16), (classes.shape[:1] + (length,), BF16),
            ((SUBLANES, width), F32),
        ],
        (middle, outward, swap(outward_other, 1), vectors, classes, targets, loss_mask),
    )

    grad_down_other = swap(grad_down, 1)
    down_parts = down_grad(activated, grad_down, grad_down_other, chips, chip_position)
    if square():
        keep_dx, send_dx, keep_dy, send_dy = down_parts
        down_first = [swap(send_dx, 2), swap(send_dy, 4)]
        (grad_down_other,) = after([grad_down_other], send_dx)
    grad_up, up_bias_part, *up_parts = up_grad(
        grad_down, grad_down_other, slope, second_low, second_other, down_full, rows, chip_position
    )
    inward, inward_other = call(
        inward_kernel,
        [((length, width), F32), ((length, width), BF16)],
        (grad_up, up_full),
        out_specs=[far_away, vmem],
        scratch=[pltpu.VMEM((length, width), F32), pltpu.SemaphoreType.DMA],
        mib=20,
    )
    got_inward = swap(inward_other, 1)
    if square():
        down_second = [
            add_low(keep_dx[1], down_first[0][1]), add_low(keep_dy[1], down_first[1][1])
        ]
        (got_inward,) = after([got_inward], down_second)
        keep_ux, send_ux, keep_uy, send_uy = up_parts
        send_ux, send_uy = after([send_ux, send_uy], down_second)
        down_got = [swap(down_second[0], 4), swap(down_second[1], 2)]
        up_first = [swap(send_ux, 2), swap(send_uy, 4)]
    grad_middle, grad_branch, grad_attended, branch_sums = call(
        branch_kernel,
        [
            ((length, width), F32), ((length, width), BF16), ((length, width), BF16),
            ((SUBLANES, width), F32),
        ],
        (got_inward, inward, middle, grad_logits, classes, output_full, vectors),
        in_specs=[vmem, far_away, far_away, vmem, vmem, vmem, vmem],
        scratch=[
            *[pltpu.VMEM((length, width), F32)] * 2,
            pltpu.SemaphoreType.DMA((length // ROWS, 2)),
        ],
        mib=24,
    )

    if square():
        attend_grads = attend_back(joined, segments, grad_attended, across, lse)
        down_got = after(down_got, attend_grads[0])
        down_narrow = [
            add_low(keep_dx[0], down_first[0][0], down_got[0]),
            add_low(keep_dy[0], down_first[1][0], down_got[1]),
        ]
        down_in = hop(down_narrow, INWARD)
        attend_grads = after(attend_grads, down_narrow)
    else:
        attend_grads = attend_back(joined, segments, grad_attended, across, lse)
    stack_shape = ((8, rows + VECTORS, 2 * width), BF16)
    *stacks, input_grad, short_sums, attend_part = call(
        functools.partial(last_kernel, 8 if square() else 0, rows, hidden, len(attend_grads) // 3),
        ([stack_shape] * 2 if square() else [])
        + [((length, width), F32), ((VECTORS, width), F32), ((width, 4 * width), BF16)],
        (
            x, first_low, *attend_grads, heads_full, attended, grad_branch,
            grad_middle, vectors, branch_sums, loss_sums, up_bias_part,
        ),
        positions,
        mib=40,
    )
    if square():
        mine, others = stacks
        mine_got = swap(others, 1)
        up_first = after(up_first, mine)
        up_second = [add_low(keep_ux[1], up_first[0][1]), add_low(keep_uy[1], up_first[1][1])]
        up_got = [swap(up_second[0], 4), swap(up_second[1], 2)]

        down_in = after(down_in, up_second)
        down_half = jnp.concatenate(add_each(down_narrow, down_in))
        (down_mid,) = hop([down_half], ACROSS)

        (mine_got,) = after([mine_got], down_half)
        both = add_low(mine, mine_got)
        side_first = [swap(both[2:4], 2), swap(both[6:8], 4)]

        up_got = after(up_got, both)
        up_narrow = [
            add_low(keep_ux[0], up_first[0][0], up_got[0]),
            add_low(keep_uy[0], up_first[1][0], up_got[1]),
        ]
        up_in = hop(up_narrow, INWARD)

        side_first = after(side_first, up_narrow)
        side_second = [add_low(both[1], side_first[0][1]), add_low(both[5], side_first[1][1])]
        side_got = [swap(side_second[0], 4), swap(side_second[1], 2)]

        (came,) = after(up_in[:1], side_second)
        up_half = [add_low(up_narrow[0], came)]
        up_mid = hop(up_half, ACROSS)

        (came,) = after(up_in[1:], up_half)
        up_half.append(add_low(up_narrow[1], came))
        up_mid += hop(up_half[1:], ACROSS)

        side_got = after(side_got, up_half[1])
        slab_narrow = [
            add_low(both[0], side_first[0][0], side_got[0]),
            add_low(both[4], side_first[1][0], side_got[1]),
        ]
        slab_in = hop(slab_narrow, INWARD)

        (down_mid,) = after([down_mid], slab_narrow)
        down_total = add_low(down_half, down_mid)
        (down_out,) = hop([down_total], OUTWARD)

        (came,) = after(up_mid[:1], down_total)
        up_total = [add_low(up_half[0], came)]
        up_out = hop(up_total, OUTWARD)

        (came,) = after(slab_in[:1], up_total)
        slab_half = [add_low(slab_narrow[0], came)]
        slab_mid = hop(slab_half, ACROSS)

        (came,) = after(up_mid[1:], slab_half)
        up_total.append(add_low(up_half[1], came))
        up_out += hop(up_total[1:], OUTWARD)

        (came,) = after(slab_in[1:], up_total[1])
        slab_half.append(add_low(slab_narrow[1], came))
        slab_mid += hop(slab_half[1:], ACROSS)

        gate = slab_half[1]
        slab_total, slab_out = [], []
        for at in range(2):
            (came,) = after([slab_mid[at]], gate)
            slab_total.append(add_low(slab_half[at], came))
            slab_out += hop(slab_total[-1:], OUTWARD)
            gate = slab_total[-1:]

        (down_out,) = after([down_out], gate)
        down_weight_sum = settle(down_total, down_out).astype(F32)
        up_out = after(up_out, down_weight_sum, slab_out[0])
        upper, lower = [settle(*pair) for pair in zip(up_total, up_out)]
        first = core == 0
        (up_weight_sum,) = call(
            functools.partial(join_kernel, hidden),
            [((rows, 2 * half), F32)],
            (jnp.where(first, upper, lower), swap(jnp.where(first, lower, upper), 1)),
            core_position,
        )
        slab_out = after(slab_out, upper, lower)
        scalar = pl.BlockSpec(memory_space=pltpu.SMEM)
        heads_sum, output_sum, short, loss_sum, token_count = call(
            functools.partial(settle_kernel, rows, hidden),
            [
                ((rows, 3 * width), F32), ((rows, width), F32), ((VECTORS, 2 * width), F32),
                ((1,), F32), ((1,), jnp.int32),
            ],
            (*slab_total, *slab_out),
            lax.axis_index("narrow").reshape(1).astype(jnp.int32),
            out_specs=[vmem, vmem, vmem, scalar, scalar],
        )
        vectors_sum = short[:, :rows]
        up_bias_grad = short[0, LANES : LANES + hidden]
        loss_sum, token_count = loss_sum.reshape(()), token_count.reshape(())
    else:
        down_weight_sum = collect_chips(down_parts[0].reshape(chips, hidden, width))
        down_weight_sum = sum_narrow(down_weight_sum).astype(F32)
        up_sum = sum_narrow(collect_chips(up_parts[0].reshape(chips, 2 * rows, half)))
        up_sum = up_sum.reshape(2, rows, chips, hidden)
        up_weight_sum = by_core(mine_of(up_sum, 0), swap(mine_of(up_sum, 0, 1), 1), 2)
        up_weight_sum = up_weight_sum.reshape(rows, 2 * half).astype(F32)
        short = short_sums.reshape(8, wide, rows).transpose(1, 0, 2).reshape(wide, 8 * rows)
        up_bias_rows = up_bias_part.reshape(chips, hidden)
        up_bias_rows = by_core(up_bias_rows, jnp.zeros_like(up_bias_rows), 1).reshape(wide, hidden)
        shared = jnp.broadcast_to(loss_sums[:1, :LANES], (wide, LANES))
        row = jnp.concatenate([short, up_bias_rows, shared], axis=1).astype(BF16)
        row = jnp.pad(row, ((0, 0), (0, 4 * width - row.shape[1])))
        slab = jnp.concatenate([attend_part.reshape(wide, rows, 4 * width), row[:, None]], axis=1)
        slab = sum_narrow(lax.psum_scatter(slab, "wide", scatter_dimension=0)).astype(F32)
        vectors_sum = slab[rows, : 8 * rows].reshape(8, rows)
        heads_sum, output_sum = slab[:rows, : 3 * width], slab[:rows, 3 * width :]
        up_bias_grad = slab[rows, 8 * rows : 8 * rows + hidden]
        loss_sum = jnp.sum(slab[rows, 8 * rows + hidden : 8 * rows + hidden + LANES])
        token_count = lax.psum(jnp.sum(loss_mask), ("narrow", "wide"))
    return (
        result_low[None],
        input_grad[None],
        vectors_sum[ATTEND_GAIN],
        vectors_sum[ATTEND_SHIFT],
        heads_sum,
        vectors_sum[QUERY_BIAS],
        vectors_sum[VALUE_BIAS],
        output_sum,
        vectors_sum[OUTPUT_BIAS],
        vectors_sum[FORWARD_GAIN],
        vectors_sum[FORWARD_SHIFT],
        up_weight_sum,
        up_bias_grad,
        down_weight_sum,
        vectors_sum[DOWN_BIAS],
        loss_sum,
        token_count,
    )


def solution(mesh):
    in_specs = (
        P(("narrow", "wide"), None, None),
        P(("narrow", "wide"), None),
        P(("narrow", "wide"), None),
        P(("narrow", "wide"), None),
        P(),
        P("wide"),
        P("wide"),
        P("wide", None),
        P("wide"),
        P("wide"),
        P("wide", None),
        P("wide"),
        P("wide"),
        P("wide"),
        P("wide", None),
        P("wide"),
        P("wide", None),
        P("wide"),
    )
    out_specs = (
        P(("narrow", "wide"), None, None),
        P(("narrow", "wide"), None, None),
        P("wide"),
        P("wide"),
        P("wide", None),
        P("wide"),
        P("wide"),
        P("wide", None),
        P("wide"),
        P("wide"),
        P("wide"),
        P("wide", None),
        P("wide"),
        P("wide", None),
        P("wide"),
        P(),
        P(),
    )
    return jax.shard_map(local, mesh=mesh, in_specs=in_specs, out_specs=out_specs, check_vma=False)
```

```python
import functools
import math

import jax
import jax.numpy as jnp
from jax import lax
from jax.experimental import pallas as pl
from jax.experimental.pallas import tpu as pltpu
from jax.sharding import PartitionSpec as P

HEADS = 20
HEAD_DIM = 32
LANES = 128
SUBLANES = 8
SEGMENTS = 8
REACH = 192
CHUNK = 256
ROWS = 128
SCALE = 1.0 / math.sqrt(HEAD_DIM)
SCALE2 = math.log2(math.e) * SCALE
F32 = jnp.float32
BF16 = jnp.bfloat16
VECTORS = 8
ATTEND_GAIN, ATTEND_SHIFT, QUERY_BIAS, VALUE_BIAS = 0, 1, 2, 3
OUTPUT_BIAS, FORWARD_GAIN, FORWARD_SHIFT, DOWN_BIAS = 4, 5, 6, 7


def nn(left, right):
    return lax.dot_general(left, right, (((1,), (0,)), ((), ())), preferred_element_type=F32)


def nt(left, right):
    return lax.dot_general(left, right, (((1,), (1,)), ((), ())), preferred_element_type=F32)


def tn(left, right):
    return lax.dot_general(left, right, (((0,), (0,)), ((), ())), preferred_element_type=F32)


def call(kernel, outs, args, positions=None, grid=None, in_specs=None, out_specs=None, scratch=(),
         mib=16):
    whole = pl.BlockSpec(memory_space=pltpu.VMEM)
    in_specs = in_specs or [whole] * len(args)
    args = [
        pltpu.with_memory_space_constraint(arg, pltpu.HBM)
        if spec.memory_space == pltpu.HBM
        else arg
        for arg, spec in zip(args, in_specs)
    ]
    out_specs = out_specs or [whole] * len(outs)
    shapes = [
        pltpu.HBM(*out) if spec.memory_space == pltpu.HBM else jax.ShapeDtypeStruct(*out)
        for out, spec in zip(outs, out_specs)
    ]
    extra = [] if positions is None else [positions]
    return pl.pallas_call(
        kernel,
        out_shape=shapes,
        grid_spec=pltpu.PrefetchScalarGridSpec(
            num_scalar_prefetch=len(extra),
            grid=grid or (),
            in_specs=in_specs,
            out_specs=out_specs,
            scratch_shapes=list(scratch),
        ),
        compiler_params=pltpu.CompilerParams(vmem_limit_bytes=mib * 1024 * 1024),
        cost_estimate=pl.CostEstimate(flops=1, bytes_accessed=1, transcendentals=0),
    )(*extra, *args)


def unit(values):
    centred = values - jnp.mean(values, axis=-1, keepdims=True)
    spread = jnp.mean(centred * centred, axis=-1, keepdims=True)
    inverse = lax.rsqrt(spread + 1e-05)
    return centred * inverse, inverse


def unit_back(grad, normal, inverse, gain):
    scaled = grad * gain
    mean = jnp.mean(scaled, axis=-1, keepdims=True)
    along = jnp.mean(scaled * normal, axis=-1, keepdims=True)
    return inverse * (scaled - mean - normal * along)


def spans(length):
    chunk = min(CHUNK, length)
    return [
        (at, at + chunk, max(0, at - REACH), min(length, at + chunk + REACH))
        for at in range(0, length, chunk)
    ]


def split3(values):
    first = values.astype(BF16).astype(F32)
    rest = values - first
    second = rest.astype(BF16).astype(F32)
    return [first, second, rest - second]


def key_marks(segment_row):
    at = lax.broadcasted_iota(jnp.int32, (LANES, segment_row.shape[1]), 0)
    ones = (at >= SEGMENTS) & (at < SEGMENTS + 3)
    return jnp.where((at == segment_row) | ones, 1.0, 0.0).astype(BF16).T


def query_marks(segment_row):
    row = lax.broadcasted_iota(jnp.int32, (SEGMENTS, segment_row.shape[1]), 0)
    return jnp.where(row == segment_row, 0.0, -1e30)


def place(rows, head, marks):
    count = rows.shape[1]
    parts = [rows, marks, jnp.zeros((LANES - marks.shape[0], count), BF16)]
    if head < LANES // HEAD_DIM - 1:
        parts.insert(1, jnp.zeros((LANES - HEAD_DIM * (head + 1), count), BF16))
    if head:
        parts.insert(0, jnp.zeros((HEAD_DIM * head, count), BF16))
    return jnp.concatenate(parts, axis=0)


def attend_kernel(row_ref, q_ref, k_ref, v_ref, out_ref, across_ref, lse_ref, marks_ref):
    @pl.when(pl.program_id(0) == 0)
    def _():
        marks_ref[...] = key_marks(row_ref[...])

    length = q_ref.shape[0]
    heads = LANES // HEAD_DIM
    queries = q_ref[...].T
    values = v_ref[...].T
    keys = jnp.concatenate([k_ref[...], marks_ref[...]], axis=1)
    blank = jnp.zeros((SUBLANES, length), F32)
    marks = jnp.concatenate([query_marks(row_ref[...]), blank], axis=0).astype(BF16)
    ones = jnp.ones((SUBLANES, length), BF16)
    bodies = [(head, span) for head in range(heads) for span in spans(length)]

    def rows(head):
        return slice(HEAD_DIM * head, HEAD_DIM * (head + 1))

    summed = [jnp.concatenate([values[rows(head)], ones], axis=0) for head in range(heads)]

    def score(head, span):
        begin, end, low, high = span
        return nn(keys[low:high], place(queries[rows(head), begin:end], head, marks[:, begin:end]))

    def finish(head, span, top, probs):
        begin, end, low, high = span
        out = nn(summed[head][:, low:high], probs)
        total = out[HEAD_DIM : HEAD_DIM + 1]
        across_ref[rows(head), begin:end] = out[:HEAD_DIM] * (1.0 / total)
        lse_ref[head : head + 1, begin:end] = (top + jnp.log2(total)) * (1.0 / SCALE2)

    scores = [score(*body) for body in bodies[:2]]
    waiting = None
    for at, body in enumerate(bodies):
        current = scores.pop(0)
        if at + 2 < len(bodies):
            scores.append(score(*bodies[at + 2]))
        top = jnp.max(current, axis=0, keepdims=True) * SCALE2
        probs = jnp.exp2(current * SCALE2 - top).astype(BF16)
        if waiting is not None:
            finish(*waiting)
        waiting = (*body, top, probs)
    finish(*waiting)
    lse_ref[heads:, :] = jnp.zeros((SUBLANES - heads, length), F32)
    out_ref[...] = across_ref[...].T.astype(BF16)


def attend_back_kernel(
    row_ref, q_ref, k_ref, v_ref, grad_ref, across_ref, lse_ref,
    gq_ref, gk_ref, gv_ref, marks_ref, turned_ref,
):
    @pl.when(pl.program_id(0) == 0)
    def _():
        marks_ref[...] = key_marks(row_ref[...])

    length = q_ref.shape[0]
    grad = grad_ref[...]
    queries = q_ref[...].T
    turned_keys = k_ref[...].T
    grads = grad.T
    keys = jnp.concatenate([k_ref[...], marks_ref[...]], axis=1)
    values = jnp.concatenate([v_ref[...], marks_ref[...]], axis=1)
    low_marks = query_marks(row_ref[...])
    blank = jnp.zeros((SUBLANES, length), F32)
    lane = lax.broadcasted_iota(jnp.int32, (1, LANES), 1) // HEAD_DIM
    heads = []
    for head in range(LANES // HEAD_DIM):
        rows = slice(HEAD_DIM * head, HEAD_DIM * (head + 1))
        inner = jnp.sum(grads[rows].astype(F32) * across_ref[rows, :], axis=0, keepdims=True)
        lse = lse_ref[head : head + 1, :]
        score_marks = jnp.concatenate([low_marks, *split3(-lse), blank[:5]], axis=0)
        inner_marks = jnp.concatenate([blank, *split3(-inner), blank[:5]], axis=0)
        zero = jnp.zeros_like(grad)
        heads.append(
            (
                rows,
                score_marks.astype(BF16),
                inner_marks.astype(BF16),
                jnp.where(lane == head, q_ref[...], zero),
                jnp.where(lane == head, grad, zero),
            )
        )
    bodies = [
        (head, at, span) for head in range(len(heads)) for at, span in enumerate(spans(length))
    ]
    sums = [[None, None] for _ in spans(length)]

    def pair(head, at, span):
        begin, end, low, high = span
        rows, score_marks, inner_marks, _, _ = heads[head]
        return (
            nn(keys[low:high], place(queries[rows, begin:end], head, score_marks[:, begin:end])),
            nn(values[low:high], place(grads[rows, begin:end], head, inner_marks[:, begin:end])),
        )

    def finish(head, at, span, score_grads, probs):
        begin, end, low, high = span
        rows, _, _, own_queries, own_grads = heads[head]
        for which, (left, right) in enumerate(
            ((score_grads, own_queries[begin:end]), (probs, own_grads[begin:end]))
        ):
            part = nn(left, right)
            sums[at][which] = part if sums[at][which] is None else sums[at][which] + part
        turned_ref[rows, begin:end] = nn(turned_keys[rows, low:high], score_grads)

    ahead = [pair(*bodies[0])]
    waiting = None
    for at, body in enumerate(bodies):
        scores, differences = ahead.pop(0)
        if at + 1 < len(bodies):
            ahead.append(pair(*bodies[at + 1]))
        probs = jnp.exp2(scores * SCALE2)
        score_grads = (probs * differences).astype(BF16)
        if waiting is not None:
            finish(*waiting)
        waiting = (*body, score_grads, probs.astype(BF16))
    finish(*waiting)
    gq_ref[...] = (turned_ref[...].T * SCALE).astype(BF16)
    for which, (ref, factor) in enumerate(((gk_ref, SCALE), (gv_ref, 1.0))):
        total = None
        for at, (_, _, low, high) in enumerate(spans(length)):
            parts = [sums[at][which]]
            if low:
                parts.insert(0, jnp.zeros((low, LANES), F32))
            if high < length:
                parts.append(jnp.zeros((length - high, LANES), F32))
            part = jnp.concatenate(parts, axis=0) if len(parts) > 1 else parts[0]
            total = part if total is None else total + part
        ref[...] = (total * factor).astype(BF16)


def attention_specs(length, width, begin=0):
    tiles = width // LANES

    def tile(at, begin=begin):
        return pl.BlockSpec((length, LANES), lambda i: (0, at + begin + i))

    return (
        tiles,
        tile,
        pl.BlockSpec((1, length), lambda i: (0, 0)),
        pl.BlockSpec((LANES, length), lambda i: (begin + i, 0)),
        pl.BlockSpec((SUBLANES, length), lambda i: (begin + i, 0)),
    )


def attend(joined, row):
    length = joined.shape[0]
    width = joined.shape[1] // 3
    tiles, tile, row_spec, across_spec, lse_spec = attention_specs(length, width)
    return call(
        attend_kernel,
        [((length, width), BF16), ((width, length), F32), ((SUBLANES * tiles, length), F32)],
        (row, joined, joined, joined),
        grid=(tiles,),
        in_specs=[row_spec, tile(0), tile(tiles), tile(2 * tiles)],
        out_specs=[tile(0), across_spec, lse_spec],
        scratch=[pltpu.VMEM((length, LANES), BF16)],
    )


def attend_back(joined, row, grad, across, lse, begin=0, end=None):
    length = joined.shape[0]
    width = joined.shape[1] // 3
    specs = attention_specs(length, width, begin)
    tiles, tile, row_spec, across_spec, lse_spec = specs
    count = (end or tiles) - begin
    return call(
        attend_back_kernel,
        [((length, count * LANES), BF16)] * 3,
        (row, joined, joined, joined, grad, across, lse),
        grid=(count,),
        in_specs=[row_spec, tile(0), tile(tiles), tile(2 * tiles), tile(0), across_spec, lse_spec],
        out_specs=[tile(0, 0)] * 3,
        scratch=[pltpu.VMEM((length, LANES), BF16), pltpu.VMEM((LANES, length), F32)],
        mib=24,
    )


def slab_kernel(heads_ref, out_ref, short_ref, up_ref, slab_ref):
    rows = heads_ref.shape[0]
    width = out_ref.shape[1]
    slab_ref[:rows, : 3 * width] = heads_ref[...]
    slab_ref[:rows, 3 * width :] = out_ref[...]
    slab_ref[rows:, :] = jnp.zeros((VECTORS, 4 * width), BF16)
    slab_ref[rows:, :rows] = short_ref[...]
    slab_ref[rows:, LANES : LANES + up_ref.shape[1]] = jnp.broadcast_to(
        up_ref[...], (VECTORS, up_ref.shape[1])
    )


def project_kernel(count, rows, hidden, position_ref, x_ref, *refs):
    slabs, refs = refs[:count], refs[count:]
    length, width = x_ref.shape
    if count:
        low_ref, joined_ref, heads_ref, out_ref, vector_ref, bias_ref, short_ref, sems = refs
        copies = []
        for at, slab in enumerate(slabs):
            begin = pl.multiple_of(position_ref[at] * rows, SUBLANES)
            here = pl.ds(begin, rows)
            for which, (source, target) in enumerate(
                (
                    (slab.at[pl.ds(0, rows), pl.ds(0, 3 * width)], heads_ref.at[here]),
                    (slab.at[pl.ds(0, rows), pl.ds(3 * width, width)], out_ref.at[here]),
                    (slab.at[pl.ds(rows, VECTORS), pl.ds(0, LANES + hidden)], short_ref.at[at]),
                )
            ):
                copy = pltpu.make_async_copy(source, target, sems.at[at, which])
                copy.start()
                copies.append(copy)
    else:
        heads_ref, vector_ref, low_ref, joined_ref = refs
    if count:
        for copy in copies:
            copy.wait()
        vectors = jnp.zeros((VECTORS, width), F32)
        for at in range(count):
            begin = position_ref[at] * rows
            short = short_ref[at, :, :LANES].astype(F32)
            lane = lax.broadcasted_iota(jnp.int32, short.shape, 1)
            short = jnp.where(lane < rows, short, 0.0)
            short = jnp.concatenate([short, jnp.zeros((VECTORS, width - LANES), F32)], axis=1)
            vectors = vectors + pltpu.roll(short, begin, 1)
            if at < count // 2:
                begin = pl.multiple_of(lax.div(position_ref[at], 2) * hidden, LANES)
                bias_ref[:, pl.ds(begin, hidden)] = short_ref[at, :, LANES:].astype(F32)
        vector_ref[...] = vectors
    zero = jnp.zeros((1, width), F32)
    vector = vector_ref[...]
    bias = jnp.concatenate(
        [vector[QUERY_BIAS : QUERY_BIAS + 1], zero, vector[VALUE_BIAS : VALUE_BIAS + 1]], axis=1
    )
    for at in range(0, length, ROWS):
        normal, _ = unit(x_ref[at : at + ROWS, :].astype(F32))
        low_ref[at : at + ROWS, :] = (
            normal * vector[ATTEND_GAIN : ATTEND_GAIN + 1]
            + vector[ATTEND_SHIFT : ATTEND_SHIFT + 1]
        ).astype(BF16)
    for at in range(0, 3 * width, width):
        here = slice(at, at + width)
        joined_ref[:, here] = (nn(low_ref[...], heads_ref[:, here]) + bias[:, here]).astype(BF16)


def middle_kernel(x_ref, attended_ref, out_ref, vector_ref, middle_ref, low_ref):
    vector = vector_ref[...]
    for at in range(0, x_ref.shape[0], ROWS):
        here = slice(at, at + ROWS)
        middle = (
            x_ref[here, :].astype(F32)
            + nn(attended_ref[here, :], out_ref[...])
            + vector[OUTPUT_BIAS : OUTPUT_BIAS + 1]
        )
        middle_ref[here, :] = middle
        normal, _ = unit(middle)
        low_ref[here, :] = (
            normal * vector[FORWARD_GAIN : FORWARD_GAIN + 1]
            + vector[FORWARD_SHIFT : FORWARD_SHIFT + 1]
        ).astype(BF16)


def up_kernel(position_ref, own_ref, other_ref, bias_ref, *refs):
    parts, (act_ref, slope_ref, full_ref) = refs[: len(refs) - 3], refs[len(refs) - 3 :]
    for at, part in enumerate(parts):
        rows = part.shape[0]
        begin = pl.multiple_of(position_ref[at] * rows, SUBLANES)
        full_ref[pl.ds(begin, rows), :] = part[...]
    weight = full_ref[...]
    bias = bias_ref[:1, :]
    length = own_ref.shape[0]
    for which, ref in enumerate((own_ref, other_ref)):
        for at in range(0, length, ROWS):
            upward = nn(ref[at : at + ROWS, :], weight) + bias
            share = 0.5 + 0.5 * lax.erf(upward * math.sqrt(0.5))
            bell = jnp.exp2((upward * upward) * (-0.5 * math.log2(math.e)))
            here = slice(which * length + at, which * length + at + ROWS)
            act_ref[here, :] = (upward * share).astype(BF16)
            slope = share + upward * (bell * (1.0 / math.sqrt(2.0 * math.pi)))
            slope_ref[here, :] = slope.astype(BF16)


def column_specs(half, block):
    block = min(block, half)

    def column(height):
        return pl.BlockSpec((height, block), lambda i, at: (0, i))

    return half // block, block, column


def whole_spec(shape):
    return pl.BlockSpec(shape, lambda i, at: (0,) * len(shape))


def up_project(own, other, bias, parts, positions, hidden):
    length, width = own.shape
    half = bias.shape[1]
    paired = parts[0].shape[1] > half
    steps, block, column = column_specs(half, hidden if paired else 512)
    whole = whole_spec((length, width))

    def part_spec(part):
        if paired:
            return pl.BlockSpec((part.shape[0], block), lambda i, at: (0, 2 * i + at[len(parts)]))
        return column(part.shape[0])

    return call(
        up_kernel,
        [((2 * length, half), BF16), ((2 * length, half), BF16), ((width, half), BF16)],
        (own, other, bias, *parts),
        positions,
        grid=(steps,),
        in_specs=[whole, whole, column(bias.shape[0])] + [part_spec(part) for part in parts],
        out_specs=[column(2 * length), column(2 * length), column(width)],
    )


def down_kernel(position_ref, act_ref, *refs):
    parts, (own_ref, other_ref, full_ref) = refs[: len(refs) - 3], refs[len(refs) - 3 :]
    length = own_ref.shape[0]
    for at, part in enumerate(parts):
        rows = part.shape[0]
        begin = pl.multiple_of(position_ref[at] * rows, SUBLANES)
        full_ref[pl.ds(begin, rows), :] = part[...]
    for which, ref in enumerate((own_ref, other_ref)):
        here = slice(which * length, (which + 1) * length)
        ref[...] = nn(act_ref[here, :], full_ref[...]).astype(ref.dtype)


def down_project(act, parts, positions):
    length = act.shape[0] // 2
    half = act.shape[1]
    width = parts[0].shape[1]
    return call(
        down_kernel,
        [((length, width), F32), ((length, width), BF16), ((half, width), BF16)],
        (act, *parts),
        positions,
        mib=20,
    )


def loss_kernel(
    middle_ref, own_ref, got_ref, vector_ref, readout_ref, target_ref, mask_ref,
    low_ref, down_ref, grad_ref, sums_ref,
):
    result = (
        middle_ref[...]
        + (own_ref[...] + got_ref[...].astype(F32))
        + vector_ref[DOWN_BIAS : DOWN_BIAS + 1, :]
    ).astype(BF16)
    low_ref[...] = result
    logits = nt(readout_ref[...], result)
    length = logits.shape[1]
    top = jnp.max(logits, axis=0, keepdims=True)
    shifted = jnp.exp(logits - top)
    total = jnp.sum(shifted, axis=0, keepdims=True)
    onehot = lax.broadcasted_iota(jnp.int32, logits.shape, 0) == target_ref[...]
    picked = jnp.sum(jnp.where(onehot, logits, 0.0), axis=0, keepdims=True)
    weight = mask_ref[...].astype(F32)
    loss = (top + jnp.log(total) - picked) * weight
    loss_lanes = jnp.zeros((1, LANES), F32)
    count_lanes = jnp.zeros((1, LANES), F32)
    for at in range(0, length, LANES):
        loss_lanes = loss_lanes + loss[:, at : at + LANES]
        count_lanes = count_lanes + weight[:, at : at + LANES]
    lanes = jnp.concatenate([loss_lanes, count_lanes], axis=0)
    lanes = jnp.concatenate([lanes, jnp.zeros((2, result.shape[1] - LANES), F32)], axis=1)
    grad_logits = (weight * (shifted / total - onehot.astype(F32))).astype(BF16)
    grad_ref[...] = grad_logits
    low = tn(grad_logits, readout_ref[...]).astype(BF16)
    down_ref[...] = low
    sums = jnp.sum(low.astype(F32), axis=0, keepdims=True)
    blank = jnp.zeros((SUBLANES - 3, result.shape[1]), F32)
    sums_ref[...] = jnp.concatenate([lanes, sums, blank], axis=0)


def down_grad_kernel(chips, position_ref, act_ref, own_ref, other_ref, *out_refs):
    length = own_ref.shape[0]
    hidden = act_ref.shape[1] // chips
    for offset in range(chips):
        if len(out_refs) == 1:
            begin = offset * hidden
        else:
            begin = pl.multiple_of((position_ref[0] ^ offset) * hidden, LANES)
        here = pl.ds(begin, hidden)
        part = tn(act_ref[:length, here], own_ref[...]) + tn(act_ref[length:, here], other_ref[...])
        part = part.astype(BF16)
        if len(out_refs) == 1:
            out_refs[0][begin : begin + hidden, :] = part
            continue
        keep_x, send_x, keep_y, send_y = out_refs
        half = hidden // 2
        (send_x if offset % 2 else keep_x)[offset // 2, :, :] = part[:half]
        (send_y if offset // 2 else keep_y)[offset % 2, :, :] = part[half:]


def down_grad(act, own, other, chips, position):
    half = act.shape[1]
    width = own.shape[1]
    if square():
        outs = [((2, half // chips // 2, width), BF16)] * 4
    else:
        outs = [((half, width), BF16)]
    return call(
        functools.partial(down_grad_kernel, chips), outs, (act, own, other), position, mib=20
    )


def up_grad_kernel(
    rows, position_ref, own_ref, other_ref, slope_ref, second_ref, second_other_ref, down_ref,
    up_ref, bias_ref, *refs,
):
    out_refs, part_ref = refs[:-1], refs[-1]
    length = own_ref.shape[0]
    total = None
    grads = []
    for which, ref in enumerate((own_ref, other_ref)):
        for at in range(0, length, 2 * ROWS):
            here = slice(which * length + at, which * length + at + 2 * ROWS)
            grad = nt(ref[at : at + 2 * ROWS, :], down_ref[...]) * slope_ref[here, :].astype(F32)
            low = grad.astype(BF16)
            up_ref[here, :] = low
            part = jnp.sum(low.astype(F32), axis=0, keepdims=True)
            total = part if total is None else total + part
    bias_ref[...] = total
    part = tn(second_ref[...], up_ref[:length, :]) + tn(second_other_ref[...], up_ref[length:, :])
    if len(out_refs) == 1:
        out_refs[0][...] = part.astype(BF16)
        return
    part_ref[...] = part
    keep_x, send_x, keep_y, send_y = out_refs
    for offset in range(4):
        begin = pl.multiple_of((position_ref[0] ^ offset) * (2 * rows), SUBLANES)
        upper = part_ref[pl.ds(begin, rows), :].astype(BF16)
        lower = part_ref[pl.ds(begin + rows, rows), :].astype(BF16)
        (send_x if offset % 2 else keep_x)[offset // 2, :, :] = upper
        (send_y if offset // 2 else keep_y)[offset % 2, :, :] = lower


def up_grad(own, other, slope, second, second_other, down_full, rows, position):
    length, width = own.shape
    half = slope.shape[1]
    steps, block, column = column_specs(half, 512)
    whole = whole_spec((length, width))
    if square():
        outs = [((2, rows, half), BF16)] * 4
        specs = [pl.BlockSpec((2, rows, block), lambda i, at: (0, 0, i))] * 4
    else:
        outs = [((width, half), BF16)]
        specs = [column(width)]
    return call(
        functools.partial(up_grad_kernel, rows),
        [((2 * length, half), BF16), ((1, half), F32), *outs],
        (own, other, slope, second, second_other, down_full),
        position,
        grid=(steps,),
        in_specs=[
            whole, whole, column(2 * length), whole, whole,
            pl.BlockSpec((block, width), lambda i, at: (i, 0)),
        ],
        out_specs=[column(2 * length), column(1), *specs],
        scratch=[pltpu.VMEM((width, block), F32)],
        mib=20,
    )


def inward_kernel(grad_ref, up_ref, own_far, other_ref, own_ref, sem):
    length = other_ref.shape[0]
    own_ref[...] = nt(grad_ref[:length, :], up_ref[...])
    copy = pltpu.make_async_copy(own_ref, own_far, sem)
    copy.start()
    other_ref[...] = nt(grad_ref[length:, :], up_ref[...]).astype(BF16)
    copy.wait()


def join_kernel(hidden, position_ref, mine_ref, other_ref, out_ref):
    for at in range(mine_ref.shape[1] // hidden):
        here = slice(hidden * at, hidden * (at + 1))
        for core, ref in enumerate((mine_ref, other_ref)):
            begin = (2 * at + (position_ref[0] + core) % 2) * hidden
            out_ref[:, pl.ds(pl.multiple_of(begin, LANES), hidden)] = ref[:, here].astype(F32)


def branch_kernel(
    got_ref, own_far, middle_far, logits_ref, classes_ref, out_ref, vector_ref,
    grad_ref, branch_ref, attended_ref, sums_ref, own_ref, middle_ref, sems,
):
    width = own_ref.shape[1]
    blocks = range(0, own_ref.shape[0], ROWS)
    copies = []
    for at in blocks:
        here = pl.ds(at, ROWS)
        copies.append(
            [
                pltpu.make_async_copy(far.at[here], ref.at[here], sems.at[at // ROWS, which])
                for which, (far, ref) in enumerate(((own_far, own_ref), (middle_far, middle_ref)))
            ]
        )
        for copy in copies[-1]:
            copy.start()
    gain = vector_ref[FORWARD_GAIN : FORWARD_GAIN + 1, :]
    sums = [jnp.zeros((1, width), F32) for _ in range(3)]
    for at in blocks:
        for copy in copies[at // ROWS]:
            copy.wait()
        here = slice(at, at + ROWS)
        grad = own_ref[here, :] + got_ref[here, :].astype(F32)
        normal, inverse = unit(middle_ref[here, :])
        result = tn(logits_ref[:, here], classes_ref[...])
        middle = result + unit_back(grad, normal, inverse, gain)
        grad_ref[here, :] = middle
        branch = middle.astype(BF16)
        branch_ref[here, :] = branch
        attended_ref[here, :] = nt(branch, out_ref[...]).astype(BF16)
        for which, part in enumerate((grad * normal, grad, branch.astype(F32))):
            sums[which] = sums[which] + jnp.sum(part, axis=0, keepdims=True)
    blank = jnp.zeros((SUBLANES - 3, width), F32)
    sums_ref[...] = jnp.concatenate([*sums, blank], axis=0)


def last_kernel(count, rows, hidden, pieces, position_ref, x_ref, low_ref, *refs):
    grad_refs, refs = refs[: 3 * pieces], refs[3 * pieces :]
    heads_ref, attended_ref, branch_ref, grad_ref, vector_ref, *refs = refs
    sums_ref, loss_ref, up_ref, *refs = refs
    stacks, (input_ref, vectors_ref, full_ref) = refs[:-3], refs[-3:]
    width = x_ref.shape[1]

    def grads(which, here):
        parts = [ref[here, :] for ref in grad_refs[which::3]]
        return jnp.concatenate(parts, axis=1) if pieces > 1 else parts[0]

    for at in range(3):
        part = tn(low_ref[...], grads(at, slice(None)))
        full_ref[:, width * at : width * (at + 1)] = part.astype(BF16)
    full_ref[:, 3 * width :] = tn(attended_ref[...], branch_ref[...]).astype(BF16)
    gain = vector_ref[ATTEND_GAIN : ATTEND_GAIN + 1, :]
    sums = [jnp.zeros((1, width), F32) for _ in range(4)]
    for at in range(0, x_ref.shape[0], ROWS):
        here = slice(at, at + ROWS)
        grad_query, grad_key, grad_value = [grads(at, here) for at in range(3)]
        grad = (
            nt(grad_query, heads_ref[:, :width])
            + nt(grad_key, heads_ref[:, width : 2 * width])
            + nt(grad_value, heads_ref[:, 2 * width :])
        )
        normal, inverse = unit(x_ref[here, :].astype(F32))
        input_ref[here, :] = grad_ref[here, :] + unit_back(grad, normal, inverse, gain)
        parts = (grad * normal, grad, grad_query.astype(F32), grad_value.astype(F32))
        for which, part in enumerate(parts):
            sums[which] = sums[which] + jnp.sum(part, axis=0, keepdims=True)
    vectors = jnp.concatenate(
        [*sums, sums_ref[2:3, :], sums_ref[0:1, :], sums_ref[1:2, :], loss_ref[2:3, :]], axis=0
    )
    vectors_ref[...] = vectors
    blank = jnp.zeros((VECTORS - 1, hidden), F32)
    lanes = jnp.concatenate([loss_ref[:2, :LANES], jnp.zeros((VECTORS - 2, LANES), F32)], axis=0)
    for at in range(count):
        stack = stacks[at // (count // 2)]
        place_at = position_ref[at]
        begin = pl.multiple_of(place_at * rows, SUBLANES)
        cuts = [
            (pick, slice(2 * width * side, 2 * width * (side + 1)))
            for side, pick in enumerate(((0, 2, 1, 3)[at % 4], 4 + at % 4))
        ]
        for pick, here in cuts:
            stack[pick, :rows, :] = full_ref[pl.ds(begin, rows), here]
        short = pltpu.roll(vectors, width - begin, 1)[:, :LANES]
        if at < count // 2:
            hidden_at = pl.multiple_of(lax.div(place_at, 2) * hidden, LANES)
            bias = jnp.concatenate([up_ref[:, pl.ds(hidden_at, hidden)], blank], axis=0)
        else:
            bias = jnp.zeros((VECTORS, hidden), F32)
        row = jnp.concatenate([short, bias, lanes], axis=1).astype(BF16)
        pad = jnp.zeros((VECTORS, 4 * width - row.shape[1]), BF16)
        row = jnp.concatenate([row, pad], axis=1)
        for pick, here in cuts:
            stack[pick, rows:, :] = row[:, here]


def settle_kernel(rows, hidden, place_ref, *refs):
    totals, outers, refs = refs[:2], refs[2:4], refs[4:]
    heads_ref, out_ref, short_ref, loss_ref, count_ref = refs
    width = out_ref.shape[1]
    inner = (place_ref[0] == 1) | (place_ref[0] == 2)
    left, right = [
        jnp.where(inner, total[...], outer[...]).astype(F32) for total, outer in zip(totals, outers)
    ]
    heads_ref[:, : 2 * width] = left[:rows]
    heads_ref[:, 2 * width :] = right[:rows, :width]
    out_ref[...] = right[:rows, width:]
    short_ref[...] = left[rows:]
    lanes = left[rows:, LANES + hidden : 2 * LANES + hidden]
    loss_ref[0] = jnp.sum(lanes[0:1])
    count_ref[0] = jnp.sum(lanes[1:2]).astype(jnp.int32)


def swap(values, bit):
    return lax.ppermute(values, "wide", [(i, i ^ bit) for i in range(lax.axis_size("wide"))])


def same_core_groups():
    chips = lax.axis_size("wide") // 2
    return [[2 * chip + core for chip in range(chips)] for core in range(2)]


def square():
    return lax.axis_size("wide") == 8


def spread_chips(shard):
    return lax.all_gather(shard, "wide", axis=0, axis_index_groups=same_core_groups())


def add_low(*parts):
    return sum(part.astype(F32) for part in parts).astype(BF16)


def collect_chips(parts):
    return lax.psum_scatter(
        parts, "wide", scatter_dimension=0, axis_index_groups=same_core_groups()
    )


def after(values, *gates):
    leaves, tree = jax.tree.flatten(values)
    held = lax.optimization_barrier((*leaves, *jax.tree.leaves(gates)))
    return jax.tree.unflatten(tree, held[: len(leaves)])


INWARD, ACROSS, OUTWARD = [(0, 1), (3, 2)], [(1, 2), (2, 1)], [(1, 0), (2, 3)]


def hop(parts, pairs):
    return [lax.ppermute(part, "narrow", pairs) for part in parts]


def add_each(left, right):
    return [add_low(a, b) for a, b in zip(left, right)]


def settle(total, outer):
    place_at = lax.axis_index("narrow")
    return jnp.where((place_at == 1) | (place_at == 2), total, outer)


def sum_narrow(shard):
    if lax.axis_size("narrow") != 4:
        return lax.psum(shard, "narrow")
    half = add_low(shard, *hop([shard], INWARD))
    total = add_low(half, *hop([half], ACROSS))
    return settle(total, *hop([total], OUTWARD))


def local(
    layer_input, segments, targets, loss_mask, readout,
    attend_gain, attend_shift, heads_weight, query_bias, value_bias, output_weight, output_bias,
    forward_gain, forward_shift, up_weight, up_bias, down_weight, down_bias,
):
    length = layer_input.shape[1]
    width = layer_input.shape[2]
    wide = lax.axis_size("wide")
    chips = wide // 2
    core = lax.axis_index("wide") % 2
    chip = lax.axis_index("wide") // 2
    rows = heads_weight.shape[0]
    hidden = up_bias.shape[0]
    half = chips * hidden
    x = layer_input[0]
    classes = readout.T
    vmem = pl.BlockSpec(memory_space=pltpu.VMEM)
    far_away = pl.BlockSpec(memory_space=pltpu.HBM)

    def by_core(mine, other, axis):
        return jnp.where(
            core == 0, jnp.stack([mine, other], axis), jnp.stack([other, mine], axis)
        )

    def mine_of(values, axis, flip=0):
        return lax.dynamic_index_in_dim(values, core ^ flip, axis, keepdims=False)

    short = jnp.stack(
        [
            attend_gain, attend_shift, query_bias, value_bias,
            output_bias, forward_gain, forward_shift, down_bias,
        ]
    )
    core_position = core.reshape(1).astype(jnp.int32)
    chip_position = chip.reshape(1).astype(jnp.int32)
    if square():
        offsets = jnp.arange(4, dtype=jnp.int32)
        (slab,) = call(
            slab_kernel,
            [((rows + VECTORS, 4 * width), BF16)],
            (heads_weight, output_weight, short, up_bias[None]),
        )
        near_x, near_y, far = swap(slab, 2), swap(slab, 4), swap(slab, 6)
        swapped = swap(slab, 1)
        devices = 2 * (chip ^ offsets) + core
        positions = jnp.concatenate([devices, devices ^ 1]).astype(jnp.int32)
        up_weight, positions = after([up_weight, positions], near_x, swapped)
        up_x, up_y = swap(up_weight, 2), swap(up_weight, 4)
        swapped_x = swap(near_x, 1)
        near_y, far = after([near_y, far], swapped_x)
        slabs = [slab, near_x, near_y, far, swapped, swapped_x, swap(near_y, 1), swap(far, 1)]
        first_low, joined, heads_full, output_full, vectors, up_bias_half = call(
            functools.partial(project_kernel, len(slabs), rows, hidden),
            [
                ((length, width), BF16), ((length, 3 * width), BF16), ((width, 3 * width), BF16),
                ((width, width), BF16), ((VECTORS, width), F32), ((VECTORS, half), F32),
            ],
            (x, *slabs),
            positions,
            in_specs=[pl.BlockSpec(memory_space=pltpu.VMEM)]
            + [pl.BlockSpec(memory_space=pltpu.HBM)] * len(slabs),
            scratch=[
                pltpu.VMEM((len(slabs), VECTORS, LANES + hidden), BF16),
                pltpu.SemaphoreType.DMA((len(slabs), 3)),
            ],
            mib=20,
        )
    else:
        tail = jnp.concatenate([short.reshape(1, 8 * rows), up_bias[None]], axis=1)
        tail = jnp.pad(tail, ((0, 0), (0, 4 * width - tail.shape[1])))
        slab = jnp.concatenate(
            [jnp.concatenate([heads_weight, output_weight], axis=1), tail], axis=0
        )
        slabs = lax.all_gather(slab, "wide", axis=0)
        attend_full = slabs[:, :rows].reshape(width, 4 * width)
        heads_full = attend_full[:, : 3 * width]
        output_full = attend_full[:, 3 * width :]
        last = slabs[:, rows].astype(F32)
        vectors = last[:, : 8 * rows].reshape(wide, 8, rows).transpose(1, 0, 2).reshape(8, width)
        up_bias_half = mine_of(last[:, 8 * rows : 8 * rows + hidden].reshape(chips, 2, hidden), 1)
        up_bias_half = jnp.broadcast_to(up_bias_half.reshape(1, half), (VECTORS, half))
        positions = jnp.zeros((1,), jnp.int32)
        first_low, joined = call(
            functools.partial(project_kernel, 0, rows, hidden),
            [((length, width), BF16), ((length, 3 * width), BF16)],
            (x, heads_full, vectors),
            positions,
            mib=20,
        )
        up_view = up_weight.reshape(rows, chips, 2, hidden)
        up_pair = by_core(
            mine_of(up_view, 2).reshape(rows, half),
            swap(mine_of(up_view, 2, 1).reshape(rows, half), 1),
            0,
        ).reshape(2 * rows, half)
        up_parts = [spread_chips(up_pair).reshape(width, half)]
        down_parts = [spread_chips(down_weight).reshape(half, width)]
        up_positions = down_positions = positions

    attended, across, lse = attend(joined, segments)
    if square():
        up_x, up_y = after([up_x, up_y], attended)
        middle_row = rows // 2
        up_parts = [
            up_weight, up_x, up_y, swap(up_y[:middle_row], 2), swap(up_x[middle_row:], 4)
        ]
        up_parts = up_parts + [swap(part, 1) for part in up_parts]
        at = jnp.arange(11, dtype=jnp.int32)
        part = at % 5
        device = 2 * (chip ^ jnp.minimum(part, 3)) + (core ^ (at // 5))
        up_positions = jnp.where(part < 3, device, 2 * device + part - 3)
        up_positions = jnp.where(at < 10, up_positions, core).astype(jnp.int32)
        middle_row = hidden // 2
        upper, lower = after(
            [down_weight[:middle_row], down_weight[middle_row:]], up_x, up_y
        )
        lower_x, upper_y = swap(lower, 2), swap(upper, 4)
        upper_x, lower_y = swap(upper, 2), swap(lower, 4)
        down_parts = [
            down_weight, upper_x, lower_x, upper_y, lower_y
        ]
        at = jnp.arange(7, dtype=jnp.int32)
        down_positions = jnp.where(at == 0, chip, 2 * (chip ^ ((at + 1) // 2)) + (at + 1) % 2)
    middle, second_low = call(
        middle_kernel,
        [((length, width), F32), ((length, width), BF16)],
        (x, attended, output_full, vectors),
    )

    second_other = swap(second_low, 1)
    activated, slope, up_full = up_project(
        second_low, second_other, up_bias_half, up_parts, up_positions, hidden
    )
    if square():
        passed_x, passed_y = after([upper_y, lower_x], activated)
        down_parts = down_parts + [swap(passed_x, 2), swap(passed_y, 4)]
    outward, outward_other, down_full = down_project(activated, down_parts, down_positions)
    result_low, grad_down, grad_logits, loss_sums = call(
        loss_kernel,
        [
            ((length, width), BF16), ((length, width), BF16), (classes.shape[:1] + (length,), BF16),
            ((SUBLANES, width), F32),
        ],
        (middle, outward, swap(outward_other, 1), vectors, classes, targets, loss_mask),
    )

    grad_down_other = swap(grad_down, 1)
    down_parts = down_grad(activated, grad_down, grad_down_other, chips, chip_position)
    if square():
        keep_dx, send_dx, keep_dy, send_dy = down_parts
        down_first = [swap(send_dx, 2), swap(send_dy, 4)]
        (grad_down_other,) = after([grad_down_other], send_dx)
    grad_up, up_bias_part, *up_parts = up_grad(
        grad_down, grad_down_other, slope, second_low, second_other, down_full, rows, chip_position
    )
    inward, inward_other = call(
        inward_kernel,
        [((length, width), F32), ((length, width), BF16)],
        (grad_up, up_full),
        out_specs=[far_away, vmem],
        scratch=[pltpu.VMEM((length, width), F32), pltpu.SemaphoreType.DMA],
        mib=20,
    )
    got_inward = swap(inward_other, 1)
    if square():
        down_second = [
            add_low(keep_dx[1], down_first[0][1]), add_low(keep_dy[1], down_first[1][1])
        ]
        (got_inward,) = after([got_inward], down_second)
        keep_ux, send_ux, keep_uy, send_uy = up_parts
        send_ux, send_uy = after([send_ux, send_uy], down_second)
        down_got = [swap(down_second[0], 4), swap(down_second[1], 2)]
        up_first = [swap(send_ux, 2), swap(send_uy, 4)]
    grad_middle, grad_branch, grad_attended, branch_sums = call(
        branch_kernel,
        [
            ((length, width), F32), ((length, width), BF16), ((length, width), BF16),
            ((SUBLANES, width), F32),
        ],
        (got_inward, inward, middle, grad_logits, classes, output_full, vectors),
        in_specs=[vmem, far_away, far_away, vmem, vmem, vmem, vmem],
        scratch=[
            *[pltpu.VMEM((length, width), F32)] * 2,
            pltpu.SemaphoreType.DMA((length // ROWS, 2)),
        ],
        mib=24,
    )

    if square():
        attend_grads = attend_back(joined, segments, grad_attended, across, lse)
        down_got = after(down_got, attend_grads[0])
        down_narrow = [
            add_low(keep_dx[0], down_first[0][0], down_got[0]),
            add_low(keep_dy[0], down_first[1][0], down_got[1]),
        ]
        down_in = hop(down_narrow, INWARD)
        attend_grads = after(attend_grads, down_narrow)
    else:
        attend_grads = attend_back(joined, segments, grad_attended, across, lse)
    stack_shape = ((8, rows + VECTORS, 2 * width), BF16)
    *stacks, input_grad, short_sums, attend_part = call(
        functools.partial(last_kernel, 8 if square() else 0, rows, hidden, len(attend_grads) // 3),
        ([stack_shape] * 2 if square() else [])
        + [((length, width), F32), ((VECTORS, width), F32), ((width, 4 * width), BF16)],
        (
            x, first_low, *attend_grads, heads_full, attended, grad_branch,
            grad_middle, vectors, branch_sums, loss_sums, up_bias_part,
        ),
        positions,
        mib=40,
    )
    if square():
        mine, others = stacks
        mine_got = swap(others, 1)
        up_first = after(up_first, mine)
        up_second = [add_low(keep_ux[1], up_first[0][1]), add_low(keep_uy[1], up_first[1][1])]
        up_got = [swap(up_second[0], 4), swap(up_second[1], 2)]

        down_in = after(down_in, up_second)
        down_half = jnp.concatenate(add_each(down_narrow, down_in))
        (down_mid,) = hop([down_half], ACROSS)

        (mine_got,) = after([mine_got], down_half)
        both = add_low(mine, mine_got)
        side_first = [swap(both[2:4], 2), swap(both[6:8], 4)]

        up_got = after(up_got, both)
        up_narrow = [
            add_low(keep_ux[0], up_first[0][0], up_got[0]),
            add_low(keep_uy[0], up_first[1][0], up_got[1]),
        ]
        up_in = hop(up_narrow, INWARD)

        side_first = after(side_first, up_narrow)
        side_second = [add_low(both[1], side_first[0][1]), add_low(both[5], side_first[1][1])]
        side_got = [swap(side_second[0], 4), swap(side_second[1], 2)]

        (down_mid,) = after([down_mid], side_second)
        down_total = add_low(down_half, down_mid)
        (down_out,) = hop([down_total], OUTWARD)

        side_got = after(side_got, down_total)
        slab_narrow = [
            add_low(both[0], side_first[0][0], side_got[0]),
            add_low(both[4], side_first[1][0], side_got[1]),
        ]
        slab_in = hop(slab_narrow, INWARD)

        (came,) = after(up_in[:1], slab_narrow)
        up_half = [add_low(up_narrow[0], came)]
        up_mid = hop(up_half, ACROSS)

        (came,) = after(up_in[1:], up_half)
        up_half.append(add_low(up_narrow[1], came))
        up_mid += hop(up_half[1:], ACROSS)

        (came,) = after(up_mid[:1], up_half[1])
        up_total = [add_low(up_half[0], came)]
        up_out = hop(up_total, OUTWARD)

        (came,) = after(slab_in[:1], up_total)
        slab_half = [add_low(slab_narrow[0], came)]
        slab_mid = hop(slab_half, ACROSS)

        (came,) = after(up_mid[1:], slab_half)
        up_total.append(add_low(up_half[1], came))
        up_out += hop(up_total[1:], OUTWARD)

        (came,) = after(slab_in[1:], up_total[1])
        slab_half.append(add_low(slab_narrow[1], came))
        slab_mid += hop(slab_half[1:], ACROSS)

        gate = slab_half[1]
        slab_total, slab_out = [], []
        for at in range(2):
            (came,) = after([slab_mid[at]], gate)
            slab_total.append(add_low(slab_half[at], came))
            slab_out += hop(slab_total[-1:], OUTWARD)
            gate = slab_total[-1:]

        (down_out,) = after([down_out], gate)
        down_weight_sum = settle(down_total, down_out).astype(F32)
        up_out = after(up_out, down_weight_sum, slab_out[0])
        upper, lower = [settle(*pair) for pair in zip(up_total, up_out)]
        first = core == 0
        (up_weight_sum,) = call(
            functools.partial(join_kernel, hidden),
            [((rows, 2 * half), F32)],
            (jnp.where(first, upper, lower), swap(jnp.where(first, lower, upper), 1)),
            core_position,
        )
        slab_out = after(slab_out, upper, lower)
        scalar = pl.BlockSpec(memory_space=pltpu.SMEM)
        heads_sum, output_sum, short, loss_sum, token_count = call(
            functools.partial(settle_kernel, rows, hidden),
            [
                ((rows, 3 * width), F32), ((rows, width), F32), ((VECTORS, 2 * width), F32),
                ((1,), F32), ((1,), jnp.int32),
            ],
            (*slab_total, *slab_out),
            lax.axis_index("narrow").reshape(1).astype(jnp.int32),
            out_specs=[vmem, vmem, vmem, scalar, scalar],
        )
        vectors_sum = short[:, :rows]
        up_bias_grad = short[0, LANES : LANES + hidden]
        loss_sum, token_count = loss_sum.reshape(()), token_count.reshape(())
    else:
        down_weight_sum = collect_chips(down_parts[0].reshape(chips, hidden, width))
        down_weight_sum = sum_narrow(down_weight_sum).astype(F32)
        up_sum = sum_narrow(collect_chips(up_parts[0].reshape(chips, 2 * rows, half)))
        up_sum = up_sum.reshape(2, rows, chips, hidden)
        up_weight_sum = by_core(mine_of(up_sum, 0), swap(mine_of(up_sum, 0, 1), 1), 2)
        up_weight_sum = up_weight_sum.reshape(rows, 2 * half).astype(F32)
        short = short_sums.reshape(8, wide, rows).transpose(1, 0, 2).reshape(wide, 8 * rows)
        up_bias_rows = up_bias_part.reshape(chips, hidden)
        up_bias_rows = by_core(up_bias_rows, jnp.zeros_like(up_bias_rows), 1).reshape(wide, hidden)
        shared = jnp.broadcast_to(loss_sums[:1, :LANES], (wide, LANES))
        row = jnp.concatenate([short, up_bias_rows, shared], axis=1).astype(BF16)
        row = jnp.pad(row, ((0, 0), (0, 4 * width - row.shape[1])))
        slab = jnp.concatenate([attend_part.reshape(wide, rows, 4 * width), row[:, None]], axis=1)
        slab = sum_narrow(lax.psum_scatter(slab, "wide", scatter_dimension=0)).astype(F32)
        vectors_sum = slab[rows, : 8 * rows].reshape(8, rows)
        heads_sum, output_sum = slab[:rows, : 3 * width], slab[:rows, 3 * width :]
        up_bias_grad = slab[rows, 8 * rows : 8 * rows + hidden]
        loss_sum = jnp.sum(slab[rows, 8 * rows + hidden : 8 * rows + hidden + LANES])
        token_count = lax.psum(jnp.sum(loss_mask), ("narrow", "wide"))
    return (
        result_low[None],
        input_grad[None],
        vectors_sum[ATTEND_GAIN],
        vectors_sum[ATTEND_SHIFT],
        heads_sum,
        vectors_sum[QUERY_BIAS],
        vectors_sum[VALUE_BIAS],
        output_sum,
        vectors_sum[OUTPUT_BIAS],
        vectors_sum[FORWARD_GAIN],
        vectors_sum[FORWARD_SHIFT],
        up_weight_sum,
        up_bias_grad,
        down_weight_sum,
        vectors_sum[DOWN_BIAS],
        loss_sum,
        token_count,
    )


def solution(mesh):
    in_specs = (
        P(("narrow", "wide"), None, None),
        P(("narrow", "wide"), None),
        P(("narrow", "wide"), None),
        P(("narrow", "wide"), None),
        P(),
        P("wide"),
        P("wide"),
        P("wide", None),
        P("wide"),
        P("wide"),
        P("wide", None),
        P("wide"),
        P("wide"),
        P("wide"),
        P("wide", None),
        P("wide"),
        P("wide", None),
        P("wide"),
    )
    out_specs = (
        P(("narrow", "wide"), None, None),
        P(("narrow", "wide"), None, None),
        P("wide"),
        P("wide"),
        P("wide", None),
        P("wide"),
        P("wide"),
        P("wide", None),
        P("wide"),
        P("wide"),
        P("wide"),
        P("wide", None),
        P("wide"),
        P("wide", None),
        P("wide"),
        P(),
        P(),
    )
    return jax.shard_map(local, mesh=mesh, in_specs=in_specs, out_specs=out_specs, check_vma=False)
```

```python
import functools
import math

import jax
import jax.numpy as jnp
from jax import lax
from jax.experimental import pallas as pl
from jax.experimental.pallas import tpu as pltpu
from jax.sharding import PartitionSpec as P

HEADS = 20
HEAD_DIM = 32
LANES = 128
SUBLANES = 8
SEGMENTS = 8
REACH = 192
CHUNK = 256
ROWS = 128
SCALE = 1.0 / math.sqrt(HEAD_DIM)
SCALE2 = math.log2(math.e) * SCALE
F32 = jnp.float32
BF16 = jnp.bfloat16
VECTORS = 8
ATTEND_GAIN, ATTEND_SHIFT, QUERY_BIAS, VALUE_BIAS = 0, 1, 2, 3
OUTPUT_BIAS, FORWARD_GAIN, FORWARD_SHIFT, DOWN_BIAS = 4, 5, 6, 7


def nn(left, right):
    return lax.dot_general(left, right, (((1,), (0,)), ((), ())), preferred_element_type=F32)


def nt(left, right):
    return lax.dot_general(left, right, (((1,), (1,)), ((), ())), preferred_element_type=F32)


def tn(left, right):
    return lax.dot_general(left, right, (((0,), (0,)), ((), ())), preferred_element_type=F32)


def call(kernel, outs, args, positions=None, grid=None, in_specs=None, out_specs=None, scratch=(),
         mib=16, aliases=None):
    whole = pl.BlockSpec(memory_space=pltpu.VMEM)
    in_specs = in_specs or [whole] * len(args)
    args = [
        pltpu.with_memory_space_constraint(arg, pltpu.HBM)
        if spec.memory_space == pltpu.HBM
        else arg
        for arg, spec in zip(args, in_specs)
    ]
    out_specs = out_specs or [whole] * len(outs)
    shapes = [
        pltpu.HBM(*out) if spec.memory_space == pltpu.HBM else jax.ShapeDtypeStruct(*out)
        for out, spec in zip(outs, out_specs)
    ]
    extra = [] if positions is None else [positions]
    return pl.pallas_call(
        kernel,
        out_shape=shapes,
        grid_spec=pltpu.PrefetchScalarGridSpec(
            num_scalar_prefetch=len(extra),
            grid=grid or (),
            in_specs=in_specs,
            out_specs=out_specs,
            scratch_shapes=list(scratch),
        ),
        compiler_params=pltpu.CompilerParams(vmem_limit_bytes=mib * 1024 * 1024),
        input_output_aliases=aliases or {},
        cost_estimate=pl.CostEstimate(flops=1, bytes_accessed=1, transcendentals=0),
    )(*extra, *args)


def unit(values):
    centred = values - jnp.mean(values, axis=-1, keepdims=True)
    spread = jnp.mean(centred * centred, axis=-1, keepdims=True)
    inverse = lax.rsqrt(spread + 1e-05)
    return centred * inverse, inverse


def unit_back(grad, normal, inverse, gain):
    scaled = grad * gain
    mean = jnp.mean(scaled, axis=-1, keepdims=True)
    along = jnp.mean(scaled * normal, axis=-1, keepdims=True)
    return inverse * (scaled - mean - normal * along)


def spans(length):
    chunk = min(CHUNK, length)
    return [
        (at, at + chunk, max(0, at - REACH), min(length, at + chunk + REACH))
        for at in range(0, length, chunk)
    ]


def split3(values):
    first = values.astype(BF16).astype(F32)
    rest = values - first
    second = rest.astype(BF16).astype(F32)
    return [first, second, rest - second]


def key_marks(segment_row):
    at = lax.broadcasted_iota(jnp.int32, (LANES, segment_row.shape[1]), 0)
    ones = (at >= SEGMENTS) & (at < SEGMENTS + 3)
    return jnp.where((at == segment_row) | ones, 1.0, 0.0).astype(BF16).T


def query_marks(segment_row):
    row = lax.broadcasted_iota(jnp.int32, (SEGMENTS, segment_row.shape[1]), 0)
    return jnp.where(row == segment_row, 0.0, -1e30)


def place(rows, head, marks):
    count = rows.shape[1]
    parts = [rows, marks, jnp.zeros((LANES - marks.shape[0], count), BF16)]
    if head < LANES // HEAD_DIM - 1:
        parts.insert(1, jnp.zeros((LANES - HEAD_DIM * (head + 1), count), BF16))
    if head:
        parts.insert(0, jnp.zeros((HEAD_DIM * head, count), BF16))
    return jnp.concatenate(parts, axis=0)


def attend_kernel(row_ref, q_ref, k_ref, v_ref, out_ref, across_ref, lse_ref, marks_ref):
    @pl.when(pl.program_id(0) == 0)
    def _():
        marks_ref[...] = key_marks(row_ref[...])

    length = q_ref.shape[0]
    heads = LANES // HEAD_DIM
    queries = q_ref[...].T
    values = v_ref[...].T
    keys = jnp.concatenate([k_ref[...], marks_ref[...]], axis=1)
    blank = jnp.zeros((SUBLANES, length), F32)
    marks = jnp.concatenate([query_marks(row_ref[...]), blank], axis=0).astype(BF16)
    ones = jnp.ones((SUBLANES, length), BF16)
    bodies = [(head, span) for head in range(heads) for span in spans(length)]

    def rows(head):
        return slice(HEAD_DIM * head, HEAD_DIM * (head + 1))

    summed = [jnp.concatenate([values[rows(head)], ones], axis=0) for head in range(heads)]

    def score(head, span):
        begin, end, low, high = span
        return nn(keys[low:high], place(queries[rows(head), begin:end], head, marks[:, begin:end]))

    def finish(head, span, top, probs):
        begin, end, low, high = span
        out = nn(summed[head][:, low:high], probs)
        total = out[HEAD_DIM : HEAD_DIM + 1]
        across_ref[rows(head), begin:end] = out[:HEAD_DIM] * (1.0 / total)
        lse_ref[head : head + 1, begin:end] = (top + jnp.log2(total)) * (1.0 / SCALE2)

    scores = [score(*body) for body in bodies[:2]]
    waiting = None
    for at, body in enumerate(bodies):
        current = scores.pop(0)
        if at + 2 < len(bodies):
            scores.append(score(*bodies[at + 2]))
        top = jnp.max(current, axis=0, keepdims=True) * SCALE2
        probs = jnp.exp2(current * SCALE2 - top).astype(BF16)
        if waiting is not None:
            finish(*waiting)
        waiting = (*body, top, probs)
    finish(*waiting)
    lse_ref[heads:, :] = jnp.zeros((SUBLANES - heads, length), F32)
    out_ref[...] = across_ref[...].T.astype(BF16)


def attend_back_kernel(
    row_ref, q_ref, k_ref, v_ref, grad_ref, across_ref, lse_ref,
    gq_ref, gk_ref, gv_ref, marks_ref, turned_ref,
):
    @pl.when(pl.program_id(0) == 0)
    def _():
        marks_ref[...] = key_marks(row_ref[...])

    length = q_ref.shape[0]
    grad = grad_ref[...]
    queries = q_ref[...].T
    turned_keys = k_ref[...].T
    grads = grad.T
    keys = jnp.concatenate([k_ref[...], marks_ref[...]], axis=1)
    values = jnp.concatenate([v_ref[...], marks_ref[...]], axis=1)
    low_marks = query_marks(row_ref[...])
    blank = jnp.zeros((SUBLANES, length), F32)
    lane = lax.broadcasted_iota(jnp.int32, (1, LANES), 1) // HEAD_DIM
    heads = []
    for head in range(LANES // HEAD_DIM):
        rows = slice(HEAD_DIM * head, HEAD_DIM * (head + 1))
        inner = jnp.sum(grads[rows].astype(F32) * across_ref[rows, :], axis=0, keepdims=True)
        lse = lse_ref[head : head + 1, :]
        score_marks = jnp.concatenate([low_marks, *split3(-lse), blank[:5]], axis=0)
        inner_marks = jnp.concatenate([blank, *split3(-inner), blank[:5]], axis=0)
        zero = jnp.zeros_like(grad)
        heads.append(
            (
                rows,
                score_marks.astype(BF16),
                inner_marks.astype(BF16),
                jnp.where(lane == head, q_ref[...], zero),
                jnp.where(lane == head, grad, zero),
            )
        )
    bodies = [
        (head, at, span) for head in range(len(heads)) for at, span in enumerate(spans(length))
    ]
    sums = [[None, None] for _ in spans(length)]

    def pair(head, at, span):
        begin, end, low, high = span
        rows, score_marks, inner_marks, _, _ = heads[head]
        return (
            nn(keys[low:high], place(queries[rows, begin:end], head, score_marks[:, begin:end])),
            nn(values[low:high], place(grads[rows, begin:end], head, inner_marks[:, begin:end])),
        )

    def finish(head, at, span, score_grads, probs):
        begin, end, low, high = span
        rows, _, _, own_queries, own_grads = heads[head]
        for which, (left, right) in enumerate(
            ((score_grads, own_queries[begin:end]), (probs, own_grads[begin:end]))
        ):
            part = nn(left, right)
            sums[at][which] = part if sums[at][which] is None else sums[at][which] + part
        turned_ref[rows, begin:end] = nn(turned_keys[rows, low:high], score_grads)

    ahead = [pair(*bodies[0])]
    waiting = None
    for at, body in enumerate(bodies):
        scores, differences = ahead.pop(0)
        if at + 1 < len(bodies):
            ahead.append(pair(*bodies[at + 1]))
        probs = jnp.exp2(scores * SCALE2)
        score_grads = (probs * differences).astype(BF16)
        if waiting is not None:
            finish(*waiting)
        waiting = (*body, score_grads, probs.astype(BF16))
    finish(*waiting)
    gq_ref[...] = (turned_ref[...].T * SCALE).astype(BF16)
    for which, (ref, factor) in enumerate(((gk_ref, SCALE), (gv_ref, 1.0))):
        total = None
        for at, (_, _, low, high) in enumerate(spans(length)):
            parts = [sums[at][which]]
            if low:
                parts.insert(0, jnp.zeros((low, LANES), F32))
            if high < length:
                parts.append(jnp.zeros((length - high, LANES), F32))
            part = jnp.concatenate(parts, axis=0) if len(parts) > 1 else parts[0]
            total = part if total is None else total + part
        ref[...] = (total * factor).astype(BF16)


def attention_specs(length, width, begin=0):
    tiles = width // LANES

    def tile(at, begin=begin):
        return pl.BlockSpec((length, LANES), lambda i: (0, at + begin + i))

    return (
        tiles,
        tile,
        pl.BlockSpec((1, length), lambda i: (0, 0)),
        pl.BlockSpec((LANES, length), lambda i: (begin + i, 0)),
        pl.BlockSpec((SUBLANES, length), lambda i: (begin + i, 0)),
    )


def attend(joined, row):
    length = joined.shape[0]
    width = joined.shape[1] // 3
    tiles, tile, row_spec, across_spec, lse_spec = attention_specs(length, width)
    return call(
        attend_kernel,
        [((length, width), BF16), ((width, length), F32), ((SUBLANES * tiles, length), F32)],
        (row, joined, joined, joined),
        grid=(tiles,),
        in_specs=[row_spec, tile(0), tile(tiles), tile(2 * tiles)],
        out_specs=[tile(0), across_spec, lse_spec],
        scratch=[pltpu.VMEM((length, LANES), BF16)],
    )


def attend_back(joined, row, grad, across, lse, begin=0, end=None):
    length = joined.shape[0]
    width = joined.shape[1] // 3
    specs = attention_specs(length, width, begin)
    tiles, tile, row_spec, across_spec, lse_spec = specs
    count = (end or tiles) - begin
    return call(
        attend_back_kernel,
        [((length, count * LANES), BF16)] * 3,
        (row, joined, joined, joined, grad, across, lse),
        grid=(count,),
        in_specs=[row_spec, tile(0), tile(tiles), tile(2 * tiles), tile(0), across_spec, lse_spec],
        out_specs=[tile(0, 0)] * 3,
        scratch=[pltpu.VMEM((length, LANES), BF16), pltpu.VMEM((LANES, length), F32)],
        mib=24,
    )


def slab_kernel(heads_ref, out_ref, short_ref, up_ref, slab_ref):
    rows = heads_ref.shape[0]
    width = out_ref.shape[1]
    slab_ref[:rows, : 3 * width] = heads_ref[...]
    slab_ref[:rows, 3 * width :] = out_ref[...]
    slab_ref[rows:, :] = jnp.zeros((VECTORS, 4 * width), BF16)
    slab_ref[rows:, :rows] = short_ref[...]
    slab_ref[rows:, LANES : LANES + up_ref.shape[1]] = jnp.broadcast_to(
        up_ref[...], (VECTORS, up_ref.shape[1])
    )


def project_kernel(count, rows, hidden, position_ref, x_ref, *refs):
    slabs, refs = refs[:count], refs[count:]
    length, width = x_ref.shape
    if count:
        low_ref, joined_ref, heads_ref, out_ref, vector_ref, bias_ref, short_ref, sems = refs
        copies = []
        for at, slab in enumerate(slabs):
            begin = pl.multiple_of(position_ref[at] * rows, SUBLANES)
            here = pl.ds(begin, rows)
            for which, (source, target) in enumerate(
                (
                    (slab.at[pl.ds(0, rows), pl.ds(0, 3 * width)], heads_ref.at[here]),
                    (slab.at[pl.ds(0, rows), pl.ds(3 * width, width)], out_ref.at[here]),
                    (slab.at[pl.ds(rows, VECTORS), pl.ds(0, LANES + hidden)], short_ref.at[at]),
                )
            ):
                copy = pltpu.make_async_copy(source, target, sems.at[at, which])
                copy.start()
                copies.append(copy)
    else:
        heads_ref, vector_ref, low_ref, joined_ref = refs
    if count:
        for copy in copies:
            copy.wait()
        vectors = jnp.zeros((VECTORS, width), F32)
        for at in range(count):
            begin = position_ref[at] * rows
            short = short_ref[at, :, :LANES].astype(F32)
            lane = lax.broadcasted_iota(jnp.int32, short.shape, 1)
            short = jnp.where(lane < rows, short, 0.0)
            short = jnp.concatenate([short, jnp.zeros((VECTORS, width - LANES), F32)], axis=1)
            vectors = vectors + pltpu.roll(short, begin, 1)
            if at < count // 2:
                begin = pl.multiple_of(lax.div(position_ref[at], 2) * hidden, LANES)
                bias_ref[:, pl.ds(begin, hidden)] = short_ref[at, :, LANES:].astype(F32)
        vector_ref[...] = vectors
    zero = jnp.zeros((1, width), F32)
    vector = vector_ref[...]
    bias = jnp.concatenate(
        [vector[QUERY_BIAS : QUERY_BIAS + 1], zero, vector[VALUE_BIAS : VALUE_BIAS + 1]], axis=1
    )
    for at in range(0, length, ROWS):
        normal, _ = unit(x_ref[at : at + ROWS, :].astype(F32))
        low_ref[at : at + ROWS, :] = (
            normal * vector[ATTEND_GAIN : ATTEND_GAIN + 1]
            + vector[ATTEND_SHIFT : ATTEND_SHIFT + 1]
        ).astype(BF16)
    for at in range(0, 3 * width, width):
        here = slice(at, at + width)
        joined_ref[:, here] = (nn(low_ref[...], heads_ref[:, here]) + bias[:, here]).astype(BF16)


def middle_kernel(x_ref, attended_ref, out_ref, vector_ref, middle_ref, low_ref):
    vector = vector_ref[...]
    for at in range(0, x_ref.shape[0], ROWS):
        here = slice(at, at + ROWS)
        middle = (
            x_ref[here, :].astype(F32)
            + nn(attended_ref[here, :], out_ref[...])
            + vector[OUTPUT_BIAS : OUTPUT_BIAS + 1]
        )
        middle_ref[here, :] = middle
        normal, _ = unit(middle)
        low_ref[here, :] = (
            normal * vector[FORWARD_GAIN : FORWARD_GAIN + 1]
            + vector[FORWARD_SHIFT : FORWARD_SHIFT + 1]
        ).astype(BF16)


def up_kernel(position_ref, own_ref, other_ref, bias_ref, *refs):
    parts, (act_ref, slope_ref, full_ref) = refs[: len(refs) - 3], refs[len(refs) - 3 :]
    for at, part in enumerate(parts):
        rows = part.shape[0]
        begin = pl.multiple_of(position_ref[at] * rows, SUBLANES)
        full_ref[pl.ds(begin, rows), :] = part[...]
    weight = full_ref[...]
    bias = bias_ref[:1, :]
    length = own_ref.shape[0]
    for which, ref in enumerate((own_ref, other_ref)):
        for at in range(0, length, ROWS):
            upward = nn(ref[at : at + ROWS, :], weight) + bias
            share = 0.5 + 0.5 * lax.erf(upward * math.sqrt(0.5))
            bell = jnp.exp2((upward * upward) * (-0.5 * math.log2(math.e)))
            here = slice(which * length + at, which * length + at + ROWS)
            act_ref[here, :] = (upward * share).astype(BF16)
            slope = share + upward * (bell * (1.0 / math.sqrt(2.0 * math.pi)))
            slope_ref[here, :] = slope.astype(BF16)


def column_specs(half, block):
    block = min(block, half)

    def column(height):
        return pl.BlockSpec((height, block), lambda i, at: (0, i))

    return half // block, block, column


def whole_spec(shape):
    return pl.BlockSpec(shape, lambda i, at: (0,) * len(shape))


def up_project(own, other, bias, parts, positions, hidden):
    length, width = own.shape
    half = bias.shape[1]
    paired = parts[0].shape[1] > half
    steps, block, column = column_specs(half, hidden if paired else 512)
    whole = whole_spec((length, width))

    def part_spec(part):
        if paired:
            return pl.BlockSpec((part.shape[0], block), lambda i, at: (0, 2 * i + at[len(parts)]))
        return column(part.shape[0])

    return call(
        up_kernel,
        [((2 * length, half), BF16), ((2 * length, half), BF16), ((width, half), BF16)],
        (own, other, bias, *parts),
        positions,
        grid=(steps,),
        in_specs=[whole, whole, column(bias.shape[0])] + [part_spec(part) for part in parts],
        out_specs=[column(2 * length), column(2 * length), column(width)],
    )


def down_kernel(position_ref, act_ref, *refs):
    parts, (own_ref, other_ref, full_ref) = refs[: len(refs) - 3], refs[len(refs) - 3 :]
    length = own_ref.shape[0]
    for at, part in enumerate(parts):
        rows = part.shape[0]
        begin = pl.multiple_of(position_ref[at] * rows, SUBLANES)
        full_ref[pl.ds(begin, rows), :] = part[...]
    for which, ref in enumerate((own_ref, other_ref)):
        here = slice(which * length, (which + 1) * length)
        ref[...] = nn(act_ref[here, :], full_ref[...]).astype(ref.dtype)


def down_project(act, parts, positions):
    length = act.shape[0] // 2
    half = act.shape[1]
    width = parts[0].shape[1]
    return call(
        down_kernel,
        [((length, width), F32), ((length, width), BF16), ((half, width), BF16)],
        (act, *parts),
        positions,
        mib=20,
    )


def down_near_kernel(position_ref, act_ref, *refs):
    parts, (sum_ref, full_ref) = refs[:-2], refs[-2:]
    size = parts[0].shape[0]
    for at, part in enumerate(parts):
        rows = part.shape[0]
        begin = pl.multiple_of(position_ref[at] * rows, SUBLANES)
        full_ref[pl.ds(begin, rows), :] = part[...]
    chips = [position_ref[0], lax.div(position_ref[1], 2), lax.div(position_ref[3], 2)]
    length = act_ref.shape[0] // 2
    for which in range(2):
        here = slice(which * length, (which + 1) * length)
        total = None
        for chip in chips:
            units = pl.ds(pl.multiple_of(chip * size, LANES), size)
            part = nn(act_ref[here, units], full_ref[units, :])
            total = part if total is None else total + part
        sum_ref[here, :] = total


def down_far_kernel(position_ref, act_ref, sum_ref, upper_ref, lower_ref, _, own_ref, other_ref, full_ref):
    rows, length = upper_ref.shape[0], own_ref.shape[0]
    size = 2 * rows
    units = pl.ds(pl.multiple_of(lax.div(position_ref[5], 2) * size, LANES), size)
    weight = jnp.concatenate([upper_ref[...], lower_ref[...]], axis=0)
    full_ref[units, :] = weight
    for which, ref in enumerate((own_ref, other_ref)):
        here = slice(which * length, (which + 1) * length)
        ref[...] = (sum_ref[here, :] + nn(act_ref[here, units], weight)).astype(ref.dtype)


def down_project_square(act, near, far, positions):
    length, half, width = act.shape[0] // 2, act.shape[1], near[0].shape[1]
    total, full = call(
        down_near_kernel,
        [((2 * length, width), F32), ((half, width), BF16)],
        (act, *near),
        positions,
        mib=24,
    )
    far = far(total)
    return call(
        down_far_kernel,
        [((length, width), F32), ((length, width), BF16), ((half, width), BF16)],
        (act, total, *far, full),
        positions,
        mib=24,
        aliases={5: 2},
    )


def loss_kernel(
    middle_ref, own_ref, got_ref, vector_ref, readout_ref, target_ref, mask_ref,
    low_ref, down_ref, grad_ref, sums_ref,
):
    result = (
        middle_ref[...]
        + (own_ref[...] + got_ref[...].astype(F32))
        + vector_ref[DOWN_BIAS : DOWN_BIAS + 1, :]
    ).astype(BF16)
    low_ref[...] = result
    logits = nt(readout_ref[...], result)
    length = logits.shape[1]
    top = jnp.max(logits, axis=0, keepdims=True)
    shifted = jnp.exp(logits - top)
    total = jnp.sum(shifted, axis=0, keepdims=True)
    onehot = lax.broadcasted_iota(jnp.int32, logits.shape, 0) == target_ref[...]
    picked = jnp.sum(jnp.where(onehot, logits, 0.0), axis=0, keepdims=True)
    weight = mask_ref[...].astype(F32)
    loss = (top + jnp.log(total) - picked) * weight
    loss_lanes = jnp.zeros((1, LANES), F32)
    count_lanes = jnp.zeros((1, LANES), F32)
    for at in range(0, length, LANES):
        loss_lanes = loss_lanes + loss[:, at : at + LANES]
        count_lanes = count_lanes + weight[:, at : at + LANES]
    lanes = jnp.concatenate([loss_lanes, count_lanes], axis=0)
    lanes = jnp.concatenate([lanes, jnp.zeros((2, result.shape[1] - LANES), F32)], axis=1)
    grad_logits = (weight * (shifted / total - onehot.astype(F32))).astype(BF16)
    grad_ref[...] = grad_logits
    low = tn(grad_logits, readout_ref[...]).astype(BF16)
    down_ref[...] = low
    sums = jnp.sum(low.astype(F32), axis=0, keepdims=True)
    blank = jnp.zeros((SUBLANES - 3, result.shape[1]), F32)
    sums_ref[...] = jnp.concatenate([lanes, sums, blank], axis=0)


def down_grad_kernel(chips, position_ref, act_ref, own_ref, other_ref, *out_refs):
    length = own_ref.shape[0]
    hidden = act_ref.shape[1] // chips
    for offset in range(chips):
        if len(out_refs) == 1:
            begin = offset * hidden
        else:
            begin = pl.multiple_of((position_ref[0] ^ offset) * hidden, LANES)
        here = pl.ds(begin, hidden)
        part = tn(act_ref[:length, here], own_ref[...]) + tn(act_ref[length:, here], other_ref[...])
        part = part.astype(BF16)
        if len(out_refs) == 1:
            out_refs[0][begin : begin + hidden, :] = part
            continue
        keep_x, send_x, keep_y, send_y = out_refs
        half = hidden // 2
        (send_x if offset % 2 else keep_x)[offset // 2, :, :] = part[:half]
        (send_y if offset // 2 else keep_y)[offset % 2, :, :] = part[half:]


def down_grad(act, own, other, chips, position):
    half = act.shape[1]
    width = own.shape[1]
    if square():
        outs = [((2, half // chips // 2, width), BF16)] * 4
    else:
        outs = [((half, width), BF16)]
    return call(
        functools.partial(down_grad_kernel, chips), outs, (act, own, other), position, mib=20
    )


def up_grad_kernel(
    rows, position_ref, own_ref, other_ref, slope_ref, second_ref, second_other_ref, down_ref,
    up_ref, bias_ref, *refs,
):
    out_refs, part_ref = refs[:-1], refs[-1]
    length = own_ref.shape[0]
    total = None
    grads = []
    for which, ref in enumerate((own_ref, other_ref)):
        for at in range(0, length, 2 * ROWS):
            here = slice(which * length + at, which * length + at + 2 * ROWS)
            grad = nt(ref[at : at + 2 * ROWS, :], down_ref[...]) * slope_ref[here, :].astype(F32)
            low = grad.astype(BF16)
            up_ref[here, :] = low
            part = jnp.sum(low.astype(F32), axis=0, keepdims=True)
            total = part if total is None else total + part
    bias_ref[...] = total
    part = tn(second_ref[...], up_ref[:length, :]) + tn(second_other_ref[...], up_ref[length:, :])
    if len(out_refs) == 1:
        out_refs[0][...] = part.astype(BF16)
        return
    part_ref[...] = part
    keep_x, send_x, keep_y, send_y = out_refs
    for offset in range(4):
        begin = pl.multiple_of((position_ref[0] ^ offset) * (2 * rows), SUBLANES)
        upper = part_ref[pl.ds(begin, rows), :].astype(BF16)
        lower = part_ref[pl.ds(begin + rows, rows), :].astype(BF16)
        (send_x if offset % 2 else keep_x)[offset // 2, :, :] = upper
        (send_y if offset // 2 else keep_y)[offset % 2, :, :] = lower


def up_grad(own, other, slope, second, second_other, down_full, rows, position):
    length, width = own.shape
    half = slope.shape[1]
    steps, block, column = column_specs(half, 512)
    whole = whole_spec((length, width))
    if square():
        outs = [((2, rows, half), BF16)] * 4
        specs = [pl.BlockSpec((2, rows, block), lambda i, at: (0, 0, i))] * 4
    else:
        outs = [((width, half), BF16)]
        specs = [column(width)]
    return call(
        functools.partial(up_grad_kernel, rows),
        [((2 * length, half), BF16), ((1, half), F32), *outs],
        (own, other, slope, second, second_other, down_full),
        position,
        grid=(steps,),
        in_specs=[
            whole, whole, column(2 * length), whole, whole,
            pl.BlockSpec((block, width), lambda i, at: (i, 0)),
        ],
        out_specs=[column(2 * length), column(1), *specs],
        scratch=[pltpu.VMEM((width, block), F32)],
        mib=20,
    )


def inward_kernel(grad_ref, up_ref, own_far, other_ref, own_ref, sem):
    length = other_ref.shape[0]
    own_ref[...] = nt(grad_ref[:length, :], up_ref[...])
    copy = pltpu.make_async_copy(own_ref, own_far, sem)
    copy.start()
    other_ref[...] = nt(grad_ref[length:, :], up_ref[...]).astype(BF16)
    copy.wait()


def join_kernel(hidden, position_ref, mine_ref, other_ref, out_ref):
    for at in range(mine_ref.shape[1] // hidden):
        here = slice(hidden * at, hidden * (at + 1))
        for core, ref in enumerate((mine_ref, other_ref)):
            begin = (2 * at + (position_ref[0] + core) % 2) * hidden
            out_ref[:, pl.ds(pl.multiple_of(begin, LANES), hidden)] = ref[:, here].astype(F32)


def branch_kernel(
    got_ref, own_far, middle_far, logits_ref, classes_ref, out_ref, vector_ref,
    grad_ref, branch_ref, attended_ref, sums_ref, own_ref, middle_ref, sems,
):
    width = own_ref.shape[1]
    blocks = range(0, own_ref.shape[0], ROWS)
    copies = []
    for at in blocks:
        here = pl.ds(at, ROWS)
        copies.append(
            [
                pltpu.make_async_copy(far.at[here], ref.at[here], sems.at[at // ROWS, which])
                for which, (far, ref) in enumerate(((own_far, own_ref), (middle_far, middle_ref)))
            ]
        )
        for copy in copies[-1]:
            copy.start()
    gain = vector_ref[FORWARD_GAIN : FORWARD_GAIN + 1, :]
    sums = [jnp.zeros((1, width), F32) for _ in range(3)]
    for at in blocks:
        for copy in copies[at // ROWS]:
            copy.wait()
        here = slice(at, at + ROWS)
        grad = own_ref[here, :] + got_ref[here, :].astype(F32)
        normal, inverse = unit(middle_ref[here, :])
        result = tn(logits_ref[:, here], classes_ref[...])
        middle = result + unit_back(grad, normal, inverse, gain)
        grad_ref[here, :] = middle
        branch = middle.astype(BF16)
        branch_ref[here, :] = branch
        attended_ref[here, :] = nt(branch, out_ref[...]).astype(BF16)
        for which, part in enumerate((grad * normal, grad, branch.astype(F32))):
            sums[which] = sums[which] + jnp.sum(part, axis=0, keepdims=True)
    blank = jnp.zeros((SUBLANES - 3, width), F32)
    sums_ref[...] = jnp.concatenate([*sums, blank], axis=0)


def last_kernel(count, rows, hidden, pieces, position_ref, x_ref, low_ref, *refs):
    grad_refs, refs = refs[: 3 * pieces], refs[3 * pieces :]
    heads_ref, attended_ref, branch_ref, grad_ref, vector_ref, *refs = refs
    sums_ref, loss_ref, up_ref, *refs = refs
    stacks, (input_ref, vectors_ref, full_ref) = refs[:-3], refs[-3:]
    width = x_ref.shape[1]

    def grads(which, here):
        parts = [ref[here, :] for ref in grad_refs[which::3]]
        return jnp.concatenate(parts, axis=1) if pieces > 1 else parts[0]

    for at in range(3):
        part = tn(low_ref[...], grads(at, slice(None)))
        full_ref[:, width * at : width * (at + 1)] = part.astype(BF16)
    full_ref[:, 3 * width :] = tn(attended_ref[...], branch_ref[...]).astype(BF16)
    gain = vector_ref[ATTEND_GAIN : ATTEND_GAIN + 1, :]
    sums = [jnp.zeros((1, width), F32) for _ in range(4)]
    for at in range(0, x_ref.shape[0], ROWS):
        here = slice(at, at + ROWS)
        grad_query, grad_key, grad_value = [grads(at, here) for at in range(3)]
        grad = (
            nt(grad_query, heads_ref[:, :width])
            + nt(grad_key, heads_ref[:, width : 2 * width])
            + nt(grad_value, heads_ref[:, 2 * width :])
        )
        normal, inverse = unit(x_ref[here, :].astype(F32))
        input_ref[here, :] = grad_ref[here, :] + unit_back(grad, normal, inverse, gain)
        parts = (grad * normal, grad, grad_query.astype(F32), grad_value.astype(F32))
        for which, part in enumerate(parts):
            sums[which] = sums[which] + jnp.sum(part, axis=0, keepdims=True)
    vectors = jnp.concatenate(
        [*sums, sums_ref[2:3, :], sums_ref[0:1, :], sums_ref[1:2, :], loss_ref[2:3, :]], axis=0
    )
    vectors_ref[...] = vectors
    blank = jnp.zeros((VECTORS - 1, hidden), F32)
    lanes = jnp.concatenate([loss_ref[:2, :LANES], jnp.zeros((VECTORS - 2, LANES), F32)], axis=0)
    for at in range(count):
        stack = stacks[at // (count // 2)]
        place_at = position_ref[at]
        begin = pl.multiple_of(place_at * rows, SUBLANES)
        cuts = [
            (pick, slice(2 * width * side, 2 * width * (side + 1)))
            for side, pick in enumerate(((0, 2, 1, 3)[at % 4], 4 + at % 4))
        ]
        for pick, here in cuts:
            stack[pick, :rows, :] = full_ref[pl.ds(begin, rows), here]
        short = pltpu.roll(vectors, width - begin, 1)[:, :LANES]
        if at < count // 2:
            hidden_at = pl.multiple_of(lax.div(place_at, 2) * hidden, LANES)
            bias = jnp.concatenate([up_ref[:, pl.ds(hidden_at, hidden)], blank], axis=0)
        else:
            bias = jnp.zeros((VECTORS, hidden), F32)
        row = jnp.concatenate([short, bias, lanes], axis=1).astype(BF16)
        pad = jnp.zeros((VECTORS, 4 * width - row.shape[1]), BF16)
        row = jnp.concatenate([row, pad], axis=1)
        for pick, here in cuts:
            stack[pick, rows:, :] = row[:, here]


def settle_kernel(rows, hidden, place_ref, *refs):
    totals, outers, refs = refs[:2], refs[2:4], refs[4:]
    heads_ref, out_ref, short_ref, loss_ref, count_ref = refs
    width = out_ref.shape[1]
    inner = (place_ref[0] == 1) | (place_ref[0] == 2)
    left, right = [
        jnp.where(inner, total[...], outer[...]).astype(F32) for total, outer in zip(totals, outers)
    ]
    heads_ref[:, : 2 * width] = left[:rows]
    heads_ref[:, 2 * width :] = right[:rows, :width]
    out_ref[...] = right[:rows, width:]
    short_ref[...] = left[rows:]
    lanes = left[rows:, LANES + hidden : 2 * LANES + hidden]
    loss_ref[0] = jnp.sum(lanes[0:1])
    count_ref[0] = jnp.sum(lanes[1:2]).astype(jnp.int32)


def swap(values, bit):
    return lax.ppermute(values, "wide", [(i, i ^ bit) for i in range(lax.axis_size("wide"))])


def same_core_groups():
    chips = lax.axis_size("wide") // 2
    return [[2 * chip + core for chip in range(chips)] for core in range(2)]


def square():
    return lax.axis_size("wide") == 8


def spread_chips(shard):
    return lax.all_gather(shard, "wide", axis=0, axis_index_groups=same_core_groups())


def add_low(*parts):
    return sum(part.astype(F32) for part in parts).astype(BF16)


def collect_chips(parts):
    return lax.psum_scatter(
        parts, "wide", scatter_dimension=0, axis_index_groups=same_core_groups()
    )


def after(values, *gates):
    leaves, tree = jax.tree.flatten(values)
    held = lax.optimization_barrier((*leaves, *jax.tree.leaves(gates)))
    return jax.tree.unflatten(tree, held[: len(leaves)])


INWARD, ACROSS, OUTWARD = [(0, 1), (3, 2)], [(1, 2), (2, 1)], [(1, 0), (2, 3)]


def hop(parts, pairs):
    return [lax.ppermute(part, "narrow", pairs) for part in parts]


def add_each(left, right):
    return [add_low(a, b) for a, b in zip(left, right)]


def settle(total, outer):
    place_at = lax.axis_index("narrow")
    return jnp.where((place_at == 1) | (place_at == 2), total, outer)


def sum_narrow(shard):
    if lax.axis_size("narrow") != 4:
        return lax.psum(shard, "narrow")
    half = add_low(shard, *hop([shard], INWARD))
    total = add_low(half, *hop([half], ACROSS))
    return settle(total, *hop([total], OUTWARD))


def local(
    layer_input, segments, targets, loss_mask, readout,
    attend_gain, attend_shift, heads_weight, query_bias, value_bias, output_weight, output_bias,
    forward_gain, forward_shift, up_weight, up_bias, down_weight, down_bias,
):
    length = layer_input.shape[1]
    width = layer_input.shape[2]
    wide = lax.axis_size("wide")
    chips = wide // 2
    core = lax.axis_index("wide") % 2
    chip = lax.axis_index("wide") // 2
    rows = heads_weight.shape[0]
    hidden = up_bias.shape[0]
    half = chips * hidden
    x = layer_input[0]
    classes = readout.T
    vmem = pl.BlockSpec(memory_space=pltpu.VMEM)
    far_away = pl.BlockSpec(memory_space=pltpu.HBM)

    def by_core(mine, other, axis):
        return jnp.where(
            core == 0, jnp.stack([mine, other], axis), jnp.stack([other, mine], axis)
        )

    def mine_of(values, axis, flip=0):
        return lax.dynamic_index_in_dim(values, core ^ flip, axis, keepdims=False)

    short = jnp.stack(
        [
            attend_gain, attend_shift, query_bias, value_bias,
            output_bias, forward_gain, forward_shift, down_bias,
        ]
    )
    core_position = core.reshape(1).astype(jnp.int32)
    chip_position = chip.reshape(1).astype(jnp.int32)
    if square():
        offsets = jnp.arange(4, dtype=jnp.int32)
        (slab,) = call(
            slab_kernel,
            [((rows + VECTORS, 4 * width), BF16)],
            (heads_weight, output_weight, short, up_bias[None]),
        )
        near_x, near_y, far = swap(slab, 2), swap(slab, 4), swap(slab, 6)
        swapped = swap(slab, 1)
        devices = 2 * (chip ^ offsets) + core
        positions = jnp.concatenate([devices, devices ^ 1]).astype(jnp.int32)
        up_weight, positions = after([up_weight, positions], near_x, swapped)
        up_x, up_y = swap(up_weight, 2), swap(up_weight, 4)
        swapped_x = swap(near_x, 1)
        near_y, far = after([near_y, far], swapped_x)
        slabs = [slab, near_x, near_y, far, swapped, swapped_x, swap(near_y, 1), swap(far, 1)]
        first_low, joined, heads_full, output_full, vectors, up_bias_half = call(
            functools.partial(project_kernel, len(slabs), rows, hidden),
            [
                ((length, width), BF16), ((length, 3 * width), BF16), ((width, 3 * width), BF16),
                ((width, width), BF16), ((VECTORS, width), F32), ((VECTORS, half), F32),
            ],
            (x, *slabs),
            positions,
            in_specs=[pl.BlockSpec(memory_space=pltpu.VMEM)]
            + [pl.BlockSpec(memory_space=pltpu.HBM)] * len(slabs),
            scratch=[
                pltpu.VMEM((len(slabs), VECTORS, LANES + hidden), BF16),
                pltpu.SemaphoreType.DMA((len(slabs), 3)),
            ],
            mib=20,
        )
    else:
        tail = jnp.concatenate([short.reshape(1, 8 * rows), up_bias[None]], axis=1)
        tail = jnp.pad(tail, ((0, 0), (0, 4 * width - tail.shape[1])))
        slab = jnp.concatenate(
            [jnp.concatenate([heads_weight, output_weight], axis=1), tail], axis=0
        )
        slabs = lax.all_gather(slab, "wide", axis=0)
        attend_full = slabs[:, :rows].reshape(width, 4 * width)
        heads_full = attend_full[:, : 3 * width]
        output_full = attend_full[:, 3 * width :]
        last = slabs[:, rows].astype(F32)
        vectors = last[:, : 8 * rows].reshape(wide, 8, rows).transpose(1, 0, 2).reshape(8, width)
        up_bias_half = mine_of(last[:, 8 * rows : 8 * rows + hidden].reshape(chips, 2, hidden), 1)
        up_bias_half = jnp.broadcast_to(up_bias_half.reshape(1, half), (VECTORS, half))
        positions = jnp.zeros((1,), jnp.int32)
        first_low, joined = call(
            functools.partial(project_kernel, 0, rows, hidden),
            [((length, width), BF16), ((length, 3 * width), BF16)],
            (x, heads_full, vectors),
            positions,
            mib=20,
        )
        up_view = up_weight.reshape(rows, chips, 2, hidden)
        up_pair = by_core(
            mine_of(up_view, 2).reshape(rows, half),
            swap(mine_of(up_view, 2, 1).reshape(rows, half), 1),
            0,
        ).reshape(2 * rows, half)
        up_parts = [spread_chips(up_pair).reshape(width, half)]
        down_parts = [spread_chips(down_weight).reshape(half, width)]
        up_positions = down_positions = positions

    attended, across, lse = attend(joined, segments)
    if square():
        up_x, up_y = after([up_x, up_y], attended)
        cut = rows // 2
        passed = [up_y[:cut], up_x[cut:]]
        (attended,) = after([attended], passed)
        near = [up_weight, up_x, up_y]
        near_swapped = [swap(part, 1) for part in near]
        passed = [swap(passed[0], 2), swap(passed[1], 4)]
        up_parts = [*near, *passed, *near_swapped, *[swap(part, 1) for part in passed]]
        at = jnp.arange(11, dtype=jnp.int32)
        part = at % 5
        device = 2 * (chip ^ jnp.minimum(part, 3)) + (core ^ (at // 5))
        up_positions = jnp.where(part < 3, device, 2 * device + part - 3)
        up_positions = jnp.where(at < 10, up_positions, core).astype(jnp.int32)
        middle_row = hidden // 2
        upper, lower = after(
            [down_weight[:middle_row], down_weight[middle_row:]], up_x, up_y
        )
        lower_x, upper_y = swap(lower, 2), swap(upper, 4)
        upper_x, lower_y = swap(upper, 2), swap(lower, 4)
        down_parts = [
            down_weight, upper_x, lower_x, upper_y, lower_y
        ]
        at = jnp.arange(7, dtype=jnp.int32)
        down_positions = jnp.where(at == 0, chip, 2 * (chip ^ ((at + 1) // 2)) + (at + 1) % 2)
    middle, second_low = call(
        middle_kernel,
        [((length, width), F32), ((length, width), BF16)],
        (x, attended, output_full, vectors),
    )

    if square():
        (second_other,) = after([second_low], near_swapped)
        second_other = swap(second_other, 1)
    else:
        second_other = swap(second_low, 1)
    activated, slope, up_full = up_project(
        second_low, second_other, up_bias_half, up_parts, up_positions, hidden
    )
    if square():
        passed_x, passed_y = after([upper_y, lower_x], activated)
        far = [swap(passed_x, 2), swap(passed_y, 4)]
        outward, outward_other, down_full = down_project_square(
            activated, down_parts, lambda total: after(far, total), down_positions
        )
    else:
        outward, outward_other, down_full = down_project(activated, down_parts, down_positions)
    result_low, grad_down, grad_logits, loss_sums = call(
        loss_kernel,
        [
            ((length, width), BF16), ((length, width), BF16), (classes.shape[:1] + (length,), BF16),
            ((SUBLANES, width), F32),
        ],
        (middle, outward, swap(outward_other, 1), vectors, classes, targets, loss_mask),
    )

    grad_down_other = swap(grad_down, 1)
    down_parts = down_grad(activated, grad_down, grad_down_other, chips, chip_position)
    if square():
        keep_dx, send_dx, keep_dy, send_dy = down_parts
        down_first = [swap(send_dx, 2), swap(send_dy, 4)]
        (grad_down_other,) = after([grad_down_other], send_dx)
    grad_up, up_bias_part, *up_parts = up_grad(
        grad_down, grad_down_other, slope, second_low, second_other, down_full, rows, chip_position
    )
    inward, inward_other = call(
        inward_kernel,
        [((length, width), F32), ((length, width), BF16)],
        (grad_up, up_full),
        out_specs=[far_away, vmem],
        scratch=[pltpu.VMEM((length, width), F32), pltpu.SemaphoreType.DMA],
        mib=20,
    )
    got_inward = swap(inward_other, 1)
    if square():
        down_second = [
            add_low(keep_dx[1], down_first[0][1]), add_low(keep_dy[1], down_first[1][1])
        ]
        (got_inward,) = after([got_inward], down_second)
        keep_ux, send_ux, keep_uy, send_uy = up_parts
        send_ux, send_uy = after([send_ux, send_uy], down_second)
        down_got = [swap(down_second[0], 4), swap(down_second[1], 2)]
        up_first = [swap(send_ux, 2), swap(send_uy, 4)]
    grad_middle, grad_branch, grad_attended, branch_sums = call(
        branch_kernel,
        [
            ((length, width), F32), ((length, width), BF16), ((length, width), BF16),
            ((SUBLANES, width), F32),
        ],
        (got_inward, inward, middle, grad_logits, classes, output_full, vectors),
        in_specs=[vmem, far_away, far_away, vmem, vmem, vmem, vmem],
        scratch=[
            *[pltpu.VMEM((length, width), F32)] * 2,
            pltpu.SemaphoreType.DMA((length // ROWS, 2)),
        ],
        mib=24,
    )

    if square():
        attend_grads = attend_back(joined, segments, grad_attended, across, lse)
        down_got = after(down_got, attend_grads[0])
        down_narrow = [
            add_low(keep_dx[0], down_first[0][0], down_got[0]),
            add_low(keep_dy[0], down_first[1][0], down_got[1]),
        ]
        down_in = hop(down_narrow, INWARD)
        attend_grads = after(attend_grads, down_narrow)
    else:
        attend_grads = attend_back(joined, segments, grad_attended, across, lse)
    stack_shape = ((8, rows + VECTORS, 2 * width), BF16)
    *stacks, input_grad, short_sums, attend_part = call(
        functools.partial(last_kernel, 8 if square() else 0, rows, hidden, len(attend_grads) // 3),
        ([stack_shape] * 2 if square() else [])
        + [((length, width), F32), ((VECTORS, width), F32), ((width, 4 * width), BF16)],
        (
            x, first_low, *attend_grads, heads_full, attended, grad_branch,
            grad_middle, vectors, branch_sums, loss_sums, up_bias_part,
        ),
        positions,
        mib=40,
    )
    if square():
        mine, others = stacks
        mine_got = swap(others, 1)
        up_first = after(up_first, mine)
        up_second = [add_low(keep_ux[1], up_first[0][1]), add_low(keep_uy[1], up_first[1][1])]
        up_got = [swap(up_second[0], 4), swap(up_second[1], 2)]

        down_in = after(down_in, up_second)
        down_half = jnp.concatenate(add_each(down_narrow, down_in))
        (down_mid,) = hop([down_half], ACROSS)

        (mine_got,) = after([mine_got], down_half)
        both = add_low(mine, mine_got)
        side_first = [swap(both[2:4], 2), swap(both[6:8], 4)]

        up_got = after(up_got, both)
        up_narrow = [
            add_low(keep_ux[0], up_first[0][0], up_got[0]),
            add_low(keep_uy[0], up_first[1][0], up_got[1]),
        ]
        up_in = hop(up_narrow, INWARD)

        side_first = after(side_first, up_narrow)
        side_second = [add_low(both[1], side_first[0][1]), add_low(both[5], side_first[1][1])]
        side_got = [swap(side_second[0], 4), swap(side_second[1], 2)]

        (down_mid,) = after([down_mid], side_second)
        down_total = add_low(down_half, down_mid)
        (down_out,) = hop([down_total], OUTWARD)

        side_got = after(side_got, down_total)
        slab_narrow = [
            add_low(both[0], side_first[0][0], side_got[0]),
            add_low(both[4], side_first[1][0], side_got[1]),
        ]
        slab_in = hop(slab_narrow, INWARD)

        (came,) = after(up_in[:1], slab_narrow)
        up_half = [add_low(up_narrow[0], came)]
        up_mid = hop(up_half, ACROSS)

        (came,) = after(up_in[1:], up_half)
        up_half.append(add_low(up_narrow[1], came))
        up_mid += hop(up_half[1:], ACROSS)

        (came,) = after(up_mid[:1], up_half[1])
        up_total = [add_low(up_half[0], came)]
        up_out = hop(up_total, OUTWARD)

        (came,) = after(slab_in[:1], up_total)
        slab_half = [add_low(slab_narrow[0], came)]
        slab_mid = hop(slab_half, ACROSS)

        (came,) = after(up_mid[1:], slab_half)
        up_total.append(add_low(up_half[1], came))
        up_out += hop(up_total[1:], OUTWARD)

        (came,) = after(slab_in[1:], up_total[1])
        slab_half.append(add_low(slab_narrow[1], came))
        slab_mid += hop(slab_half[1:], ACROSS)

        gate = slab_half[1]
        slab_total, slab_out = [], []
        for at in range(2):
            (came,) = after([slab_mid[at]], gate)
            slab_total.append(add_low(slab_half[at], came))
            slab_out += hop(slab_total[-1:], OUTWARD)
            gate = slab_total[-1:]

        (down_out,) = after([down_out], gate)
        down_weight_sum = settle(down_total, down_out).astype(F32)
        up_out = after(up_out, down_weight_sum, slab_out[0])
        upper, lower = [settle(*pair) for pair in zip(up_total, up_out)]
        first = core == 0
        (up_weight_sum,) = call(
            functools.partial(join_kernel, hidden),
            [((rows, 2 * half), F32)],
            (jnp.where(first, upper, lower), swap(jnp.where(first, lower, upper), 1)),
            core_position,
        )
        slab_out = after(slab_out, upper, lower)
        scalar = pl.BlockSpec(memory_space=pltpu.SMEM)
        heads_sum, output_sum, short, loss_sum, token_count = call(
            functools.partial(settle_kernel, rows, hidden),
            [
                ((rows, 3 * width), F32), ((rows, width), F32), ((VECTORS, 2 * width), F32),
                ((1,), F32), ((1,), jnp.int32),
            ],
            (*slab_total, *slab_out),
            lax.axis_index("narrow").reshape(1).astype(jnp.int32),
            out_specs=[vmem, vmem, vmem, scalar, scalar],
        )
        vectors_sum = short[:, :rows]
        up_bias_grad = short[0, LANES : LANES + hidden]
        loss_sum, token_count = loss_sum.reshape(()), token_count.reshape(())
    else:
        down_weight_sum = collect_chips(down_parts[0].reshape(chips, hidden, width))
        down_weight_sum = sum_narrow(down_weight_sum).astype(F32)
        up_sum = sum_narrow(collect_chips(up_parts[0].reshape(chips, 2 * rows, half)))
        up_sum = up_sum.reshape(2, rows, chips, hidden)
        up_weight_sum = by_core(mine_of(up_sum, 0), swap(mine_of(up_sum, 0, 1), 1), 2)
        up_weight_sum = up_weight_sum.reshape(rows, 2 * half).astype(F32)
        short = short_sums.reshape(8, wide, rows).transpose(1, 0, 2).reshape(wide, 8 * rows)
        up_bias_rows = up_bias_part.reshape(chips, hidden)
        up_bias_rows = by_core(up_bias_rows, jnp.zeros_like(up_bias_rows), 1).reshape(wide, hidden)
        shared = jnp.broadcast_to(loss_sums[:1, :LANES], (wide, LANES))
        row = jnp.concatenate([short, up_bias_rows, shared], axis=1).astype(BF16)
        row = jnp.pad(row, ((0, 0), (0, 4 * width - row.shape[1])))
        slab = jnp.concatenate([attend_part.reshape(wide, rows, 4 * width), row[:, None]], axis=1)
        slab = sum_narrow(lax.psum_scatter(slab, "wide", scatter_dimension=0)).astype(F32)
        vectors_sum = slab[rows, : 8 * rows].reshape(8, rows)
        heads_sum, output_sum = slab[:rows, : 3 * width], slab[:rows, 3 * width :]
        up_bias_grad = slab[rows, 8 * rows : 8 * rows + hidden]
        loss_sum = jnp.sum(slab[rows, 8 * rows + hidden : 8 * rows + hidden + LANES])
        token_count = lax.psum(jnp.sum(loss_mask), ("narrow", "wide"))
    return (
        result_low[None],
        input_grad[None],
        vectors_sum[ATTEND_GAIN],
        vectors_sum[ATTEND_SHIFT],
        heads_sum,
        vectors_sum[QUERY_BIAS],
        vectors_sum[VALUE_BIAS],
        output_sum,
        vectors_sum[OUTPUT_BIAS],
        vectors_sum[FORWARD_GAIN],
        vectors_sum[FORWARD_SHIFT],
        up_weight_sum,
        up_bias_grad,
        down_weight_sum,
        vectors_sum[DOWN_BIAS],
        loss_sum,
        token_count,
    )


def solution(mesh):
    in_specs = (
        P(("narrow", "wide"), None, None),
        P(("narrow", "wide"), None),
        P(("narrow", "wide"), None),
        P(("narrow", "wide"), None),
        P(),
        P("wide"),
        P("wide"),
        P("wide", None),
        P("wide"),
        P("wide"),
        P("wide", None),
        P("wide"),
        P("wide"),
        P("wide"),
        P("wide", None),
        P("wide"),
        P("wide", None),
        P("wide"),
    )
    out_specs = (
        P(("narrow", "wide"), None, None),
        P(("narrow", "wide"), None, None),
        P("wide"),
        P("wide"),
        P("wide", None),
        P("wide"),
        P("wide"),
        P("wide", None),
        P("wide"),
        P("wide"),
        P("wide"),
        P("wide", None),
        P("wide"),
        P("wide", None),
        P("wide"),
        P(),
        P(),
    )
    return jax.shard_map(local, mesh=mesh, in_specs=in_specs, out_specs=out_specs, check_vma=False)
```

```python
import functools
import math

import jax
import jax.numpy as jnp
from jax import lax
from jax.experimental import pallas as pl
from jax.experimental.pallas import tpu as pltpu
from jax.sharding import PartitionSpec as P

HEADS = 20
HEAD_DIM = 32
LANES = 128
SUBLANES = 8
SEGMENTS = 8
REACH = 192
CHUNK = 256
ROWS = 128
SCALE = 1.0 / math.sqrt(HEAD_DIM)
SCALE2 = math.log2(math.e) * SCALE
F32 = jnp.float32
BF16 = jnp.bfloat16
VECTORS = 8
ATTEND_GAIN, ATTEND_SHIFT, QUERY_BIAS, VALUE_BIAS = 0, 1, 2, 3
OUTPUT_BIAS, FORWARD_GAIN, FORWARD_SHIFT, DOWN_BIAS = 4, 5, 6, 7


def nn(left, right):
    return lax.dot_general(left, right, (((1,), (0,)), ((), ())), preferred_element_type=F32)


def nt(left, right):
    return lax.dot_general(left, right, (((1,), (1,)), ((), ())), preferred_element_type=F32)


def tn(left, right):
    return lax.dot_general(left, right, (((0,), (0,)), ((), ())), preferred_element_type=F32)


def call(kernel, outs, args, positions=None, grid=None, in_specs=None, out_specs=None, scratch=(),
         mib=16, aliases=None):
    whole = pl.BlockSpec(memory_space=pltpu.VMEM)
    in_specs = in_specs or [whole] * len(args)
    args = [
        pltpu.with_memory_space_constraint(arg, pltpu.HBM)
        if spec.memory_space == pltpu.HBM
        else arg
        for arg, spec in zip(args, in_specs)
    ]
    out_specs = out_specs or [whole] * len(outs)
    shapes = [
        pltpu.HBM(*out) if spec.memory_space == pltpu.HBM else jax.ShapeDtypeStruct(*out)
        for out, spec in zip(outs, out_specs)
    ]
    extra = [] if positions is None else [positions]
    return pl.pallas_call(
        kernel,
        out_shape=shapes,
        grid_spec=pltpu.PrefetchScalarGridSpec(
            num_scalar_prefetch=len(extra),
            grid=grid or (),
            in_specs=in_specs,
            out_specs=out_specs,
            scratch_shapes=list(scratch),
        ),
        compiler_params=pltpu.CompilerParams(vmem_limit_bytes=mib * 1024 * 1024),
        input_output_aliases=aliases or {},
        cost_estimate=pl.CostEstimate(flops=1, bytes_accessed=1, transcendentals=0),
    )(*extra, *args)


def unit(values):
    centred = values - jnp.mean(values, axis=-1, keepdims=True)
    spread = jnp.mean(centred * centred, axis=-1, keepdims=True)
    inverse = lax.rsqrt(spread + 1e-05)
    return centred * inverse, inverse


def unit_back(grad, normal, inverse, gain):
    scaled = grad * gain
    mean = jnp.mean(scaled, axis=-1, keepdims=True)
    along = jnp.mean(scaled * normal, axis=-1, keepdims=True)
    return inverse * (scaled - mean - normal * along)


def spans(length):
    chunk = min(CHUNK, length)
    return [
        (at, at + chunk, max(0, at - REACH), min(length, at + chunk + REACH))
        for at in range(0, length, chunk)
    ]


def split3(values):
    first = values.astype(BF16).astype(F32)
    rest = values - first
    second = rest.astype(BF16).astype(F32)
    return [first, second, rest - second]


def key_marks(segment_row):
    at = lax.broadcasted_iota(jnp.int32, (LANES, segment_row.shape[1]), 0)
    ones = (at >= SEGMENTS) & (at < SEGMENTS + 3)
    return jnp.where((at == segment_row) | ones, 1.0, 0.0).astype(BF16).T


def query_marks(segment_row):
    row = lax.broadcasted_iota(jnp.int32, (SEGMENTS, segment_row.shape[1]), 0)
    return jnp.where(row == segment_row, 0.0, -1e30)


def place(rows, head, marks):
    count = rows.shape[1]
    parts = [rows, marks, jnp.zeros((LANES - marks.shape[0], count), BF16)]
    if head < LANES // HEAD_DIM - 1:
        parts.insert(1, jnp.zeros((LANES - HEAD_DIM * (head + 1), count), BF16))
    if head:
        parts.insert(0, jnp.zeros((HEAD_DIM * head, count), BF16))
    return jnp.concatenate(parts, axis=0)


def attend_kernel(row_ref, q_ref, k_ref, v_ref, out_ref, across_ref, lse_ref, marks_ref):
    @pl.when(pl.program_id(0) == 0)
    def _():
        marks_ref[...] = key_marks(row_ref[...])

    length = q_ref.shape[0]
    heads = LANES // HEAD_DIM
    queries = q_ref[...].T
    values = v_ref[...].T
    keys = jnp.concatenate([k_ref[...], marks_ref[...]], axis=1)
    blank = jnp.zeros((SUBLANES, length), F32)
    marks = jnp.concatenate([query_marks(row_ref[...]), blank], axis=0).astype(BF16)
    ones = jnp.ones((SUBLANES, length), BF16)
    bodies = [(head, span) for head in range(heads) for span in spans(length)]

    def rows(head):
        return slice(HEAD_DIM * head, HEAD_DIM * (head + 1))

    summed = [jnp.concatenate([values[rows(head)], ones], axis=0) for head in range(heads)]

    def score(head, span):
        begin, end, low, high = span
        return nn(keys[low:high], place(queries[rows(head), begin:end], head, marks[:, begin:end]))

    def finish(head, span, top, probs):
        begin, end, low, high = span
        out = nn(summed[head][:, low:high], probs)
        total = out[HEAD_DIM : HEAD_DIM + 1]
        across_ref[rows(head), begin:end] = out[:HEAD_DIM] * (1.0 / total)
        lse_ref[head : head + 1, begin:end] = (top + jnp.log2(total)) * (1.0 / SCALE2)

    scores = [score(*body) for body in bodies[:2]]
    waiting = None
    for at, body in enumerate(bodies):
        current = scores.pop(0)
        if at + 2 < len(bodies):
            scores.append(score(*bodies[at + 2]))
        top = jnp.max(current, axis=0, keepdims=True) * SCALE2
        probs = jnp.exp2(current * SCALE2 - top).astype(BF16)
        if waiting is not None:
            finish(*waiting)
        waiting = (*body, top, probs)
    finish(*waiting)
    lse_ref[heads:, :] = jnp.zeros((SUBLANES - heads, length), F32)
    out_ref[...] = across_ref[...].T.astype(BF16)


def attend_back_kernel(
    row_ref, q_ref, k_ref, v_ref, grad_ref, across_ref, lse_ref,
    gq_ref, gk_ref, gv_ref, marks_ref, turned_ref,
):
    @pl.when(pl.program_id(0) == 0)
    def _():
        marks_ref[...] = key_marks(row_ref[...])

    length = q_ref.shape[0]
    grad = grad_ref[...]
    queries = q_ref[...].T
    turned_keys = k_ref[...].T
    grads = grad.T
    keys = jnp.concatenate([k_ref[...], marks_ref[...]], axis=1)
    values = jnp.concatenate([v_ref[...], marks_ref[...]], axis=1)
    low_marks = query_marks(row_ref[...])
    blank = jnp.zeros((SUBLANES, length), F32)
    lane = lax.broadcasted_iota(jnp.int32, (1, LANES), 1) // HEAD_DIM
    heads = []
    for head in range(LANES // HEAD_DIM):
        rows = slice(HEAD_DIM * head, HEAD_DIM * (head + 1))
        inner = jnp.sum(grads[rows].astype(F32) * across_ref[rows, :], axis=0, keepdims=True)
        lse = lse_ref[head : head + 1, :]
        score_marks = jnp.concatenate([low_marks, *split3(-lse), blank[:5]], axis=0)
        inner_marks = jnp.concatenate([blank, *split3(-inner), blank[:5]], axis=0)
        zero = jnp.zeros_like(grad)
        heads.append(
            (
                rows,
                score_marks.astype(BF16),
                inner_marks.astype(BF16),
                jnp.where(lane == head, q_ref[...], zero),
                jnp.where(lane == head, grad, zero),
            )
        )
    bodies = [
        (head, at, span) for head in range(len(heads)) for at, span in enumerate(spans(length))
    ]
    sums = [[None, None] for _ in spans(length)]

    def pair(head, at, span):
        begin, end, low, high = span
        rows, score_marks, inner_marks, _, _ = heads[head]
        return (
            nn(keys[low:high], place(queries[rows, begin:end], head, score_marks[:, begin:end])),
            nn(values[low:high], place(grads[rows, begin:end], head, inner_marks[:, begin:end])),
        )

    def finish(head, at, span, score_grads, probs):
        begin, end, low, high = span
        rows, _, _, own_queries, own_grads = heads[head]
        for which, (left, right) in enumerate(
            ((score_grads, own_queries[begin:end]), (probs, own_grads[begin:end]))
        ):
            part = nn(left, right)
            sums[at][which] = part if sums[at][which] is None else sums[at][which] + part
        turned_ref[rows, begin:end] = nn(turned_keys[rows, low:high], score_grads)

    ahead = [pair(*bodies[0])]
    waiting = None
    for at, body in enumerate(bodies):
        scores, differences = ahead.pop(0)
        if at + 1 < len(bodies):
            ahead.append(pair(*bodies[at + 1]))
        probs = jnp.exp2(scores * SCALE2)
        score_grads = (probs * differences).astype(BF16)
        if waiting is not None:
            finish(*waiting)
        waiting = (*body, score_grads, probs.astype(BF16))
    finish(*waiting)
    gq_ref[...] = (turned_ref[...].T * SCALE).astype(BF16)
    for which, (ref, factor) in enumerate(((gk_ref, SCALE), (gv_ref, 1.0))):
        total = None
        for at, (_, _, low, high) in enumerate(spans(length)):
            parts = [sums[at][which]]
            if low:
                parts.insert(0, jnp.zeros((low, LANES), F32))
            if high < length:
                parts.append(jnp.zeros((length - high, LANES), F32))
            part = jnp.concatenate(parts, axis=0) if len(parts) > 1 else parts[0]
            total = part if total is None else total + part
        ref[...] = (total * factor).astype(BF16)


def attention_specs(length, width, begin=0):
    tiles = width // LANES

    def tile(at, begin=begin):
        return pl.BlockSpec((length, LANES), lambda i: (0, at + begin + i))

    return (
        tiles,
        tile,
        pl.BlockSpec((1, length), lambda i: (0, 0)),
        pl.BlockSpec((LANES, length), lambda i: (begin + i, 0)),
        pl.BlockSpec((SUBLANES, length), lambda i: (begin + i, 0)),
    )


def attend(joined, row):
    length = joined.shape[0]
    width = joined.shape[1] // 3
    tiles, tile, row_spec, across_spec, lse_spec = attention_specs(length, width)
    return call(
        attend_kernel,
        [((length, width), BF16), ((width, length), F32), ((SUBLANES * tiles, length), F32)],
        (row, joined, joined, joined),
        grid=(tiles,),
        in_specs=[row_spec, tile(0), tile(tiles), tile(2 * tiles)],
        out_specs=[tile(0), across_spec, lse_spec],
        scratch=[pltpu.VMEM((length, LANES), BF16)],
    )


def attend_back(joined, row, grad, across, lse, begin=0, end=None):
    length = joined.shape[0]
    width = joined.shape[1] // 3
    specs = attention_specs(length, width, begin)
    tiles, tile, row_spec, across_spec, lse_spec = specs
    count = (end or tiles) - begin
    return call(
        attend_back_kernel,
        [((length, count * LANES), BF16)] * 3,
        (row, joined, joined, joined, grad, across, lse),
        grid=(count,),
        in_specs=[row_spec, tile(0), tile(tiles), tile(2 * tiles), tile(0), across_spec, lse_spec],
        out_specs=[tile(0, 0)] * 3,
        scratch=[pltpu.VMEM((length, LANES), BF16), pltpu.VMEM((LANES, length), F32)],
        mib=24,
    )


def slab_kernel(heads_ref, out_ref, short_ref, up_ref, slab_ref):
    rows = heads_ref.shape[0]
    width = out_ref.shape[1]
    slab_ref[:rows, : 3 * width] = heads_ref[...]
    slab_ref[:rows, 3 * width :] = out_ref[...]
    slab_ref[rows:, :] = jnp.zeros((VECTORS, 4 * width), BF16)
    slab_ref[rows:, :rows] = short_ref[...]
    slab_ref[rows:, LANES : LANES + up_ref.shape[1]] = jnp.broadcast_to(
        up_ref[...], (VECTORS, up_ref.shape[1])
    )


def project_kernel(count, rows, hidden, position_ref, x_ref, *refs):
    slabs, refs = refs[:count], refs[count:]
    length, width = x_ref.shape
    if count:
        low_ref, joined_ref, heads_ref, out_ref, vector_ref, bias_ref, short_ref, sems = refs
        copies = []
        for at, slab in enumerate(slabs):
            begin = pl.multiple_of(position_ref[at] * rows, SUBLANES)
            here = pl.ds(begin, rows)
            for which, (source, target) in enumerate(
                (
                    (slab.at[pl.ds(0, rows), pl.ds(0, 3 * width)], heads_ref.at[here]),
                    (slab.at[pl.ds(0, rows), pl.ds(3 * width, width)], out_ref.at[here]),
                    (slab.at[pl.ds(rows, VECTORS), pl.ds(0, LANES + hidden)], short_ref.at[at]),
                )
            ):
                copy = pltpu.make_async_copy(source, target, sems.at[at, which])
                copy.start()
                copies.append(copy)
    else:
        heads_ref, vector_ref, low_ref, joined_ref = refs
    if count:
        for copy in copies:
            copy.wait()
        vectors = jnp.zeros((VECTORS, width), F32)
        for at in range(count):
            begin = position_ref[at] * rows
            short = short_ref[at, :, :LANES].astype(F32)
            lane = lax.broadcasted_iota(jnp.int32, short.shape, 1)
            short = jnp.where(lane < rows, short, 0.0)
            short = jnp.concatenate([short, jnp.zeros((VECTORS, width - LANES), F32)], axis=1)
            vectors = vectors + pltpu.roll(short, begin, 1)
            if at < count // 2:
                begin = pl.multiple_of(lax.div(position_ref[at], 2) * hidden, LANES)
                bias_ref[:, pl.ds(begin, hidden)] = short_ref[at, :, LANES:].astype(F32)
        vector_ref[...] = vectors
    zero = jnp.zeros((1, width), F32)
    vector = vector_ref[...]
    bias = jnp.concatenate(
        [vector[QUERY_BIAS : QUERY_BIAS + 1], zero, vector[VALUE_BIAS : VALUE_BIAS + 1]], axis=1
    )
    for at in range(0, length, ROWS):
        normal, _ = unit(x_ref[at : at + ROWS, :].astype(F32))
        low_ref[at : at + ROWS, :] = (
            normal * vector[ATTEND_GAIN : ATTEND_GAIN + 1]
            + vector[ATTEND_SHIFT : ATTEND_SHIFT + 1]
        ).astype(BF16)
    for at in range(0, 3 * width, width):
        here = slice(at, at + width)
        joined_ref[:, here] = (nn(low_ref[...], heads_ref[:, here]) + bias[:, here]).astype(BF16)


def middle_kernel(x_ref, attended_ref, out_ref, vector_ref, middle_ref, low_ref):
    vector = vector_ref[...]
    for at in range(0, x_ref.shape[0], ROWS):
        here = slice(at, at + ROWS)
        middle = (
            x_ref[here, :].astype(F32)
            + nn(attended_ref[here, :], out_ref[...])
            + vector[OUTPUT_BIAS : OUTPUT_BIAS + 1]
        )
        middle_ref[here, :] = middle
        normal, _ = unit(middle)
        low_ref[here, :] = (
            normal * vector[FORWARD_GAIN : FORWARD_GAIN + 1]
            + vector[FORWARD_SHIFT : FORWARD_SHIFT + 1]
        ).astype(BF16)


def up_kernel(position_ref, own_ref, other_ref, bias_ref, *refs):
    parts, (act_ref, slope_ref, full_ref) = refs[: len(refs) - 3], refs[len(refs) - 3 :]
    for at, part in enumerate(parts):
        rows = part.shape[0]
        begin = pl.multiple_of(position_ref[at] * rows, SUBLANES)
        full_ref[pl.ds(begin, rows), :] = part[...]
    weight = full_ref[...]
    bias = bias_ref[:1, :]
    length = own_ref.shape[0]
    for which, ref in enumerate((own_ref, other_ref)):
        for at in range(0, length, ROWS):
            upward = nn(ref[at : at + ROWS, :], weight) + bias
            share = 0.5 + 0.5 * lax.erf(upward * math.sqrt(0.5))
            bell = jnp.exp2((upward * upward) * (-0.5 * math.log2(math.e)))
            here = slice(which * length + at, which * length + at + ROWS)
            act_ref[here, :] = (upward * share).astype(BF16)
            slope = share + upward * (bell * (1.0 / math.sqrt(2.0 * math.pi)))
            slope_ref[here, :] = slope.astype(BF16)


def column_specs(half, block):
    block = min(block, half)

    def column(height):
        return pl.BlockSpec((height, block), lambda i, at: (0, i))

    return half // block, block, column


def whole_spec(shape):
    return pl.BlockSpec(shape, lambda i, at: (0,) * len(shape))


def up_project(own, other, bias, parts, positions, hidden):
    length, width = own.shape
    half = bias.shape[1]
    paired = parts[0].shape[1] > half
    steps, block, column = column_specs(half, hidden if paired else 512)
    whole = whole_spec((length, width))

    def part_spec(part):
        if paired:
            return pl.BlockSpec((part.shape[0], block), lambda i, at: (0, 2 * i + at[len(parts)]))
        return column(part.shape[0])

    return call(
        up_kernel,
        [((2 * length, half), BF16), ((2 * length, half), BF16), ((width, half), BF16)],
        (own, other, bias, *parts),
        positions,
        grid=(steps,),
        in_specs=[whole, whole, column(bias.shape[0])] + [part_spec(part) for part in parts],
        out_specs=[column(2 * length), column(2 * length), column(width)],
    )


def down_kernel(position_ref, act_ref, *refs):
    parts, (own_ref, other_ref, full_ref) = refs[: len(refs) - 3], refs[len(refs) - 3 :]
    length = own_ref.shape[0]
    for at, part in enumerate(parts):
        rows = part.shape[0]
        begin = pl.multiple_of(position_ref[at] * rows, SUBLANES)
        full_ref[pl.ds(begin, rows), :] = part[...]
    for which, ref in enumerate((own_ref, other_ref)):
        here = slice(which * length, (which + 1) * length)
        ref[...] = nn(act_ref[here, :], full_ref[...]).astype(ref.dtype)


def down_project(act, parts, positions):
    length = act.shape[0] // 2
    half = act.shape[1]
    width = parts[0].shape[1]
    return call(
        down_kernel,
        [((length, width), F32), ((length, width), BF16), ((half, width), BF16)],
        (act, *parts),
        positions,
        mib=20,
    )


def down_near_kernel(position_ref, act_ref, *refs):
    parts, (sum_ref, full_ref) = refs[:-2], refs[-2:]
    size = parts[0].shape[0]
    for at, part in enumerate(parts):
        rows = part.shape[0]
        begin = pl.multiple_of(position_ref[at] * rows, SUBLANES)
        full_ref[pl.ds(begin, rows), :] = part[...]
    chips = [position_ref[0], lax.div(position_ref[1], 2), lax.div(position_ref[3], 2)]
    length = act_ref.shape[0] // 2
    for which in range(2):
        here = slice(which * length, (which + 1) * length)
        total = None
        for chip in chips:
            units = pl.ds(pl.multiple_of(chip * size, LANES), size)
            part = nn(act_ref[here, units], full_ref[units, :])
            total = part if total is None else total + part
        sum_ref[here, :] = total


def down_far_kernel(position_ref, act_ref, sum_ref, upper_ref, lower_ref, _, own_ref, other_ref, full_ref):
    rows, length = upper_ref.shape[0], own_ref.shape[0]
    size = 2 * rows
    units = pl.ds(pl.multiple_of(lax.div(position_ref[5], 2) * size, LANES), size)
    weight = jnp.concatenate([upper_ref[...], lower_ref[...]], axis=0)
    full_ref[units, :] = weight
    for which, ref in enumerate((own_ref, other_ref)):
        here = slice(which * length, (which + 1) * length)
        ref[...] = (sum_ref[here, :] + nn(act_ref[here, units], weight)).astype(ref.dtype)


def down_project_square(act, near, far, positions):
    length, half, width = act.shape[0] // 2, act.shape[1], near[0].shape[1]
    total, full = call(
        down_near_kernel,
        [((2 * length, width), F32), ((half, width), BF16)],
        (act, *near),
        positions,
        mib=24,
    )
    far = far(total)
    return call(
        down_far_kernel,
        [((length, width), F32), ((length, width), BF16), ((half, width), BF16)],
        (act, total, *far, full),
        positions,
        mib=24,
        aliases={5: 2},
    )


def loss_kernel(
    middle_ref, own_ref, got_ref, vector_ref, readout_ref, target_ref, mask_ref,
    low_ref, down_ref, grad_ref, sums_ref,
):
    result = (
        middle_ref[...]
        + (own_ref[...] + got_ref[...].astype(F32))
        + vector_ref[DOWN_BIAS : DOWN_BIAS + 1, :]
    ).astype(BF16)
    low_ref[...] = result
    logits = nt(readout_ref[...], result)
    length = logits.shape[1]
    top = jnp.max(logits, axis=0, keepdims=True)
    shifted = jnp.exp(logits - top)
    total = jnp.sum(shifted, axis=0, keepdims=True)
    onehot = lax.broadcasted_iota(jnp.int32, logits.shape, 0) == target_ref[...]
    picked = jnp.sum(jnp.where(onehot, logits, 0.0), axis=0, keepdims=True)
    weight = mask_ref[...].astype(F32)
    loss = (top + jnp.log(total) - picked) * weight
    loss_lanes = jnp.zeros((1, LANES), F32)
    count_lanes = jnp.zeros((1, LANES), F32)
    for at in range(0, length, LANES):
        loss_lanes = loss_lanes + loss[:, at : at + LANES]
        count_lanes = count_lanes + weight[:, at : at + LANES]
    lanes = jnp.concatenate([loss_lanes, count_lanes], axis=0)
    lanes = jnp.concatenate([lanes, jnp.zeros((2, result.shape[1] - LANES), F32)], axis=1)
    grad_logits = (weight * (shifted / total - onehot.astype(F32))).astype(BF16)
    grad_ref[...] = grad_logits
    low = tn(grad_logits, readout_ref[...]).astype(BF16)
    down_ref[...] = low
    sums = jnp.sum(low.astype(F32), axis=0, keepdims=True)
    blank = jnp.zeros((SUBLANES - 3, result.shape[1]), F32)
    sums_ref[...] = jnp.concatenate([lanes, sums, blank], axis=0)


def down_grad_kernel(chips, position_ref, act_ref, own_ref, other_ref, *out_refs):
    length = own_ref.shape[0]
    hidden = act_ref.shape[1] // chips
    for offset in range(chips):
        if len(out_refs) == 1:
            begin = offset * hidden
        else:
            begin = pl.multiple_of((position_ref[0] ^ offset) * hidden, LANES)
        here = pl.ds(begin, hidden)
        part = tn(act_ref[:length, here], own_ref[...]) + tn(act_ref[length:, here], other_ref[...])
        part = part.astype(BF16)
        if len(out_refs) == 1:
            out_refs[0][begin : begin + hidden, :] = part
            continue
        keep_x, send_x, keep_y, send_y = out_refs
        half = hidden // 2
        (send_x if offset % 2 else keep_x)[offset // 2, :, :] = part[:half]
        (send_y if offset // 2 else keep_y)[offset % 2, :, :] = part[half:]


def down_grad(act, own, other, chips, position):
    half = act.shape[1]
    width = own.shape[1]
    if square():
        outs = [((2, half // chips // 2, width), BF16)] * 4
    else:
        outs = [((half, width), BF16)]
    return call(
        functools.partial(down_grad_kernel, chips), outs, (act, own, other), position, mib=20
    )


def up_grad_kernel(
    rows, position_ref, own_ref, other_ref, slope_ref, second_ref, second_other_ref, down_ref,
    up_ref, bias_ref, *refs,
):
    out_refs, part_ref = refs[:-1], refs[-1]
    length = own_ref.shape[0]
    total = None
    grads = []
    for which, ref in enumerate((own_ref, other_ref)):
        for at in range(0, length, 2 * ROWS):
            here = slice(which * length + at, which * length + at + 2 * ROWS)
            grad = nt(ref[at : at + 2 * ROWS, :], down_ref[...]) * slope_ref[here, :].astype(F32)
            low = grad.astype(BF16)
            up_ref[here, :] = low
            part = jnp.sum(low.astype(F32), axis=0, keepdims=True)
            total = part if total is None else total + part
    bias_ref[...] = total
    part = tn(second_ref[...], up_ref[:length, :]) + tn(second_other_ref[...], up_ref[length:, :])
    if len(out_refs) == 1:
        out_refs[0][...] = part.astype(BF16)
        return
    part_ref[...] = part
    keep_x, send_x, keep_y, send_y = out_refs
    for offset in range(4):
        begin = pl.multiple_of((position_ref[0] ^ offset) * (2 * rows), SUBLANES)
        upper = part_ref[pl.ds(begin, rows), :].astype(BF16)
        lower = part_ref[pl.ds(begin + rows, rows), :].astype(BF16)
        (send_x if offset % 2 else keep_x)[offset // 2, :, :] = upper
        (send_y if offset // 2 else keep_y)[offset % 2, :, :] = lower


def up_grad(own, other, slope, second, second_other, down_full, rows, position):
    length, width = own.shape
    half = slope.shape[1]
    steps, block, column = column_specs(half, 512)
    whole = whole_spec((length, width))
    if square():
        outs = [((2, rows, half), BF16)] * 4
        specs = [pl.BlockSpec((2, rows, block), lambda i, at: (0, 0, i))] * 4
    else:
        outs = [((width, half), BF16)]
        specs = [column(width)]
    return call(
        functools.partial(up_grad_kernel, rows),
        [((2 * length, half), BF16), ((1, half), F32), *outs],
        (own, other, slope, second, second_other, down_full),
        position,
        grid=(steps,),
        in_specs=[
            whole, whole, column(2 * length), whole, whole,
            pl.BlockSpec((block, width), lambda i, at: (i, 0)),
        ],
        out_specs=[column(2 * length), column(1), *specs],
        scratch=[pltpu.VMEM((width, block), F32)],
        mib=20,
    )


def inward_kernel(grad_ref, up_ref, own_far, other_ref, own_ref, sem):
    length = other_ref.shape[0]
    own_ref[...] = nt(grad_ref[:length, :], up_ref[...])
    copy = pltpu.make_async_copy(own_ref, own_far, sem)
    copy.start()
    other_ref[...] = nt(grad_ref[length:, :], up_ref[...]).astype(BF16)
    copy.wait()


def join_kernel(hidden, position_ref, mine_ref, other_ref, out_ref):
    for at in range(mine_ref.shape[1] // hidden):
        here = slice(hidden * at, hidden * (at + 1))
        for core, ref in enumerate((mine_ref, other_ref)):
            begin = (2 * at + (position_ref[0] + core) % 2) * hidden
            out_ref[:, pl.ds(pl.multiple_of(begin, LANES), hidden)] = ref[:, here].astype(F32)


def branch_kernel(
    got_ref, own_far, middle_far, logits_ref, classes_ref, out_ref, vector_ref,
    grad_ref, branch_ref, attended_ref, sums_ref, own_ref, middle_ref, sems,
):
    width = own_ref.shape[1]
    blocks = range(0, own_ref.shape[0], ROWS)
    copies = []
    for at in blocks:
        here = pl.ds(at, ROWS)
        copies.append(
            [
                pltpu.make_async_copy(far.at[here], ref.at[here], sems.at[at // ROWS, which])
                for which, (far, ref) in enumerate(((own_far, own_ref), (middle_far, middle_ref)))
            ]
        )
        for copy in copies[-1]:
            copy.start()
    gain = vector_ref[FORWARD_GAIN : FORWARD_GAIN + 1, :]
    sums = [jnp.zeros((1, width), F32) for _ in range(3)]
    for at in blocks:
        for copy in copies[at // ROWS]:
            copy.wait()
        here = slice(at, at + ROWS)
        grad = own_ref[here, :] + got_ref[here, :].astype(F32)
        normal, inverse = unit(middle_ref[here, :])
        result = tn(logits_ref[:, here], classes_ref[...])
        middle = result + unit_back(grad, normal, inverse, gain)
        grad_ref[here, :] = middle
        branch = middle.astype(BF16)
        branch_ref[here, :] = branch
        attended_ref[here, :] = nt(branch, out_ref[...]).astype(BF16)
        for which, part in enumerate((grad * normal, grad, branch.astype(F32))):
            sums[which] = sums[which] + jnp.sum(part, axis=0, keepdims=True)
    blank = jnp.zeros((SUBLANES - 3, width), F32)
    sums_ref[...] = jnp.concatenate([*sums, blank], axis=0)


def last_kernel(count, rows, hidden, pieces, position_ref, x_ref, low_ref, *refs):
    grad_refs, refs = refs[: 3 * pieces], refs[3 * pieces :]
    heads_ref, attended_ref, branch_ref, grad_ref, vector_ref, *refs = refs
    sums_ref, loss_ref, up_ref, *refs = refs
    stacks, (input_ref, vectors_ref, full_ref) = refs[:-3], refs[-3:]
    width = x_ref.shape[1]

    def grads(which, here):
        parts = [ref[here, :] for ref in grad_refs[which::3]]
        return jnp.concatenate(parts, axis=1) if pieces > 1 else parts[0]

    for at in range(3):
        part = tn(low_ref[...], grads(at, slice(None)))
        full_ref[:, width * at : width * (at + 1)] = part.astype(BF16)
    full_ref[:, 3 * width :] = tn(attended_ref[...], branch_ref[...]).astype(BF16)
    gain = vector_ref[ATTEND_GAIN : ATTEND_GAIN + 1, :]

    def block(at, sums):
        here = pl.ds(pl.multiple_of(at * ROWS, ROWS), ROWS)
        grad_query, grad_key, grad_value = [grads(which, here) for which in range(3)]
        grad = (
            nt(grad_query, heads_ref[:, :width])
            + nt(grad_key, heads_ref[:, width : 2 * width])
            + nt(grad_value, heads_ref[:, 2 * width :])
        )
        normal, inverse = unit(x_ref[here, :].astype(F32))
        input_ref[here, :] = grad_ref[here, :] + unit_back(grad, normal, inverse, gain)
        parts = (grad * normal, grad, grad_query.astype(F32), grad_value.astype(F32))
        return tuple(
            total + jnp.sum(part, axis=0, keepdims=True) for total, part in zip(sums, parts)
        )

    zero = jnp.zeros((1, width), F32)
    sums = lax.fori_loop(0, x_ref.shape[0] // ROWS, block, (zero,) * 4)
    vectors = jnp.concatenate(
        [*sums, sums_ref[2:3, :], sums_ref[0:1, :], sums_ref[1:2, :], loss_ref[2:3, :]], axis=0
    )
    vectors_ref[...] = vectors
    blank = jnp.zeros((VECTORS - 1, hidden), F32)
    lanes = jnp.concatenate([loss_ref[:2, :LANES], jnp.zeros((VECTORS - 2, LANES), F32)], axis=0)
    for which, stack in enumerate(stacks):

        def slab(step, carry, which=which, stack=stack):
            place_at = position_ref[which * (count // 2) + step]
            begin = pl.multiple_of(place_at * rows, SUBLANES)
            short = pltpu.roll(vectors, width - begin, 1)[:, :LANES]
            if which == 0:
                hidden_at = pl.multiple_of(lax.div(place_at, 2) * hidden, LANES)
                bias = jnp.concatenate([up_ref[:, pl.ds(hidden_at, hidden)], blank], axis=0)
            else:
                bias = jnp.zeros((VECTORS, hidden), F32)
            row = jnp.concatenate([short, bias, lanes], axis=1).astype(BF16)
            pad = jnp.zeros((VECTORS, 4 * width - row.shape[1]), BF16)
            row = jnp.concatenate([row, pad], axis=1)
            picks = (2 * (step % 2) + step // 2, 4 + step)
            for side, pick in enumerate(picks):
                here = slice(2 * width * side, 2 * width * (side + 1))
                stack[pick, :rows, :] = full_ref[pl.ds(begin, rows), here]
                stack[pick, rows:, :] = row[:, here]
            return carry

        lax.fori_loop(0, count // 2, slab, 0)


def settle_kernel(rows, hidden, place_ref, *refs):
    totals, outers, refs = refs[:2], refs[2:4], refs[4:]
    heads_ref, out_ref, short_ref, loss_ref, count_ref = refs
    width = out_ref.shape[1]
    inner = (place_ref[0] == 1) | (place_ref[0] == 2)
    left, right = [
        jnp.where(inner, total[...], outer[...]).astype(F32) for total, outer in zip(totals, outers)
    ]
    heads_ref[:, : 2 * width] = left[:rows]
    heads_ref[:, 2 * width :] = right[:rows, :width]
    out_ref[...] = right[:rows, width:]
    short_ref[...] = left[rows:]
    lanes = left[rows:, LANES + hidden : 2 * LANES + hidden]
    loss_ref[0] = jnp.sum(lanes[0:1])
    count_ref[0] = jnp.sum(lanes[1:2]).astype(jnp.int32)


def swap(values, bit):
    return lax.ppermute(values, "wide", [(i, i ^ bit) for i in range(lax.axis_size("wide"))])


def same_core_groups():
    chips = lax.axis_size("wide") // 2
    return [[2 * chip + core for chip in range(chips)] for core in range(2)]


def square():
    return lax.axis_size("wide") == 8


def spread_chips(shard):
    return lax.all_gather(shard, "wide", axis=0, axis_index_groups=same_core_groups())


def add_low(*parts):
    return sum(part.astype(F32) for part in parts).astype(BF16)


def collect_chips(parts):
    return lax.psum_scatter(
        parts, "wide", scatter_dimension=0, axis_index_groups=same_core_groups()
    )


def after(values, *gates):
    leaves, tree = jax.tree.flatten(values)
    held = lax.optimization_barrier((*leaves, *jax.tree.leaves(gates)))
    return jax.tree.unflatten(tree, held[: len(leaves)])


INWARD, ACROSS, OUTWARD = [(0, 1), (3, 2)], [(1, 2), (2, 1)], [(1, 0), (2, 3)]


def hop(parts, pairs):
    return [lax.ppermute(part, "narrow", pairs) for part in parts]


def add_each(left, right):
    return [add_low(a, b) for a, b in zip(left, right)]


def settle(total, outer):
    place_at = lax.axis_index("narrow")
    return jnp.where((place_at == 1) | (place_at == 2), total, outer)


def sum_narrow(shard):
    if lax.axis_size("narrow") != 4:
        return lax.psum(shard, "narrow")
    half = add_low(shard, *hop([shard], INWARD))
    total = add_low(half, *hop([half], ACROSS))
    return settle(total, *hop([total], OUTWARD))


def local(
    layer_input, segments, targets, loss_mask, readout,
    attend_gain, attend_shift, heads_weight, query_bias, value_bias, output_weight, output_bias,
    forward_gain, forward_shift, up_weight, up_bias, down_weight, down_bias,
):
    length = layer_input.shape[1]
    width = layer_input.shape[2]
    wide = lax.axis_size("wide")
    chips = wide // 2
    core = lax.axis_index("wide") % 2
    chip = lax.axis_index("wide") // 2
    rows = heads_weight.shape[0]
    hidden = up_bias.shape[0]
    half = chips * hidden
    x = layer_input[0]
    classes = readout.T
    vmem = pl.BlockSpec(memory_space=pltpu.VMEM)
    far_away = pl.BlockSpec(memory_space=pltpu.HBM)

    def by_core(mine, other, axis):
        return jnp.where(
            core == 0, jnp.stack([mine, other], axis), jnp.stack([other, mine], axis)
        )

    def mine_of(values, axis, flip=0):
        return lax.dynamic_index_in_dim(values, core ^ flip, axis, keepdims=False)

    short = jnp.stack(
        [
            attend_gain, attend_shift, query_bias, value_bias,
            output_bias, forward_gain, forward_shift, down_bias,
        ]
    )
    core_position = core.reshape(1).astype(jnp.int32)
    chip_position = chip.reshape(1).astype(jnp.int32)
    if square():
        offsets = jnp.arange(4, dtype=jnp.int32)
        (slab,) = call(
            slab_kernel,
            [((rows + VECTORS, 4 * width), BF16)],
            (heads_weight, output_weight, short, up_bias[None]),
        )
        near_x, near_y, far = swap(slab, 2), swap(slab, 4), swap(slab, 6)
        swapped = swap(slab, 1)
        devices = 2 * (chip ^ offsets) + core
        positions = jnp.concatenate([devices, devices ^ 1]).astype(jnp.int32)
        up_weight, positions = after([up_weight, positions], near_x, swapped)
        up_x, up_y = swap(up_weight, 2), swap(up_weight, 4)
        swapped_x = swap(near_x, 1)
        near_y, far = after([near_y, far], swapped_x)
        slabs = [slab, near_x, near_y, far, swapped, swapped_x, swap(near_y, 1), swap(far, 1)]
        first_low, joined, heads_full, output_full, vectors, up_bias_half = call(
            functools.partial(project_kernel, len(slabs), rows, hidden),
            [
                ((length, width), BF16), ((length, 3 * width), BF16), ((width, 3 * width), BF16),
                ((width, width), BF16), ((VECTORS, width), F32), ((VECTORS, half), F32),
            ],
            (x, *slabs),
            positions,
            in_specs=[pl.BlockSpec(memory_space=pltpu.VMEM)]
            + [pl.BlockSpec(memory_space=pltpu.HBM)] * len(slabs),
            scratch=[
                pltpu.VMEM((len(slabs), VECTORS, LANES + hidden), BF16),
                pltpu.SemaphoreType.DMA((len(slabs), 3)),
            ],
            mib=20,
        )
    else:
        tail = jnp.concatenate([short.reshape(1, 8 * rows), up_bias[None]], axis=1)
        tail = jnp.pad(tail, ((0, 0), (0, 4 * width - tail.shape[1])))
        slab = jnp.concatenate(
            [jnp.concatenate([heads_weight, output_weight], axis=1), tail], axis=0
        )
        slabs = lax.all_gather(slab, "wide", axis=0)
        attend_full = slabs[:, :rows].reshape(width, 4 * width)
        heads_full = attend_full[:, : 3 * width]
        output_full = attend_full[:, 3 * width :]
        last = slabs[:, rows].astype(F32)
        vectors = last[:, : 8 * rows].reshape(wide, 8, rows).transpose(1, 0, 2).reshape(8, width)
        up_bias_half = mine_of(last[:, 8 * rows : 8 * rows + hidden].reshape(chips, 2, hidden), 1)
        up_bias_half = jnp.broadcast_to(up_bias_half.reshape(1, half), (VECTORS, half))
        positions = jnp.zeros((1,), jnp.int32)
        first_low, joined = call(
            functools.partial(project_kernel, 0, rows, hidden),
            [((length, width), BF16), ((length, 3 * width), BF16)],
            (x, heads_full, vectors),
            positions,
            mib=20,
        )
        up_view = up_weight.reshape(rows, chips, 2, hidden)
        up_pair = by_core(
            mine_of(up_view, 2).reshape(rows, half),
            swap(mine_of(up_view, 2, 1).reshape(rows, half), 1),
            0,
        ).reshape(2 * rows, half)
        up_parts = [spread_chips(up_pair).reshape(width, half)]
        down_parts = [spread_chips(down_weight).reshape(half, width)]
        up_positions = down_positions = positions

    attended, across, lse = attend(joined, segments)
    if square():
        up_x, up_y = after([up_x, up_y], attended)
        cut = rows // 2
        passed = [up_y[:cut], up_x[cut:]]
        (attended,) = after([attended], passed)
        near = [up_weight, up_x, up_y]
        near_swapped = [swap(part, 1) for part in near]
        passed = [swap(passed[0], 2), swap(passed[1], 4)]
        up_parts = [*near, *passed, *near_swapped, *[swap(part, 1) for part in passed]]
        at = jnp.arange(11, dtype=jnp.int32)
        part = at % 5
        device = 2 * (chip ^ jnp.minimum(part, 3)) + (core ^ (at // 5))
        up_positions = jnp.where(part < 3, device, 2 * device + part - 3)
        up_positions = jnp.where(at < 10, up_positions, core).astype(jnp.int32)
        middle_row = hidden // 2
        upper, lower = after(
            [down_weight[:middle_row], down_weight[middle_row:]], up_x, up_y
        )
        lower_x, upper_y = swap(lower, 2), swap(upper, 4)
        upper_x, lower_y = swap(upper, 2), swap(lower, 4)
        down_parts = [
            down_weight, upper_x, lower_x, upper_y, lower_y
        ]
        at = jnp.arange(7, dtype=jnp.int32)
        down_positions = jnp.where(at == 0, chip, 2 * (chip ^ ((at + 1) // 2)) + (at + 1) % 2)
    middle, second_low = call(
        middle_kernel,
        [((length, width), F32), ((length, width), BF16)],
        (x, attended, output_full, vectors),
    )

    if square():
        (second_other,) = after([second_low], near_swapped)
        second_other = swap(second_other, 1)
    else:
        second_other = swap(second_low, 1)
    activated, slope, up_full = up_project(
        second_low, second_other, up_bias_half, up_parts, up_positions, hidden
    )
    if square():
        passed_x, passed_y = after([upper_y, lower_x], activated)
        far = [swap(passed_x, 2), swap(passed_y, 4)]
        outward, outward_other, down_full = down_project_square(
            activated, down_parts, lambda total: after(far, total), down_positions
        )
    else:
        outward, outward_other, down_full = down_project(activated, down_parts, down_positions)
    result_low, grad_down, grad_logits, loss_sums = call(
        loss_kernel,
        [
            ((length, width), BF16), ((length, width), BF16), (classes.shape[:1] + (length,), BF16),
            ((SUBLANES, width), F32),
        ],
        (middle, outward, swap(outward_other, 1), vectors, classes, targets, loss_mask),
    )

    grad_down_other = swap(grad_down, 1)
    down_parts = down_grad(activated, grad_down, grad_down_other, chips, chip_position)
    if square():
        keep_dx, send_dx, keep_dy, send_dy = down_parts
        down_first = [swap(send_dx, 2), swap(send_dy, 4)]
        (grad_down_other,) = after([grad_down_other], send_dx)
    grad_up, up_bias_part, *up_parts = up_grad(
        grad_down, grad_down_other, slope, second_low, second_other, down_full, rows, chip_position
    )
    inward, inward_other = call(
        inward_kernel,
        [((length, width), F32), ((length, width), BF16)],
        (grad_up, up_full),
        out_specs=[far_away, vmem],
        scratch=[pltpu.VMEM((length, width), F32), pltpu.SemaphoreType.DMA],
        mib=20,
    )
    got_inward = swap(inward_other, 1)
    if square():
        down_second = [
            add_low(keep_dx[1], down_first[0][1]), add_low(keep_dy[1], down_first[1][1])
        ]
        (got_inward,) = after([got_inward], down_second)
        keep_ux, send_ux, keep_uy, send_uy = up_parts
        send_ux, send_uy = after([send_ux, send_uy], down_second)
        down_got = [swap(down_second[0], 4), swap(down_second[1], 2)]
        up_first = [swap(send_ux, 2), swap(send_uy, 4)]
    grad_middle, grad_branch, grad_attended, branch_sums = call(
        branch_kernel,
        [
            ((length, width), F32), ((length, width), BF16), ((length, width), BF16),
            ((SUBLANES, width), F32),
        ],
        (got_inward, inward, middle, grad_logits, classes, output_full, vectors),
        in_specs=[vmem, far_away, far_away, vmem, vmem, vmem, vmem],
        scratch=[
            *[pltpu.VMEM((length, width), F32)] * 2,
            pltpu.SemaphoreType.DMA((length // ROWS, 2)),
        ],
        mib=24,
    )

    if square():
        attend_grads = attend_back(joined, segments, grad_attended, across, lse)
        down_got = after(down_got, attend_grads[0])
        down_narrow = [
            add_low(keep_dx[0], down_first[0][0], down_got[0]),
            add_low(keep_dy[0], down_first[1][0], down_got[1]),
        ]
        down_in = hop(down_narrow, INWARD)
        attend_grads = after(attend_grads, down_narrow)
    else:
        attend_grads = attend_back(joined, segments, grad_attended, across, lse)
    stack_shape = ((8, rows + VECTORS, 2 * width), BF16)
    *stacks, input_grad, short_sums, attend_part = call(
        functools.partial(last_kernel, 8 if square() else 0, rows, hidden, len(attend_grads) // 3),
        ([stack_shape] * 2 if square() else [])
        + [((length, width), F32), ((VECTORS, width), F32), ((width, 4 * width), BF16)],
        (
            x, first_low, *attend_grads, heads_full, attended, grad_branch,
            grad_middle, vectors, branch_sums, loss_sums, up_bias_part,
        ),
        positions,
        mib=40,
    )
    if square():
        mine, others = stacks
        mine_got = swap(others, 1)
        up_first = after(up_first, mine)
        up_second = [add_low(keep_ux[1], up_first[0][1]), add_low(keep_uy[1], up_first[1][1])]
        up_got = [swap(up_second[0], 4), swap(up_second[1], 2)]

        down_in = after(down_in, up_second)
        down_half = jnp.concatenate(add_each(down_narrow, down_in))
        (down_mid,) = hop([down_half], ACROSS)

        (mine_got,) = after([mine_got], down_half)
        both = add_low(mine, mine_got)
        side_first = [swap(both[2:4], 2), swap(both[6:8], 4)]

        up_got = after(up_got, both)
        up_narrow = [
            add_low(keep_ux[0], up_first[0][0], up_got[0]),
            add_low(keep_uy[0], up_first[1][0], up_got[1]),
        ]
        up_in = hop(up_narrow, INWARD)

        side_first = after(side_first, up_narrow)
        side_second = [add_low(both[1], side_first[0][1]), add_low(both[5], side_first[1][1])]
        side_got = [swap(side_second[0], 4), swap(side_second[1], 2)]

        (down_mid,) = after([down_mid], side_second)
        down_total = add_low(down_half, down_mid)
        (down_out,) = hop([down_total], OUTWARD)

        side_got = after(side_got, down_total)
        slab_narrow = [
            add_low(both[0], side_first[0][0], side_got[0]),
            add_low(both[4], side_first[1][0], side_got[1]),
        ]
        slab_in = hop(slab_narrow, INWARD)

        (came,) = after(up_in[:1], slab_narrow)
        up_half = [add_low(up_narrow[0], came)]
        up_mid = hop(up_half, ACROSS)

        (came,) = after(up_in[1:], up_half)
        up_half.append(add_low(up_narrow[1], came))
        up_mid += hop(up_half[1:], ACROSS)

        (came,) = after(up_mid[:1], up_half[1])
        up_total = [add_low(up_half[0], came)]
        up_out = hop(up_total, OUTWARD)

        (came,) = after(slab_in[:1], up_total)
        slab_half = [add_low(slab_narrow[0], came)]
        slab_mid = hop(slab_half, ACROSS)

        (came,) = after(up_mid[1:], slab_half)
        up_total.append(add_low(up_half[1], came))
        up_out += hop(up_total[1:], OUTWARD)

        (came,) = after(slab_in[1:], up_total[1])
        slab_half.append(add_low(slab_narrow[1], came))
        slab_mid += hop(slab_half[1:], ACROSS)

        gate = slab_half[1]
        slab_total, slab_out = [], []
        for at in range(2):
            (came,) = after([slab_mid[at]], gate)
            slab_total.append(add_low(slab_half[at], came))
            slab_out += hop(slab_total[-1:], OUTWARD)
            gate = slab_total[-1:]

        (down_out,) = after([down_out], gate)
        down_weight_sum = settle(down_total, down_out).astype(F32)
        up_out = after(up_out, down_weight_sum, slab_out[0])
        upper, lower = [settle(*pair) for pair in zip(up_total, up_out)]
        first = core == 0
        (up_weight_sum,) = call(
            functools.partial(join_kernel, hidden),
            [((rows, 2 * half), F32)],
            (jnp.where(first, upper, lower), swap(jnp.where(first, lower, upper), 1)),
            core_position,
        )
        slab_out = after(slab_out, upper, lower)
        scalar = pl.BlockSpec(memory_space=pltpu.SMEM)
        heads_sum, output_sum, short, loss_sum, token_count = call(
            functools.partial(settle_kernel, rows, hidden),
            [
                ((rows, 3 * width), F32), ((rows, width), F32), ((VECTORS, 2 * width), F32),
                ((1,), F32), ((1,), jnp.int32),
            ],
            (*slab_total, *slab_out),
            lax.axis_index("narrow").reshape(1).astype(jnp.int32),
            out_specs=[vmem, vmem, vmem, scalar, scalar],
        )
        vectors_sum = short[:, :rows]
        up_bias_grad = short[0, LANES : LANES + hidden]
        loss_sum, token_count = loss_sum.reshape(()), token_count.reshape(())
    else:
        down_weight_sum = collect_chips(down_parts[0].reshape(chips, hidden, width))
        down_weight_sum = sum_narrow(down_weight_sum).astype(F32)
        up_sum = sum_narrow(collect_chips(up_parts[0].reshape(chips, 2 * rows, half)))
        up_sum = up_sum.reshape(2, rows, chips, hidden)
        up_weight_sum = by_core(mine_of(up_sum, 0), swap(mine_of(up_sum, 0, 1), 1), 2)
        up_weight_sum = up_weight_sum.reshape(rows, 2 * half).astype(F32)
        short = short_sums.reshape(8, wide, rows).transpose(1, 0, 2).reshape(wide, 8 * rows)
        up_bias_rows = up_bias_part.reshape(chips, hidden)
        up_bias_rows = by_core(up_bias_rows, jnp.zeros_like(up_bias_rows), 1).reshape(wide, hidden)
        shared = jnp.broadcast_to(loss_sums[:1, :LANES], (wide, LANES))
        row = jnp.concatenate([short, up_bias_rows, shared], axis=1).astype(BF16)
        row = jnp.pad(row, ((0, 0), (0, 4 * width - row.shape[1])))
        slab = jnp.concatenate([attend_part.reshape(wide, rows, 4 * width), row[:, None]], axis=1)
        slab = sum_narrow(lax.psum_scatter(slab, "wide", scatter_dimension=0)).astype(F32)
        vectors_sum = slab[rows, : 8 * rows].reshape(8, rows)
        heads_sum, output_sum = slab[:rows, : 3 * width], slab[:rows, 3 * width :]
        up_bias_grad = slab[rows, 8 * rows : 8 * rows + hidden]
        loss_sum = jnp.sum(slab[rows, 8 * rows + hidden : 8 * rows + hidden + LANES])
        token_count = lax.psum(jnp.sum(loss_mask), ("narrow", "wide"))
    return (
        result_low[None],
        input_grad[None],
        vectors_sum[ATTEND_GAIN],
        vectors_sum[ATTEND_SHIFT],
        heads_sum,
        vectors_sum[QUERY_BIAS],
        vectors_sum[VALUE_BIAS],
        output_sum,
        vectors_sum[OUTPUT_BIAS],
        vectors_sum[FORWARD_GAIN],
        vectors_sum[FORWARD_SHIFT],
        up_weight_sum,
        up_bias_grad,
        down_weight_sum,
        vectors_sum[DOWN_BIAS],
        loss_sum,
        token_count,
    )


def solution(mesh):
    in_specs = (
        P(("narrow", "wide"), None, None),
        P(("narrow", "wide"), None),
        P(("narrow", "wide"), None),
        P(("narrow", "wide"), None),
        P(),
        P("wide"),
        P("wide"),
        P("wide", None),
        P("wide"),
        P("wide"),
        P("wide", None),
        P("wide"),
        P("wide"),
        P("wide"),
        P("wide", None),
        P("wide"),
        P("wide", None),
        P("wide"),
    )
    out_specs = (
        P(("narrow", "wide"), None, None),
        P(("narrow", "wide"), None, None),
        P("wide"),
        P("wide"),
        P("wide", None),
        P("wide"),
        P("wide"),
        P("wide", None),
        P("wide"),
        P("wide"),
        P("wide"),
        P("wide", None),
        P("wide"),
        P("wide", None),
        P("wide"),
        P(),
        P(),
    )
    return jax.shard_map(local, mesh=mesh, in_specs=in_specs, out_specs=out_specs, check_vma=False)
```

```python
import functools
import math

import jax
import jax.numpy as jnp
from jax import lax
from jax.experimental import pallas as pl
from jax.experimental.pallas import tpu as pltpu
from jax.sharding import PartitionSpec as P

HEADS = 20
HEAD_DIM = 32
LANES = 128
SUBLANES = 8
SEGMENTS = 8
REACH = 192
CHUNK = 256
ROWS = 128
SCALE = 1.0 / math.sqrt(HEAD_DIM)
SCALE2 = math.log2(math.e) * SCALE
F32 = jnp.float32
BF16 = jnp.bfloat16
VECTORS = 8
ATTEND_GAIN, ATTEND_SHIFT, QUERY_BIAS, VALUE_BIAS = 0, 1, 2, 3
OUTPUT_BIAS, FORWARD_GAIN, FORWARD_SHIFT, DOWN_BIAS = 4, 5, 6, 7


def nn(left, right):
    return lax.dot_general(left, right, (((1,), (0,)), ((), ())), preferred_element_type=F32)


def nt(left, right):
    return lax.dot_general(left, right, (((1,), (1,)), ((), ())), preferred_element_type=F32)


def tn(left, right):
    return lax.dot_general(left, right, (((0,), (0,)), ((), ())), preferred_element_type=F32)


def call(kernel, outs, args, positions=None, grid=None, in_specs=None, out_specs=None, scratch=(),
         mib=16, aliases=None):
    whole = pl.BlockSpec(memory_space=pltpu.VMEM)
    in_specs = in_specs or [whole] * len(args)
    args = [
        pltpu.with_memory_space_constraint(arg, pltpu.HBM)
        if spec.memory_space == pltpu.HBM
        else arg
        for arg, spec in zip(args, in_specs)
    ]
    out_specs = out_specs or [whole] * len(outs)
    shapes = [
        pltpu.HBM(*out) if spec.memory_space == pltpu.HBM else jax.ShapeDtypeStruct(*out)
        for out, spec in zip(outs, out_specs)
    ]
    extra = [] if positions is None else [positions]
    return pl.pallas_call(
        kernel,
        out_shape=shapes,
        grid_spec=pltpu.PrefetchScalarGridSpec(
            num_scalar_prefetch=len(extra),
            grid=grid or (),
            in_specs=in_specs,
            out_specs=out_specs,
            scratch_shapes=list(scratch),
        ),
        compiler_params=pltpu.CompilerParams(vmem_limit_bytes=mib * 1024 * 1024),
        input_output_aliases=aliases or {},
        cost_estimate=pl.CostEstimate(flops=1, bytes_accessed=1, transcendentals=0),
    )(*extra, *args)


def unit(values):
    centred = values - jnp.mean(values, axis=-1, keepdims=True)
    spread = jnp.mean(centred * centred, axis=-1, keepdims=True)
    inverse = lax.rsqrt(spread + 1e-05)
    return centred * inverse, inverse


def unit_back(grad, normal, inverse, gain):
    scaled = grad * gain
    mean = jnp.mean(scaled, axis=-1, keepdims=True)
    along = jnp.mean(scaled * normal, axis=-1, keepdims=True)
    return inverse * (scaled - mean - normal * along)


def spans(length):
    chunk = min(CHUNK, length)
    return [
        (at, at + chunk, max(0, at - REACH), min(length, at + chunk + REACH))
        for at in range(0, length, chunk)
    ]


def split3(values):
    first = values.astype(BF16).astype(F32)
    rest = values - first
    second = rest.astype(BF16).astype(F32)
    return [first, second, rest - second]


def key_marks(segment_row):
    at = lax.broadcasted_iota(jnp.int32, (LANES, segment_row.shape[1]), 0)
    ones = (at >= SEGMENTS) & (at < SEGMENTS + 3)
    return jnp.where((at == segment_row) | ones, 1.0, 0.0).astype(BF16).T


def query_marks(segment_row):
    row = lax.broadcasted_iota(jnp.int32, (SEGMENTS, segment_row.shape[1]), 0)
    return jnp.where(row == segment_row, 0.0, -1e30)


def place(rows, head, marks):
    count = rows.shape[1]
    parts = [rows, marks, jnp.zeros((LANES - marks.shape[0], count), BF16)]
    if head < LANES // HEAD_DIM - 1:
        parts.insert(1, jnp.zeros((LANES - HEAD_DIM * (head + 1), count), BF16))
    if head:
        parts.insert(0, jnp.zeros((HEAD_DIM * head, count), BF16))
    return jnp.concatenate(parts, axis=0)


def attend_kernel(row_ref, q_ref, k_ref, v_ref, out_ref, across_ref, lse_ref, marks_ref):
    @pl.when(pl.program_id(0) == 0)
    def _():
        marks_ref[...] = key_marks(row_ref[...])

    length = q_ref.shape[0]
    heads = LANES // HEAD_DIM
    queries = q_ref[...].T
    values = v_ref[...].T
    keys = jnp.concatenate([k_ref[...], marks_ref[...]], axis=1)
    blank = jnp.zeros((SUBLANES, length), F32)
    marks = jnp.concatenate([query_marks(row_ref[...]), blank], axis=0).astype(BF16)
    ones = jnp.ones((SUBLANES, length), BF16)
    bodies = [(head, span) for head in range(heads) for span in spans(length)]

    def rows(head):
        return slice(HEAD_DIM * head, HEAD_DIM * (head + 1))

    summed = [jnp.concatenate([values[rows(head)], ones], axis=0) for head in range(heads)]

    def score(head, span):
        begin, end, low, high = span
        return nn(keys[low:high], place(queries[rows(head), begin:end], head, marks[:, begin:end]))

    def finish(head, span, top, probs):
        begin, end, low, high = span
        out = nn(summed[head][:, low:high], probs)
        total = out[HEAD_DIM : HEAD_DIM + 1]
        across_ref[rows(head), begin:end] = out[:HEAD_DIM] * (1.0 / total)
        lse_ref[head : head + 1, begin:end] = (top + jnp.log2(total)) * (1.0 / SCALE2)

    scores = [score(*body) for body in bodies[:2]]
    waiting = None
    for at, body in enumerate(bodies):
        current = scores.pop(0)
        if at + 2 < len(bodies):
            scores.append(score(*bodies[at + 2]))
        top = jnp.max(current, axis=0, keepdims=True) * SCALE2
        probs = jnp.exp2(current * SCALE2 - top).astype(BF16)
        if waiting is not None:
            finish(*waiting)
        waiting = (*body, top, probs)
    finish(*waiting)
    lse_ref[heads:, :] = jnp.zeros((SUBLANES - heads, length), F32)
    out_ref[...] = across_ref[...].T.astype(BF16)


def attend_back_kernel(
    row_ref, q_ref, k_ref, v_ref, grad_ref, across_ref, lse_ref,
    gq_ref, gk_ref, gv_ref, marks_ref, turned_ref,
):
    @pl.when(pl.program_id(0) == 0)
    def _():
        marks_ref[...] = key_marks(row_ref[...])

    length = q_ref.shape[0]
    grad = grad_ref[...]
    queries = q_ref[...].T
    turned_keys = k_ref[...].T
    grads = grad.T
    keys = jnp.concatenate([k_ref[...], marks_ref[...]], axis=1)
    values = jnp.concatenate([v_ref[...], marks_ref[...]], axis=1)
    low_marks = query_marks(row_ref[...])
    blank = jnp.zeros((SUBLANES, length), F32)
    lane = lax.broadcasted_iota(jnp.int32, (1, LANES), 1) // HEAD_DIM
    heads = []
    for head in range(LANES // HEAD_DIM):
        rows = slice(HEAD_DIM * head, HEAD_DIM * (head + 1))
        inner = jnp.sum(grads[rows].astype(F32) * across_ref[rows, :], axis=0, keepdims=True)
        lse = lse_ref[head : head + 1, :]
        score_marks = jnp.concatenate([low_marks, *split3(-lse), blank[:5]], axis=0)
        inner_marks = jnp.concatenate([blank, *split3(-inner), blank[:5]], axis=0)
        zero = jnp.zeros_like(grad)
        heads.append(
            (
                rows,
                score_marks.astype(BF16),
                inner_marks.astype(BF16),
                jnp.where(lane == head, q_ref[...], zero),
                jnp.where(lane == head, grad, zero),
            )
        )
    bodies = [
        (head, at, span) for head in range(len(heads)) for at, span in enumerate(spans(length))
    ]
    sums = [[None, None] for _ in spans(length)]

    def pair(head, at, span):
        begin, end, low, high = span
        rows, score_marks, inner_marks, _, _ = heads[head]
        return (
            nn(keys[low:high], place(queries[rows, begin:end], head, score_marks[:, begin:end])),
            nn(values[low:high], place(grads[rows, begin:end], head, inner_marks[:, begin:end])),
        )

    def finish(head, at, span, score_grads, probs):
        begin, end, low, high = span
        rows, _, _, own_queries, own_grads = heads[head]
        for which, (left, right) in enumerate(
            ((score_grads, own_queries[begin:end]), (probs, own_grads[begin:end]))
        ):
            part = nn(left, right)
            sums[at][which] = part if sums[at][which] is None else sums[at][which] + part
        turned_ref[rows, begin:end] = nn(turned_keys[rows, low:high], score_grads)

    ahead = [pair(*bodies[0])]
    waiting = None
    for at, body in enumerate(bodies):
        scores, differences = ahead.pop(0)
        if at + 1 < len(bodies):
            ahead.append(pair(*bodies[at + 1]))
        probs = jnp.exp2(scores * SCALE2)
        score_grads = (probs * differences).astype(BF16)
        if waiting is not None:
            finish(*waiting)
        waiting = (*body, score_grads, probs.astype(BF16))
    finish(*waiting)
    gq_ref[...] = (turned_ref[...].T * SCALE).astype(BF16)
    for which, (ref, factor) in enumerate(((gk_ref, SCALE), (gv_ref, 1.0))):
        total = None
        for at, (_, _, low, high) in enumerate(spans(length)):
            parts = [sums[at][which]]
            if low:
                parts.insert(0, jnp.zeros((low, LANES), F32))
            if high < length:
                parts.append(jnp.zeros((length - high, LANES), F32))
            part = jnp.concatenate(parts, axis=0) if len(parts) > 1 else parts[0]
            total = part if total is None else total + part
        ref[...] = (total * factor).astype(BF16)


def attention_specs(length, width, begin=0):
    tiles = width // LANES

    def tile(at, begin=begin):
        return pl.BlockSpec((length, LANES), lambda i: (0, at + begin + i))

    return (
        tiles,
        tile,
        pl.BlockSpec((1, length), lambda i: (0, 0)),
        pl.BlockSpec((LANES, length), lambda i: (begin + i, 0)),
        pl.BlockSpec((SUBLANES, length), lambda i: (begin + i, 0)),
    )


def attend(joined, row):
    length = joined.shape[0]
    width = joined.shape[1] // 3
    tiles, tile, row_spec, across_spec, lse_spec = attention_specs(length, width)
    return call(
        attend_kernel,
        [((length, width), BF16), ((width, length), F32), ((SUBLANES * tiles, length), F32)],
        (row, joined, joined, joined),
        grid=(tiles,),
        in_specs=[row_spec, tile(0), tile(tiles), tile(2 * tiles)],
        out_specs=[tile(0), across_spec, lse_spec],
        scratch=[pltpu.VMEM((length, LANES), BF16)],
    )


def attend_back(joined, row, grad, across, lse, begin=0, end=None):
    length = joined.shape[0]
    width = joined.shape[1] // 3
    specs = attention_specs(length, width, begin)
    tiles, tile, row_spec, across_spec, lse_spec = specs
    count = (end or tiles) - begin
    return call(
        attend_back_kernel,
        [((length, count * LANES), BF16)] * 3,
        (row, joined, joined, joined, grad, across, lse),
        grid=(count,),
        in_specs=[row_spec, tile(0), tile(tiles), tile(2 * tiles), tile(0), across_spec, lse_spec],
        out_specs=[tile(0, 0)] * 3,
        scratch=[pltpu.VMEM((length, LANES), BF16), pltpu.VMEM((LANES, length), F32)],
        mib=24,
    )


def slab_kernel(heads_far, out_far, short_ref, up_ref, slab_ref, sems):
    rows = heads_far.shape[0]
    width = out_far.shape[1]
    copies = [
        pltpu.make_async_copy(far, slab_ref.at[pl.ds(0, rows), here], sems.at[at])
        for at, (far, here) in enumerate(
            ((heads_far, pl.ds(0, 3 * width)), (out_far, pl.ds(3 * width, width)))
        )
    ]
    for copy in copies:
        copy.start()
    slab_ref[rows:, :] = jnp.zeros((VECTORS, 4 * width), BF16)
    slab_ref[rows:, :rows] = short_ref[...]
    slab_ref[rows:, LANES : LANES + up_ref.shape[1]] = jnp.broadcast_to(
        up_ref[...], (VECTORS, up_ref.shape[1])
    )
    for copy in copies:
        copy.wait()


def project_kernel(count, rows, hidden, position_ref, x_far, *refs):
    slabs, refs = refs[:count], refs[count:]
    length, width = x_far.shape
    x_ref = x_far
    if count:
        low_ref, joined_ref, heads_ref, out_ref, vector_ref, bias_ref, *refs = refs
        short_ref, x_ref, sems, x_sem = refs
        copies = [pltpu.make_async_copy(x_far, x_ref, x_sem)]
        copies[0].start()
        for at, slab in enumerate(slabs):
            begin = pl.multiple_of(position_ref[at] * rows, SUBLANES)
            here = pl.ds(begin, rows)
            for which, (source, target) in enumerate(
                (
                    (slab.at[pl.ds(0, rows), pl.ds(0, 3 * width)], heads_ref.at[here]),
                    (slab.at[pl.ds(0, rows), pl.ds(3 * width, width)], out_ref.at[here]),
                    (slab.at[pl.ds(rows, VECTORS), pl.ds(0, LANES + hidden)], short_ref.at[at]),
                )
            ):
                copy = pltpu.make_async_copy(source, target, sems.at[at, which])
                copy.start()
                copies.append(copy)
    else:
        heads_ref, vector_ref, low_ref, joined_ref = refs
    if count:
        for copy in copies:
            copy.wait()
        vectors = jnp.zeros((VECTORS, width), F32)
        for at in range(count):
            begin = position_ref[at] * rows
            short = short_ref[at, :, :LANES].astype(F32)
            lane = lax.broadcasted_iota(jnp.int32, short.shape, 1)
            short = jnp.where(lane < rows, short, 0.0)
            short = jnp.concatenate([short, jnp.zeros((VECTORS, width - LANES), F32)], axis=1)
            vectors = vectors + pltpu.roll(short, begin, 1)
            if at < count // 2:
                begin = pl.multiple_of(lax.div(position_ref[at], 2) * hidden, LANES)
                bias_ref[:, pl.ds(begin, hidden)] = short_ref[at, :, LANES:].astype(F32)
        vector_ref[...] = vectors
    zero = jnp.zeros((1, width), F32)
    vector = vector_ref[...]
    bias = jnp.concatenate(
        [vector[QUERY_BIAS : QUERY_BIAS + 1], zero, vector[VALUE_BIAS : VALUE_BIAS + 1]], axis=1
    )
    for at in range(0, length, ROWS):
        normal, _ = unit(x_ref[at : at + ROWS, :].astype(F32))
        low_ref[at : at + ROWS, :] = (
            normal * vector[ATTEND_GAIN : ATTEND_GAIN + 1]
            + vector[ATTEND_SHIFT : ATTEND_SHIFT + 1]
        ).astype(BF16)
    for at in range(0, 3 * width, width):
        here = slice(at, at + width)
        joined_ref[:, here] = (nn(low_ref[...], heads_ref[:, here]) + bias[:, here]).astype(BF16)


def middle_kernel(x_ref, attended_ref, out_ref, vector_ref, middle_ref, low_ref):
    vector = vector_ref[...]
    for at in range(0, x_ref.shape[0], ROWS):
        here = slice(at, at + ROWS)
        middle = (
            x_ref[here, :].astype(F32)
            + nn(attended_ref[here, :], out_ref[...])
            + vector[OUTPUT_BIAS : OUTPUT_BIAS + 1]
        )
        middle_ref[here, :] = middle
        normal, _ = unit(middle)
        low_ref[here, :] = (
            normal * vector[FORWARD_GAIN : FORWARD_GAIN + 1]
            + vector[FORWARD_SHIFT : FORWARD_SHIFT + 1]
        ).astype(BF16)


def up_kernel(position_ref, own_ref, other_ref, bias_ref, *refs):
    parts, (act_ref, slope_ref, full_ref) = refs[: len(refs) - 3], refs[len(refs) - 3 :]
    for at, part in enumerate(parts):
        rows = part.shape[0]
        begin = pl.multiple_of(position_ref[at] * rows, SUBLANES)
        full_ref[pl.ds(begin, rows), :] = part[...]
    weight = full_ref[...]
    bias = bias_ref[:1, :]
    length = own_ref.shape[0]
    for which, ref in enumerate((own_ref, other_ref)):
        for at in range(0, length, ROWS):
            upward = nn(ref[at : at + ROWS, :], weight) + bias
            share = 0.5 + 0.5 * lax.erf(upward * math.sqrt(0.5))
            bell = jnp.exp2((upward * upward) * (-0.5 * math.log2(math.e)))
            here = slice(which * length + at, which * length + at + ROWS)
            act_ref[here, :] = (upward * share).astype(BF16)
            slope = share + upward * (bell * (1.0 / math.sqrt(2.0 * math.pi)))
            slope_ref[here, :] = slope.astype(BF16)


def column_specs(half, block):
    block = min(block, half)

    def column(height):
        return pl.BlockSpec((height, block), lambda i, at: (0, i))

    return half // block, block, column


def whole_spec(shape):
    return pl.BlockSpec(shape, lambda i, at: (0,) * len(shape))


def up_project(own, other, bias, parts, positions, hidden):
    length, width = own.shape
    half = bias.shape[1]
    paired = parts[0].shape[1] > half
    steps, block, column = column_specs(half, hidden if paired else 512)
    whole = whole_spec((length, width))

    def part_spec(part):
        if paired:
            return pl.BlockSpec((part.shape[0], block), lambda i, at: (0, 2 * i + at[len(parts)]))
        return column(part.shape[0])

    return call(
        up_kernel,
        [((2 * length, half), BF16), ((2 * length, half), BF16), ((width, half), BF16)],
        (own, other, bias, *parts),
        positions,
        grid=(steps,),
        in_specs=[whole, whole, column(bias.shape[0])] + [part_spec(part) for part in parts],
        out_specs=[column(2 * length), column(2 * length), column(width)],
    )


def down_kernel(position_ref, act_ref, *refs):
    parts, (own_ref, other_ref, full_ref) = refs[: len(refs) - 3], refs[len(refs) - 3 :]
    length = own_ref.shape[0]
    for at, part in enumerate(parts):
        rows = part.shape[0]
        begin = pl.multiple_of(position_ref[at] * rows, SUBLANES)
        full_ref[pl.ds(begin, rows), :] = part[...]
    for which, ref in enumerate((own_ref, other_ref)):
        here = slice(which * length, (which + 1) * length)
        ref[...] = nn(act_ref[here, :], full_ref[...]).astype(ref.dtype)


def down_project(act, parts, positions):
    length = act.shape[0] // 2
    half = act.shape[1]
    width = parts[0].shape[1]
    return call(
        down_kernel,
        [((length, width), F32), ((length, width), BF16), ((half, width), BF16)],
        (act, *parts),
        positions,
        mib=20,
    )


def down_near_kernel(position_ref, act_ref, *refs):
    parts, (sum_ref, full_ref) = refs[:-2], refs[-2:]
    size = parts[0].shape[0]
    for at, part in enumerate(parts):
        rows = part.shape[0]
        begin = pl.multiple_of(position_ref[at] * rows, SUBLANES)
        full_ref[pl.ds(begin, rows), :] = part[...]
    chips = [position_ref[0], lax.div(position_ref[1], 2), lax.div(position_ref[3], 2)]
    length = act_ref.shape[0] // 2
    for which in range(2):
        here = slice(which * length, (which + 1) * length)
        total = None
        for chip in chips:
            units = pl.ds(pl.multiple_of(chip * size, LANES), size)
            part = nn(act_ref[here, units], full_ref[units, :])
            total = part if total is None else total + part
        sum_ref[here, :] = total


def down_far_kernel(position_ref, act_ref, sum_ref, upper_ref, lower_ref, _, own_ref, other_ref, full_ref):
    rows, length = upper_ref.shape[0], own_ref.shape[0]
    size = 2 * rows
    units = pl.ds(pl.multiple_of(lax.div(position_ref[5], 2) * size, LANES), size)
    weight = jnp.concatenate([upper_ref[...], lower_ref[...]], axis=0)
    full_ref[units, :] = weight
    for which, ref in enumerate((own_ref, other_ref)):
        here = slice(which * length, (which + 1) * length)
        ref[...] = (sum_ref[here, :] + nn(act_ref[here, units], weight)).astype(ref.dtype)


def down_project_square(act, near, far, positions):
    length, half, width = act.shape[0] // 2, act.shape[1], near[0].shape[1]
    total, full = call(
        down_near_kernel,
        [((2 * length, width), F32), ((half, width), BF16)],
        (act, *near),
        positions,
        mib=24,
    )
    far = far(total)
    return call(
        down_far_kernel,
        [((length, width), F32), ((length, width), BF16), ((half, width), BF16)],
        (act, total, *far, full),
        positions,
        mib=24,
        aliases={5: 2},
    )


def loss_kernel(
    middle_ref, own_ref, got_ref, vector_ref, readout_ref, target_ref, mask_ref,
    low_ref, down_ref, grad_ref, sums_ref,
):
    result = (
        middle_ref[...]
        + (own_ref[...] + got_ref[...].astype(F32))
        + vector_ref[DOWN_BIAS : DOWN_BIAS + 1, :]
    ).astype(BF16)
    low_ref[...] = result
    logits = nt(readout_ref[...], result)
    length = logits.shape[1]
    top = jnp.max(logits, axis=0, keepdims=True)
    shifted = jnp.exp(logits - top)
    total = jnp.sum(shifted, axis=0, keepdims=True)
    onehot = lax.broadcasted_iota(jnp.int32, logits.shape, 0) == target_ref[...]
    picked = jnp.sum(jnp.where(onehot, logits, 0.0), axis=0, keepdims=True)
    weight = mask_ref[...].astype(F32)
    loss = (top + jnp.log(total) - picked) * weight
    loss_lanes = jnp.zeros((1, LANES), F32)
    count_lanes = jnp.zeros((1, LANES), F32)
    for at in range(0, length, LANES):
        loss_lanes = loss_lanes + loss[:, at : at + LANES]
        count_lanes = count_lanes + weight[:, at : at + LANES]
    lanes = jnp.concatenate([loss_lanes, count_lanes], axis=0)
    lanes = jnp.concatenate([lanes, jnp.zeros((2, result.shape[1] - LANES), F32)], axis=1)
    grad_logits = (weight * (shifted / total - onehot.astype(F32))).astype(BF16)
    grad_ref[...] = grad_logits
    low = tn(grad_logits, readout_ref[...]).astype(BF16)
    down_ref[...] = low
    sums = jnp.sum(low.astype(F32), axis=0, keepdims=True)
    blank = jnp.zeros((SUBLANES - 3, result.shape[1]), F32)
    sums_ref[...] = jnp.concatenate([lanes, sums, blank], axis=0)


def down_grad_kernel(chips, position_ref, act_ref, own_ref, other_ref, *out_refs):
    length = own_ref.shape[0]
    hidden = act_ref.shape[1] // chips
    for offset in range(chips):
        if len(out_refs) == 1:
            begin = offset * hidden
        else:
            begin = pl.multiple_of((position_ref[0] ^ offset) * hidden, LANES)
        here = pl.ds(begin, hidden)
        part = tn(act_ref[:length, here], own_ref[...]) + tn(act_ref[length:, here], other_ref[...])
        part = part.astype(BF16)
        if len(out_refs) == 1:
            out_refs[0][begin : begin + hidden, :] = part
            continue
        keep_x, send_x, keep_y, send_y = out_refs
        half = hidden // 2
        (send_x if offset % 2 else keep_x)[offset // 2, :, :] = part[:half]
        (send_y if offset // 2 else keep_y)[offset % 2, :, :] = part[half:]


def down_grad(act, own, other, chips, position):
    half = act.shape[1]
    width = own.shape[1]
    if square():
        outs = [((2, half // chips // 2, width), BF16)] * 4
    else:
        outs = [((half, width), BF16)]
    return call(
        functools.partial(down_grad_kernel, chips), outs, (act, own, other), position, mib=20
    )


def up_grad_kernel(
    rows, position_ref, own_ref, other_ref, slope_ref, second_ref, second_other_ref, down_ref,
    up_ref, bias_ref, *refs,
):
    out_refs, part_ref = refs[:-1], refs[-1]
    length = own_ref.shape[0]
    total = None
    grads = []
    for which, ref in enumerate((own_ref, other_ref)):
        for at in range(0, length, 2 * ROWS):
            here = slice(which * length + at, which * length + at + 2 * ROWS)
            grad = nt(ref[at : at + 2 * ROWS, :], down_ref[...]) * slope_ref[here, :].astype(F32)
            low = grad.astype(BF16)
            up_ref[here, :] = low
            part = jnp.sum(low.astype(F32), axis=0, keepdims=True)
            total = part if total is None else total + part
    bias_ref[...] = total
    part = tn(second_ref[...], up_ref[:length, :]) + tn(second_other_ref[...], up_ref[length:, :])
    if len(out_refs) == 1:
        out_refs[0][...] = part.astype(BF16)
        return
    part_ref[...] = part
    keep_x, send_x, keep_y, send_y = out_refs
    for offset in range(4):
        begin = pl.multiple_of((position_ref[0] ^ offset) * (2 * rows), SUBLANES)
        upper = part_ref[pl.ds(begin, rows), :].astype(BF16)
        lower = part_ref[pl.ds(begin + rows, rows), :].astype(BF16)
        (send_x if offset % 2 else keep_x)[offset // 2, :, :] = upper
        (send_y if offset // 2 else keep_y)[offset % 2, :, :] = lower


def up_grad(own, other, slope, second, second_other, down_full, rows, position):
    length, width = own.shape
    half = slope.shape[1]
    steps, block, column = column_specs(half, 512)
    whole = whole_spec((length, width))
    if square():
        outs = [((2, rows, half), BF16)] * 4
        specs = [pl.BlockSpec((2, rows, block), lambda i, at: (0, 0, i))] * 4
    else:
        outs = [((width, half), BF16)]
        specs = [column(width)]
    return call(
        functools.partial(up_grad_kernel, rows),
        [((2 * length, half), BF16), ((1, half), F32), *outs],
        (own, other, slope, second, second_other, down_full),
        position,
        grid=(steps,),
        in_specs=[
            whole, whole, column(2 * length), whole, whole,
            pl.BlockSpec((block, width), lambda i, at: (i, 0)),
        ],
        out_specs=[column(2 * length), column(1), *specs],
        scratch=[pltpu.VMEM((width, block), F32)],
        mib=20,
    )


def inward_kernel(grad_ref, up_ref, own_far, other_ref, own_ref, sem):
    length = other_ref.shape[0]
    own_ref[...] = nt(grad_ref[:length, :], up_ref[...])
    copy = pltpu.make_async_copy(own_ref, own_far, sem)
    copy.start()
    other_ref[...] = nt(grad_ref[length:, :], up_ref[...]).astype(BF16)
    copy.wait()


def join_kernel(hidden, position_ref, mine_ref, other_ref, out_ref):
    for at in range(mine_ref.shape[1] // hidden):
        here = slice(hidden * at, hidden * (at + 1))
        for core, ref in enumerate((mine_ref, other_ref)):
            begin = (2 * at + (position_ref[0] + core) % 2) * hidden
            out_ref[:, pl.ds(pl.multiple_of(begin, LANES), hidden)] = ref[:, here].astype(F32)


def branch_kernel(
    got_ref, own_far, middle_far, logits_ref, classes_ref, out_ref, vector_ref,
    grad_ref, branch_ref, attended_ref, sums_ref, own_ref, middle_ref, sems,
):
    width = own_ref.shape[1]
    blocks = range(0, own_ref.shape[0], ROWS)
    copies = []
    for at in blocks:
        here = pl.ds(at, ROWS)
        copies.append(
            [
                pltpu.make_async_copy(far.at[here], ref.at[here], sems.at[at // ROWS, which])
                for which, (far, ref) in enumerate(((own_far, own_ref), (middle_far, middle_ref)))
            ]
        )
        for copy in copies[-1]:
            copy.start()
    gain = vector_ref[FORWARD_GAIN : FORWARD_GAIN + 1, :]
    sums = [jnp.zeros((1, width), F32) for _ in range(3)]
    for at in blocks:
        for copy in copies[at // ROWS]:
            copy.wait()
        here = slice(at, at + ROWS)
        grad = own_ref[here, :] + got_ref[here, :].astype(F32)
        normal, inverse = unit(middle_ref[here, :])
        result = tn(logits_ref[:, here], classes_ref[...])
        middle = result + unit_back(grad, normal, inverse, gain)
        grad_ref[here, :] = middle
        branch = middle.astype(BF16)
        branch_ref[here, :] = branch
        attended_ref[here, :] = nt(branch, out_ref[...]).astype(BF16)
        for which, part in enumerate((grad * normal, grad, branch.astype(F32))):
            sums[which] = sums[which] + jnp.sum(part, axis=0, keepdims=True)
    blank = jnp.zeros((SUBLANES - 3, width), F32)
    sums_ref[...] = jnp.concatenate([*sums, blank], axis=0)


def last_kernel(count, rows, hidden, pieces, position_ref, x_ref, low_ref, *refs):
    grad_refs, refs = refs[: 3 * pieces], refs[3 * pieces :]
    heads_ref, attended_ref, branch_ref, grad_ref, vector_ref, *refs = refs
    sums_ref, loss_ref, up_ref, *refs = refs
    stacks, (input_ref, vectors_ref, full_ref) = refs[:-3], refs[-3:]
    width = x_ref.shape[1]

    def grads(which, here):
        parts = [ref[here, :] for ref in grad_refs[which::3]]
        return jnp.concatenate(parts, axis=1) if pieces > 1 else parts[0]

    for at in range(3):
        part = tn(low_ref[...], grads(at, slice(None)))
        full_ref[:, width * at : width * (at + 1)] = part.astype(BF16)
    full_ref[:, 3 * width :] = tn(attended_ref[...], branch_ref[...]).astype(BF16)
    gain = vector_ref[ATTEND_GAIN : ATTEND_GAIN + 1, :]

    def block(at, sums):
        here = pl.ds(pl.multiple_of(at * ROWS, ROWS), ROWS)
        grad_query, grad_key, grad_value = [grads(which, here) for which in range(3)]
        grad = (
            nt(grad_query, heads_ref[:, :width])
            + nt(grad_key, heads_ref[:, width : 2 * width])
            + nt(grad_value, heads_ref[:, 2 * width :])
        )
        normal, inverse = unit(x_ref[here, :].astype(F32))
        input_ref[here, :] = grad_ref[here, :] + unit_back(grad, normal, inverse, gain)
        parts = (grad * normal, grad, grad_query.astype(F32), grad_value.astype(F32))
        return tuple(
            total + jnp.sum(part, axis=0, keepdims=True) for total, part in zip(sums, parts)
        )

    zero = jnp.zeros((1, width), F32)
    sums = lax.fori_loop(0, x_ref.shape[0] // ROWS, block, (zero,) * 4)
    vectors = jnp.concatenate(
        [*sums, sums_ref[2:3, :], sums_ref[0:1, :], sums_ref[1:2, :], loss_ref[2:3, :]], axis=0
    )
    vectors_ref[...] = vectors
    blank = jnp.zeros((VECTORS - 1, hidden), F32)
    lanes = jnp.concatenate([loss_ref[:2, :LANES], jnp.zeros((VECTORS - 2, LANES), F32)], axis=0)
    for which, stack in enumerate(stacks):

        def slab(step, carry, which=which, stack=stack):
            place_at = position_ref[which * (count // 2) + step]
            begin = pl.multiple_of(place_at * rows, SUBLANES)
            short = pltpu.roll(vectors, width - begin, 1)[:, :LANES]
            if which == 0:
                hidden_at = pl.multiple_of(lax.div(place_at, 2) * hidden, LANES)
                bias = jnp.concatenate([up_ref[:, pl.ds(hidden_at, hidden)], blank], axis=0)
            else:
                bias = jnp.zeros((VECTORS, hidden), F32)
            row = jnp.concatenate([short, bias, lanes], axis=1).astype(BF16)
            pad = jnp.zeros((VECTORS, 4 * width - row.shape[1]), BF16)
            row = jnp.concatenate([row, pad], axis=1)
            picks = (2 * (step % 2) + step // 2, 4 + step)
            for side, pick in enumerate(picks):
                here = slice(2 * width * side, 2 * width * (side + 1))
                stack[pick, :rows, :] = full_ref[pl.ds(begin, rows), here]
                stack[pick, rows:, :] = row[:, here]
            return carry

        lax.fori_loop(0, count // 2, slab, 0)


def settle_kernel(rows, hidden, place_ref, *refs):
    totals, outers, refs = refs[:2], refs[2:4], refs[4:]
    heads_ref, out_ref, short_ref, loss_ref, count_ref = refs
    width = out_ref.shape[1]
    inner = (place_ref[0] == 1) | (place_ref[0] == 2)
    left, right = [
        jnp.where(inner, total[...], outer[...]).astype(F32) for total, outer in zip(totals, outers)
    ]
    heads_ref[:, : 2 * width] = left[:rows]
    heads_ref[:, 2 * width :] = right[:rows, :width]
    out_ref[...] = right[:rows, width:]
    short_ref[...] = left[rows:]
    lanes = left[rows:, LANES + hidden : 2 * LANES + hidden]
    loss_ref[0] = jnp.sum(lanes[0:1])
    count_ref[0] = jnp.sum(lanes[1:2]).astype(jnp.int32)


def swap(values, bit):
    return lax.ppermute(values, "wide", [(i, i ^ bit) for i in range(lax.axis_size("wide"))])


def same_core_groups():
    chips = lax.axis_size("wide") // 2
    return [[2 * chip + core for chip in range(chips)] for core in range(2)]


def square():
    return lax.axis_size("wide") == 8


def spread_chips(shard):
    return lax.all_gather(shard, "wide", axis=0, axis_index_groups=same_core_groups())


def add_low(*parts):
    return sum(part.astype(F32) for part in parts).astype(BF16)


def collect_chips(parts):
    return lax.psum_scatter(
        parts, "wide", scatter_dimension=0, axis_index_groups=same_core_groups()
    )


def after(values, *gates):
    leaves, tree = jax.tree.flatten(values)
    held = lax.optimization_barrier((*leaves, *jax.tree.leaves(gates)))
    return jax.tree.unflatten(tree, held[: len(leaves)])


INWARD, ACROSS, OUTWARD = [(0, 1), (3, 2)], [(1, 2), (2, 1)], [(1, 0), (2, 3)]


def hop(parts, pairs):
    return [lax.ppermute(part, "narrow", pairs) for part in parts]


def add_each(left, right):
    return [add_low(a, b) for a, b in zip(left, right)]


def settle(total, outer):
    place_at = lax.axis_index("narrow")
    return jnp.where((place_at == 1) | (place_at == 2), total, outer)


def sum_narrow(shard):
    if lax.axis_size("narrow") != 4:
        return lax.psum(shard, "narrow")
    half = add_low(shard, *hop([shard], INWARD))
    total = add_low(half, *hop([half], ACROSS))
    return settle(total, *hop([total], OUTWARD))


def local(
    layer_input, segments, targets, loss_mask, readout,
    attend_gain, attend_shift, heads_weight, query_bias, value_bias, output_weight, output_bias,
    forward_gain, forward_shift, up_weight, up_bias, down_weight, down_bias,
):
    length = layer_input.shape[1]
    width = layer_input.shape[2]
    wide = lax.axis_size("wide")
    chips = wide // 2
    core = lax.axis_index("wide") % 2
    chip = lax.axis_index("wide") // 2
    rows = heads_weight.shape[0]
    hidden = up_bias.shape[0]
    half = chips * hidden
    x = layer_input[0]
    classes = readout.T
    vmem = pl.BlockSpec(memory_space=pltpu.VMEM)
    far_away = pl.BlockSpec(memory_space=pltpu.HBM)

    def by_core(mine, other, axis):
        return jnp.where(
            core == 0, jnp.stack([mine, other], axis), jnp.stack([other, mine], axis)
        )

    def mine_of(values, axis, flip=0):
        return lax.dynamic_index_in_dim(values, core ^ flip, axis, keepdims=False)

    short = jnp.stack(
        [
            attend_gain, attend_shift, query_bias, value_bias,
            output_bias, forward_gain, forward_shift, down_bias,
        ]
    )
    core_position = core.reshape(1).astype(jnp.int32)
    chip_position = chip.reshape(1).astype(jnp.int32)
    if square():
        offsets = jnp.arange(4, dtype=jnp.int32)
        (slab,) = call(
            slab_kernel,
            [((rows + VECTORS, 4 * width), BF16)],
            (heads_weight, output_weight, short, up_bias[None]),
            in_specs=[far_away, far_away, vmem, vmem],
            scratch=[pltpu.SemaphoreType.DMA((2,))],
        )
        near_x, near_y, far = swap(slab, 2), swap(slab, 4), swap(slab, 6)
        swapped = swap(slab, 1)
        devices = 2 * (chip ^ offsets) + core
        positions = jnp.concatenate([devices, devices ^ 1]).astype(jnp.int32)
        up_weight, positions = after([up_weight, positions], near_x, swapped)
        up_x, up_y = swap(up_weight, 2), swap(up_weight, 4)
        swapped_x = swap(near_x, 1)
        near_y, far = after([near_y, far], swapped_x)
        slabs = [slab, near_x, near_y, far, swapped, swapped_x, swap(near_y, 1), swap(far, 1)]
        first_low, joined, heads_full, output_full, vectors, up_bias_half = call(
            functools.partial(project_kernel, len(slabs), rows, hidden),
            [
                ((length, width), BF16), ((length, 3 * width), BF16), ((width, 3 * width), BF16),
                ((width, width), BF16), ((VECTORS, width), F32), ((VECTORS, half), F32),
            ],
            (x, *slabs),
            positions,
            in_specs=[far_away] * (1 + len(slabs)),
            scratch=[
                pltpu.VMEM((len(slabs), VECTORS, LANES + hidden), BF16),
                pltpu.VMEM((length, width), BF16),
                pltpu.SemaphoreType.DMA((len(slabs), 3)),
                pltpu.SemaphoreType.DMA,
            ],
            mib=20,
        )
    else:
        tail = jnp.concatenate([short.reshape(1, 8 * rows), up_bias[None]], axis=1)
        tail = jnp.pad(tail, ((0, 0), (0, 4 * width - tail.shape[1])))
        slab = jnp.concatenate(
            [jnp.concatenate([heads_weight, output_weight], axis=1), tail], axis=0
        )
        slabs = lax.all_gather(slab, "wide", axis=0)
        attend_full = slabs[:, :rows].reshape(width, 4 * width)
        heads_full = attend_full[:, : 3 * width]
        output_full = attend_full[:, 3 * width :]
        last = slabs[:, rows].astype(F32)
        vectors = last[:, : 8 * rows].reshape(wide, 8, rows).transpose(1, 0, 2).reshape(8, width)
        up_bias_half = mine_of(last[:, 8 * rows : 8 * rows + hidden].reshape(chips, 2, hidden), 1)
        up_bias_half = jnp.broadcast_to(up_bias_half.reshape(1, half), (VECTORS, half))
        positions = jnp.zeros((1,), jnp.int32)
        first_low, joined = call(
            functools.partial(project_kernel, 0, rows, hidden),
            [((length, width), BF16), ((length, 3 * width), BF16)],
            (x, heads_full, vectors),
            positions,
            mib=20,
        )
        up_view = up_weight.reshape(rows, chips, 2, hidden)
        up_pair = by_core(
            mine_of(up_view, 2).reshape(rows, half),
            swap(mine_of(up_view, 2, 1).reshape(rows, half), 1),
            0,
        ).reshape(2 * rows, half)
        up_parts = [spread_chips(up_pair).reshape(width, half)]
        down_parts = [spread_chips(down_weight).reshape(half, width)]
        up_positions = down_positions = positions

    attended, across, lse = attend(joined, segments)
    if square():
        up_x, up_y = after([up_x, up_y], attended)
        cut = rows // 2
        passed = [up_y[:cut], up_x[cut:]]
        (attended,) = after([attended], passed)
        near = [up_weight, up_x, up_y]
        near_swapped = [swap(part, 1) for part in near]
        passed = [swap(passed[0], 2), swap(passed[1], 4)]
        up_parts = [*near, *passed, *near_swapped, *[swap(part, 1) for part in passed]]
        at = jnp.arange(11, dtype=jnp.int32)
        part = at % 5
        device = 2 * (chip ^ jnp.minimum(part, 3)) + (core ^ (at // 5))
        up_positions = jnp.where(part < 3, device, 2 * device + part - 3)
        up_positions = jnp.where(at < 10, up_positions, core).astype(jnp.int32)
        middle_row = hidden // 2
        upper, lower = after(
            [down_weight[:middle_row], down_weight[middle_row:]], up_x, up_y
        )
        lower_x, upper_y = swap(lower, 2), swap(upper, 4)
        upper_x, lower_y = swap(upper, 2), swap(lower, 4)
        down_parts = [
            down_weight, upper_x, lower_x, upper_y, lower_y
        ]
        at = jnp.arange(7, dtype=jnp.int32)
        down_positions = jnp.where(at == 0, chip, 2 * (chip ^ ((at + 1) // 2)) + (at + 1) % 2)
    middle, second_low = call(
        middle_kernel,
        [((length, width), F32), ((length, width), BF16)],
        (x, attended, output_full, vectors),
    )

    if square():
        (second_other,) = after([second_low], near_swapped)
        second_other = swap(second_other, 1)
    else:
        second_other = swap(second_low, 1)
    activated, slope, up_full = up_project(
        second_low, second_other, up_bias_half, up_parts, up_positions, hidden
    )
    if square():
        passed_x, passed_y = after([upper_y, lower_x], activated)
        far = [swap(passed_x, 2), swap(passed_y, 4)]
        outward, outward_other, down_full = down_project_square(
            activated, down_parts, lambda total: after(far, total), down_positions
        )
    else:
        outward, outward_other, down_full = down_project(activated, down_parts, down_positions)
    result_low, grad_down, grad_logits, loss_sums = call(
        loss_kernel,
        [
            ((length, width), BF16), ((length, width), BF16), (classes.shape[:1] + (length,), BF16),
            ((SUBLANES, width), F32),
        ],
        (middle, outward, swap(outward_other, 1), vectors, classes, targets, loss_mask),
    )

    grad_down_other = swap(grad_down, 1)
    down_parts = down_grad(activated, grad_down, grad_down_other, chips, chip_position)
    if square():
        keep_dx, send_dx, keep_dy, send_dy = down_parts
        down_first = [swap(send_dx, 2), swap(send_dy, 4)]
        (grad_down_other,) = after([grad_down_other], send_dx)
    grad_up, up_bias_part, *up_parts = up_grad(
        grad_down, grad_down_other, slope, second_low, second_other, down_full, rows, chip_position
    )
    inward, inward_other = call(
        inward_kernel,
        [((length, width), F32), ((length, width), BF16)],
        (grad_up, up_full),
        out_specs=[far_away, vmem],
        scratch=[pltpu.VMEM((length, width), F32), pltpu.SemaphoreType.DMA],
        mib=20,
    )
    got_inward = swap(inward_other, 1)
    if square():
        down_second = [
            add_low(keep_dx[1], down_first[0][1]), add_low(keep_dy[1], down_first[1][1])
        ]
        (got_inward,) = after([got_inward], down_second)
        keep_ux, send_ux, keep_uy, send_uy = up_parts
        send_ux, send_uy = after([send_ux, send_uy], down_second)
        down_got = [swap(down_second[0], 4), swap(down_second[1], 2)]
        up_first = [swap(send_ux, 2), swap(send_uy, 4)]
    grad_middle, grad_branch, grad_attended, branch_sums = call(
        branch_kernel,
        [
            ((length, width), F32), ((length, width), BF16), ((length, width), BF16),
            ((SUBLANES, width), F32),
        ],
        (got_inward, inward, middle, grad_logits, classes, output_full, vectors),
        in_specs=[vmem, far_away, far_away, vmem, vmem, vmem, vmem],
        scratch=[
            *[pltpu.VMEM((length, width), F32)] * 2,
            pltpu.SemaphoreType.DMA((length // ROWS, 2)),
        ],
        mib=24,
    )

    if square():
        attend_grads = attend_back(joined, segments, grad_attended, across, lse)
        down_got = after(down_got, attend_grads[0])
        down_narrow = [
            add_low(keep_dx[0], down_first[0][0], down_got[0]),
            add_low(keep_dy[0], down_first[1][0], down_got[1]),
        ]
        down_in = hop(down_narrow, INWARD)
        attend_grads = after(attend_grads, down_narrow)
    else:
        attend_grads = attend_back(joined, segments, grad_attended, across, lse)
    stack_shape = ((8, rows + VECTORS, 2 * width), BF16)
    *stacks, input_grad, short_sums, attend_part = call(
        functools.partial(last_kernel, 8 if square() else 0, rows, hidden, len(attend_grads) // 3),
        ([stack_shape] * 2 if square() else [])
        + [((length, width), F32), ((VECTORS, width), F32), ((width, 4 * width), BF16)],
        (
            x, first_low, *attend_grads, heads_full, attended, grad_branch,
            grad_middle, vectors, branch_sums, loss_sums, up_bias_part,
        ),
        positions,
        mib=40,
    )
    if square():
        mine, others = stacks
        mine_got = swap(others, 1)
        up_first = after(up_first, mine)
        up_second = [add_low(keep_ux[1], up_first[0][1]), add_low(keep_uy[1], up_first[1][1])]
        up_got = [swap(up_second[0], 4), swap(up_second[1], 2)]

        down_in = after(down_in, up_second)
        down_half = jnp.concatenate(add_each(down_narrow, down_in))
        (down_mid,) = hop([down_half], ACROSS)

        (mine_got,) = after([mine_got], down_half)
        both = add_low(mine, mine_got)
        side_first = [swap(both[2:4], 2), swap(both[6:8], 4)]

        up_got = after(up_got, both)
        up_narrow = [
            add_low(keep_ux[0], up_first[0][0], up_got[0]),
            add_low(keep_uy[0], up_first[1][0], up_got[1]),
        ]
        up_in = hop(up_narrow, INWARD)

        side_first = after(side_first, up_narrow)
        side_second = [add_low(both[1], side_first[0][1]), add_low(both[5], side_first[1][1])]
        side_got = [swap(side_second[0], 4), swap(side_second[1], 2)]

        (down_mid,) = after([down_mid], side_second)
        down_total = add_low(down_half, down_mid)
        (down_out,) = hop([down_total], OUTWARD)

        side_got = after(side_got, down_total)
        slab_narrow = [
            add_low(both[0], side_first[0][0], side_got[0]),
            add_low(both[4], side_first[1][0], side_got[1]),
        ]
        slab_in = hop(slab_narrow, INWARD)

        (came,) = after(up_in[:1], slab_narrow)
        up_half = [add_low(up_narrow[0], came)]
        up_mid = hop(up_half, ACROSS)

        (came,) = after(up_in[1:], up_half)
        up_half.append(add_low(up_narrow[1], came))
        up_mid += hop(up_half[1:], ACROSS)

        (came,) = after(up_mid[:1], up_half[1])
        up_total = [add_low(up_half[0], came)]
        up_out = hop(up_total, OUTWARD)

        (came,) = after(slab_in[:1], up_total)
        slab_half = [add_low(slab_narrow[0], came)]
        slab_mid = hop(slab_half, ACROSS)

        (came,) = after(up_mid[1:], slab_half)
        up_total.append(add_low(up_half[1], came))
        up_out += hop(up_total[1:], OUTWARD)

        (came,) = after(slab_in[1:], up_total[1])
        slab_half.append(add_low(slab_narrow[1], came))
        slab_mid += hop(slab_half[1:], ACROSS)

        gate = slab_half[1]
        slab_total, slab_out = [], []
        for at in range(2):
            (came,) = after([slab_mid[at]], gate)
            slab_total.append(add_low(slab_half[at], came))
            slab_out += hop(slab_total[-1:], OUTWARD)
            gate = slab_total[-1:]

        (down_out,) = after([down_out], gate)
        down_weight_sum = settle(down_total, down_out).astype(F32)
        up_out = after(up_out, down_weight_sum, slab_out[0])
        upper, lower = [settle(*pair) for pair in zip(up_total, up_out)]
        first = core == 0
        (up_weight_sum,) = call(
            functools.partial(join_kernel, hidden),
            [((rows, 2 * half), F32)],
            (jnp.where(first, upper, lower), swap(jnp.where(first, lower, upper), 1)),
            core_position,
        )
        slab_out = after(slab_out, upper, lower)
        scalar = pl.BlockSpec(memory_space=pltpu.SMEM)
        heads_sum, output_sum, short, loss_sum, token_count = call(
            functools.partial(settle_kernel, rows, hidden),
            [
                ((rows, 3 * width), F32), ((rows, width), F32), ((VECTORS, 2 * width), F32),
                ((1,), F32), ((1,), jnp.int32),
            ],
            (*slab_total, *slab_out),
            lax.axis_index("narrow").reshape(1).astype(jnp.int32),
            out_specs=[vmem, vmem, vmem, scalar, scalar],
        )
        vectors_sum = short[:, :rows]
        up_bias_grad = short[0, LANES : LANES + hidden]
        loss_sum, token_count = loss_sum.reshape(()), token_count.reshape(())
    else:
        down_weight_sum = collect_chips(down_parts[0].reshape(chips, hidden, width))
        down_weight_sum = sum_narrow(down_weight_sum).astype(F32)
        up_sum = sum_narrow(collect_chips(up_parts[0].reshape(chips, 2 * rows, half)))
        up_sum = up_sum.reshape(2, rows, chips, hidden)
        up_weight_sum = by_core(mine_of(up_sum, 0), swap(mine_of(up_sum, 0, 1), 1), 2)
        up_weight_sum = up_weight_sum.reshape(rows, 2 * half).astype(F32)
        short = short_sums.reshape(8, wide, rows).transpose(1, 0, 2).reshape(wide, 8 * rows)
        up_bias_rows = up_bias_part.reshape(chips, hidden)
        up_bias_rows = by_core(up_bias_rows, jnp.zeros_like(up_bias_rows), 1).reshape(wide, hidden)
        shared = jnp.broadcast_to(loss_sums[:1, :LANES], (wide, LANES))
        row = jnp.concatenate([short, up_bias_rows, shared], axis=1).astype(BF16)
        row = jnp.pad(row, ((0, 0), (0, 4 * width - row.shape[1])))
        slab = jnp.concatenate([attend_part.reshape(wide, rows, 4 * width), row[:, None]], axis=1)
        slab = sum_narrow(lax.psum_scatter(slab, "wide", scatter_dimension=0)).astype(F32)
        vectors_sum = slab[rows, : 8 * rows].reshape(8, rows)
        heads_sum, output_sum = slab[:rows, : 3 * width], slab[:rows, 3 * width :]
        up_bias_grad = slab[rows, 8 * rows : 8 * rows + hidden]
        loss_sum = jnp.sum(slab[rows, 8 * rows + hidden : 8 * rows + hidden + LANES])
        token_count = lax.psum(jnp.sum(loss_mask), ("narrow", "wide"))
    return (
        result_low[None],
        input_grad[None],
        vectors_sum[ATTEND_GAIN],
        vectors_sum[ATTEND_SHIFT],
        heads_sum,
        vectors_sum[QUERY_BIAS],
        vectors_sum[VALUE_BIAS],
        output_sum,
        vectors_sum[OUTPUT_BIAS],
        vectors_sum[FORWARD_GAIN],
        vectors_sum[FORWARD_SHIFT],
        up_weight_sum,
        up_bias_grad,
        down_weight_sum,
        vectors_sum[DOWN_BIAS],
        loss_sum,
        token_count,
    )


def solution(mesh):
    in_specs = (
        P(("narrow", "wide"), None, None),
        P(("narrow", "wide"), None),
        P(("narrow", "wide"), None),
        P(("narrow", "wide"), None),
        P(),
        P("wide"),
        P("wide"),
        P("wide", None),
        P("wide"),
        P("wide"),
        P("wide", None),
        P("wide"),
        P("wide"),
        P("wide"),
        P("wide", None),
        P("wide"),
        P("wide", None),
        P("wide"),
    )
    out_specs = (
        P(("narrow", "wide"), None, None),
        P(("narrow", "wide"), None, None),
        P("wide"),
        P("wide"),
        P("wide", None),
        P("wide"),
        P("wide"),
        P("wide", None),
        P("wide"),
        P("wide"),
        P("wide"),
        P("wide", None),
        P("wide"),
        P("wide", None),
        P("wide"),
        P(),
        P(),
    )
    return jax.shard_map(local, mesh=mesh, in_specs=in_specs, out_specs=out_specs, check_vma=False)
```

```python
import functools
import math

import jax
import jax.numpy as jnp
from jax import lax
from jax.experimental import pallas as pl
from jax.experimental.pallas import tpu as pltpu
from jax.sharding import PartitionSpec as P

HEADS = 20
HEAD_DIM = 32
LANES = 128
SUBLANES = 8
SEGMENTS = 8
REACH = 192
CHUNK = 256
ROWS = 128
SCALE = 1.0 / math.sqrt(HEAD_DIM)
SCALE2 = math.log2(math.e) * SCALE
F32 = jnp.float32
BF16 = jnp.bfloat16
VECTORS = 8
ATTEND_GAIN, ATTEND_SHIFT, QUERY_BIAS, VALUE_BIAS = 0, 1, 2, 3
OUTPUT_BIAS, FORWARD_GAIN, FORWARD_SHIFT, DOWN_BIAS = 4, 5, 6, 7


def nn(left, right):
    return lax.dot_general(left, right, (((1,), (0,)), ((), ())), preferred_element_type=F32)


def nt(left, right):
    return lax.dot_general(left, right, (((1,), (1,)), ((), ())), preferred_element_type=F32)


def tn(left, right):
    return lax.dot_general(left, right, (((0,), (0,)), ((), ())), preferred_element_type=F32)


def call(kernel, outs, args, positions=None, grid=None, in_specs=None, out_specs=None, scratch=(),
         mib=16, aliases=None):
    whole = pl.BlockSpec(memory_space=pltpu.VMEM)
    in_specs = in_specs or [whole] * len(args)
    args = [
        pltpu.with_memory_space_constraint(arg, pltpu.HBM)
        if spec.memory_space == pltpu.HBM
        else arg
        for arg, spec in zip(args, in_specs)
    ]
    out_specs = out_specs or [whole] * len(outs)
    shapes = [
        pltpu.HBM(*out) if spec.memory_space == pltpu.HBM else jax.ShapeDtypeStruct(*out)
        for out, spec in zip(outs, out_specs)
    ]
    extra = [] if positions is None else [positions]
    return pl.pallas_call(
        kernel,
        out_shape=shapes,
        grid_spec=pltpu.PrefetchScalarGridSpec(
            num_scalar_prefetch=len(extra),
            grid=grid or (),
            in_specs=in_specs,
            out_specs=out_specs,
            scratch_shapes=list(scratch),
        ),
        compiler_params=pltpu.CompilerParams(vmem_limit_bytes=mib * 1024 * 1024),
        input_output_aliases=aliases or {},
        cost_estimate=pl.CostEstimate(flops=1, bytes_accessed=1, transcendentals=0),
    )(*extra, *args)


def unit(values):
    centred = values - jnp.mean(values, axis=-1, keepdims=True)
    spread = jnp.mean(centred * centred, axis=-1, keepdims=True)
    inverse = lax.rsqrt(spread + 1e-05)
    return centred * inverse, inverse


def unit_back(grad, normal, inverse, gain):
    scaled = grad * gain
    mean = jnp.mean(scaled, axis=-1, keepdims=True)
    along = jnp.mean(scaled * normal, axis=-1, keepdims=True)
    return inverse * (scaled - mean - normal * along)


def spans(length):
    chunk = min(CHUNK, length)
    return [
        (at, at + chunk, max(0, at - REACH), min(length, at + chunk + REACH))
        for at in range(0, length, chunk)
    ]


def split3(values):
    first = values.astype(BF16).astype(F32)
    rest = values - first
    second = rest.astype(BF16).astype(F32)
    return [first, second, rest - second]


def key_marks(segment_row):
    at = lax.broadcasted_iota(jnp.int32, (LANES, segment_row.shape[1]), 0)
    ones = (at >= SEGMENTS) & (at < SEGMENTS + 3)
    return jnp.where((at == segment_row) | ones, 1.0, 0.0).astype(BF16).T


def query_marks(segment_row):
    row = lax.broadcasted_iota(jnp.int32, (SEGMENTS, segment_row.shape[1]), 0)
    return jnp.where(row == segment_row, 0.0, -1e30)


def place(rows, head, marks):
    count = rows.shape[1]
    parts = [rows, marks, jnp.zeros((LANES - marks.shape[0], count), BF16)]
    if head < LANES // HEAD_DIM - 1:
        parts.insert(1, jnp.zeros((LANES - HEAD_DIM * (head + 1), count), BF16))
    if head:
        parts.insert(0, jnp.zeros((HEAD_DIM * head, count), BF16))
    return jnp.concatenate(parts, axis=0)


def attend_kernel(row_ref, q_ref, k_ref, v_ref, out_ref, across_ref, lse_ref, marks_ref):
    @pl.when(pl.program_id(0) == 0)
    def _():
        marks_ref[...] = key_marks(row_ref[...])

    length = q_ref.shape[0]
    heads = LANES // HEAD_DIM
    queries = q_ref[...].T
    values = v_ref[...].T
    keys = jnp.concatenate([k_ref[...], marks_ref[...]], axis=1)
    blank = jnp.zeros((SUBLANES, length), F32)
    marks = jnp.concatenate([query_marks(row_ref[...]), blank], axis=0).astype(BF16)
    ones = jnp.ones((SUBLANES, length), BF16)
    bodies = [(head, span) for head in range(heads) for span in spans(length)]

    def rows(head):
        return slice(HEAD_DIM * head, HEAD_DIM * (head + 1))

    summed = [jnp.concatenate([values[rows(head)], ones], axis=0) for head in range(heads)]

    def score(head, span):
        begin, end, low, high = span
        return nn(keys[low:high], place(queries[rows(head), begin:end], head, marks[:, begin:end]))

    def finish(head, span, top, probs):
        begin, end, low, high = span
        out = nn(summed[head][:, low:high], probs)
        total = out[HEAD_DIM : HEAD_DIM + 1]
        across_ref[rows(head), begin:end] = out[:HEAD_DIM] * (1.0 / total)
        lse_ref[head : head + 1, begin:end] = (top + jnp.log2(total)) * (1.0 / SCALE2)

    scores = [score(*body) for body in bodies[:2]]
    waiting = None
    for at, body in enumerate(bodies):
        current = scores.pop(0)
        if at + 2 < len(bodies):
            scores.append(score(*bodies[at + 2]))
        top = jnp.max(current, axis=0, keepdims=True) * SCALE2
        probs = jnp.exp2(current * SCALE2 - top).astype(BF16)
        if waiting is not None:
            finish(*waiting)
        waiting = (*body, top, probs)
    finish(*waiting)
    lse_ref[heads:, :] = jnp.zeros((SUBLANES - heads, length), F32)
    out_ref[...] = across_ref[...].T.astype(BF16)


def attend_back_kernel(
    row_ref, q_ref, k_ref, v_ref, grad_ref, across_ref, lse_ref,
    gq_ref, gk_ref, gv_ref, marks_ref, turned_ref,
):
    @pl.when(pl.program_id(0) == 0)
    def _():
        marks_ref[...] = key_marks(row_ref[...])

    length = q_ref.shape[0]
    grad = grad_ref[...]
    queries = q_ref[...].T
    turned_keys = k_ref[...].T
    grads = grad.T
    keys = jnp.concatenate([k_ref[...], marks_ref[...]], axis=1)
    values = jnp.concatenate([v_ref[...], marks_ref[...]], axis=1)
    low_marks = query_marks(row_ref[...])
    blank = jnp.zeros((SUBLANES, length), F32)
    lane = lax.broadcasted_iota(jnp.int32, (1, LANES), 1) // HEAD_DIM
    heads = []
    for head in range(LANES // HEAD_DIM):
        rows = slice(HEAD_DIM * head, HEAD_DIM * (head + 1))
        inner = jnp.sum(grads[rows].astype(F32) * across_ref[rows, :], axis=0, keepdims=True)
        lse = lse_ref[head : head + 1, :]
        score_marks = jnp.concatenate([low_marks, *split3(-lse), blank[:5]], axis=0)
        inner_marks = jnp.concatenate([blank, *split3(-inner), blank[:5]], axis=0)
        zero = jnp.zeros_like(grad)
        heads.append(
            (
                rows,
                score_marks.astype(BF16),
                inner_marks.astype(BF16),
                jnp.where(lane == head, q_ref[...], zero),
                jnp.where(lane == head, grad, zero),
            )
        )
    bodies = [
        (head, at, span) for head in range(len(heads)) for at, span in enumerate(spans(length))
    ]
    sums = [[None, None] for _ in spans(length)]

    def pair(head, at, span):
        begin, end, low, high = span
        rows, score_marks, inner_marks, _, _ = heads[head]
        return (
            nn(keys[low:high], place(queries[rows, begin:end], head, score_marks[:, begin:end])),
            nn(values[low:high], place(grads[rows, begin:end], head, inner_marks[:, begin:end])),
        )

    def finish(head, at, span, score_grads, probs):
        begin, end, low, high = span
        rows, _, _, own_queries, own_grads = heads[head]
        for which, (left, right) in enumerate(
            ((score_grads, own_queries[begin:end]), (probs, own_grads[begin:end]))
        ):
            part = nn(left, right)
            sums[at][which] = part if sums[at][which] is None else sums[at][which] + part
        turned_ref[rows, begin:end] = nn(turned_keys[rows, low:high], score_grads)

    ahead = [pair(*bodies[0])]
    waiting = None
    for at, body in enumerate(bodies):
        scores, differences = ahead.pop(0)
        if at + 1 < len(bodies):
            ahead.append(pair(*bodies[at + 1]))
        probs = jnp.exp2(scores * SCALE2)
        score_grads = (probs * differences).astype(BF16)
        if waiting is not None:
            finish(*waiting)
        waiting = (*body, score_grads, probs.astype(BF16))
    finish(*waiting)
    gq_ref[...] = (turned_ref[...].T * SCALE).astype(BF16)
    for which, (ref, factor) in enumerate(((gk_ref, SCALE), (gv_ref, 1.0))):
        total = None
        for at, (_, _, low, high) in enumerate(spans(length)):
            parts = [sums[at][which]]
            if low:
                parts.insert(0, jnp.zeros((low, LANES), F32))
            if high < length:
                parts.append(jnp.zeros((length - high, LANES), F32))
            part = jnp.concatenate(parts, axis=0) if len(parts) > 1 else parts[0]
            total = part if total is None else total + part
        ref[...] = (total * factor).astype(BF16)


def attention_specs(length, width, begin=0):
    tiles = width // LANES

    def tile(at, begin=begin):
        return pl.BlockSpec((length, LANES), lambda i: (0, at + begin + i))

    return (
        tiles,
        tile,
        pl.BlockSpec((1, length), lambda i: (0, 0)),
        pl.BlockSpec((LANES, length), lambda i: (begin + i, 0)),
        pl.BlockSpec((SUBLANES, length), lambda i: (begin + i, 0)),
    )


def attend(joined, row):
    length = joined.shape[0]
    width = joined.shape[1] // 3
    tiles, tile, row_spec, across_spec, lse_spec = attention_specs(length, width)
    return call(
        attend_kernel,
        [((length, width), BF16), ((width, length), F32), ((SUBLANES * tiles, length), F32)],
        (row, joined, joined, joined),
        grid=(tiles,),
        in_specs=[row_spec, tile(0), tile(tiles), tile(2 * tiles)],
        out_specs=[tile(0), across_spec, lse_spec],
        scratch=[pltpu.VMEM((length, LANES), BF16)],
    )


def attend_back(joined, row, grad, across, lse, begin=0, end=None):
    length = joined.shape[0]
    width = joined.shape[1] // 3
    specs = attention_specs(length, width, begin)
    tiles, tile, row_spec, across_spec, lse_spec = specs
    count = (end or tiles) - begin
    return call(
        attend_back_kernel,
        [((length, count * LANES), BF16)] * 3,
        (row, joined, joined, joined, grad, across, lse),
        grid=(count,),
        in_specs=[row_spec, tile(0), tile(tiles), tile(2 * tiles), tile(0), across_spec, lse_spec],
        out_specs=[tile(0, 0)] * 3,
        scratch=[pltpu.VMEM((length, LANES), BF16), pltpu.VMEM((LANES, length), F32)],
        mib=24,
    )


def slab_kernel(heads_far, out_far, short_ref, up_ref, slab_ref, sems):
    rows = heads_far.shape[0]
    width = out_far.shape[1]
    copies = [
        pltpu.make_async_copy(far, slab_ref.at[pl.ds(0, rows), here], sems.at[at])
        for at, (far, here) in enumerate(
            ((heads_far, pl.ds(0, 3 * width)), (out_far, pl.ds(3 * width, width)))
        )
    ]
    for copy in copies:
        copy.start()
    slab_ref[rows:, :] = jnp.zeros((VECTORS, 4 * width), BF16)
    slab_ref[rows:, :rows] = short_ref[...]
    slab_ref[rows:, LANES : LANES + up_ref.shape[1]] = jnp.broadcast_to(
        up_ref[...], (VECTORS, up_ref.shape[1])
    )
    for copy in copies:
        copy.wait()


def project_kernel(count, rows, hidden, position_ref, x_far, *refs):
    slabs, refs = refs[:count], refs[count:]
    length, width = x_far.shape
    x_ref = x_far
    if count:
        low_ref, joined_ref, heads_ref, out_ref, vector_ref, bias_ref, *refs = refs
        short_ref, x_ref, sems, x_sem = refs
        copies = [pltpu.make_async_copy(x_far, x_ref, x_sem)]
        copies[0].start()
        for at, slab in enumerate(slabs):
            begin = pl.multiple_of(position_ref[at] * rows, SUBLANES)
            here = pl.ds(begin, rows)
            for which, (source, target) in enumerate(
                (
                    (slab.at[pl.ds(0, rows), pl.ds(0, 3 * width)], heads_ref.at[here]),
                    (slab.at[pl.ds(0, rows), pl.ds(3 * width, width)], out_ref.at[here]),
                    (slab.at[pl.ds(rows, VECTORS), pl.ds(0, LANES + hidden)], short_ref.at[at]),
                )
            ):
                copy = pltpu.make_async_copy(source, target, sems.at[at, which])
                copy.start()
                copies.append(copy)
    else:
        heads_ref, vector_ref, low_ref, joined_ref = refs
    if count:
        for copy in copies:
            copy.wait()
        vectors = jnp.zeros((VECTORS, width), F32)
        for at in range(count):
            begin = position_ref[at] * rows
            short = short_ref[at, :, :LANES].astype(F32)
            lane = lax.broadcasted_iota(jnp.int32, short.shape, 1)
            short = jnp.where(lane < rows, short, 0.0)
            short = jnp.concatenate([short, jnp.zeros((VECTORS, width - LANES), F32)], axis=1)
            vectors = vectors + pltpu.roll(short, begin, 1)
            if at < count // 2:
                begin = pl.multiple_of(lax.div(position_ref[at], 2) * hidden, LANES)
                bias_ref[:, pl.ds(begin, hidden)] = short_ref[at, :, LANES:].astype(F32)
        vector_ref[...] = vectors
    zero = jnp.zeros((1, width), F32)
    vector = vector_ref[...]
    bias = jnp.concatenate(
        [vector[QUERY_BIAS : QUERY_BIAS + 1], zero, vector[VALUE_BIAS : VALUE_BIAS + 1]], axis=1
    )
    for at in range(0, length, ROWS):
        normal, _ = unit(x_ref[at : at + ROWS, :].astype(F32))
        low_ref[at : at + ROWS, :] = (
            normal * vector[ATTEND_GAIN : ATTEND_GAIN + 1]
            + vector[ATTEND_SHIFT : ATTEND_SHIFT + 1]
        ).astype(BF16)
    for at in range(0, 3 * width, width):
        here = slice(at, at + width)
        joined_ref[:, here] = (nn(low_ref[...], heads_ref[:, here]) + bias[:, here]).astype(BF16)


def middle_kernel(x_ref, attended_ref, out_ref, vector_ref, middle_ref, low_ref):
    vector = vector_ref[...]
    for at in range(0, x_ref.shape[0], ROWS):
        here = slice(at, at + ROWS)
        middle = (
            x_ref[here, :].astype(F32)
            + nn(attended_ref[here, :], out_ref[...])
            + vector[OUTPUT_BIAS : OUTPUT_BIAS + 1]
        )
        middle_ref[here, :] = middle
        normal, _ = unit(middle)
        low_ref[here, :] = (
            normal * vector[FORWARD_GAIN : FORWARD_GAIN + 1]
            + vector[FORWARD_SHIFT : FORWARD_SHIFT + 1]
        ).astype(BF16)


def up_kernel(position_ref, own_ref, other_ref, bias_ref, *refs):
    parts, (act_ref, slope_ref, full_ref) = refs[: len(refs) - 3], refs[len(refs) - 3 :]
    for at, part in enumerate(parts):
        rows = part.shape[0]
        begin = pl.multiple_of(position_ref[at] * rows, SUBLANES)
        full_ref[pl.ds(begin, rows), :] = part[...]
    weight = full_ref[...]
    bias = bias_ref[:1, :]
    length = own_ref.shape[0]
    for which, ref in enumerate((own_ref, other_ref)):
        for at in range(0, length, ROWS):
            upward = nn(ref[at : at + ROWS, :], weight) + bias
            share = 0.5 + 0.5 * lax.erf(upward * math.sqrt(0.5))
            bell = jnp.exp2((upward * upward) * (-0.5 * math.log2(math.e)))
            here = slice(which * length + at, which * length + at + ROWS)
            act_ref[here, :] = (upward * share).astype(BF16)
            slope = share + upward * (bell * (1.0 / math.sqrt(2.0 * math.pi)))
            slope_ref[here, :] = slope.astype(BF16)


def column_specs(half, block):
    block = min(block, half)

    def column(height):
        return pl.BlockSpec((height, block), lambda i, at: (0, i))

    return half // block, block, column


def whole_spec(shape):
    return pl.BlockSpec(shape, lambda i, at: (0,) * len(shape))


def up_project(own, other, bias, parts, positions, hidden):
    length, width = own.shape
    half = bias.shape[1]
    paired = parts[0].shape[1] > half
    steps, block, column = column_specs(half, hidden if paired else 512)
    whole = whole_spec((length, width))

    def part_spec(part):
        if paired:
            return pl.BlockSpec((part.shape[0], block), lambda i, at: (0, 2 * i + at[len(parts)]))
        return column(part.shape[0])

    return call(
        up_kernel,
        [((2 * length, half), BF16), ((2 * length, half), BF16), ((width, half), BF16)],
        (own, other, bias, *parts),
        positions,
        grid=(steps,),
        in_specs=[whole, whole, column(bias.shape[0])] + [part_spec(part) for part in parts],
        out_specs=[column(2 * length), column(2 * length), column(width)],
    )


def down_kernel(position_ref, act_ref, *refs):
    parts, (own_ref, other_ref, full_ref) = refs[: len(refs) - 3], refs[len(refs) - 3 :]
    length = own_ref.shape[0]
    for at, part in enumerate(parts):
        rows = part.shape[0]
        begin = pl.multiple_of(position_ref[at] * rows, SUBLANES)
        full_ref[pl.ds(begin, rows), :] = part[...]
    for which, ref in enumerate((own_ref, other_ref)):
        here = slice(which * length, (which + 1) * length)
        ref[...] = nn(act_ref[here, :], full_ref[...]).astype(ref.dtype)


def down_project(act, parts, positions):
    length = act.shape[0] // 2
    half = act.shape[1]
    width = parts[0].shape[1]
    return call(
        down_kernel,
        [((length, width), F32), ((length, width), BF16), ((half, width), BF16)],
        (act, *parts),
        positions,
        mib=20,
    )


def down_near_kernel(position_ref, act_ref, *refs):
    parts, (sum_ref, full_ref) = refs[:-2], refs[-2:]
    size = parts[0].shape[0]
    for at, part in enumerate(parts):
        rows = part.shape[0]
        begin = pl.multiple_of(position_ref[at] * rows, SUBLANES)
        full_ref[pl.ds(begin, rows), :] = part[...]
    chips = [position_ref[0], lax.div(position_ref[1], 2), lax.div(position_ref[3], 2)]
    length = act_ref.shape[0] // 2
    for which in range(2):
        here = slice(which * length, (which + 1) * length)
        total = None
        for chip in chips:
            units = pl.ds(pl.multiple_of(chip * size, LANES), size)
            part = nn(act_ref[here, units], full_ref[units, :])
            total = part if total is None else total + part
        sum_ref[here, :] = total


def down_far_kernel(position_ref, act_ref, sum_ref, upper_ref, lower_ref, _, own_ref, other_ref, full_ref):
    rows, length = upper_ref.shape[0], own_ref.shape[0]
    size = 2 * rows
    units = pl.ds(pl.multiple_of(lax.div(position_ref[5], 2) * size, LANES), size)
    weight = jnp.concatenate([upper_ref[...], lower_ref[...]], axis=0)
    full_ref[units, :] = weight
    for which, ref in enumerate((own_ref, other_ref)):
        here = slice(which * length, (which + 1) * length)
        ref[...] = (sum_ref[here, :] + nn(act_ref[here, units], weight)).astype(ref.dtype)


def down_project_square(act, near, far, positions):
    length, half, width = act.shape[0] // 2, act.shape[1], near[0].shape[1]
    total, full = call(
        down_near_kernel,
        [((2 * length, width), F32), ((half, width), BF16)],
        (act, *near),
        positions,
        mib=24,
    )
    far = far(total)
    return call(
        down_far_kernel,
        [((length, width), F32), ((length, width), BF16), ((half, width), BF16)],
        (act, total, *far, full),
        positions,
        mib=24,
        aliases={5: 2},
    )


def loss_kernel(
    middle_ref, own_ref, got_ref, vector_ref, readout_ref, target_ref, mask_ref,
    low_ref, down_ref, grad_ref, sums_ref,
):
    result = (
        middle_ref[...]
        + (own_ref[...] + got_ref[...].astype(F32))
        + vector_ref[DOWN_BIAS : DOWN_BIAS + 1, :]
    ).astype(BF16)
    low_ref[...] = result
    logits = nt(readout_ref[...], result)
    length = logits.shape[1]
    top = jnp.max(logits, axis=0, keepdims=True)
    shifted = jnp.exp(logits - top)
    total = jnp.sum(shifted, axis=0, keepdims=True)
    onehot = lax.broadcasted_iota(jnp.int32, logits.shape, 0) == target_ref[...]
    picked = jnp.sum(jnp.where(onehot, logits, 0.0), axis=0, keepdims=True)
    weight = mask_ref[...].astype(F32)
    loss = (top + jnp.log(total) - picked) * weight
    loss_lanes = jnp.zeros((1, LANES), F32)
    count_lanes = jnp.zeros((1, LANES), F32)
    for at in range(0, length, LANES):
        loss_lanes = loss_lanes + loss[:, at : at + LANES]
        count_lanes = count_lanes + weight[:, at : at + LANES]
    lanes = jnp.concatenate([loss_lanes, count_lanes], axis=0)
    lanes = jnp.concatenate([lanes, jnp.zeros((2, result.shape[1] - LANES), F32)], axis=1)
    grad_logits = (weight * (shifted / total - onehot.astype(F32))).astype(BF16)
    grad_ref[...] = grad_logits
    low = tn(grad_logits, readout_ref[...]).astype(BF16)
    down_ref[...] = low
    sums = jnp.sum(low.astype(F32), axis=0, keepdims=True)
    blank = jnp.zeros((SUBLANES - 3, result.shape[1]), F32)
    sums_ref[...] = jnp.concatenate([lanes, sums, blank], axis=0)


def down_grad_kernel(chips, position_ref, act_ref, own_ref, other_ref, *out_refs):
    length = own_ref.shape[0]
    hidden = act_ref.shape[1] // chips
    for offset in range(chips):
        if len(out_refs) == 1:
            begin = offset * hidden
        else:
            begin = pl.multiple_of((position_ref[0] ^ offset) * hidden, LANES)
        here = pl.ds(begin, hidden)
        part = tn(act_ref[:length, here], own_ref[...]) + tn(act_ref[length:, here], other_ref[...])
        part = part.astype(BF16)
        if len(out_refs) == 1:
            out_refs[0][begin : begin + hidden, :] = part
            continue
        keep_x, send_x, keep_y, send_y = out_refs
        half = hidden // 2
        (send_x if offset % 2 else keep_x)[offset // 2, :, :] = part[:half]
        (send_y if offset // 2 else keep_y)[offset % 2, :, :] = part[half:]


def down_grad(act, own, other, chips, position):
    half = act.shape[1]
    width = own.shape[1]
    if square():
        outs = [((2, half // chips // 2, width), BF16)] * 4
    else:
        outs = [((half, width), BF16)]
    return call(
        functools.partial(down_grad_kernel, chips), outs, (act, own, other), position, mib=20
    )


def up_grad_kernel(
    rows, position_ref, own_ref, other_ref, slope_ref, second_ref, second_other_ref, down_ref,
    up_ref, bias_ref, *refs,
):
    out_refs, part_ref = refs[:-1], refs[-1]
    length = own_ref.shape[0]
    total = None
    grads = []
    for which, ref in enumerate((own_ref, other_ref)):
        for at in range(0, length, 2 * ROWS):
            here = slice(which * length + at, which * length + at + 2 * ROWS)
            grad = nt(ref[at : at + 2 * ROWS, :], down_ref[...]) * slope_ref[here, :].astype(F32)
            low = grad.astype(BF16)
            up_ref[here, :] = low
            part = jnp.sum(low.astype(F32), axis=0, keepdims=True)
            total = part if total is None else total + part
    bias_ref[...] = total
    part = tn(second_ref[...], up_ref[:length, :]) + tn(second_other_ref[...], up_ref[length:, :])
    if len(out_refs) == 1:
        out_refs[0][...] = part.astype(BF16)
        return
    part_ref[...] = part
    keep_x, send_x, keep_y, send_y = out_refs
    for offset in range(4):
        begin = pl.multiple_of((position_ref[0] ^ offset) * (2 * rows), SUBLANES)
        upper = part_ref[pl.ds(begin, rows), :].astype(BF16)
        lower = part_ref[pl.ds(begin + rows, rows), :].astype(BF16)
        (send_x if offset % 2 else keep_x)[offset // 2, :, :] = upper
        (send_y if offset // 2 else keep_y)[offset % 2, :, :] = lower


def up_grad(own, other, slope, second, second_other, down_full, rows, position):
    length, width = own.shape
    half = slope.shape[1]
    steps, block, column = column_specs(half, 512)
    whole = whole_spec((length, width))
    if square():
        outs = [((2, rows, half), BF16)] * 4
        specs = [pl.BlockSpec((2, rows, block), lambda i, at: (0, 0, i))] * 4
    else:
        outs = [((width, half), BF16)]
        specs = [column(width)]
    return call(
        functools.partial(up_grad_kernel, rows),
        [((2 * length, half), BF16), ((1, half), F32), *outs],
        (own, other, slope, second, second_other, down_full),
        position,
        grid=(steps,),
        in_specs=[
            whole, whole, column(2 * length), whole, whole,
            pl.BlockSpec((block, width), lambda i, at: (i, 0)),
        ],
        out_specs=[column(2 * length), column(1), *specs],
        scratch=[pltpu.VMEM((width, block), F32)],
        mib=20,
    )


def inward_kernel(grad_ref, up_ref, own_far, other_ref, own_ref, sem):
    length = other_ref.shape[0]
    own_ref[...] = nt(grad_ref[:length, :], up_ref[...])
    copy = pltpu.make_async_copy(own_ref, own_far, sem)
    copy.start()
    other_ref[...] = nt(grad_ref[length:, :], up_ref[...]).astype(BF16)
    copy.wait()


def join_kernel(hidden, position_ref, mine_ref, other_ref, out_ref):
    for at in range(mine_ref.shape[1] // hidden):
        here = slice(hidden * at, hidden * (at + 1))
        for core, ref in enumerate((mine_ref, other_ref)):
            begin = (2 * at + (position_ref[0] + core) % 2) * hidden
            out_ref[:, pl.ds(pl.multiple_of(begin, LANES), hidden)] = ref[:, here].astype(F32)


def branch_kernel(
    got_ref, own_far, middle_far, logits_ref, classes_ref, out_ref, vector_ref,
    grad_ref, branch_ref, attended_ref, sums_ref, own_ref, middle_ref, sems,
):
    width = own_ref.shape[1]
    blocks = range(0, own_ref.shape[0], ROWS)
    copies = []
    for at in blocks:
        here = pl.ds(at, ROWS)
        copies.append(
            [
                pltpu.make_async_copy(far.at[here], ref.at[here], sems.at[at // ROWS, which])
                for which, (far, ref) in enumerate(((own_far, own_ref), (middle_far, middle_ref)))
            ]
        )
        for copy in copies[-1]:
            copy.start()
    gain = vector_ref[FORWARD_GAIN : FORWARD_GAIN + 1, :]
    sums = [jnp.zeros((1, width), F32) for _ in range(3)]
    for at in blocks:
        for copy in copies[at // ROWS]:
            copy.wait()
        here = slice(at, at + ROWS)
        grad = own_ref[here, :] + got_ref[here, :].astype(F32)
        normal, inverse = unit(middle_ref[here, :])
        result = tn(logits_ref[:, here], classes_ref[...])
        middle = result + unit_back(grad, normal, inverse, gain)
        grad_ref[here, :] = middle
        branch = middle.astype(BF16)
        branch_ref[here, :] = branch
        attended_ref[here, :] = nt(branch, out_ref[...]).astype(BF16)
        for which, part in enumerate((grad * normal, grad, branch.astype(F32))):
            sums[which] = sums[which] + jnp.sum(part, axis=0, keepdims=True)
    blank = jnp.zeros((SUBLANES - 3, width), F32)
    sums_ref[...] = jnp.concatenate([*sums, blank], axis=0)


def last_kernel(count, rows, hidden, pieces, position_ref, x_ref, low_ref, *refs):
    grad_refs, refs = refs[: 3 * pieces], refs[3 * pieces :]
    heads_ref, attended_ref, branch_ref, grad_ref, vector_ref, *refs = refs
    sums_ref, loss_ref, up_ref, *refs = refs
    stacks, (input_ref, vectors_ref, full_ref) = refs[:-3], refs[-3:]
    width = x_ref.shape[1]

    def grads(which, here):
        parts = [ref[here, :] for ref in grad_refs[which::3]]
        return jnp.concatenate(parts, axis=1) if pieces > 1 else parts[0]

    for at in range(3):
        part = tn(low_ref[...], grads(at, slice(None)))
        full_ref[:, width * at : width * (at + 1)] = part.astype(BF16)
    full_ref[:, 3 * width :] = tn(attended_ref[...], branch_ref[...]).astype(BF16)
    gain = vector_ref[ATTEND_GAIN : ATTEND_GAIN + 1, :]

    def block(at, sums):
        here = pl.ds(pl.multiple_of(at * ROWS, ROWS), ROWS)
        grad_query, grad_key, grad_value = [grads(which, here) for which in range(3)]
        grad = (
            nt(grad_query, heads_ref[:, :width])
            + nt(grad_key, heads_ref[:, width : 2 * width])
            + nt(grad_value, heads_ref[:, 2 * width :])
        )
        normal, inverse = unit(x_ref[here, :].astype(F32))
        input_ref[here, :] = grad_ref[here, :] + unit_back(grad, normal, inverse, gain)
        parts = (grad * normal, grad, grad_query.astype(F32), grad_value.astype(F32))
        return tuple(
            total + jnp.sum(part, axis=0, keepdims=True) for total, part in zip(sums, parts)
        )

    zero = jnp.zeros((1, width), F32)
    sums = lax.fori_loop(0, x_ref.shape[0] // ROWS, block, (zero,) * 4)
    vectors = jnp.concatenate(
        [*sums, sums_ref[2:3, :], sums_ref[0:1, :], sums_ref[1:2, :], loss_ref[2:3, :]], axis=0
    )
    vectors_ref[...] = vectors
    blank = jnp.zeros((VECTORS - 1, hidden), F32)
    lanes = jnp.concatenate([loss_ref[:2, :LANES], jnp.zeros((VECTORS - 2, LANES), F32)], axis=0)
    for which, stack in enumerate(stacks):

        def slab(step, carry, which=which, stack=stack):
            place_at = position_ref[which * (count // 2) + step]
            begin = pl.multiple_of(place_at * rows, SUBLANES)
            short = pltpu.roll(vectors, width - begin, 1)[:, :LANES]
            if which == 0:
                hidden_at = pl.multiple_of(lax.div(place_at, 2) * hidden, LANES)
                bias = jnp.concatenate([up_ref[:, pl.ds(hidden_at, hidden)], blank], axis=0)
            else:
                bias = jnp.zeros((VECTORS, hidden), F32)
            row = jnp.concatenate([short, bias, lanes], axis=1).astype(BF16)
            pad = jnp.zeros((VECTORS, 4 * width - row.shape[1]), BF16)
            row = jnp.concatenate([row, pad], axis=1)
            picks = (2 * (step % 2) + step // 2, 4 + step)
            for side, pick in enumerate(picks):
                here = slice(2 * width * side, 2 * width * (side + 1))
                stack[pick, :rows, :] = full_ref[pl.ds(begin, rows), here]
                stack[pick, rows:, :] = row[:, here]
            return carry

        lax.fori_loop(0, count // 2, slab, 0)


def settle_kernel(rows, hidden, place_ref, *refs):
    totals, outers, refs = refs[:2], refs[2:4], refs[4:]
    heads_ref, out_ref, up_ref, loss_ref, count_ref, *short_refs = refs
    width = out_ref.shape[1]
    inner = (place_ref[0] == 1) | (place_ref[0] == 2)
    left, right = [
        jnp.where(inner, total[...], outer[...]).astype(F32) for total, outer in zip(totals, outers)
    ]
    heads_ref[:, : 2 * width] = left[:rows]
    heads_ref[:, 2 * width :] = right[:rows, :width]
    out_ref[...] = right[:rows, width:]
    up_ref[...] = left[rows, LANES : LANES + hidden]
    for at, ref in enumerate(short_refs):
        ref[...] = left[rows + at, :rows]
    lanes = left[rows:, LANES + hidden : 2 * LANES + hidden]
    loss_ref[0] = jnp.sum(lanes[0:1])
    count_ref[0] = jnp.sum(lanes[1:2]).astype(jnp.int32)


def swap(values, bit):
    return lax.ppermute(values, "wide", [(i, i ^ bit) for i in range(lax.axis_size("wide"))])


def same_core_groups():
    chips = lax.axis_size("wide") // 2
    return [[2 * chip + core for chip in range(chips)] for core in range(2)]


def square():
    return lax.axis_size("wide") == 8


def spread_chips(shard):
    return lax.all_gather(shard, "wide", axis=0, axis_index_groups=same_core_groups())


def add_low(*parts):
    return sum(part.astype(F32) for part in parts).astype(BF16)


def collect_chips(parts):
    return lax.psum_scatter(
        parts, "wide", scatter_dimension=0, axis_index_groups=same_core_groups()
    )


def after(values, *gates):
    leaves, tree = jax.tree.flatten(values)
    held = lax.optimization_barrier((*leaves, *jax.tree.leaves(gates)))
    return jax.tree.unflatten(tree, held[: len(leaves)])


INWARD, ACROSS, OUTWARD = [(0, 1), (3, 2)], [(1, 2), (2, 1)], [(1, 0), (2, 3)]


def hop(parts, pairs):
    return [lax.ppermute(part, "narrow", pairs) for part in parts]


def add_each(left, right):
    return [add_low(a, b) for a, b in zip(left, right)]


def settle(total, outer):
    place_at = lax.axis_index("narrow")
    return jnp.where((place_at == 1) | (place_at == 2), total, outer)


def sum_narrow(shard):
    if lax.axis_size("narrow") != 4:
        return lax.psum(shard, "narrow")
    half = add_low(shard, *hop([shard], INWARD))
    total = add_low(half, *hop([half], ACROSS))
    return settle(total, *hop([total], OUTWARD))


def local(
    layer_input, segments, targets, loss_mask, readout,
    attend_gain, attend_shift, heads_weight, query_bias, value_bias, output_weight, output_bias,
    forward_gain, forward_shift, up_weight, up_bias, down_weight, down_bias,
):
    length = layer_input.shape[1]
    width = layer_input.shape[2]
    wide = lax.axis_size("wide")
    chips = wide // 2
    core = lax.axis_index("wide") % 2
    chip = lax.axis_index("wide") // 2
    rows = heads_weight.shape[0]
    hidden = up_bias.shape[0]
    half = chips * hidden
    x = layer_input[0]
    classes = readout.T
    vmem = pl.BlockSpec(memory_space=pltpu.VMEM)
    far_away = pl.BlockSpec(memory_space=pltpu.HBM)

    def by_core(mine, other, axis):
        return jnp.where(
            core == 0, jnp.stack([mine, other], axis), jnp.stack([other, mine], axis)
        )

    def mine_of(values, axis, flip=0):
        return lax.dynamic_index_in_dim(values, core ^ flip, axis, keepdims=False)

    short = jnp.stack(
        [
            attend_gain, attend_shift, query_bias, value_bias,
            output_bias, forward_gain, forward_shift, down_bias,
        ]
    )
    core_position = core.reshape(1).astype(jnp.int32)
    chip_position = chip.reshape(1).astype(jnp.int32)
    if square():
        offsets = jnp.arange(4, dtype=jnp.int32)
        (slab,) = call(
            slab_kernel,
            [((rows + VECTORS, 4 * width), BF16)],
            (heads_weight, output_weight, short, up_bias[None]),
            in_specs=[far_away, far_away, vmem, vmem],
            scratch=[pltpu.SemaphoreType.DMA((2,))],
        )
        near_x, near_y, far = swap(slab, 2), swap(slab, 4), swap(slab, 6)
        swapped = swap(slab, 1)
        devices = 2 * (chip ^ offsets) + core
        positions = jnp.concatenate([devices, devices ^ 1]).astype(jnp.int32)
        up_weight, positions = after([up_weight, positions], near_x, swapped)
        up_x, up_y = swap(up_weight, 2), swap(up_weight, 4)
        swapped_x = swap(near_x, 1)
        near_y, far = after([near_y, far], swapped_x)
        slabs = [slab, near_x, near_y, far, swapped, swapped_x, swap(near_y, 1), swap(far, 1)]
        first_low, joined, heads_full, output_full, vectors, up_bias_half = call(
            functools.partial(project_kernel, len(slabs), rows, hidden),
            [
                ((length, width), BF16), ((length, 3 * width), BF16), ((width, 3 * width), BF16),
                ((width, width), BF16), ((VECTORS, width), F32), ((VECTORS, half), F32),
            ],
            (x, *slabs),
            positions,
            in_specs=[far_away] * (1 + len(slabs)),
            scratch=[
                pltpu.VMEM((len(slabs), VECTORS, LANES + hidden), BF16),
                pltpu.VMEM((length, width), BF16),
                pltpu.SemaphoreType.DMA((len(slabs), 3)),
                pltpu.SemaphoreType.DMA,
            ],
            mib=20,
        )
    else:
        tail = jnp.concatenate([short.reshape(1, 8 * rows), up_bias[None]], axis=1)
        tail = jnp.pad(tail, ((0, 0), (0, 4 * width - tail.shape[1])))
        slab = jnp.concatenate(
            [jnp.concatenate([heads_weight, output_weight], axis=1), tail], axis=0
        )
        slabs = lax.all_gather(slab, "wide", axis=0)
        attend_full = slabs[:, :rows].reshape(width, 4 * width)
        heads_full = attend_full[:, : 3 * width]
        output_full = attend_full[:, 3 * width :]
        last = slabs[:, rows].astype(F32)
        vectors = last[:, : 8 * rows].reshape(wide, 8, rows).transpose(1, 0, 2).reshape(8, width)
        up_bias_half = mine_of(last[:, 8 * rows : 8 * rows + hidden].reshape(chips, 2, hidden), 1)
        up_bias_half = jnp.broadcast_to(up_bias_half.reshape(1, half), (VECTORS, half))
        positions = jnp.zeros((1,), jnp.int32)
        first_low, joined = call(
            functools.partial(project_kernel, 0, rows, hidden),
            [((length, width), BF16), ((length, 3 * width), BF16)],
            (x, heads_full, vectors),
            positions,
            mib=20,
        )
        up_view = up_weight.reshape(rows, chips, 2, hidden)
        up_pair = by_core(
            mine_of(up_view, 2).reshape(rows, half),
            swap(mine_of(up_view, 2, 1).reshape(rows, half), 1),
            0,
        ).reshape(2 * rows, half)
        up_parts = [spread_chips(up_pair).reshape(width, half)]
        down_parts = [spread_chips(down_weight).reshape(half, width)]
        up_positions = down_positions = positions

    attended, across, lse = attend(joined, segments)
    if square():
        up_x, up_y = after([up_x, up_y], attended)
        cut = rows // 2
        passed = [up_y[:cut], up_x[cut:]]
        (attended,) = after([attended], passed)
        near = [up_weight, up_x, up_y]
        near_swapped = [swap(part, 1) for part in near]
        passed = [swap(passed[0], 2), swap(passed[1], 4)]
        up_parts = [*near, *passed, *near_swapped, *[swap(part, 1) for part in passed]]
        at = jnp.arange(11, dtype=jnp.int32)
        part = at % 5
        device = 2 * (chip ^ jnp.minimum(part, 3)) + (core ^ (at // 5))
        up_positions = jnp.where(part < 3, device, 2 * device + part - 3)
        up_positions = jnp.where(at < 10, up_positions, core).astype(jnp.int32)
        middle_row = hidden // 2
        upper, lower = after(
            [down_weight[:middle_row], down_weight[middle_row:]], up_x, up_y
        )
        lower_x, upper_y = swap(lower, 2), swap(upper, 4)
        upper_x, lower_y = swap(upper, 2), swap(lower, 4)
        down_parts = [
            down_weight, upper_x, lower_x, upper_y, lower_y
        ]
        at = jnp.arange(7, dtype=jnp.int32)
        down_positions = jnp.where(at == 0, chip, 2 * (chip ^ ((at + 1) // 2)) + (at + 1) % 2)
    middle, second_low = call(
        middle_kernel,
        [((length, width), F32), ((length, width), BF16)],
        (x, attended, output_full, vectors),
    )

    if square():
        (second_other,) = after([second_low], near_swapped)
        second_other = swap(second_other, 1)
    else:
        second_other = swap(second_low, 1)
    activated, slope, up_full = up_project(
        second_low, second_other, up_bias_half, up_parts, up_positions, hidden
    )
    if square():
        passed_x, passed_y = after([upper_y, lower_x], activated)
        far = [swap(passed_x, 2), swap(passed_y, 4)]
        outward, outward_other, down_full = down_project_square(
            activated, down_parts, lambda total: after(far, total), down_positions
        )
    else:
        outward, outward_other, down_full = down_project(activated, down_parts, down_positions)
    result_low, grad_down, grad_logits, loss_sums = call(
        loss_kernel,
        [
            ((length, width), BF16), ((length, width), BF16), (classes.shape[:1] + (length,), BF16),
            ((SUBLANES, width), F32),
        ],
        (middle, outward, swap(outward_other, 1), vectors, classes, targets, loss_mask),
    )

    grad_down_other = swap(grad_down, 1)
    down_parts = down_grad(activated, grad_down, grad_down_other, chips, chip_position)
    if square():
        keep_dx, send_dx, keep_dy, send_dy = down_parts
        down_first = [swap(send_dx, 2), swap(send_dy, 4)]
        (grad_down_other,) = after([grad_down_other], send_dx)
    grad_up, up_bias_part, *up_parts = up_grad(
        grad_down, grad_down_other, slope, second_low, second_other, down_full, rows, chip_position
    )
    inward, inward_other = call(
        inward_kernel,
        [((length, width), F32), ((length, width), BF16)],
        (grad_up, up_full),
        out_specs=[far_away, vmem],
        scratch=[pltpu.VMEM((length, width), F32), pltpu.SemaphoreType.DMA],
        mib=20,
    )
    got_inward = swap(inward_other, 1)
    if square():
        down_second = [
            add_low(keep_dx[1], down_first[0][1]), add_low(keep_dy[1], down_first[1][1])
        ]
        (got_inward,) = after([got_inward], down_second)
        keep_ux, send_ux, keep_uy, send_uy = up_parts
        send_ux, send_uy = after([send_ux, send_uy], down_second)
        down_got = [swap(down_second[0], 4), swap(down_second[1], 2)]
        up_first = [swap(send_ux, 2), swap(send_uy, 4)]
    grad_middle, grad_branch, grad_attended, branch_sums = call(
        branch_kernel,
        [
            ((length, width), F32), ((length, width), BF16), ((length, width), BF16),
            ((SUBLANES, width), F32),
        ],
        (got_inward, inward, middle, grad_logits, classes, output_full, vectors),
        in_specs=[vmem, far_away, far_away, vmem, vmem, vmem, vmem],
        scratch=[
            *[pltpu.VMEM((length, width), F32)] * 2,
            pltpu.SemaphoreType.DMA((length // ROWS, 2)),
        ],
        mib=24,
    )

    if square():
        attend_grads = attend_back(joined, segments, grad_attended, across, lse)
        down_got = after(down_got, attend_grads[0])
        down_narrow = [
            add_low(keep_dx[0], down_first[0][0], down_got[0]),
            add_low(keep_dy[0], down_first[1][0], down_got[1]),
        ]
        down_in = hop(down_narrow, INWARD)
        attend_grads = after(attend_grads, down_narrow)
    else:
        attend_grads = attend_back(joined, segments, grad_attended, across, lse)
    stack_shape = ((8, rows + VECTORS, 2 * width), BF16)
    *stacks, input_grad, short_sums, attend_part = call(
        functools.partial(last_kernel, 8 if square() else 0, rows, hidden, len(attend_grads) // 3),
        ([stack_shape] * 2 if square() else [])
        + [((length, width), F32), ((VECTORS, width), F32), ((width, 4 * width), BF16)],
        (
            x, first_low, *attend_grads, heads_full, attended, grad_branch,
            grad_middle, vectors, branch_sums, loss_sums, up_bias_part,
        ),
        positions,
        mib=40,
    )
    if square():
        mine, others = stacks
        mine_got = swap(others, 1)
        up_first = after(up_first, mine)
        up_second = [add_low(keep_ux[1], up_first[0][1]), add_low(keep_uy[1], up_first[1][1])]
        up_got = [swap(up_second[0], 4), swap(up_second[1], 2)]

        down_in = after(down_in, up_second)
        down_half = jnp.concatenate(add_each(down_narrow, down_in))
        (down_mid,) = hop([down_half], ACROSS)

        (mine_got,) = after([mine_got], down_half)
        both = add_low(mine, mine_got)
        side_first = [swap(both[2:4], 2), swap(both[6:8], 4)]

        up_got = after(up_got, both)
        up_narrow = [
            add_low(keep_ux[0], up_first[0][0], up_got[0]),
            add_low(keep_uy[0], up_first[1][0], up_got[1]),
        ]
        up_in = hop(up_narrow, INWARD)

        side_first = after(side_first, up_narrow)
        side_second = [add_low(both[1], side_first[0][1]), add_low(both[5], side_first[1][1])]
        side_got = [swap(side_second[0], 4), swap(side_second[1], 2)]

        (down_mid,) = after([down_mid], side_second)
        down_total = add_low(down_half, down_mid)
        (down_out,) = hop([down_total], OUTWARD)

        side_got = after(side_got, down_total)
        slab_narrow = [
            add_low(both[0], side_first[0][0], side_got[0]),
            add_low(both[4], side_first[1][0], side_got[1]),
        ]
        slab_in = hop(slab_narrow, INWARD)

        (came,) = after(up_in[:1], slab_narrow)
        up_half = [add_low(up_narrow[0], came)]
        up_mid = hop(up_half, ACROSS)

        (came,) = after(up_in[1:], up_half)
        up_half.append(add_low(up_narrow[1], came))
        up_mid += hop(up_half[1:], ACROSS)

        (came,) = after(up_mid[:1], up_half[1])
        up_total = [add_low(up_half[0], came)]
        up_out = hop(up_total, OUTWARD)

        (came,) = after(slab_in[:1], up_total)
        slab_half = [add_low(slab_narrow[0], came)]
        slab_mid = hop(slab_half, ACROSS)

        (came,) = after(up_mid[1:], slab_half)
        up_total.append(add_low(up_half[1], came))
        up_out += hop(up_total[1:], OUTWARD)

        (came,) = after(slab_in[1:], up_total[1])
        slab_half.append(add_low(slab_narrow[1], came))
        slab_mid += hop(slab_half[1:], ACROSS)

        gate = slab_half[1]
        slab_total, slab_out = [], []
        for at in range(2):
            (came,) = after([slab_mid[at]], gate)
            slab_total.append(add_low(slab_half[at], came))
            slab_out += hop(slab_total[-1:], OUTWARD)
            gate = slab_total[-1:]

        (down_out,) = after([down_out], gate)
        down_weight_sum = settle(down_total, down_out).astype(F32)
        up_out = after(up_out, down_weight_sum, slab_out[0])
        upper, lower = [settle(*pair) for pair in zip(up_total, up_out)]
        first = core == 0
        crossed = swap(jnp.where(first, lower, upper), 1)
        (up_weight_sum,) = call(
            functools.partial(join_kernel, hidden),
            [((rows, 2 * half), F32)],
            (jnp.where(first, upper, lower), crossed),
            core_position,
        )
        slab_out = after(slab_out, crossed)
        scalar = pl.BlockSpec(memory_space=pltpu.SMEM)
        heads_sum, output_sum, up_bias_grad, loss_sum, token_count, *vectors_sum = call(
            functools.partial(settle_kernel, rows, hidden),
            [
                ((rows, 3 * width), F32), ((rows, width), F32), ((hidden,), F32),
                ((1,), F32), ((1,), jnp.int32), *[((rows,), F32)] * VECTORS,
            ],
            (*slab_total, *slab_out),
            lax.axis_index("narrow").reshape(1).astype(jnp.int32),
            out_specs=[vmem, vmem, vmem, scalar, scalar, *[vmem] * VECTORS],
        )
        loss_sum, token_count = loss_sum.reshape(()), token_count.reshape(())
    else:
        down_weight_sum = collect_chips(down_parts[0].reshape(chips, hidden, width))
        down_weight_sum = sum_narrow(down_weight_sum).astype(F32)
        up_sum = sum_narrow(collect_chips(up_parts[0].reshape(chips, 2 * rows, half)))
        up_sum = up_sum.reshape(2, rows, chips, hidden)
        up_weight_sum = by_core(mine_of(up_sum, 0), swap(mine_of(up_sum, 0, 1), 1), 2)
        up_weight_sum = up_weight_sum.reshape(rows, 2 * half).astype(F32)
        short = short_sums.reshape(8, wide, rows).transpose(1, 0, 2).reshape(wide, 8 * rows)
        up_bias_rows = up_bias_part.reshape(chips, hidden)
        up_bias_rows = by_core(up_bias_rows, jnp.zeros_like(up_bias_rows), 1).reshape(wide, hidden)
        shared = jnp.broadcast_to(loss_sums[:1, :LANES], (wide, LANES))
        row = jnp.concatenate([short, up_bias_rows, shared], axis=1).astype(BF16)
        row = jnp.pad(row, ((0, 0), (0, 4 * width - row.shape[1])))
        slab = jnp.concatenate([attend_part.reshape(wide, rows, 4 * width), row[:, None]], axis=1)
        slab = sum_narrow(lax.psum_scatter(slab, "wide", scatter_dimension=0)).astype(F32)
        vectors_sum = slab[rows, : 8 * rows].reshape(8, rows)
        heads_sum, output_sum = slab[:rows, : 3 * width], slab[:rows, 3 * width :]
        up_bias_grad = slab[rows, 8 * rows : 8 * rows + hidden]
        loss_sum = jnp.sum(slab[rows, 8 * rows + hidden : 8 * rows + hidden + LANES])
        token_count = lax.psum(jnp.sum(loss_mask), ("narrow", "wide"))
    return (
        result_low[None],
        input_grad[None],
        vectors_sum[ATTEND_GAIN],
        vectors_sum[ATTEND_SHIFT],
        heads_sum,
        vectors_sum[QUERY_BIAS],
        vectors_sum[VALUE_BIAS],
        output_sum,
        vectors_sum[OUTPUT_BIAS],
        vectors_sum[FORWARD_GAIN],
        vectors_sum[FORWARD_SHIFT],
        up_weight_sum,
        up_bias_grad,
        down_weight_sum,
        vectors_sum[DOWN_BIAS],
        loss_sum,
        token_count,
    )


def solution(mesh):
    in_specs = (
        P(("narrow", "wide"), None, None),
        P(("narrow", "wide"), None),
        P(("narrow", "wide"), None),
        P(("narrow", "wide"), None),
        P(),
        P("wide"),
        P("wide"),
        P("wide", None),
        P("wide"),
        P("wide"),
        P("wide", None),
        P("wide"),
        P("wide"),
        P("wide"),
        P("wide", None),
        P("wide"),
        P("wide", None),
        P("wide"),
    )
    out_specs = (
        P(("narrow", "wide"), None, None),
        P(("narrow", "wide"), None, None),
        P("wide"),
        P("wide"),
        P("wide", None),
        P("wide"),
        P("wide"),
        P("wide", None),
        P("wide"),
        P("wide"),
        P("wide"),
        P("wide", None),
        P("wide"),
        P("wide", None),
        P("wide"),
        P(),
        P(),
    )
    return jax.shard_map(local, mesh=mesh, in_specs=in_specs, out_specs=out_specs, check_vma=False)
```
